32 devices in a mesh: task: 2 (over x), batch: 16 (over z, y, core).
Axes of the slice: x: 2, y: 2, z: 4, core: 2. Of those that a mesh axis runs over, the one named last changes fastest.
Arguments:
- inputs: bfloat16 [2, 128, 256, 2048], P('task', 'batch')
- crop_cuts: int32 [2, 128, 2], P('task', 'batch'), may hold values from 2 to 13
- threshold: bfloat16 [2, 128, 256, 2048], P('task', 'batch'), may hold values from 0 to 1
- w_reduce: bfloat16 [2048, 512], replicated, may hold values from -0.125 to 0.125
- w_spatial: bfloat16 [9, 512, 512], replicated, may hold values from -0.09375 to 0.09375
- w_expand: bfloat16 [512, 2048], replicated, may hold values from -0.25 to 0.25
- w_heads: bfloat16 [2, 2048, 256], P('task'), may hold values from -0.125 to 0.125
- gain_one: float32 [512], replicated, may hold values from 0.1 to 1.9
- bias_one: float32 [512], replicated, may hold values from -3 to 3
- gain_two: float32 [512], replicated, may hold values from 0.1 to 1.9
- bias_two: float32 [512], replicated, may hold values from -3 to 3
- gain_three: float32 [2048], replicated, may hold values from 0.1 to 1.9
- bias_three: float32 [2048], replicated, may hold values from -3 to 3
- cotangent: bfloat16 [2, 2, 128, 256, 256], P('task', None, 'batch')
Outputs:
- heads: float32 [2, 2, 128, 256, 256], P('task', None, 'batch')
- grad_inputs: bfloat16 [2, 128, 256, 2048], P('task', 'batch')
- grad_reduce: float32 [2048, 512], replicated
- grad_spatial: float32 [9, 512, 512], replicated
- grad_expand: float32 [512, 2048], replicated
- grad_heads: float32 [2, 2048, 256], P('task')
- grad_gain_one: float32 [512], replicated
- grad_bias_one: float32 [512], replicated
- grad_gain_two: float32 [512], replicated
- grad_bias_two: float32 [512], replicated
- grad_gain_three: float32 [2048], replicated
- grad_bias_three: float32 [2048], replicated
The draws below stay inside these ranges and needn't reach their ends.
Inputs may be any that keep to these rules, and one draw needn't show every extreme that they name: `crop_cuts`: each entry is a row cut followed by a column cut of its canvas.
All inputs are finite; a program needn't handle non-finite values.
Results may differ from the reference program's by a relative error of at most 0.014.
Values may be sent and summed in bfloat16 or wider, within the bound.
A program may use at most 384 MiB of HBM per device.

```python
import jax
import jax.numpy as jnp
from jax import lax

D = 2048
M = 512
HO = 256
SIDE = 16
TASKS = 2
HALVES = 2
CANVASES = 128


def draw_inputs(key, part):
    first, second = jax.random.split(key, 2)
    shape = (HALVES, CANVASES, SIDE * SIDE, D)
    channel = jnp.exp(jax.random.uniform(second, (D,), jnp.float32, jnp.log(0.3), jnp.log(3.0)))
    ramp = 0.6 + 1.2 * jnp.arange(CANVASES, dtype=jnp.float32) / max(CANVASES - 1, 1)
    base = jnp.clip(jax.random.normal(first, shape, jnp.float32), -6.0, 6.0)
    return (base * channel * ramp[None, :, None, None]).astype(jnp.bfloat16)


def draw_cotangent(key, part):
    first = jax.random.fold_in(key, 0)
    shape = (TASKS, HALVES, CANVASES, SIDE * SIDE, HO)
    ramp = 0.6 + 1.2 * jnp.arange(CANVASES, dtype=jnp.float32) / max(CANVASES - 1, 1)
    base = jnp.clip(jax.random.normal(first, shape, jnp.float32), -6.0, 6.0)
    return (base * ramp[None, None, :, None, None]).astype(jnp.bfloat16)


def with_ends(values, key, low, largest):
    shape = values.shape
    place = [jax.random.randint(jax.random.fold_in(key, axis), (), 0, shape[axis]) for axis in range(len(shape))]
    values = values.at[tuple(place)].set(low)
    longest = shape.index(max(shape))
    place[longest] = (place[longest] + 1) % shape[longest]
    return values.at[tuple(place)].set(largest)


def shard_levels(own_key, dims, cuts, least, high):
    factor_of = 1.0
    for position, blocks in cuts:
        heights = jax.random.uniform(jax.random.fold_in(jax.random.fold_in(own_key, 6), position), (blocks,), jnp.float32, least / len(cuts), high / len(cuts))
        factor_of = factor_of * jnp.repeat(jnp.exp(heights), dims[position] // blocks).reshape((-1,) + (1,) * (len(dims) - 1 - position))
    return factor_of


def gaussian(own_key, extent, scale, reach, pieces=(), kind=jnp.bfloat16):
    values = jax.random.normal(own_key, extent, jnp.float32) * scale
    if len(pieces) > 0:
        values = shard_levels(own_key, extent, pieces, -0.22, 0.18) * values
    return jnp.clip(values, min=-reach, max=reach).astype(kind)


def setup_inputs(seed: int = 0) -> dict:
    key_of = jax.random.split(jax.random.key(seed), 15)
    return {
        "inputs": draw_inputs(jax.random.fold_in(key_of[14], 71), 0),
        "crop_cuts": with_ends(jax.random.randint(key_of[1], (HALVES, CANVASES, 2), 2, SIDE - 2), jax.random.fold_in(key_of[1], 1), 2, (SIDE - 2) - 1).astype(jnp.int32),
        "threshold": jnp.clip(1.0 * jax.random.uniform(key_of[2], (HALVES, CANVASES, SIDE * SIDE, D), jnp.float32) ** shard_levels(key_of[2], (HALVES, CANVASES, SIDE * SIDE, D), ((0, 2), (1, 16)), -0.2, 0.2), 0.0, 1.0).astype(jnp.bfloat16),
        "w_reduce": gaussian(key_of[3], (D, M), D ** -0.5, 0.125),
        "w_spatial": gaussian(key_of[4], (9, M, M), (9 * M) ** -0.5, 0.09375),
        "w_expand": gaussian(key_of[5], (M, D), M ** -0.5, 0.25),
        "w_heads": gaussian(key_of[6], (TASKS, D, HO), D ** -0.5, 0.125, ((0, 2),)),
        "gain_one": jnp.clip(1.0 + 0.18 * jax.random.normal(key_of[7], (M,), jnp.float32), 0.1, 1.9),
        "bias_one": gaussian(key_of[8], (M,), 0.5, 3.0, (), jnp.float32),
        "gain_two": jnp.clip(1.0 + 0.18 * jax.random.normal(key_of[9], (M,), jnp.float32), 0.1, 1.9),
        "bias_two": gaussian(key_of[10], (M,), 0.5, 3.0, (), jnp.float32),
        "gain_three": jnp.clip(1.0 + 0.18 * jax.random.normal(key_of[11], (D,), jnp.float32), 0.1, 1.9),
        "bias_three": gaussian(key_of[12], (D,), 0.5, 3.0, (), jnp.float32),
        "cotangent": draw_cotangent(jax.random.fold_in(key_of[14], 71), 0),
    }


HIGH = lax.Precision.HIGHEST
OFFSETS = ((-1, -1), (-1, 0), (-1, 1), (0, -1), (0, 0), (0, 1), (1, -1), (1, 0), (1, 1))
EPS = 1e-05
FLOOR = 0.1
SOFT = 0.25

@jax.custom_vjp
def low(v):
    return lax.optimization_barrier(v.astype(jnp.bfloat16)).astype(jnp.float32)

@jax.custom_vjp
def low_back(v):
    return v

def low_keep(v):
    return (low(v), None)

def low_pass(kept, grad):
    return (grad,)

def back_keep(v):
    return (v, None)

def back_low(kept, grad):
    return (low(grad),)
low.defvjp(low_keep, low_pass)
low_back.defvjp(back_keep, back_low)

def smooth(value):
    return jax.nn.gelu(value, approximate=False)

def displace(array, down, right, first, fill):
    widths = [(0, 0)] * array.ndim
    widths[first] = (1, 1)
    widths[first + 1] = (1, 1)
    padded = jnp.pad(array, widths, constant_values=fill)
    rows_here = array.shape[first]
    cols_here = array.shape[first + 1]
    padded = lax.slice_in_dim(padded, 1 + down, 1 + down + rows_here, axis=first)
    return lax.slice_in_dim(padded, 1 + right, 1 + right + cols_here, axis=first + 1)

def tap_valid(cuts, side):
    lines = jnp.arange(side, dtype=jnp.int32)
    upper = (lines[None, :, None] >= cuts[:, 0, None, None]).astype(jnp.int32)
    left = (lines[None, None, :] >= cuts[:, 1, None, None]).astype(jnp.int32)
    ident = upper * 2 + left
    return [ident == displace(ident, down, right, 1, -1) for down, right in OFFSETS]

def spatial(flat, weights, valid, canvases):
    grid = flat.reshape(canvases, SIDE, SIDE, -1)
    total = jnp.zeros((flat.shape[0], weights.shape[2]), jnp.float32)
    for index, (down, right) in enumerate(OFFSETS):
        moved = jnp.where(valid[index][..., None], displace(grid, down, right, 1, 0.0), 0.0)
        total = total + jnp.dot(moved.reshape(flat.shape), weights[index], precision=HIGH)
    return total

def bnorm(hidden, gain, bias):
    centre = lax.optimization_barrier(jnp.mean(hidden, axis=0))
    spread = lax.optimization_barrier(jnp.mean(jnp.square(hidden - centre), axis=0))
    return (hidden - centre) * lax.rsqrt(spread + EPS) * gain + bias

def reference(inputs, crop_cuts, threshold, w_reduce, w_spatial, w_expand, w_heads, gain_one, bias_one, gain_two, bias_two, gain_three, bias_three, cotangent):
    canvases = HALVES * CANVASES
    valid = tap_valid(crop_cuts.reshape(canvases, 2), SIDE)
    flat = inputs.astype(jnp.float32).reshape(-1, D)

    def trunk(source, wone, wtwo, wthree, gone, bone, gtwo, btwo, gthree, bthree):
        hone = low_back(jnp.dot(source, wone, precision=HIGH))
        qone = low(smooth(bnorm(hone, gone, bone)))
        htwo = low_back(spatial(qone, wtwo, valid, canvases))
        qtwo = low(smooth(bnorm(htwo, gtwo, btwo)))
        hthree = low_back(jnp.dot(qtwo, wthree, precision=HIGH))
        return low(smooth(bnorm(hthree, gthree, bthree) + source))
    trunk_out, trunk_back = jax.vjp(trunk, flat, w_reduce.astype(jnp.float32), w_spatial.astype(jnp.float32), w_expand.astype(jnp.float32), gain_one, bias_one, gain_two, bias_two, gain_three, bias_three)

    def head(feature, weight):
        return jnp.dot(low_back(feature), weight, precision=HIGH)
    outputs = []
    grads_trunk = []
    grads_head = []
    for task_id in range(TASKS):
        result, head_back = jax.vjp(head, trunk_out, w_heads[task_id].astype(jnp.float32))
        feature_grad, weight_grad = head_back(cotangent[task_id].astype(jnp.float32).reshape(-1, HO))
        outputs.append(result)
        grads_trunk.append(feature_grad)
        grads_head.append(weight_grad)
    stacked = jnp.stack(grads_trunk)
    limit = threshold.astype(jnp.float32).reshape(-1, D)
    purity = 0.5 * (1.0 + lax.optimization_barrier(jnp.sum(stacked, axis=0)) / jnp.maximum(lax.optimization_barrier(jnp.sum(jnp.abs(stacked), axis=0)), FLOOR))
    keep = jnp.clip((purity - limit) / SOFT + 0.5, 0.0, 1.0)
    merged = lax.optimization_barrier(jnp.sum(jnp.where(stacked > 0, keep * stacked, (1.0 - keep) * stacked), axis=0))
    grads = trunk_back(merged)
    heads = jnp.stack(outputs).reshape(TASKS, HALVES, CANVASES, SIDE * SIDE, HO)
    grad_inputs = grads[0].astype(jnp.bfloat16).reshape(HALVES, CANVASES, SIDE * SIDE, D)
    return (heads, grad_inputs, grads[1], grads[2], grads[3], jnp.stack(grads_head), grads[4], grads[5], grads[6], grads[7], grads[8], grads[9])
```

```python
import functools

import jax
import jax.numpy as jnp
from jax import lax
from jax.experimental import pallas as pl
from jax.experimental.pallas import tpu as pltpu
from jax.sharding import PartitionSpec as P

SIDE = 16
EPS = 1e-05
FLOOR = 0.1
SOFT = 0.25
ROOT_HALF = 0.7071067811865476
DENSITY = 0.3989422804014327
ROWS_ROWS = (((0,), (0,)), ((), ()))
COLS_COLS = (((1,), (1,)), ((), ()))
MESH = pl.DeviceIdType.MESH
LOW = 4


def bulk(value):
    return 0.5 * (1.0 + lax.erf(value * ROOT_HALF))


def slope(value):
    return bulk(value) + value * jnp.exp(-0.5 * value * value) * DENSITY


def centred_join(total, spread, share):
    groups = total.shape[0]
    whole = jnp.sum(total, axis=0)
    means = total / share
    centre = whole / (share * groups)
    return whole, jnp.sum(spread, axis=0) + share * jnp.sum(jnp.square(means - centre), axis=0)


def stats_kernel(rows, forward, tasks, batch, local, out, near, far, middle, near_send, near_recv, far_send, far_recv):
    task = lax.axis_index("task")
    place = lax.axis_index("batch")
    high = place // LOW
    low = lax.rem(place, LOW)
    near_size = tasks * LOW
    far_size = batch // LOW
    me_near = task * LOW + low

    def near_peer(step):
        slot = lax.rem(me_near + step, near_size)
        return slot, (slot // LOW, high * LOW + lax.rem(slot, LOW))

    def far_peer(step):
        slot = lax.rem(high + step, far_size)
        return slot, (task, slot * LOW + low)

    def join(held, count, share):
        half = local.shape[0] // 2
        total = held[:, :half]
        spread = held[:, half:]
        if forward:
            return centred_join(total, spread, share)
        return jnp.sum(total, axis=0), jnp.sum(spread, axis=0)

    barrier = pltpu.get_barrier_semaphore()
    for step in range(1, near_size):
        pl.semaphore_signal(barrier, inc=1, device_id=near_peer(step)[1], device_id_type=MESH)
    for step in range(1, far_size):
        pl.semaphore_signal(barrier, inc=1, device_id=far_peer(step)[1], device_id_type=MESH)
    pl.semaphore_wait(barrier, near_size + far_size - 2)

    def run(size, peer, me, source, held, send, recv):
        copies = []
        for step in range(1, size):
            slot, device = peer(step)
            copy = pltpu.make_async_remote_copy(
                src_ref=source,
                dst_ref=held.at[me],
                send_sem=send.at[step],
                recv_sem=recv.at[me],
                device_id=device,
                device_id_type=MESH,
            )
            copy.start()
            copies.append(copy)
        for step in range(1, size):
            slot, device = peer(step)
            pltpu.make_async_remote_copy(
                src_ref=source,
                dst_ref=held.at[slot],
                send_sem=send.at[step],
                recv_sem=recv.at[slot],
                device_id=device,
                device_id_type=MESH,
            ).wait_recv()
        for copy in copies:
            copy.wait_send()

    half = local.shape[0] // 2
    near[me_near] = local[...]
    run(near_size, near_peer, me_near, local, near, near_send, near_recv)
    total, spread = join(near[...], near_size, float(rows))
    middle[:half] = total
    middle[half:] = spread
    far[high] = middle[...]
    run(far_size, far_peer, high, middle, far, far_send, far_recv)
    total, spread = join(far[...], far_size, float(rows * near_size))
    out[:half] = total
    out[half:] = spread


def reduce_stats(first, second, rows, forward, ident):
    tasks = lax.axis_size("task")
    batch = lax.axis_size("batch")
    width = first.shape[0]
    local = jnp.concatenate([first.reshape(-1, 128), second.reshape(-1, 128)], axis=0)
    shape = local.shape
    near_size = tasks * LOW
    far_size = batch // LOW
    out = pl.pallas_call(
        functools.partial(stats_kernel, rows, forward, tasks, batch),
        out_shape=jax.ShapeDtypeStruct(shape, jnp.float32),
        in_specs=[pl.BlockSpec(memory_space=pltpu.VMEM)],
        out_specs=pl.BlockSpec(memory_space=pltpu.VMEM),
        scratch_shapes=[
            pltpu.VMEM((near_size,) + shape, jnp.float32),
            pltpu.VMEM((far_size,) + shape, jnp.float32),
            pltpu.VMEM(shape, jnp.float32),
            pltpu.SemaphoreType.DMA((near_size,)),
            pltpu.SemaphoreType.DMA((near_size,)),
            pltpu.SemaphoreType.DMA((far_size,)),
            pltpu.SemaphoreType.DMA((far_size,)),
        ],
        compiler_params=pltpu.CompilerParams(collective_id=ident, has_side_effects=True),
        name="stats_%d" % ident,
    )(local)
    half = shape[0] // 2
    return out[:half].reshape(width), out[half:].reshape(width)


def norm_forward(hidden, gain, bias, ident):
    rows = hidden.shape[0]
    count = lax.axis_size("task") * lax.axis_size("batch") * rows
    total = jnp.sum(hidden, axis=0)
    spread = jnp.sum(jnp.square(hidden - total / rows), axis=0)
    total, spread = reduce_stats(total, spread, rows, True, ident)
    centre = total / count
    scale = lax.rsqrt(spread / count + EPS)
    normed = (hidden - centre) * scale
    return normed * gain + bias, normed, scale


def norm_backward(upstream, normed, scale, gain, ident):
    rows = upstream.shape[0]
    count = lax.axis_size("task") * lax.axis_size("batch") * rows
    bias_grad, gain_grad = reduce_stats(
        jnp.sum(upstream, axis=0), jnp.sum(upstream * normed, axis=0), rows, False, ident
    )
    hidden_grad = gain * scale * (upstream - bias_grad / count - normed * gain_grad / count)
    return hidden_grad.astype(jnp.bfloat16), gain_grad, bias_grad


def moved(array, down, right):
    rows, cols = array.shape[1:3]
    padded = jnp.pad(array, ((0, 0), (1, 1), (1, 1), (0, 0)))
    return padded[:, 1 + down : 1 + down + rows, 1 + right : 1 + right + cols]


def body(
    inputs,
    crop_cuts,
    threshold,
    w_reduce,
    w_spatial,
    w_expand,
    w_heads,
    gain_one,
    bias_one,
    gain_two,
    bias_two,
    gain_three,
    bias_three,
    cotangent,
):
    low = jnp.bfloat16
    full = jnp.float32
    canvases, pixels, width = inputs.shape[1:]
    mid = w_reduce.shape[1]
    rows = canvases * pixels
    out_width = w_heads.shape[2]
    task = lax.axis_index("task")
    swap = [(0, 1), (1, 0)]
    cot = cotangent.reshape(2, rows, out_width)
    cot_mine = lax.dynamic_index_in_dim(cot, task, 0, keepdims=False)
    cot_send = lax.dynamic_index_in_dim(cot, 1 - task, 0, keepdims=False)
    cot_peer = lax.ppermute(cot_send, "task", swap)
    heads_mine = w_heads[0]
    heads_peer = lax.ppermute(heads_mine, "task", swap)

    lines = jnp.arange(SIDE, dtype=jnp.int32)
    cuts = crop_cuts.reshape(canvases, 2)
    row_edge = lines[None, :] == cuts[:, 0:1]
    col_edge = lines[None, :] == cuts[:, 1:2]
    from_above = jnp.logical_not(row_edge | (lines == 0)[None, :]).astype(low)
    from_left = jnp.logical_not(col_edge | (lines == 0)[None, :]).astype(low)
    from_below = jnp.pad(from_above[:, 1:], ((0, 0), (0, 1)))
    from_right = jnp.pad(from_left[:, 1:], ((0, 0), (0, 1)))
    by_row = lambda mask: mask[:, :, None, None]
    by_col = lambda mask: mask[:, None, :, None]

    flat_in = inputs.reshape(rows, width)
    h_one = jnp.dot(flat_in, w_reduce, preferred_element_type=full)
    n_one, xh_one, inv_one = norm_forward(h_one, gain_one, bias_one, 0)
    q_one = (n_one * bulk(n_one)).astype(low).reshape(canvases, SIDE, SIDE, mid)
    sides = jnp.concatenate(
        [moved(q_one, 0, -1) * by_col(from_left), q_one, moved(q_one, 0, 1) * by_col(from_right)],
        axis=-1,
    )
    taps = w_spatial.reshape(3, 3 * mid, mid)
    h_two = (
        jnp.dot((moved(sides, -1, 0) * by_row(from_above)).reshape(rows, -1), taps[0], preferred_element_type=full)
        + jnp.dot(sides.reshape(rows, -1), taps[1], preferred_element_type=full)
        + jnp.dot((moved(sides, 1, 0) * by_row(from_below)).reshape(rows, -1), taps[2], preferred_element_type=full)
    )
    n_two, xh_two, inv_two = norm_forward(h_two, gain_two, bias_two, 1)
    q_two = (n_two * bulk(n_two)).astype(low)
    h_three = jnp.dot(q_two, w_expand, preferred_element_type=full)
    n_three, xh_three, inv_three = norm_forward(h_three, gain_three, bias_three, 2)
    before = n_three + flat_in.astype(full)
    trunk = (before * bulk(before)).astype(low)

    out_mine = jnp.dot(trunk, heads_mine, preferred_element_type=full)
    out_sent = jnp.dot(trunk, heads_peer, preferred_element_type=full).astype(low)
    out_peer = lax.ppermute(out_sent, "task", swap).astype(full)
    first = jnp.where(task == 0, out_mine, out_peer)
    second = jnp.where(task == 0, out_peer, out_mine)
    head_out = jnp.stack([first, second]).reshape(1, 2, canvases, pixels, out_width)

    grad_mine = lax.dot_general(trunk, cot_mine, ROWS_ROWS, preferred_element_type=full)
    grad_sent = lax.dot_general(trunk, cot_peer, ROWS_ROWS, preferred_element_type=full)
    grad_other = lax.ppermute(grad_sent.astype(low), "task", swap).astype(full)
    grad_heads = lax.psum((grad_mine + grad_other).astype(low), "batch").astype(full)[None]

    g_mine = lax.dot_general(cot_mine, heads_mine, COLS_COLS, preferred_element_type=full)
    g_peer = lax.dot_general(cot_peer, heads_peer, COLS_COLS, preferred_element_type=full)
    g_mine = g_mine.astype(low).astype(full)
    g_peer = g_peer.astype(low).astype(full)
    both = g_mine + g_peer
    size = jnp.abs(g_mine) + jnp.abs(g_peer)
    purity = 0.5 * (1.0 + both / jnp.maximum(size, FLOOR))
    keep = jnp.clip((purity - threshold.reshape(rows, width).astype(full)) / SOFT + 0.5, 0.0, 1.0)
    merged = 0.5 * (both - size) + keep * size

    flow = merged * slope(before)
    dh_three, dg_three, db_three = norm_backward(flow, xh_three, inv_three, gain_three, 3)
    grad_expand = lax.dot_general(q_two, dh_three, ROWS_ROWS, preferred_element_type=full)
    grad_expand = lax.psum(grad_expand.astype(low), ("task", "batch")).astype(full)
    dq_two = lax.dot_general(dh_three, w_expand, COLS_COLS, preferred_element_type=full)
    dh_two, dg_two, db_two = norm_backward(dq_two * slope(n_two), xh_two, inv_two, gain_two, 4)
    up = dh_two.reshape(canvases, SIDE, SIDE, mid)
    lanes = jnp.concatenate(
        [moved(up * by_row(from_above), 1, 0), up, moved(up * by_row(from_below), -1, 0)], axis=-1
    ).reshape(rows, 3 * mid)
    across = w_spatial.reshape(3, 3, mid, mid)
    pieces = [
        lax.dot_general(
            lanes,
            across[:, b].transpose(1, 0, 2).reshape(mid, 3 * mid),
            COLS_COLS,
            preferred_element_type=full,
        ).reshape(up.shape)
        for b in range(3)
    ]
    dq_one = (
        pieces[1]
        + moved(pieces[0] * by_col(from_left).astype(full), 0, 1)
        + moved(pieces[2] * by_col(from_right).astype(full), 0, -1)
    ).reshape(rows, mid)
    dh_one, dg_one, db_one = norm_backward(dq_one * slope(n_one), xh_one, inv_one, gain_one, 5)
    grad_spatial = lax.dot_general(
        sides.reshape(rows, 3 * mid), lanes, ROWS_ROWS, preferred_element_type=full
    )
    grad_spatial = lax.psum(grad_spatial.astype(low), ("task", "batch"))
    grad_spatial = (
        grad_spatial.reshape(3, mid, 3, mid).transpose(2, 0, 1, 3).reshape(w_spatial.shape).astype(full)
    )
    grad_reduce = lax.dot_general(flat_in, dh_one, ROWS_ROWS, preferred_element_type=full)
    grad_reduce = lax.psum(grad_reduce.astype(low), ("task", "batch")).astype(full)
    grad_inputs = (
        flow + lax.dot_general(dh_one, w_reduce, COLS_COLS, preferred_element_type=full)
    ).astype(low)
    return (
        head_out,
        grad_inputs.reshape(inputs.shape),
        grad_reduce,
        grad_spatial,
        grad_expand,
        grad_heads,
        dg_one,
        db_one,
        dg_two,
        db_two,
        dg_three,
        db_three,
    )


def solution(mesh):
    in_specs = (
        P("task", "batch", None, None),
        P("task", "batch", None),
        P("task", "batch", None, None),
        P(),
        P(),
        P(),
        P("task", None, None),
        P(),
        P(),
        P(),
        P(),
        P(),
        P(),
        P("task", None, "batch", None, None),
    )
    out_specs = (
        P("task", None, "batch", None, None),
        P("task", "batch", None, None),
        P(),
        P(),
        P(),
        P("task", None, None),
        P(),
        P(),
        P(),
        P(),
        P(),
        P(),
    )
    return jax.shard_map(body, mesh=mesh, in_specs=in_specs, out_specs=out_specs, check_vma=False)
```

```python
import functools
import math

import jax
import jax.numpy as jnp
from jax import lax
from jax.experimental import pallas as pl
from jax.experimental.pallas import tpu as pltpu
from jax.sharding import PartitionSpec as P

SIDE = 16
EPS = 1e-05
FLOOR = 0.1
SOFT = 0.25
ROOT_HALF = 0.7071067811865476
DENSITY = 0.3989422804014327
ROWS_ROWS = (((0,), (0,)), ((), ()))
COLS_COLS = (((1,), (1,)), ((), ()))
MESH = pl.DeviceIdType.MESH
LOW = 4


def bulk(value):
    return 0.5 * (1.0 + lax.erf(value * ROOT_HALF))


def slope(value):
    return bulk(value) + value * jnp.exp(-0.5 * value * value) * DENSITY


def centred_join(total, spread, share):
    groups = total.shape[0]
    whole = jnp.sum(total, axis=0)
    means = total / share
    centre = whole / (share * groups)
    return whole, jnp.sum(spread, axis=0) + share * jnp.sum(jnp.square(means - centre), axis=0)


def stats_kernel(rows, forward, tasks, batch, local, out, near, far, middle, near_send, near_recv, far_send, far_recv):
    task = lax.axis_index("task")
    place = lax.axis_index("batch")
    high = place // LOW
    low = lax.rem(place, LOW)
    near_size = tasks * LOW
    far_size = batch // LOW
    me_near = task * LOW + low

    def near_peer(step):
        slot = lax.rem(me_near + step, near_size)
        return slot, (slot // LOW, high * LOW + lax.rem(slot, LOW))

    def far_peer(step):
        slot = lax.rem(high + step, far_size)
        return slot, (task, slot * LOW + low)

    def join(held, count, share):
        half = local.shape[0] // 2
        total = held[:, :half]
        spread = held[:, half:]
        if forward:
            return centred_join(total, spread, share)
        return jnp.sum(total, axis=0), jnp.sum(spread, axis=0)

    barrier = pltpu.get_barrier_semaphore()
    for step in range(1, near_size):
        pl.semaphore_signal(barrier, inc=1, device_id=near_peer(step)[1], device_id_type=MESH)
    for step in range(1, far_size):
        pl.semaphore_signal(barrier, inc=1, device_id=far_peer(step)[1], device_id_type=MESH)
    pl.semaphore_wait(barrier, near_size + far_size - 2)

    def run(size, peer, me, source, held, send, recv):
        copies = []
        for step in range(1, size):
            slot, device = peer(step)
            copy = pltpu.make_async_remote_copy(
                src_ref=source,
                dst_ref=held.at[me],
                send_sem=send.at[step],
                recv_sem=recv.at[me],
                device_id=device,
                device_id_type=MESH,
            )
            copy.start()
            copies.append(copy)
        for step in range(1, size):
            slot, device = peer(step)
            pltpu.make_async_remote_copy(
                src_ref=source,
                dst_ref=held.at[slot],
                send_sem=send.at[step],
                recv_sem=recv.at[slot],
                device_id=device,
                device_id_type=MESH,
            ).wait_recv()
        for copy in copies:
            copy.wait_send()

    half = local.shape[0] // 2
    near[me_near] = local[...]
    run(near_size, near_peer, me_near, local, near, near_send, near_recv)
    total, spread = join(near[...], near_size, float(rows))
    middle[:half] = total
    middle[half:] = spread
    far[high] = middle[...]
    run(far_size, far_peer, high, middle, far, far_send, far_recv)
    total, spread = join(far[...], far_size, float(rows * near_size))
    out[:half] = total
    out[half:] = spread


def reduce_stats(first, second, rows, forward, ident):
    tasks = lax.axis_size("task")
    batch = lax.axis_size("batch")
    width = first.shape[0]
    local = jnp.concatenate([first.reshape(-1, 128), second.reshape(-1, 128)], axis=0)
    shape = local.shape
    near_size = tasks * LOW
    far_size = batch // LOW
    out = pl.pallas_call(
        functools.partial(stats_kernel, rows, forward, tasks, batch),
        out_shape=jax.ShapeDtypeStruct(shape, jnp.float32),
        in_specs=[pl.BlockSpec(memory_space=pltpu.VMEM)],
        out_specs=pl.BlockSpec(memory_space=pltpu.VMEM),
        scratch_shapes=[
            pltpu.VMEM((near_size,) + shape, jnp.float32),
            pltpu.VMEM((far_size,) + shape, jnp.float32),
            pltpu.VMEM(shape, jnp.float32),
            pltpu.SemaphoreType.DMA((near_size,)),
            pltpu.SemaphoreType.DMA((near_size,)),
            pltpu.SemaphoreType.DMA((far_size,)),
            pltpu.SemaphoreType.DMA((far_size,)),
        ],
        compiler_params=pltpu.CompilerParams(collective_id=ident, has_side_effects=True),
        name="stats_%d" % ident,
    )(local)
    half = shape[0] // 2
    return out[:half].reshape(width), out[half:].reshape(width)


class Reduction:
    def __init__(self, grid, work, result, room, send, recv, far_send, far_recv, wide):
        self.grid, self.work, self.result, self.room = grid, work, result, room
        self.send, self.recv, self.far_send, self.far_recv = send, recv, far_send, far_recv
        self.wide = wide
        self.rows, self.cols = work.shape
        sizes = self.sizes(self.rows, self.cols, wide, grid.far)
        self.flat = sizes[3] == sizes[2] and grid.far > 1
        self.copies = {}

    @staticmethod
    def sizes(rows, cols, wide, far):
        if wide:
            core = (rows, cols // 2)
            first = (rows, cols // 8)
            second = (rows, cols // 16)
        else:
            core = (rows // 2, cols)
            first = (rows // 2, cols // 4)
            second = (rows // 4, cols // 4)
        if second[0] % (8 * far):
            return core, first, second, second
        return core, first, second, (second[0] // far, second[1])

    @staticmethod
    def room_shapes(rows, cols, wide, far):
        core, first, second, last = Reduction.sizes(rows, cols, wide, far)
        return [
            pltpu.VMEM(core, jnp.bfloat16),
            pltpu.VMEM((2,) + first, jnp.bfloat16),
            pltpu.VMEM((2,) + second, jnp.bfloat16),
            pltpu.VMEM((2, far) + last, jnp.bfloat16),
            pltpu.SemaphoreType.DMA((10,)),
            pltpu.SemaphoreType.DMA((10,)),
            pltpu.SemaphoreType.DMA((4, far)),
            pltpu.SemaphoreType.DMA((4, far)),
        ]

    def view(self, core, part=None, first=None, second=None, piece=None, done=False):
        grid = self.grid
        sizes = self.sizes(self.rows, self.cols, self.wide, grid.far)
        row = col = 0
        if self.wide:
            col = core * (self.cols // 2)
            shape = sizes[0]
            if part is not None:
                col = col + part * (self.cols // 4) + first * (self.cols // 8)
                shape = sizes[1]
            if second is not None:
                col = col + second * (self.cols // 16)
                shape = sizes[2]
        else:
            row = core * (self.rows // 2)
            shape = sizes[0]
            if part is not None:
                col = part * (self.cols // 2) + first * (self.cols // 4)
                shape = sizes[1]
            if second is not None:
                row = row + second * (self.rows // 4)
                shape = sizes[2]
        if piece is not None and not self.flat:
            row = row + piece * sizes[3][0]
            shape = sizes[3]
        if not isinstance(row, int):
            row = pl.multiple_of(row, shape[0] & -shape[0])
        if not isinstance(col, int):
            col = pl.multiple_of(col, 128)
        ref = self.result if done else self.work
        return ref.at[pl.ds(row, shape[0]), pl.ds(col, shape[1])]

    def swap(self, index, source, target, device):
        copy = pltpu.make_async_remote_copy(
            src_ref=source,
            dst_ref=target,
            send_sem=self.send.at[index],
            recv_sem=self.recv.at[index],
            device_id=device,
            device_id_type=MESH,
        )
        copy.start()
        self.copies[index] = copy

    def settle(self, *indices):
        for index in indices:
            self.copies.pop(index).wait()

    def add(self, target, sources):
        rows = target.shape[0]
        step = math.gcd(rows, 64)

        def one(i, carry):
            span = pl.ds(pl.multiple_of(i * step, step), step)
            total = sources[0][span].astype(jnp.float32)
            for source in sources[1:]:
                total = total + source[span].astype(jnp.float32)
            target[span] = total.astype(jnp.bfloat16)
            return carry

        lax.fori_loop(0, rows // step, one, 0)

    def join(self, mine, received):
        self.add(mine, [mine, received])

    def far_copy(self, part, step, back, inward):
        grid = self.grid
        bits = grid.bits(part)
        slot = lax.rem(grid.high + step, grid.far)
        owner = slot if inward else grid.high
        if back:
            source = self.view(grid.core, part, bits[0], bits[1], grid.high, True)
            target = self.view(grid.core, part, bits[0], bits[1], owner, True)
        else:
            source = self.view(grid.core, part, bits[0], bits[1], slot)
            target = self.room[3].at[part, owner]
        line = 2 * part + (1 if back else 0)
        return pltpu.make_async_remote_copy(
            src_ref=source,
            dst_ref=target,
            send_sem=self.far_send.at[line, step],
            recv_sem=self.far_recv.at[line, owner],
            device_id=(grid.task, slot * LOW + grid.low),
            device_id_type=MESH,
        )

    def far_start(self, back):
        for part in range(2):
            for step in range(1, self.grid.far):
                self.far_copy(part, step, back, False).start()

    def far_settle(self, back):
        for part in range(2):
            for step in range(1, self.grid.far):
                self.far_copy(part, step, back, True).wait_recv()
                self.far_copy(part, step, back, False).wait_send()

    def stage(self, index):
        grid = self.grid
        other = 1 - grid.core
        if index == 0:
            self.swap(0, self.view(other), self.room[0], grid.core_peer)
        elif index == 1:
            self.settle(0)
            self.join(self.view(grid.core), self.room[0])
            for part in range(2):
                bit = grid.bits(part)[0]
                self.swap(1 + part, self.view(grid.core, part, 1 - bit), self.room[1].at[part], grid.peers(part)[0])
        elif index == 2:
            self.settle(1, 2)
            for part in range(2):
                bits = grid.bits(part)
                self.join(self.view(grid.core, part, bits[0]), self.room[1].at[part])
                self.swap(
                    3 + part,
                    self.view(grid.core, part, bits[0], 1 - bits[1]),
                    self.room[2].at[part],
                    grid.peers(part)[1],
                )
        elif index == 3:
            self.settle(3, 4)
            for part in range(2):
                bits = grid.bits(part)
                self.join(self.view(grid.core, part, bits[0], bits[1]), self.room[2].at[part])
            self.far_start(False)
        elif index == 4:
            self.far_settle(False)
            for part in range(2):
                bits = grid.bits(part)
                mine = self.view(grid.core, part, bits[0], bits[1], grid.high)
                self.room[3][part, grid.high] = mine[...]
                self.add(
                    self.view(grid.core, part, bits[0], bits[1], grid.high, True),
                    [self.room[3].at[part, slot] for slot in range(grid.far)],
                )
            if not self.flat:
                self.far_start(True)
        elif index == 5:
            if not self.flat:
                self.far_settle(True)
            for part in range(2):
                bits = grid.bits(part)
                mine = self.view(grid.core, part, bits[0], bits[1], done=True)
                self.swap(5 + part, mine, mine, grid.peers(part)[1])
        elif index == 6:
            self.settle(5, 6)
            for part in range(2):
                mine = self.view(grid.core, part, grid.bits(part)[0], done=True)
                self.swap(7 + part, mine, mine, grid.peers(part)[0])
        elif index == 7:
            self.settle(7, 8)
            mine = self.view(grid.core, done=True)
            self.swap(9, mine, mine, grid.core_peer)
        elif index == 8:
            self.settle(9)


class Grid:
    def __init__(self, batch):
        self.task = lax.axis_index("task")
        place = lax.axis_index("batch")
        self.far = batch // LOW
        self.high = place // LOW
        self.low = lax.rem(place, LOW)
        self.core = lax.rem(place, 2)
        self.y = lax.rem(place // 2, 2)
        base = place - self.low
        self.core_peer = (self.task, base + self.y * 2 + (1 - self.core))
        self.x_peer = (1 - self.task, place)
        self.y_peer = (self.task, base + (1 - self.y) * 2 + self.core)

    def bits(self, part):
        return (self.task, self.y) if part == 0 else (self.y, self.task)

    def peers(self, part):
        return (self.x_peer, self.y_peer) if part == 0 else (self.y_peer, self.x_peer)

    def far_peers(self):
        return [
            (self.task, lax.rem(self.high + step, self.far) * LOW + self.low) for step in range(1, self.far)
        ]

    def meet(self):
        barrier = pltpu.get_barrier_semaphore()
        everyone = [self.core_peer, self.x_peer, self.y_peer] + self.far_peers()
        for device in everyone:
            pl.semaphore_signal(barrier, inc=1, device_id=device, device_id_type=MESH)
        return lambda: pl.semaphore_wait(barrier, len(everyone))


def sum_kernel(shapes, batch, *refs):
    count = len(shapes)
    sources, results = refs[:count], refs[count : 2 * count]
    refs = refs[2 * count :]
    works, refs = refs[:count], refs[count:]
    totals, refs = refs[:count], refs[count:]
    local, refs = refs[0], refs[1:]
    grid = Grid(batch)
    wait = grid.meet()
    chunks = []
    loads = []
    number = 0
    for item, (rows, cols, pieces, wide) in enumerate(shapes):
        width = cols // pieces
        for piece in range(pieces):
            span = pl.ds(piece * width, width)
            load = pltpu.make_async_copy(
                sources[item].at[:, span], works[item].at[:, span], local.at[number]
            )
            load.start()
            store = pltpu.make_async_copy(
                totals[item].at[:, span], results[item].at[:, span], local.at[number]
            )
            loads.append((load, store))
            room = refs[8 * number : 8 * number + 8]
            chunks.append(
                Reduction(grid, works[item].at[:, span], totals[item].at[:, span], room[:4], room[4], room[5], room[6], room[7], wide)
            )
            number += 1
    wait()
    for wave in range(number + 8):
        for stage in range(8, -1, -1):
            chunk = wave - stage
            if 0 <= chunk < number:
                if stage == 0:
                    loads[chunk][0].wait()
                chunks[chunk].stage(stage)
                if stage == 8:
                    loads[chunk][1].start()
    for load, store in loads:
        store.wait()


def sum_all(arrays, pieces, wides, ident):
    batch = lax.axis_size("batch")
    far = batch // LOW
    shapes = [a.shape + (p, w) for a, p, w in zip(arrays, pieces, wides)]
    rooms = []
    for rows, cols, piece, wide in shapes:
        for _ in range(piece):
            rooms += Reduction.room_shapes(rows, cols // piece, wide, far)
    return pl.pallas_call(
        functools.partial(sum_kernel, shapes, batch),
        out_shape=[jax.ShapeDtypeStruct(a.shape, jnp.bfloat16) for a in arrays],
        in_specs=[pl.BlockSpec(memory_space=pl.ANY)] * len(arrays),
        out_specs=[pl.BlockSpec(memory_space=pl.ANY)] * len(arrays),
        scratch_shapes=[pltpu.VMEM(a.shape, jnp.bfloat16) for a in arrays + arrays]
        + [pltpu.SemaphoreType.DMA((sum(pieces),))]
        + rooms,
        compiler_params=pltpu.CompilerParams(
            collective_id=ident, has_side_effects=True, vmem_limit_bytes=56 * 2**20
        ),
        name="sum_all",
    )(*arrays)


def norm_forward(hidden, gain, bias, ident):
    rows = hidden.shape[0]
    count = lax.axis_size("task") * lax.axis_size("batch") * rows
    total = jnp.sum(hidden, axis=0)
    spread = jnp.sum(jnp.square(hidden - total / rows), axis=0)
    total, spread = reduce_stats(total, spread, rows, True, ident)
    centre = total / count
    scale = lax.rsqrt(spread / count + EPS)
    normed = (hidden - centre) * scale
    return normed * gain + bias, normed, scale


def norm_backward(upstream, normed, scale, gain, ident):
    rows = upstream.shape[0]
    count = lax.axis_size("task") * lax.axis_size("batch") * rows
    bias_grad, gain_grad = reduce_stats(
        jnp.sum(upstream, axis=0), jnp.sum(upstream * normed, axis=0), rows, False, ident
    )
    hidden_grad = gain * scale * (upstream - bias_grad / count - normed * gain_grad / count)
    return hidden_grad.astype(jnp.bfloat16), gain_grad, bias_grad


def moved(array, down, right):
    rows, cols = array.shape[1:3]
    padded = jnp.pad(array, ((0, 0), (1, 1), (1, 1), (0, 0)))
    return padded[:, 1 + down : 1 + down + rows, 1 + right : 1 + right + cols]


def body(
    inputs,
    crop_cuts,
    threshold,
    w_reduce,
    w_spatial,
    w_expand,
    w_heads,
    gain_one,
    bias_one,
    gain_two,
    bias_two,
    gain_three,
    bias_three,
    cotangent,
):
    low = jnp.bfloat16
    full = jnp.float32
    canvases, pixels, width = inputs.shape[1:]
    mid = w_reduce.shape[1]
    rows = canvases * pixels
    out_width = w_heads.shape[2]
    task = lax.axis_index("task")
    swap = [(0, 1), (1, 0)]
    lines = jnp.arange(SIDE, dtype=jnp.int32)
    cuts = crop_cuts.reshape(canvases, 2)
    row_edge = lines[None, :] == cuts[:, 0:1]
    col_edge = lines[None, :] == cuts[:, 1:2]
    from_above = jnp.logical_not(row_edge | (lines == 0)[None, :]).astype(low)
    from_left = jnp.logical_not(col_edge | (lines == 0)[None, :]).astype(low)
    from_below = jnp.pad(from_above[:, 1:], ((0, 0), (0, 1)))
    from_right = jnp.pad(from_left[:, 1:], ((0, 0), (0, 1)))
    by_row = lambda mask: mask[:, :, None, None]
    by_col = lambda mask: mask[:, None, :, None]

    flat_in = inputs.reshape(rows, width)
    h_one = jnp.dot(flat_in, w_reduce, preferred_element_type=full)
    n_one, xh_one, inv_one = norm_forward(h_one, gain_one, bias_one, 0)
    cot = cotangent.reshape(2, rows, out_width)
    cot_mine = lax.dynamic_index_in_dim(cot, task, 0, keepdims=False)
    cot_send = lax.dynamic_index_in_dim(cot, 1 - task, 0, keepdims=False)
    cot_send, inv_one = lax.optimization_barrier((cot_send, inv_one))
    cot_peer = lax.ppermute(cot_send, "task", swap)
    q_one = (n_one * bulk(n_one)).astype(low).reshape(canvases, SIDE, SIDE, mid)
    sides = jnp.concatenate(
        [moved(q_one, 0, -1) * by_col(from_left), q_one, moved(q_one, 0, 1) * by_col(from_right)],
        axis=-1,
    )
    taps = w_spatial.reshape(3, 3 * mid, mid)
    h_two = (
        jnp.dot((moved(sides, -1, 0) * by_row(from_above)).reshape(rows, -1), taps[0], preferred_element_type=full)
        + jnp.dot(sides.reshape(rows, -1), taps[1], preferred_element_type=full)
        + jnp.dot((moved(sides, 1, 0) * by_row(from_below)).reshape(rows, -1), taps[2], preferred_element_type=full)
    )
    n_two, xh_two, inv_two = norm_forward(h_two, gain_two, bias_two, 1)
    heads_mine = w_heads[0]
    heads_sent, inv_two = lax.optimization_barrier((heads_mine, inv_two))
    heads_peer = lax.ppermute(heads_sent, "task", swap)
    q_two = (n_two * bulk(n_two)).astype(low)
    h_three = jnp.dot(q_two, w_expand, preferred_element_type=full)
    n_three, xh_three, inv_three = norm_forward(h_three, gain_three, bias_three, 2)
    before = n_three + flat_in.astype(full)
    trunk = (before * bulk(before)).astype(low)

    first_task = task == 0
    cots = [jnp.where(first_task, cot_mine, cot_peer), jnp.where(first_task, cot_peer, cot_mine)]
    tops = [jnp.where(first_task, heads_mine, heads_peer), jnp.where(first_task, heads_peer, heads_mine)]
    cot_both = jnp.concatenate(cots, axis=1)
    out_mine = jnp.dot(trunk, heads_mine, preferred_element_type=full)
    out_sent = jnp.dot(trunk, heads_peer, preferred_element_type=full).astype(low)
    out_peer = lax.ppermute(out_sent, "task", swap).astype(full)
    first = jnp.where(first_task, out_mine, out_peer)
    second = jnp.where(first_task, out_peer, out_mine)
    head_out = jnp.stack([first, second]).reshape(1, 2, canvases, pixels, out_width)
    grad_heads = lax.dot_general(trunk, cot_both, ROWS_ROWS, preferred_element_type=full)

    g_mine = lax.dot_general(cot_mine, heads_mine, COLS_COLS, preferred_element_type=full)
    g_peer = lax.dot_general(cot_peer, heads_peer, COLS_COLS, preferred_element_type=full)
    g_mine = g_mine.astype(low).astype(full)
    g_peer = g_peer.astype(low).astype(full)
    both = g_mine + g_peer
    size = jnp.abs(g_mine) + jnp.abs(g_peer)
    purity = 0.5 * (1.0 + both / jnp.maximum(size, FLOOR))
    keep = jnp.clip((purity - threshold.reshape(rows, width).astype(full)) / SOFT + 0.5, 0.0, 1.0)
    merged = 0.5 * (both - size) + keep * size

    flow = merged * slope(before)
    dh_three, dg_three, db_three = norm_backward(flow, xh_three, inv_three, gain_three, 3)
    grad_expand = lax.dot_general(q_two, dh_three, ROWS_ROWS, preferred_element_type=full)
    dq_two = lax.dot_general(dh_three, w_expand, COLS_COLS, preferred_element_type=full)
    dh_two, dg_two, db_two = norm_backward(dq_two * slope(n_two), xh_two, inv_two, gain_two, 4)
    up = dh_two.reshape(canvases, SIDE, SIDE, mid)
    lanes = jnp.concatenate(
        [moved(up * by_row(from_above), 1, 0), up, moved(up * by_row(from_below), -1, 0)], axis=-1
    ).reshape(rows, 3 * mid)
    across = w_spatial.reshape(3, 3, mid, mid)
    pieces = [
        lax.dot_general(
            lanes,
            across[:, b].transpose(1, 0, 2).reshape(mid, 3 * mid),
            COLS_COLS,
            preferred_element_type=full,
        ).reshape(up.shape)
        for b in range(3)
    ]
    dq_one = (
        pieces[1]
        + moved(pieces[0] * by_col(from_left).astype(full), 0, 1)
        + moved(pieces[2] * by_col(from_right).astype(full), 0, -1)
    ).reshape(rows, mid)
    dh_one, dg_one, db_one = norm_backward(dq_one * slope(n_one), xh_one, inv_one, gain_one, 5)
    grad_spatial = lax.dot_general(
        sides.reshape(rows, 3 * mid), lanes, ROWS_ROWS, preferred_element_type=full
    )
    grad_reduce = lax.dot_general(flat_in, dh_one, ROWS_ROWS, preferred_element_type=full)
    grad_heads, grad_expand, grad_spatial, grad_reduce = sum_all(
        [g.astype(low) for g in (grad_heads, grad_expand, grad_spatial, grad_reduce)],
        [1, 1, 3, 1],
        [False, True, False, False],
        6,
    )
    grad_spatial = (
        grad_spatial.reshape(3, mid, 3, mid).transpose(2, 0, 1, 3).reshape(w_spatial.shape).astype(full)
    )
    grad_heads = lax.dynamic_slice_in_dim(grad_heads, task * out_width, out_width, axis=1).astype(full)[None]
    grad_expand = grad_expand.astype(full)
    grad_reduce = grad_reduce.astype(full)
    grad_inputs = (
        flow + lax.dot_general(dh_one, w_reduce, COLS_COLS, preferred_element_type=full)
    ).astype(low)
    return (
        head_out,
        grad_inputs.reshape(inputs.shape),
        grad_reduce,
        grad_spatial,
        grad_expand,
        grad_heads,
        dg_one,
        db_one,
        dg_two,
        db_two,
        dg_three,
        db_three,
    )


def solution(mesh):
    in_specs = (
        P("task", "batch", None, None),
        P("task", "batch", None),
        P("task", "batch", None, None),
        P(),
        P(),
        P(),
        P("task", None, None),
        P(),
        P(),
        P(),
        P(),
        P(),
        P(),
        P("task", None, "batch", None, None),
    )
    out_specs = (
        P("task", None, "batch", None, None),
        P("task", "batch", None, None),
        P(),
        P(),
        P(),
        P("task", None, None),
        P(),
        P(),
        P(),
        P(),
        P(),
        P(),
    )
    return jax.shard_map(body, mesh=mesh, in_specs=in_specs, out_specs=out_specs, check_vma=False)
```

```python
import functools
import math

import jax
import jax.numpy as jnp
from jax import lax
from jax.experimental import pallas as pl
from jax.experimental.pallas import tpu as pltpu
from jax.sharding import PartitionSpec as P

SIDE = 16
EPS = 1e-05
FLOOR = 0.1
SOFT = 0.25
ROOT_HALF = 0.7071067811865476
DENSITY = 0.3989422804014327
LOG2E = 1.4426950408889634
ERF_P = 0.3275911
ERF_A = (0.254829592, -0.284496736, 1.421413741, -1.453152027, 1.061405429)
ROWS_ROWS = (((0,), (0,)), ((), ()))
COLS_COLS = (((1,), (1,)), ((), ()))
MESH = pl.DeviceIdType.MESH
LOW = 4
VMEM_BYTES = 62 * 2**20


class Reduction:
    def __init__(self, grid, work, result, core, first, second, last, send, recv, far_send, far_recv, wide):
        self.grid, self.work, self.result, self.room = grid, work, result, (core, first, second, last)
        self.send, self.recv, self.far_send, self.far_recv = send, recv, far_send, far_recv
        self.wide = wide
        self.rows, self.cols = work.shape
        sizes = self.sizes(self.rows, self.cols, wide, grid.far)
        self.flat = sizes[3] == sizes[2] and grid.far > 1
        self.copies = {}

    @staticmethod
    def sizes(rows, cols, wide, far):
        if wide:
            core = (rows, cols // 2)
            first = (rows, cols // 8)
            second = (rows, cols // 16)
        else:
            core = (rows // 2, cols)
            first = (rows // 2, cols // 4)
            second = (rows // 4, cols // 4)
        if second[0] % (8 * far):
            return core, first, second, second
        return core, first, second, (second[0] // far, second[1])

    @staticmethod
    def room_shapes(rows, cols, wide, far):
        core, first, second, last = Reduction.sizes(rows, cols, wide, far)
        return [
            pltpu.VMEM(core, jnp.bfloat16),
            pltpu.VMEM((2,) + first, jnp.bfloat16),
            pltpu.VMEM((2,) + second, jnp.bfloat16),
            pltpu.VMEM((2, far) + last, jnp.bfloat16),
            pltpu.SemaphoreType.DMA((10,)),
            pltpu.SemaphoreType.DMA((10,)),
            pltpu.SemaphoreType.DMA((4, far)),
            pltpu.SemaphoreType.DMA((4, far)),
        ]

    def view(self, core, part=None, first=None, second=None, piece=None, done=False):
        grid = self.grid
        sizes = self.sizes(self.rows, self.cols, self.wide, grid.far)
        row = col = 0
        if self.wide:
            col = core * (self.cols // 2)
            shape = sizes[0]
            if part is not None:
                col = col + part * (self.cols // 4) + first * (self.cols // 8)
                shape = sizes[1]
            if second is not None:
                col = col + second * (self.cols // 16)
                shape = sizes[2]
        else:
            row = core * (self.rows // 2)
            shape = sizes[0]
            if part is not None:
                col = part * (self.cols // 2) + first * (self.cols // 4)
                shape = sizes[1]
            if second is not None:
                row = row + second * (self.rows // 4)
                shape = sizes[2]
        if piece is not None and not self.flat:
            row = row + piece * sizes[3][0]
            shape = sizes[3]
        if not isinstance(row, int):
            row = pl.multiple_of(row, shape[0] & -shape[0])
        if not isinstance(col, int):
            col = pl.multiple_of(col, 128)
        ref = self.result if done else self.work
        return ref.at[pl.ds(row, shape[0]), pl.ds(col, shape[1])]

    def swap(self, index, source, target, device):
        copy = pltpu.make_async_remote_copy(
            src_ref=source,
            dst_ref=target,
            send_sem=self.send.at[index],
            recv_sem=self.recv.at[index],
            device_id=device,
            device_id_type=MESH,
        )
        copy.start()
        self.copies[index] = copy

    def settle(self, *indices):
        for index in indices:
            self.copies.pop(index).wait()

    def add(self, target, sources):
        rows = target.shape[0]
        step = math.gcd(rows, 64)

        def one(i, carry):
            span = pl.ds(pl.multiple_of(i * step, step), step)
            total = sources[0][span].astype(jnp.float32)
            for source in sources[1:]:
                total = total + source[span].astype(jnp.float32)
            target[span] = total.astype(jnp.bfloat16)
            return carry

        lax.fori_loop(0, rows // step, one, 0)

    def join(self, mine, received):
        self.add(mine, [mine, received])

    def far_copy(self, part, step, back, inward):
        grid = self.grid
        bits = grid.bits(part)
        slot = lax.rem(grid.high + step, grid.far)
        owner = slot if inward else grid.high
        if back:
            source = self.view(grid.core, part, bits[0], bits[1], grid.high, True)
            target = self.view(grid.core, part, bits[0], bits[1], owner, True)
        else:
            source = self.view(grid.core, part, bits[0], bits[1], slot)
            target = self.room[3].at[part, owner]
        line = 2 * part + (1 if back else 0)
        return pltpu.make_async_remote_copy(
            src_ref=source,
            dst_ref=target,
            send_sem=self.far_send.at[line, step],
            recv_sem=self.far_recv.at[line, owner],
            device_id=(grid.task, slot * LOW + grid.low),
            device_id_type=MESH,
        )

    def far_start(self, back):
        for part in range(2):
            for step in range(1, self.grid.far):
                self.far_copy(part, step, back, False).start()

    def far_settle(self, back):
        for part in range(2):
            for step in range(1, self.grid.far):
                self.far_copy(part, step, back, True).wait_recv()
                self.far_copy(part, step, back, False).wait_send()

    def stage(self, index):
        grid = self.grid
        other = 1 - grid.core
        if index == 0:
            self.swap(0, self.view(other), self.room[0], grid.core_peer)
        elif index == 1:
            self.settle(0)
            self.join(self.view(grid.core), self.room[0])
            for part in range(2):
                bit = grid.bits(part)[0]
                self.swap(1 + part, self.view(grid.core, part, 1 - bit), self.room[1].at[part], grid.peers(part)[0])
        elif index == 2:
            self.settle(1, 2)
            for part in range(2):
                bits = grid.bits(part)
                self.join(self.view(grid.core, part, bits[0]), self.room[1].at[part])
                self.swap(
                    3 + part,
                    self.view(grid.core, part, bits[0], 1 - bits[1]),
                    self.room[2].at[part],
                    grid.peers(part)[1],
                )
        elif index == 3:
            self.settle(3, 4)
            for part in range(2):
                bits = grid.bits(part)
                self.join(self.view(grid.core, part, bits[0], bits[1]), self.room[2].at[part])
            self.far_start(False)
        elif index == 4:
            self.far_settle(False)
            for part in range(2):
                bits = grid.bits(part)
                mine = self.view(grid.core, part, bits[0], bits[1], grid.high)
                self.room[3][part, grid.high] = mine[...]
                self.add(
                    self.view(grid.core, part, bits[0], bits[1], grid.high, True),
                    [self.room[3].at[part, slot] for slot in range(grid.far)],
                )
            if not self.flat:
                self.far_start(True)
        elif index == 5:
            if not self.flat:
                self.far_settle(True)
            for part in range(2):
                bits = grid.bits(part)
                mine = self.view(grid.core, part, bits[0], bits[1], done=True)
                self.swap(5 + part, mine, mine, grid.peers(part)[1])
        elif index == 6:
            self.settle(5, 6)
            for part in range(2):
                mine = self.view(grid.core, part, grid.bits(part)[0], done=True)
                self.swap(7 + part, mine, mine, grid.peers(part)[0])
        elif index == 7:
            self.settle(7, 8)
            mine = self.view(grid.core, done=True)
            self.swap(9, mine, mine, grid.core_peer)
        elif index == 8:
            self.settle(9)


class Grid:
    def __init__(self, batch):
        self.task = lax.axis_index("task")
        place = lax.axis_index("batch")
        self.far = batch // LOW
        self.high = place // LOW
        self.low = lax.rem(place, LOW)
        self.core = lax.rem(place, 2)
        self.y = lax.rem(place // 2, 2)
        base = place - self.low
        self.core_peer = (self.task, base + self.y * 2 + (1 - self.core))
        self.x_peer = (1 - self.task, place)
        self.y_peer = (self.task, base + (1 - self.y) * 2 + self.core)

    def bits(self, part):
        return (self.task, self.y) if part == 0 else (self.y, self.task)

    def peers(self, part):
        return (self.x_peer, self.y_peer) if part == 0 else (self.y_peer, self.x_peer)

    def far_peers(self):
        return [
            (self.task, lax.rem(self.high + step, self.far) * LOW + self.low) for step in range(1, self.far)
        ]

    def meet(self):
        barrier = pltpu.get_barrier_semaphore()
        everyone = [self.core_peer, self.x_peer, self.y_peer] + self.far_peers()
        for device in everyone:
            pl.semaphore_signal(barrier, inc=1, device_id=device, device_id_type=MESH)
        return lambda: pl.semaphore_wait(barrier, len(everyone))


def sum_kernel(shapes, batch, *refs):
    count = len(shapes)
    sources, results = refs[:count], refs[count : 2 * count]
    refs = refs[2 * count :]
    works, refs = refs[:count], refs[count:]
    totals, refs = refs[:count], refs[count:]
    local, refs = refs[0], refs[1:]
    grid = Grid(batch)
    wait = grid.meet()
    chunks = []
    loads = []
    number = 0
    for item, (rows, cols, pieces, wide) in enumerate(shapes):
        height = rows // pieces
        for piece in range(pieces):
            span = pl.ds(piece * height, height)
            load = pltpu.make_async_copy(sources[item].at[span], works[item].at[span], local.at[number])
            load.start()
            store = pltpu.make_async_copy(totals[item].at[span], results[item].at[span], local.at[number])
            loads.append((load, store))
            room = refs[8 * number : 8 * number + 8]
            chunks.append(Reduction(grid, works[item].at[span], totals[item].at[span], *room, wide))
            number += 1
    wait()
    for wave in range(number + 8):
        for stage in range(8, -1, -1):
            chunk = wave - stage
            if 0 <= chunk < number:
                if stage == 0:
                    loads[chunk][0].wait()
                chunks[chunk].stage(stage)
                if stage == 8:
                    loads[chunk][1].start()
    for load, store in loads:
        store.wait()


def sum_all(arrays, pieces, wides, ident):
    batch = lax.axis_size("batch")
    far = batch // LOW
    shapes = [a.shape + (p, w) for a, p, w in zip(arrays, pieces, wides)]
    rooms = []
    for rows, cols, piece, wide in shapes:
        for _ in range(piece):
            rooms += Reduction.room_shapes(rows // piece, cols, wide, far)
    return pl.pallas_call(
        functools.partial(sum_kernel, shapes, batch),
        out_shape=[jax.ShapeDtypeStruct(a.shape, jnp.bfloat16) for a in arrays],
        in_specs=[pl.BlockSpec(memory_space=pl.ANY)] * len(arrays),
        out_specs=[pl.BlockSpec(memory_space=pl.ANY)] * len(arrays),
        scratch_shapes=[pltpu.VMEM(a.shape, jnp.bfloat16) for a in arrays + arrays]
        + [pltpu.SemaphoreType.DMA((sum(pieces),))]
        + rooms,
        compiler_params=pltpu.CompilerParams(
            collective_id=ident, has_side_effects=True, vmem_limit_bytes=VMEM_BYTES
        ),
        name="sum_all",
    )(*arrays)


class Exchange:
    def __init__(self, tasks, batch, near, far, near_send, near_recv, far_send, far_recv):
        place = lax.axis_index("batch")
        self.task = lax.axis_index("task")
        self.high = place // LOW
        self.low = lax.rem(place, LOW)
        self.near_size = tasks * LOW
        self.far_size = batch // LOW
        self.me_near = self.task * LOW + self.low
        self.near, self.far = near, far
        self.near_sems, self.far_sems = (near_send, near_recv), (far_send, far_recv)

    @staticmethod
    def scratch(tasks, batch, width):
        near_size, far_size = tasks * LOW, batch // LOW
        return [
            pltpu.VMEM((near_size + 1, 2, width), jnp.float32),
            pltpu.VMEM((far_size + 1, 2, width), jnp.float32),
            pltpu.SemaphoreType.DMA((near_size,)),
            pltpu.SemaphoreType.DMA((near_size,)),
            pltpu.SemaphoreType.DMA((far_size,)),
            pltpu.SemaphoreType.DMA((far_size,)),
        ]

    def near_peer(self, step):
        slot = lax.rem(self.me_near + step, self.near_size)
        return slot, (slot // LOW, self.high * LOW + lax.rem(slot, LOW))

    def far_peer(self, step):
        slot = lax.rem(self.high + step, self.far_size)
        return slot, (self.task, slot * LOW + self.low)

    def peers(self):
        near = [self.near_peer(step)[1] for step in range(1, self.near_size)]
        return near + [self.far_peer(step)[1] for step in range(1, self.far_size)]

    def greet(self):
        barrier = pltpu.get_barrier_semaphore()
        for device in self.peers():
            pl.semaphore_signal(barrier, inc=1, device_id=device, device_id_type=MESH)

    def met(self):
        pl.semaphore_wait(pltpu.get_barrier_semaphore(), self.near_size + self.far_size - 2)

    def hop(self, size, peer, me, held, sems):
        def copy(step, slot):
            return pltpu.make_async_remote_copy(
                src_ref=held.at[size],
                dst_ref=held.at[slot],
                send_sem=sems[0].at[step],
                recv_sem=sems[1].at[slot],
                device_id=peer(step)[1],
                device_id_type=MESH,
            )

        for step in range(1, size):
            copy(step, me).start()
        held[me] = held[size]
        for step in range(1, size):
            copy(step, peer(step)[0]).wait_recv()
        for step in range(1, size):
            copy(step, me).wait_send()
        return held[:size]

    def run(self, total, spread, rows, forward):
        self.near[self.near_size, 0:1] = total
        self.near[self.near_size, 1:2] = spread
        held = self.hop(self.near_size, self.near_peer, self.me_near, self.near, self.near_sems)
        total, spread = join(held, float(rows), forward)
        self.far[self.far_size, 0:1] = total
        self.far[self.far_size, 1:2] = spread
        held = self.hop(self.far_size, self.far_peer, self.high, self.far, self.far_sems)
        return join(held, float(rows * self.near_size), forward)


def join(held, share, forward):
    sums = held[:, 0, :]
    total = jnp.sum(sums, axis=0, keepdims=True)
    spread = jnp.sum(held[:, 1, :], axis=0, keepdims=True)
    if forward:
        groups = held.shape[0]
        away = sums * (1.0 / share) - total * (1.0 / (share * groups))
        spread = spread + share * jnp.sum(away * away, axis=0, keepdims=True)
    return total, spread


def stats_kernel(rows, forward, tasks, batch, stat_ref, vec_ref, out_ref, *scratch):
    exchange = Exchange(tasks, batch, *scratch)
    exchange.greet()
    count = rows * tasks * batch
    first = jnp.sum(stat_ref[:8], axis=0, keepdims=True)
    second = jnp.sum(stat_ref[8:16], axis=0, keepdims=True)
    exchange.met()
    out_ref[:8] = vec_ref[...]
    if forward:
        local = first + rows * stat_ref[16:17]
        total, spread = exchange.run(local, second - first * first * (1.0 / rows), rows, True)
        scale = lax.rsqrt(spread * (1.0 / count) + EPS)
        out_ref[0:1] = total * (1.0 / count)
        out_ref[1:2] = scale
        out_ref[4:5] = scale * vec_ref[2:3]
    else:
        total, spread = exchange.run(first, second, rows, False)
        out_ref[5:6] = total * (1.0 / count)
        out_ref[6:7] = spread * (1.0 / count)
        out_ref[8:9] = total
        out_ref[9:10] = spread


def reduce_stats(stat, vec, rows, forward, ident):
    tasks = lax.axis_size("task")
    batch = lax.axis_size("batch")
    width = stat.shape[1]
    return pl.pallas_call(
        functools.partial(stats_kernel, rows, forward, tasks, batch),
        out_shape=jax.ShapeDtypeStruct((16, width), jnp.float32),
        in_specs=[pl.BlockSpec(memory_space=pltpu.VMEM)] * 2,
        out_specs=pl.BlockSpec(memory_space=pltpu.VMEM),
        scratch_shapes=Exchange.scratch(tasks, batch, width),
        compiler_params=pltpu.CompilerParams(collective_id=ident, has_side_effects=True),
        name="stats_%d" % ident,
    )(stat, vec[:8])


def tail_and_bell(value):
    bell = jnp.exp2(value * value * (-0.5 * LOG2E))
    away = jnp.abs(value)
    ratio = 1.0 / (1.0 + away * (ERF_P * ROOT_HALF))
    poly = ERF_A[4]
    for factor in ERF_A[3::-1]:
        poly = poly * ratio + factor
    tail = 0.5 * poly * ratio * bell
    return jnp.where(value >= 0, 1.0 - tail, tail), bell


def fold(array):
    total = array[:8]
    for start in range(8, array.shape[0], 8):
        total = total + array[start : start + 8]
    return total


def crown_kernel(
    piece, h_ref, x_ref, thr_ref, cot_ref, cot_peer_ref, top_ref, top_peer_ref, vec_ref,
    out_ref, sent_ref, flow_ref, gradt_ref, stat_ref, z_ref, acc_ref,
):
    step = pl.program_id(0)
    rows, width = x_ref.shape
    half = cot_ref.shape[1]

    @pl.when(step == 0)
    def _():
        stat_ref[...] = jnp.zeros_like(stat_ref)
        acc_ref[...] = jnp.zeros_like(acc_ref)

    for start in range(0, width, piece):
        cols = pl.ds(start, piece)
        g_one = lax.dot_general(
            cot_ref[...], top_ref[cols], COLS_COLS, preferred_element_type=jnp.float32
        ).astype(jnp.bfloat16).astype(jnp.float32)
        g_two = lax.dot_general(
            cot_peer_ref[...], top_peer_ref[cols], COLS_COLS, preferred_element_type=jnp.float32
        ).astype(jnp.bfloat16).astype(jnp.float32)
        total = g_one + g_two
        size = jnp.abs(g_one) + jnp.abs(g_two)
        share = total / jnp.maximum(size, FLOOR)
        limit = thr_ref[:, cols].astype(jnp.float32)
        keep = jnp.clip((0.5 / SOFT) * share + ((0.5 / SOFT + 0.5) - limit * (1.0 / SOFT)), 0.0, 1.0)
        merged = 0.5 * (total - size) + keep * size
        normed = (h_ref[:, cols] - vec_ref[0:1, cols]) * vec_ref[1:2, cols]
        before = normed * vec_ref[2:3, cols] + vec_ref[3:4, cols] + x_ref[:, cols].astype(jnp.float32)
        phi, bell = tail_and_bell(before)
        z_ref[:, cols] = (before * phi).astype(jnp.bfloat16)
        flow = merged * (phi + before * bell * DENSITY)
        flow_ref[:, cols] = flow.astype(flow_ref.dtype)
        stat_ref[:8, cols] += fold(flow)
        stat_ref[8:, cols] += fold(flow * normed)
    out_ref[...] = jnp.dot(z_ref[...], top_ref[...], preferred_element_type=jnp.float32)
    sent_ref[...] = jnp.dot(z_ref[...], top_peer_ref[...], preferred_element_type=jnp.float32).astype(jnp.bfloat16)
    acc_ref[:half] += lax.dot_general(cot_ref[...], z_ref[...], ROWS_ROWS, preferred_element_type=jnp.float32)
    acc_ref[half:] += lax.dot_general(cot_peer_ref[...], z_ref[...], ROWS_ROWS, preferred_element_type=jnp.float32)

    @pl.when(step == pl.num_programs(0) - 1)
    def _():
        task = lax.axis_index("task")
        gradt_ref[pl.ds(task * half, half)] = acc_ref[:half].astype(jnp.bfloat16)
        gradt_ref[pl.ds((1 - task) * half, half)] = acc_ref[half:].astype(jnp.bfloat16)


def wide(mask, width):
    return jnp.concatenate([mask] * (width // mask.shape[1]), axis=1)


def gather_stats(stat_ref, hidden, first):
    @pl.when(first)
    def _():
        stat_ref[:16] = jnp.zeros_like(stat_ref[:16])
        mean = jnp.sum(hidden, axis=0, keepdims=True) / hidden.shape[0]
        stat_ref[16:] = jnp.broadcast_to(mean, stat_ref[16:].shape)

    away = hidden - stat_ref[16:17]
    stat_ref[:8] += fold(away)
    stat_ref[8:16] += fold(away * away)


def normal(hidden, vec_ref):
    return (hidden - vec_ref[0:1]) * vec_ref[1:2]


def squeeze_kernel(x_ref, w_ref, out_ref, stat_ref):
    hidden = jnp.dot(x_ref[...], w_ref[...], preferred_element_type=jnp.float32)
    out_ref[...] = hidden
    gather_stats(stat_ref, hidden, pl.program_id(0) == 0)


def mesh_kernel(h_ref, vec_ref, mask_ref, w_ref, out_ref, side_ref, stat_ref, pad_ref):
    rows, mid = h_ref.shape
    inner = pl.ds(SIDE, rows)
    before = normal(h_ref[...], vec_ref) * vec_ref[2:3] + vec_ref[3:4]
    phi, _ = tail_and_bell(before)
    low = (before * phi).astype(jnp.bfloat16)
    kept = low.astype(jnp.float32)
    left = wide(mask_ref[:, :128].astype(jnp.float32), mid)
    right = wide(mask_ref[:, 128:256].astype(jnp.float32), mid)

    @pl.when(pl.program_id(0) == 0)
    def _():
        pad_ref[:SIDE] = jnp.zeros_like(pad_ref[:SIDE])
        pad_ref[SIDE + rows :] = jnp.zeros_like(pad_ref[:SIDE])

    pad_ref[inner, :mid] = (pltpu.roll(kept, 1, 0) * left).astype(jnp.bfloat16)
    pad_ref[inner, mid : 2 * mid] = low
    pad_ref[inner, 2 * mid :] = (pltpu.roll(kept, rows - 1, 0) * right).astype(jnp.bfloat16)
    side_ref[...] = pad_ref[inner]
    above = wide(mask_ref[:, 256:384], 3 * mid)
    below = wide(mask_ref[:, 384:], 3 * mid)
    hidden = jnp.dot(pad_ref[inner], w_ref[3 * mid : 6 * mid], preferred_element_type=jnp.float32)
    hidden += jnp.dot(pad_ref[:rows] * above, w_ref[: 3 * mid], preferred_element_type=jnp.float32)
    hidden += jnp.dot(pad_ref[2 * SIDE :] * below, w_ref[6 * mid :], preferred_element_type=jnp.float32)
    out_ref[...] = hidden
    gather_stats(stat_ref, hidden, pl.program_id(0) == 0)


def widen_kernel(h_ref, vec_ref, w_ref, out_ref, low_ref, stat_ref):
    before = normal(h_ref[...], vec_ref) * vec_ref[2:3] + vec_ref[3:4]
    phi, _ = tail_and_bell(before)
    low = (before * phi).astype(jnp.bfloat16)
    low_ref[...] = low
    hidden = jnp.dot(low, w_ref[...], preferred_element_type=jnp.float32)
    out_ref[...] = hidden
    gather_stats(stat_ref, hidden, pl.program_id(0) == 0)


def norm_grad(upstream, normed, vec_ref):
    return vec_ref[4:5] * (upstream - vec_ref[5:6] - normed * vec_ref[6:7])


def act_slope(value):
    phi, bell = tail_and_bell(value)
    return phi + value * bell * DENSITY


def gather_flow(stat_ref, flow, normed, first):
    @pl.when(first)
    def _():
        stat_ref[...] = jnp.zeros_like(stat_ref)

    stat_ref[:8] += fold(flow)
    stat_ref[8:16] += fold(flow * normed)


def narrow_kernel(flow_ref, h_ref, vec_ref, two_ref, vectwo_ref, low_ref, w_ref, out_ref, grad_ref, stat_ref, acc_ref):
    first = pl.program_id(0) == 0
    dh = norm_grad(flow_ref[...].astype(jnp.float32), normal(h_ref[...], vec_ref), vec_ref).astype(jnp.bfloat16)
    dq = lax.dot_general(dh, w_ref[...], COLS_COLS, preferred_element_type=jnp.float32)
    normed = normal(two_ref[...], vectwo_ref)
    flow = dq * act_slope(normed * vectwo_ref[2:3] + vectwo_ref[3:4])
    out_ref[...] = flow
    gather_flow(stat_ref, flow, normed, first)
    part = lax.dot_general(low_ref[...], dh, ROWS_ROWS, preferred_element_type=jnp.float32)
    accumulate(acc_ref, grad_ref, part)


def accumulate(acc_ref, grad_ref, part):
    step = pl.program_id(0)
    last = pl.num_programs(0) - 1

    @pl.when(step == 0)
    def _():
        acc_ref[...] = part

    @pl.when((step > 0) & (step < last))
    def _():
        acc_ref[...] += part

    @pl.when(step == last)
    def _():
        grad_ref[...] = (acc_ref[...] + part).astype(jnp.bfloat16)


def unmesh_kernel(flow_ref, two_ref, vec_ref, one_ref, vecone_ref, side_ref, mask_ref, w_ref, out_ref, grad_ref, stat_ref, lane_ref, acc_ref):
    step = pl.program_id(0)
    last = pl.num_programs(0) - 1
    rows, mid = flow_ref.shape
    dh = norm_grad(flow_ref[...], normal(two_ref[...], vec_ref), vec_ref)
    above = wide(mask_ref[:, 256:384].astype(jnp.float32), mid)
    below = wide(mask_ref[:, 384:].astype(jnp.float32), mid)

    @pl.when(step == 0)
    def _():
        lane_ref[rows - SIDE :, :mid] = jnp.zeros((SIDE, mid), jnp.bfloat16)
        lane_ref[:SIDE, 2 * mid :] = jnp.zeros((SIDE, mid), jnp.bfloat16)

    lane_ref[: rows - SIDE, :mid] = (dh * above)[SIDE:].astype(jnp.bfloat16)
    lane_ref[:, mid : 2 * mid] = dh.astype(jnp.bfloat16)
    lane_ref[SIDE:, 2 * mid :] = (dh * below)[: rows - SIDE].astype(jnp.bfloat16)
    pieces = []
    for b in range(3):
        total = None
        for a in range(3):
            part = lax.dot_general(
                lane_ref[:, a * mid : (a + 1) * mid], w_ref[3 * a + b], COLS_COLS, preferred_element_type=jnp.float32
            )
            total = part if total is None else total + part
        pieces.append(total)
    left = wide(mask_ref[:, :128].astype(jnp.float32), mid)
    right = wide(mask_ref[:, 128:256].astype(jnp.float32), mid)
    dq = pieces[1] + pltpu.roll(pieces[0] * left, rows - 1, 0) + pltpu.roll(pieces[2] * right, 1, 0)
    normed = normal(one_ref[...], vecone_ref)
    flow = dq * act_slope(normed * vecone_ref[2:3] + vecone_ref[3:4])
    out_ref[...] = flow
    gather_flow(stat_ref, flow, normed, step == 0)
    for a in range(3):
        part = lax.dot_general(
            side_ref[...], lane_ref[:, a * mid : (a + 1) * mid], ROWS_ROWS, preferred_element_type=jnp.float32
        )
        span = pl.ds(a * 3 * mid, 3 * mid)
        accumulate(acc_ref.at[span], grad_ref.at[span], part)


def finish_kernel(flow_ref, one_ref, vec_ref, up_ref, x_ref, w_ref, out_ref, grad_ref, acc_ref):
    dh = norm_grad(flow_ref[...], normal(one_ref[...], vec_ref), vec_ref).astype(jnp.bfloat16)
    back = lax.dot_general(dh, w_ref[...], COLS_COLS, preferred_element_type=jnp.float32)
    out_ref[...] = (up_ref[...].astype(jnp.float32) + back).astype(jnp.bfloat16)
    accumulate(acc_ref, grad_ref, lax.dot_general(dh, x_ref[...], ROWS_ROWS, preferred_element_type=jnp.float32))


def tiled(kernel, tile, rows, moving, fixed, outs, stats, scratch, name):
    def block(array):
        return pl.BlockSpec((tile,) + array.shape[1:], lambda i: (i,) + (0,) * (len(array.shape) - 1))

    def whole(array):
        zeros = (0,) * len(array.shape)
        return pl.BlockSpec(array.shape, lambda i: zeros)

    return pl.pallas_call(
        kernel,
        grid=(rows // tile,),
        out_shape=outs + stats,
        in_specs=[block(a) if m else whole(a) for a, m in zip(moving, fixed)],
        out_specs=[block(a) for a in outs] + [whole(a) for a in stats],
        scratch_shapes=scratch,
        compiler_params=pltpu.CompilerParams(vmem_limit_bytes=VMEM_BYTES),
        name=name,
    )(*moving)


def shape32(*shape):
    return jax.ShapeDtypeStruct(shape, jnp.float32)


def shape16(*shape):
    return jax.ShapeDtypeStruct(shape, jnp.bfloat16)


def squeeze(flat_in, w_reduce, tile):
    rows, mid = flat_in.shape[0], w_reduce.shape[1]
    return tiled(squeeze_kernel, tile, rows, [flat_in, w_reduce], [1, 0], [shape32(rows, mid)], [shape32(24, mid)], [], "squeeze")


def mesh_forward(h_one, vec, masks, taps, tile):
    rows, mid = h_one.shape
    return tiled(
        mesh_kernel, tile, rows, [h_one, vec, masks, taps], [1, 0, 1, 0],
        [shape32(rows, mid), shape16(rows, 3 * mid)], [shape32(24, mid)],
        [pltpu.VMEM((tile + 2 * SIDE, 3 * mid), jnp.bfloat16)], "mesh_forward",
    )


def widen(h_two, vec, w_expand, tile):
    rows, mid = h_two.shape
    width = w_expand.shape[1]
    return tiled(
        widen_kernel, tile, rows, [h_two, vec, w_expand], [1, 0, 0],
        [shape32(rows, width), shape16(rows, mid)], [shape32(24, width)], [], "widen",
    )


def narrow(flow, h_three, vec_three, h_two, vec_two, q_two, w_expand, tile):
    rows, mid = h_two.shape
    width = w_expand.shape[1]
    return tiled(
        narrow_kernel, tile, rows, [flow, h_three, vec_three, h_two, vec_two, q_two, w_expand], [1, 1, 0, 1, 0, 1, 0],
        [shape32(rows, mid)], [shape16(mid, width), shape32(16, mid)], [pltpu.VMEM((mid, width), jnp.float32)], "narrow",
    )


def mesh_backward(flow, h_two, vec_two, h_one, vec_one, sides, masks, w_spatial, tile):
    rows, mid = h_two.shape
    return tiled(
        unmesh_kernel, tile, rows, [flow, h_two, vec_two, h_one, vec_one, sides, masks, w_spatial], [1, 1, 0, 1, 0, 1, 1, 0],
        [shape32(rows, mid)], [shape16(9 * mid, mid), shape32(16, mid)],
        [pltpu.VMEM((tile, 3 * mid), jnp.bfloat16), pltpu.VMEM((9 * mid, mid), jnp.float32)], "mesh_backward",
    )


def finish(flow, h_one, vec_one, up, flat_in, w_reduce, tile):
    rows, mid = h_one.shape
    width = flat_in.shape[1]
    return tiled(
        finish_kernel, tile, rows, [flow, h_one, vec_one, up, flat_in, w_reduce], [1, 1, 0, 1, 1, 0],
        [shape16(rows, width)], [shape16(mid, width)], [pltpu.VMEM((mid, width), jnp.float32)], "finish",
    )


def crown(h_three, flat_in, limits, cot, cot_peer, top, top_peer, vec, tile, piece):
    rows, width = flat_in.shape
    half = cot.shape[1]
    return tiled(
        functools.partial(crown_kernel, piece), tile, rows,
        [h_three, flat_in, limits, cot, cot_peer, top, top_peer, vec], [1, 1, 1, 1, 1, 0, 0, 0],
        [shape32(rows, half), shape16(rows, half), shape16(rows, width)],
        [shape16(2 * half, width), shape32(16, width)],
        [pltpu.VMEM((tile, width), jnp.bfloat16), pltpu.VMEM((2 * half, width), jnp.float32)],
        "crown",
    )


def body(
    inputs,
    crop_cuts,
    threshold,
    w_reduce,
    w_spatial,
    w_expand,
    w_heads,
    gain_one,
    bias_one,
    gain_two,
    bias_two,
    gain_three,
    bias_three,
    cotangent,
):
    low = jnp.bfloat16
    full = jnp.float32
    canvases, pixels, width = inputs.shape[1:]
    mid = w_reduce.shape[1]
    rows = canvases * pixels
    half = w_heads.shape[2]
    task = lax.axis_index("task")
    swap = [(0, 1), (1, 0)]
    cot = cotangent.reshape(2, rows, half)
    cot_mine = lax.dynamic_index_in_dim(cot, task, 0, keepdims=False)
    cot_sent = lax.dynamic_index_in_dim(cot, 1 - task, 0, keepdims=False)
    top_mine = w_heads[0]

    def params(gain, bias):
        zero = jnp.zeros_like(gain)
        return jnp.stack([zero, zero, gain, bias, zero, zero, zero, zero])

    lines = jnp.arange(SIDE, dtype=jnp.int32)
    cuts = crop_cuts.reshape(canvases, 2)
    from_above = jnp.logical_not((lines == cuts[:, 0:1]) | (lines == 0)[None, :])
    from_left = jnp.logical_not((lines == cuts[:, 1:2]) | (lines == 0)[None, :])
    from_below = jnp.pad(from_above[:, 1:], ((0, 0), (0, 1)))
    from_right = jnp.pad(from_left[:, 1:], ((0, 0), (0, 1)))
    shape = (canvases, SIDE, SIDE, 128)
    masks = jnp.concatenate(
        [jnp.broadcast_to(m[:, None, :, None], shape) for m in (from_left, from_right)]
        + [jnp.broadcast_to(m[:, :, None, None], shape) for m in (from_above, from_below)],
        axis=3,
    ).astype(low).reshape(rows, 512)

    flat_in = inputs.reshape(rows, width)
    h_one, stat = squeeze(flat_in, w_reduce, min(rows, 512))
    vec_one = reduce_stats(stat, params(gain_one, bias_one), rows, True, 0)
    cot_sent, vec_one = lax.optimization_barrier((cot_sent, vec_one))
    cot_peer = lax.ppermute(cot_sent, "task", swap)
    h_two, sides, stat = mesh_forward(h_one, vec_one, masks, w_spatial.reshape(9 * mid, mid), pixels)
    vec_two = reduce_stats(stat, params(gain_two, bias_two), rows, True, 1)
    top_sent, vec_two = lax.optimization_barrier((top_mine, vec_two))
    top_peer = lax.ppermute(top_sent, "task", swap)
    h_three, q_two, stat = widen(h_two, vec_two, w_expand, pixels)
    vec_three = reduce_stats(stat, params(gain_three, bias_three), rows, True, 2)
    out_mine, out_sent, flow, grad_heads, stat = crown(
        h_three, flat_in, threshold.reshape(rows, width), cot_mine, cot_peer, top_mine, top_peer, vec_three, pixels, 256
    )
    out_peer = lax.ppermute(out_sent, "task", swap).astype(full)
    first = jnp.where(task == 0, out_mine, out_peer)
    second = jnp.where(task == 0, out_peer, out_mine)
    head_out = jnp.stack([first, second]).reshape(1, 2, canvases, pixels, half)
    vec_three = reduce_stats(stat, vec_three, rows, False, 3)
    flow_two, grad_expand, stat = narrow(flow, h_three, vec_three, h_two, vec_two, q_two, w_expand, min(rows, 512))
    vec_two = reduce_stats(stat, vec_two, rows, False, 4)
    flow_one, grad_spatial, stat = mesh_backward(
        flow_two, h_two, vec_two, h_one, vec_one, sides, masks, w_spatial, min(rows, 512)
    )
    vec_one = reduce_stats(stat, vec_one, rows, False, 5)
    grad_inputs, grad_reduce = finish(flow_one, h_one, vec_one, flow, flat_in, w_reduce, min(rows, 512))
    grad_heads, grad_expand, grad_spatial, grad_reduce = sum_all(
        [grad_heads, grad_expand, grad_spatial, grad_reduce], [1, 1, 3, 1], [True, True, False, True], 6
    )
    grad_heads = lax.dynamic_slice_in_dim(grad_heads, task * half, half, axis=0)
    return (
        head_out,
        grad_inputs.reshape(inputs.shape),
        grad_reduce.T.astype(full),
        grad_spatial.reshape(w_spatial.shape).astype(full),
        grad_expand.astype(full),
        grad_heads.T.astype(full)[None],
        vec_one[9],
        vec_one[8],
        vec_two[9],
        vec_two[8],
        vec_three[9],
        vec_three[8],
    )


def solution(mesh):
    in_specs = (
        P("task", "batch", None, None),
        P("task", "batch", None),
        P("task", "batch", None, None),
        P(),
        P(),
        P(),
        P("task", None, None),
        P(),
        P(),
        P(),
        P(),
        P(),
        P(),
        P("task", None, "batch", None, None),
    )
    out_specs = (
        P("task", None, "batch", None, None),
        P("task", "batch", None, None),
        P(),
        P(),
        P(),
        P("task", None, None),
        P(),
        P(),
        P(),
        P(),
        P(),
        P(),
    )
    return jax.shard_map(body, mesh=mesh, in_specs=in_specs, out_specs=out_specs, check_vma=False)
```

```python
import functools
import math

import jax
import jax.numpy as jnp
from jax import lax
from jax.experimental import pallas as pl
from jax.experimental.pallas import tpu as pltpu
from jax.sharding import PartitionSpec as P

SIDE = 16
EPS = 1e-05
FLOOR = 0.1
SOFT = 0.25
ROOT_HALF = 0.7071067811865476
DENSITY = 0.3989422804014327
LOG2E = 1.4426950408889634
ERF_P = 0.3275911
ERF_A = (0.254829592, -0.284496736, 1.421413741, -1.453152027, 1.061405429)
ROWS_ROWS = (((0,), (0,)), ((), ()))
COLS_COLS = (((1,), (1,)), ((), ()))
MESH = pl.DeviceIdType.MESH
LOW = 4
VMEM_BYTES = 62 * 2**20


class Reduction:
    def __init__(self, grid, work, result, core, first, second, last, send, recv, far_send, far_recv, wide):
        self.grid, self.work, self.result, self.room = grid, work, result, (core, first, second, last)
        self.send, self.recv, self.far_send, self.far_recv = send, recv, far_send, far_recv
        self.wide = wide
        self.rows, self.cols = work.shape
        sizes = self.sizes(self.rows, self.cols, wide, grid.far)
        self.flat = sizes[3] == sizes[2] and grid.far > 1
        self.copies = {}

    @staticmethod
    def sizes(rows, cols, wide, far):
        if wide:
            core = (rows, cols // 2)
            first = (rows, cols // 8)
            second = (rows, cols // 16)
        else:
            core = (rows // 2, cols)
            first = (rows // 2, cols // 4)
            second = (rows // 4, cols // 4)
        if second[0] % (8 * far):
            return core, first, second, second
        return core, first, second, (second[0] // far, second[1])

    @staticmethod
    def room_shapes(rows, cols, wide, far):
        core, first, second, last = Reduction.sizes(rows, cols, wide, far)
        return [
            pltpu.VMEM(core, jnp.bfloat16),
            pltpu.VMEM((2,) + first, jnp.bfloat16),
            pltpu.VMEM((2,) + second, jnp.bfloat16),
            pltpu.VMEM((2, far) + last, jnp.bfloat16),
            pltpu.SemaphoreType.DMA((10,)),
            pltpu.SemaphoreType.DMA((10,)),
            pltpu.SemaphoreType.DMA((4, far)),
            pltpu.SemaphoreType.DMA((4, far)),
        ]

    def view(self, core, part=None, first=None, second=None, piece=None, done=False):
        grid = self.grid
        sizes = self.sizes(self.rows, self.cols, self.wide, grid.far)
        row = col = 0
        if self.wide:
            col = core * (self.cols // 2)
            shape = sizes[0]
            if part is not None:
                col = col + part * (self.cols // 4) + first * (self.cols // 8)
                shape = sizes[1]
            if second is not None:
                col = col + second * (self.cols // 16)
                shape = sizes[2]
        else:
            row = core * (self.rows // 2)
            shape = sizes[0]
            if part is not None:
                col = part * (self.cols // 2) + first * (self.cols // 4)
                shape = sizes[1]
            if second is not None:
                row = row + second * (self.rows // 4)
                shape = sizes[2]
        if piece is not None and not self.flat:
            row = row + piece * sizes[3][0]
            shape = sizes[3]
        if not isinstance(row, int):
            row = pl.multiple_of(row, shape[0] & -shape[0])
        if not isinstance(col, int):
            col = pl.multiple_of(col, 128)
        ref = self.result if done else self.work
        return ref.at[pl.ds(row, shape[0]), pl.ds(col, shape[1])]

    def swap(self, index, source, target, device):
        copy = pltpu.make_async_remote_copy(
            src_ref=source,
            dst_ref=target,
            send_sem=self.send.at[index],
            recv_sem=self.recv.at[index],
            device_id=device,
            device_id_type=MESH,
        )
        copy.start()
        self.copies[index] = copy

    def settle(self, *indices):
        for index in indices:
            self.copies.pop(index).wait()

    def add(self, target, sources):
        rows = target.shape[0]
        step = math.gcd(rows, 64)

        def one(i, carry):
            span = pl.ds(pl.multiple_of(i * step, step), step)
            total = sources[0][span].astype(jnp.float32)
            for source in sources[1:]:
                total = total + source[span].astype(jnp.float32)
            target[span] = total.astype(jnp.bfloat16)
            return carry

        lax.fori_loop(0, rows // step, one, 0)

    def join(self, mine, received):
        self.add(mine, [mine, received])

    def far_copy(self, part, step, back, inward):
        grid = self.grid
        bits = grid.bits(part)
        slot = lax.rem(grid.high + step, grid.far)
        owner = slot if inward else grid.high
        if back:
            source = self.view(grid.core, part, bits[0], bits[1], grid.high, True)
            target = self.view(grid.core, part, bits[0], bits[1], owner, True)
        else:
            source = self.view(grid.core, part, bits[0], bits[1], slot)
            target = self.room[3].at[part, owner]
        line = 2 * part + (1 if back else 0)
        return pltpu.make_async_remote_copy(
            src_ref=source,
            dst_ref=target,
            send_sem=self.far_send.at[line, step],
            recv_sem=self.far_recv.at[line, owner],
            device_id=(grid.task, slot * LOW + grid.low),
            device_id_type=MESH,
        )

    def far_start(self, back):
        for part in range(2):
            for step in range(1, self.grid.far):
                self.far_copy(part, step, back, False).start()

    def far_settle(self, back):
        for part in range(2):
            for step in range(1, self.grid.far):
                self.far_copy(part, step, back, True).wait_recv()
                self.far_copy(part, step, back, False).wait_send()

    def stage(self, index):
        grid = self.grid
        other = 1 - grid.core
        if index == 0:
            self.swap(0, self.view(other), self.room[0], grid.core_peer)
        elif index == 1:
            self.settle(0)
            self.join(self.view(grid.core), self.room[0])
            for part in range(2):
                bit = grid.bits(part)[0]
                self.swap(1 + part, self.view(grid.core, part, 1 - bit), self.room[1].at[part], grid.peers(part)[0])
        elif index == 2:
            self.settle(1, 2)
            for part in range(2):
                bits = grid.bits(part)
                self.join(self.view(grid.core, part, bits[0]), self.room[1].at[part])
                self.swap(
                    3 + part,
                    self.view(grid.core, part, bits[0], 1 - bits[1]),
                    self.room[2].at[part],
                    grid.peers(part)[1],
                )
        elif index == 3:
            self.settle(3, 4)
            for part in range(2):
                bits = grid.bits(part)
                self.join(self.view(grid.core, part, bits[0], bits[1]), self.room[2].at[part])
            self.far_start(False)
        elif index == 4:
            self.far_settle(False)
            for part in range(2):
                bits = grid.bits(part)
                mine = self.view(grid.core, part, bits[0], bits[1], grid.high)
                self.room[3][part, grid.high] = mine[...]
                self.add(
                    self.view(grid.core, part, bits[0], bits[1], grid.high, True),
                    [self.room[3].at[part, slot] for slot in range(grid.far)],
                )
            if not self.flat:
                self.far_start(True)
        elif index == 5:
            if not self.flat:
                self.far_settle(True)
            for part in range(2):
                bits = grid.bits(part)
                mine = self.view(grid.core, part, bits[0], bits[1], done=True)
                self.swap(5 + part, mine, mine, grid.peers(part)[1])
        elif index == 6:
            self.settle(5, 6)
            for part in range(2):
                mine = self.view(grid.core, part, grid.bits(part)[0], done=True)
                self.swap(7 + part, mine, mine, grid.peers(part)[0])
        elif index == 7:
            self.settle(7, 8)
            mine = self.view(grid.core, done=True)
            self.swap(9, mine, mine, grid.core_peer)
        elif index == 8:
            self.settle(9)


class Grid:
    def __init__(self, batch):
        self.task = lax.axis_index("task")
        place = lax.axis_index("batch")
        self.far = batch // LOW
        self.high = place // LOW
        self.low = lax.rem(place, LOW)
        self.core = lax.rem(place, 2)
        self.y = lax.rem(place // 2, 2)
        base = place - self.low
        self.core_peer = (self.task, base + self.y * 2 + (1 - self.core))
        self.x_peer = (1 - self.task, place)
        self.y_peer = (self.task, base + (1 - self.y) * 2 + self.core)

    def bits(self, part):
        return (self.task, self.y) if part == 0 else (self.y, self.task)

    def peers(self, part):
        return (self.x_peer, self.y_peer) if part == 0 else (self.y_peer, self.x_peer)

    def far_peers(self):
        return [
            (self.task, lax.rem(self.high + step, self.far) * LOW + self.low) for step in range(1, self.far)
        ]

    def meet(self):
        barrier = pltpu.get_barrier_semaphore()
        everyone = [self.core_peer, self.x_peer, self.y_peer] + self.far_peers()
        for device in everyone:
            pl.semaphore_signal(barrier, inc=1, device_id=device, device_id_type=MESH)
        return lambda: pl.semaphore_wait(barrier, len(everyone))


def sum_kernel(shapes, batch, *refs):
    count = len(shapes)
    sources, results = refs[:count], refs[count : 2 * count]
    refs = refs[2 * count :]
    works, refs = refs[:count], refs[count:]
    totals, refs = refs[:count], refs[count:]
    local, refs = refs[0], refs[1:]
    grid = Grid(batch)
    wait = grid.meet()
    chunks = []
    loads = []
    number = 0
    for item, (rows, cols, pieces, wide) in enumerate(shapes):
        height = rows // pieces
        for piece in range(pieces):
            span = pl.ds(piece * height, height)
            load = pltpu.make_async_copy(sources[item].at[span], works[item].at[span], local.at[number])
            load.start()
            store = pltpu.make_async_copy(totals[item].at[span], results[item].at[span], local.at[number])
            loads.append((load, store))
            room = refs[8 * number : 8 * number + 8]
            chunks.append(Reduction(grid, works[item].at[span], totals[item].at[span], *room, wide))
            number += 1
    wait()
    for wave in range(number + 8):
        for stage in range(8, -1, -1):
            chunk = wave - stage
            if 0 <= chunk < number:
                if stage == 0:
                    loads[chunk][0].wait()
                chunks[chunk].stage(stage)
                if stage == 8:
                    loads[chunk][1].start()
    for load, store in loads:
        store.wait()


def sum_all(arrays, pieces, wides, ident):
    batch = lax.axis_size("batch")
    far = batch // LOW
    shapes = [a.shape + (p, w) for a, p, w in zip(arrays, pieces, wides)]
    rooms = []
    for rows, cols, piece, wide in shapes:
        for _ in range(piece):
            rooms += Reduction.room_shapes(rows // piece, cols, wide, far)
    return pl.pallas_call(
        functools.partial(sum_kernel, shapes, batch),
        out_shape=[jax.ShapeDtypeStruct(a.shape, jnp.bfloat16) for a in arrays],
        in_specs=[pl.BlockSpec(memory_space=pl.ANY)] * len(arrays),
        out_specs=[pl.BlockSpec(memory_space=pl.ANY)] * len(arrays),
        scratch_shapes=[pltpu.VMEM(a.shape, jnp.bfloat16) for a in arrays + arrays]
        + [pltpu.SemaphoreType.DMA((sum(pieces),))]
        + rooms,
        compiler_params=pltpu.CompilerParams(
            collective_id=ident, has_side_effects=True, vmem_limit_bytes=VMEM_BYTES
        ),
        name="sum_all",
    )(*arrays)


class Exchange:
    def __init__(self, tasks, batch, near, far, near_send, near_recv, far_send, far_recv):
        place = lax.axis_index("batch")
        self.task = lax.axis_index("task")
        self.high = place // LOW
        self.low = lax.rem(place, LOW)
        self.near_size = tasks * LOW
        self.far_size = batch // LOW
        self.me_near = self.task * LOW + self.low
        self.near, self.far = near, far
        self.near_sems, self.far_sems = (near_send, near_recv), (far_send, far_recv)

    @staticmethod
    def scratch(tasks, batch, width):
        near_size, far_size = tasks * LOW, batch // LOW
        return [
            pltpu.VMEM((near_size + 1, 2, width), jnp.float32),
            pltpu.VMEM((far_size + 1, 2, width), jnp.float32),
            pltpu.SemaphoreType.DMA((near_size,)),
            pltpu.SemaphoreType.DMA((near_size,)),
            pltpu.SemaphoreType.DMA((far_size,)),
            pltpu.SemaphoreType.DMA((far_size,)),
        ]

    def near_peer(self, step):
        slot = lax.rem(self.me_near + step, self.near_size)
        return slot, (slot // LOW, self.high * LOW + lax.rem(slot, LOW))

    def far_peer(self, step):
        slot = lax.rem(self.high + step, self.far_size)
        return slot, (self.task, slot * LOW + self.low)

    def peers(self):
        near = [self.near_peer(step)[1] for step in range(1, self.near_size)]
        return near + [self.far_peer(step)[1] for step in range(1, self.far_size)]

    def greet(self):
        barrier = pltpu.get_barrier_semaphore()
        for device in self.peers():
            pl.semaphore_signal(barrier, inc=1, device_id=device, device_id_type=MESH)

    def met(self):
        pl.semaphore_wait(pltpu.get_barrier_semaphore(), self.near_size + self.far_size - 2)

    def hop(self, size, peer, me, held, sems):
        def copy(step, slot):
            return pltpu.make_async_remote_copy(
                src_ref=held.at[size],
                dst_ref=held.at[slot],
                send_sem=sems[0].at[step],
                recv_sem=sems[1].at[slot],
                device_id=peer(step)[1],
                device_id_type=MESH,
            )

        for step in range(1, size):
            copy(step, me).start()
        held[me] = held[size]
        for step in range(1, size):
            copy(step, peer(step)[0]).wait_recv()
        for step in range(1, size):
            copy(step, me).wait_send()
        return held[:size]

    def run(self, total, spread, rows, forward):
        self.near[self.near_size, 0:1] = total
        self.near[self.near_size, 1:2] = spread
        held = self.hop(self.near_size, self.near_peer, self.me_near, self.near, self.near_sems)
        total, spread = join(held, float(rows), forward)
        self.far[self.far_size, 0:1] = total
        self.far[self.far_size, 1:2] = spread
        held = self.hop(self.far_size, self.far_peer, self.high, self.far, self.far_sems)
        return join(held, float(rows * self.near_size), forward)


def join(held, share, forward):
    sums = held[:, 0, :]
    total = jnp.sum(sums, axis=0, keepdims=True)
    spread = jnp.sum(held[:, 1, :], axis=0, keepdims=True)
    if forward:
        groups = held.shape[0]
        away = sums * (1.0 / share) - total * (1.0 / (share * groups))
        spread = spread + share * jnp.sum(away * away, axis=0, keepdims=True)
    return total, spread


def settle_stats(exchange, stat_ref, vec_ref, out_ref, rows, count, forward):
    first = jnp.sum(stat_ref[:8], axis=0, keepdims=True)
    second = jnp.sum(stat_ref[8:16], axis=0, keepdims=True)
    out_ref[:8] = vec_ref[:8]
    if forward:
        local = first + rows * stat_ref[16:17]
        total, spread = exchange.run(local, second - first * first * (1.0 / rows), rows, True)
        scale = lax.rsqrt(spread * (1.0 / count) + EPS)
        out_ref[0:1] = total * (1.0 / count)
        out_ref[1:2] = scale
        out_ref[4:5] = scale * vec_ref[2:3]
        out_ref[8:] = jnp.zeros_like(out_ref[8:])
    else:
        total, spread = exchange.run(first, second, rows, False)
        out_ref[5:6] = total * (1.0 / count)
        out_ref[6:7] = spread * (1.0 / count)
        out_ref[8:9] = total
        out_ref[9:10] = spread
        out_ref[10:] = jnp.zeros_like(out_ref[10:])


def tail_and_bell(value):
    bell = jnp.exp2(value * value * (-0.5 * LOG2E))
    away = jnp.abs(value)
    ratio = 1.0 / (1.0 + away * (ERF_P * ROOT_HALF))
    poly = ERF_A[4]
    for factor in ERF_A[3::-1]:
        poly = poly * ratio + factor
    tail = 0.5 * poly * ratio * bell
    return jnp.where(value >= 0, 1.0 - tail, tail), bell


def fold(array):
    total = array[:8]
    for start in range(8, array.shape[0], 8):
        total = total + array[start : start + 8]
    return total


def crown_kernel(
    piece, h_ref, x_ref, thr_ref, cot_ref, cot_peer_ref, top_ref, top_peer_ref, vec_ref,
    out_ref, flow_ref, gradt_ref, came_ref, stat_ref, z_ref, acc_ref, sent_ref, sems,
):
    step = pl.program_id(0)
    rows, width = x_ref.shape
    half = cot_ref.shape[1]
    task = lax.axis_index("task")
    last = pl.num_programs(0) - 1

    def send(index):
        span = pl.ds(pl.multiple_of(index * rows, rows), rows)
        return across(sent_ref.at[span], came_ref.at[span], sems.at[index])

    @pl.when(step > 0)
    def _():
        send(step - 1).start()

    @pl.when(step == 0)
    def _():
        stat_ref[...] = jnp.zeros_like(stat_ref)
        acc_ref[...] = jnp.zeros_like(acc_ref)

    for start in range(0, width, piece):
        cols = pl.ds(start, piece)
        g_one = lax.dot_general(
            cot_ref[...], top_ref[cols], COLS_COLS, preferred_element_type=jnp.float32
        ).astype(jnp.bfloat16).astype(jnp.float32)
        g_two = lax.dot_general(
            cot_peer_ref[...], top_peer_ref[cols], COLS_COLS, preferred_element_type=jnp.float32
        ).astype(jnp.bfloat16).astype(jnp.float32)
        total = g_one + g_two
        size = jnp.abs(g_one) + jnp.abs(g_two)
        share = total / jnp.maximum(size, FLOOR)
        limit = thr_ref[:, cols].astype(jnp.float32)
        keep = jnp.clip((0.5 / SOFT) * share + ((0.5 / SOFT + 0.5) - limit * (1.0 / SOFT)), 0.0, 1.0)
        merged = 0.5 * (total - size) + keep * size
        normed = (h_ref[:, cols] - vec_ref[0:1, cols]) * vec_ref[1:2, cols]
        before = normed * vec_ref[2:3, cols] + vec_ref[3:4, cols] + x_ref[:, cols].astype(jnp.float32)
        phi, bell = tail_and_bell(before)
        z_ref[:, cols] = (before * phi).astype(jnp.bfloat16)
        flow = merged * (phi + before * bell * DENSITY)
        flow_ref[:, cols] = flow.astype(flow_ref.dtype)
        stat_ref[:8, cols] += fold(flow)
        stat_ref[8:, cols] += fold(flow * normed)
    out_ref[...] = jnp.dot(z_ref[...], top_ref[...], preferred_element_type=jnp.float32)
    sent_ref[pl.ds(pl.multiple_of(step * rows, rows), rows)] = jnp.dot(
        z_ref[...], top_peer_ref[...], preferred_element_type=jnp.float32
    ).astype(jnp.bfloat16)
    acc_ref[:half] += lax.dot_general(cot_ref[...], z_ref[...], ROWS_ROWS, preferred_element_type=jnp.float32)
    acc_ref[half:] += lax.dot_general(cot_peer_ref[...], z_ref[...], ROWS_ROWS, preferred_element_type=jnp.float32)

    @pl.when(step == last)
    def _():
        gradt_ref[pl.ds(task * half, half)] = acc_ref[:half].astype(jnp.bfloat16)
        gradt_ref[pl.ds((1 - task) * half, half)] = acc_ref[half:].astype(jnp.bfloat16)
        send(last).start()

    def after():
        lax.fori_loop(0, last + 1, lambda index, carry: (send(index).wait(), carry)[1], 0)

    return after


def wide(mask, width):
    return jnp.concatenate([mask] * (width // mask.shape[1]), axis=1)


def gather_stats(stat_ref, hidden, first):
    @pl.when(first)
    def _():
        stat_ref[:16] = jnp.zeros_like(stat_ref[:16])
        mean = jnp.sum(hidden, axis=0, keepdims=True) / hidden.shape[0]
        stat_ref[16:] = jnp.broadcast_to(mean, stat_ref[16:].shape)

    away = hidden - stat_ref[16:17]
    stat_ref[:8] += fold(away)
    stat_ref[8:16] += fold(away * away)


def normal(hidden, vec_ref):
    return (hidden - vec_ref[0:1]) * vec_ref[1:2]


def squeeze_kernel(x_ref, w_ref, out_ref, stat_ref):
    hidden = jnp.dot(x_ref[...], w_ref[...], preferred_element_type=jnp.float32)
    out_ref[...] = hidden
    gather_stats(stat_ref, hidden, pl.program_id(0) == 0)


def mesh_kernel(h_ref, vec_ref, mask_ref, w_ref, out_ref, side_ref, stat_ref, pad_ref):
    rows, mid = h_ref.shape
    inner = pl.ds(SIDE, rows)
    before = normal(h_ref[...], vec_ref) * vec_ref[2:3] + vec_ref[3:4]
    phi, _ = tail_and_bell(before)
    low = (before * phi).astype(jnp.bfloat16)
    kept = low.astype(jnp.float32)
    left = wide(mask_ref[:, :128].astype(jnp.float32), mid)
    right = wide(mask_ref[:, 128:256].astype(jnp.float32), mid)

    @pl.when(pl.program_id(0) == 0)
    def _():
        pad_ref[:SIDE] = jnp.zeros_like(pad_ref[:SIDE])
        pad_ref[SIDE + rows :] = jnp.zeros_like(pad_ref[:SIDE])

    pad_ref[inner, :mid] = (pltpu.roll(kept, 1, 0) * left).astype(jnp.bfloat16)
    pad_ref[inner, mid : 2 * mid] = low
    pad_ref[inner, 2 * mid :] = (pltpu.roll(kept, rows - 1, 0) * right).astype(jnp.bfloat16)
    side_ref[...] = pad_ref[inner]
    above = wide(mask_ref[:, 256:384], 3 * mid)
    below = wide(mask_ref[:, 384:], 3 * mid)
    hidden = jnp.dot(pad_ref[inner], w_ref[3 * mid : 6 * mid], preferred_element_type=jnp.float32)
    hidden += jnp.dot(pad_ref[:rows] * above, w_ref[: 3 * mid], preferred_element_type=jnp.float32)
    hidden += jnp.dot(pad_ref[2 * SIDE :] * below, w_ref[6 * mid :], preferred_element_type=jnp.float32)
    out_ref[...] = hidden
    gather_stats(stat_ref, hidden, pl.program_id(0) == 0)


def widen_kernel(h_ref, vec_ref, w_ref, out_ref, low_ref, stat_ref):
    before = normal(h_ref[...], vec_ref) * vec_ref[2:3] + vec_ref[3:4]
    phi, _ = tail_and_bell(before)
    low = (before * phi).astype(jnp.bfloat16)
    low_ref[...] = low
    hidden = jnp.dot(low, w_ref[...], preferred_element_type=jnp.float32)
    out_ref[...] = hidden
    gather_stats(stat_ref, hidden, pl.program_id(0) == 0)


def norm_grad(upstream, normed, vec_ref):
    return vec_ref[4:5] * (upstream - vec_ref[5:6] - normed * vec_ref[6:7])


def act_slope(value):
    phi, bell = tail_and_bell(value)
    return phi + value * bell * DENSITY


def gather_flow(stat_ref, flow, normed, first):
    @pl.when(first)
    def _():
        stat_ref[...] = jnp.zeros_like(stat_ref)

    stat_ref[:8] += fold(flow)
    stat_ref[8:16] += fold(flow * normed)


def narrow_kernel(flow_ref, h_ref, vec_ref, two_ref, vectwo_ref, low_ref, w_ref, out_ref, grad_ref, stat_ref, acc_ref):
    first = pl.program_id(0) == 0
    dh = norm_grad(flow_ref[...].astype(jnp.float32), normal(h_ref[...], vec_ref), vec_ref).astype(jnp.bfloat16)
    dq = lax.dot_general(dh, w_ref[...], COLS_COLS, preferred_element_type=jnp.float32)
    normed = normal(two_ref[...], vectwo_ref)
    flow = dq * act_slope(normed * vectwo_ref[2:3] + vectwo_ref[3:4])
    out_ref[...] = flow
    gather_flow(stat_ref, flow, normed, first)
    part = lax.dot_general(low_ref[...], dh, ROWS_ROWS, preferred_element_type=jnp.float32)
    accumulate(acc_ref, grad_ref, part)


def accumulate(acc_ref, grad_ref, part):
    step = pl.program_id(0)
    last = pl.num_programs(0) - 1

    @pl.when(step == 0)
    def _():
        acc_ref[...] = part

    @pl.when((step > 0) & (step < last))
    def _():
        acc_ref[...] += part

    @pl.when(step == last)
    def _():
        grad_ref[...] = (acc_ref[...] + part).astype(jnp.bfloat16)


def unmesh_kernel(flow_ref, two_ref, vec_ref, one_ref, vecone_ref, side_ref, mask_ref, w_ref, out_ref, grad_ref, stat_ref, lane_ref, acc_ref):
    step = pl.program_id(0)
    last = pl.num_programs(0) - 1
    rows, mid = flow_ref.shape
    dh = norm_grad(flow_ref[...], normal(two_ref[...], vec_ref), vec_ref)
    above = wide(mask_ref[:, 256:384].astype(jnp.float32), mid)
    below = wide(mask_ref[:, 384:].astype(jnp.float32), mid)

    @pl.when(step == 0)
    def _():
        lane_ref[rows - SIDE :, :mid] = jnp.zeros((SIDE, mid), jnp.bfloat16)
        lane_ref[:SIDE, 2 * mid :] = jnp.zeros((SIDE, mid), jnp.bfloat16)

    lane_ref[: rows - SIDE, :mid] = (dh * above)[SIDE:].astype(jnp.bfloat16)
    lane_ref[:, mid : 2 * mid] = dh.astype(jnp.bfloat16)
    lane_ref[SIDE:, 2 * mid :] = (dh * below)[: rows - SIDE].astype(jnp.bfloat16)
    pieces = []
    for b in range(3):
        total = None
        for a in range(3):
            part = lax.dot_general(
                lane_ref[:, a * mid : (a + 1) * mid], w_ref[3 * a + b], COLS_COLS, preferred_element_type=jnp.float32
            )
            total = part if total is None else total + part
        pieces.append(total)
    left = wide(mask_ref[:, :128].astype(jnp.float32), mid)
    right = wide(mask_ref[:, 128:256].astype(jnp.float32), mid)
    dq = pieces[1] + pltpu.roll(pieces[0] * left, rows - 1, 0) + pltpu.roll(pieces[2] * right, 1, 0)
    normed = normal(one_ref[...], vecone_ref)
    flow = dq * act_slope(normed * vecone_ref[2:3] + vecone_ref[3:4])
    out_ref[...] = flow
    gather_flow(stat_ref, flow, normed, step == 0)
    for a in range(3):
        part = lax.dot_general(
            side_ref[...], lane_ref[:, a * mid : (a + 1) * mid], ROWS_ROWS, preferred_element_type=jnp.float32
        )
        span = pl.ds(a * 3 * mid, 3 * mid)
        accumulate(acc_ref.at[span], grad_ref.at[span], part)


def finish_kernel(flow_ref, one_ref, vec_ref, up_ref, x_ref, w_ref, out_ref, grad_ref, acc_ref):
    dh = norm_grad(flow_ref[...], normal(one_ref[...], vec_ref), vec_ref).astype(jnp.bfloat16)
    back = lax.dot_general(dh, w_ref[...], COLS_COLS, preferred_element_type=jnp.float32)
    out_ref[...] = (up_ref[...].astype(jnp.float32) + back).astype(jnp.bfloat16)
    accumulate(acc_ref, grad_ref, lax.dot_general(dh, x_ref[...], ROWS_ROWS, preferred_element_type=jnp.float32))


def across(source, target, sems):
    return pltpu.make_async_remote_copy(
        src_ref=source,
        dst_ref=target,
        send_sem=sems.at[0],
        recv_sem=sems.at[1],
        device_id=(1 - lax.axis_index("task"), lax.axis_index("batch")),
        device_id_type=MESH,
    )


def tiled(kernel, tile, moving, flags, outs, fixed, scratch, name, stats=None, send=None, far=()):
    tasks = lax.axis_size("task")
    batch = lax.axis_size("batch")
    rows = moving[0].shape[0]

    def block(array):
        return pl.BlockSpec((tile,) + array.shape[1:], lambda i: (i,) + (0,) * (len(array.shape) - 1))

    def whole(array):
        zeros = (0,) * len(array.shape)
        return pl.BlockSpec(array.shape, lambda i: zeros)

    hbm = pl.BlockSpec(memory_space=pl.ANY)
    operands = list(moving)
    in_specs = [block(a) if m else whole(a) for a, m in zip(moving, flags)]
    out_shape = outs + fixed + list(far)
    out_specs = [block(a) for a in outs] + [whole(a) for a in fixed] + [hbm for a in far]
    scratch = list(scratch)
    params = dict(vmem_limit_bytes=VMEM_BYTES)
    ins, made, held = len(operands), len(out_shape), len(scratch)
    run = kernel
    if stats is not None:
        vec, forward, ident = stats
        width = vec.shape[1]
        params.update(collective_id=ident, has_side_effects=True)
        operands.append(vec)
        in_specs.append(whole(vec))
        out_shape = out_shape + [shape32(16, width)]
        out_specs = out_specs + [whole(out_shape[-1])]
        scratch = scratch + [pltpu.VMEM((24 if forward else 16, width), jnp.float32)]
        scratch = scratch + Exchange.scratch(tasks, batch, width)
        if send is not None:
            operands.append(send)
            in_specs.append(hbm)
            out_shape = out_shape + [jax.ShapeDtypeStruct(send.shape, send.dtype)]
            out_specs = out_specs + [hbm]
            scratch = scratch + [pltpu.SemaphoreType.DMA((2,))]

        def run(*refs):
            refs = list(refs)
            take = lambda n: [refs.pop(0) for _ in range(n)]
            used = take(ins)
            vec_ref = take(1)[0]
            source = take(1)[0] if send is not None else None
            given = take(made)
            out_ref = take(1)[0]
            target = take(1)[0] if send is not None else None
            own = take(held)
            stat_ref = take(1)[0]
            exchange = Exchange(tasks, batch, *take(6))
            step = pl.program_id(0)
            last = pl.num_programs(0) - 1

            @pl.when(step == 0)
            def _():
                exchange.greet()

            early = send is not None or len(far) > 0
            if early:

                @pl.when(step == 1)
                def _():
                    exchange.met()
                    if send is not None:
                        across(source, target, refs[0]).start()

            after = kernel(*used, *given, stat_ref, *own)

            @pl.when(step == last)
            def _():
                if not early:
                    exchange.met()
                settle_stats(exchange, stat_ref, vec_ref, out_ref, rows, rows * tasks * batch, forward)
                if send is not None:
                    across(source, target, refs[0]).wait()
                if after is not None:
                    after()

    return pl.pallas_call(
        run,
        grid=(rows // tile,),
        out_shape=out_shape,
        in_specs=in_specs,
        out_specs=out_specs,
        scratch_shapes=scratch,
        compiler_params=pltpu.CompilerParams(**params),
        name=name,
    )(*operands)


def shape32(*shape):
    return jax.ShapeDtypeStruct(shape, jnp.float32)


def shape16(*shape):
    return jax.ShapeDtypeStruct(shape, jnp.bfloat16)


def squeeze(flat_in, w_reduce, stats, tile):
    rows, mid = flat_in.shape[0], w_reduce.shape[1]
    return tiled(squeeze_kernel, tile, [flat_in, w_reduce], [1, 0], [shape32(rows, mid)], [], [], "squeeze", stats)


def mesh_forward(h_one, vec, masks, taps, stats, send, tile):
    rows, mid = h_one.shape
    return tiled(
        mesh_kernel, tile, [h_one, vec, masks, taps], [1, 0, 1, 0],
        [shape32(rows, mid), shape16(rows, 3 * mid)], [],
        [pltpu.VMEM((tile + 2 * SIDE, 3 * mid), jnp.bfloat16)], "mesh_forward", stats, send,
    )


def widen(h_two, vec, w_expand, stats, send, tile):
    rows, mid = h_two.shape
    width = w_expand.shape[1]
    return tiled(
        widen_kernel, tile, [h_two, vec, w_expand], [1, 0, 0],
        [shape32(rows, width), shape16(rows, mid)], [], [], "widen", stats, send,
    )


def narrow(flow, h_three, vec_three, h_two, vec_two, q_two, w_expand, stats, tile):
    rows, mid = h_two.shape
    width = w_expand.shape[1]
    return tiled(
        narrow_kernel, tile, [flow, h_three, vec_three, h_two, vec_two, q_two, w_expand], [1, 1, 0, 1, 0, 1, 0],
        [shape32(rows, mid)], [shape16(mid, width)], [pltpu.VMEM((mid, width), jnp.float32)], "narrow", stats,
    )


def mesh_backward(flow, h_two, vec_two, h_one, vec_one, sides, masks, w_spatial, stats, tile):
    rows, mid = h_two.shape
    return tiled(
        unmesh_kernel, tile, [flow, h_two, vec_two, h_one, vec_one, sides, masks, w_spatial], [1, 1, 0, 1, 0, 1, 1, 0],
        [shape32(rows, mid)], [shape16(9 * mid, mid)],
        [pltpu.VMEM((tile, 3 * mid), jnp.bfloat16), pltpu.VMEM((9 * mid, mid), jnp.float32)], "mesh_backward", stats,
    )


def finish(flow, h_one, vec_one, up, flat_in, w_reduce, tile):
    rows, mid = h_one.shape
    width = flat_in.shape[1]
    return tiled(
        finish_kernel, tile, [flow, h_one, vec_one, up, flat_in, w_reduce], [1, 1, 0, 1, 1, 0],
        [shape16(rows, width)], [shape16(mid, width)], [pltpu.VMEM((mid, width), jnp.float32)], "finish",
    )


def crown(h_three, flat_in, limits, cot, cot_peer, top, top_peer, vec, stats, tile, piece):
    rows, width = flat_in.shape
    half = cot.shape[1]
    return tiled(
        functools.partial(crown_kernel, piece), tile,
        [h_three, flat_in, limits, cot, cot_peer, top, top_peer, vec], [1, 1, 1, 1, 1, 0, 0, 0],
        [shape32(rows, half), shape16(rows, width)], [shape16(2 * half, width)],
        [
            pltpu.VMEM((tile, width), jnp.bfloat16),
            pltpu.VMEM((2 * half, width), jnp.float32),
            pltpu.VMEM((rows, half), jnp.bfloat16),
            pltpu.SemaphoreType.DMA((rows // tile, 2)),
        ],
        "crown", stats, None, [shape16(rows, half)],
    )


def body(
    inputs,
    crop_cuts,
    threshold,
    w_reduce,
    w_spatial,
    w_expand,
    w_heads,
    gain_one,
    bias_one,
    gain_two,
    bias_two,
    gain_three,
    bias_three,
    cotangent,
):
    low = jnp.bfloat16
    full = jnp.float32
    canvases, pixels, width = inputs.shape[1:]
    mid = w_reduce.shape[1]
    rows = canvases * pixels
    half = w_heads.shape[2]
    task = lax.axis_index("task")
    cot = cotangent.reshape(2, rows, half)
    cot_mine = lax.dynamic_index_in_dim(cot, task, 0, keepdims=False)
    cot_sent = lax.dynamic_index_in_dim(cot, 1 - task, 0, keepdims=False)
    top_mine = w_heads[0]

    def params(gain, bias):
        zero = jnp.zeros_like(gain)
        return jnp.stack([zero, zero, gain, bias, zero, zero, zero, zero])

    lines = jnp.arange(SIDE, dtype=jnp.int32)
    cuts = crop_cuts.reshape(canvases, 2)
    from_above = jnp.logical_not((lines == cuts[:, 0:1]) | (lines == 0)[None, :])
    from_left = jnp.logical_not((lines == cuts[:, 1:2]) | (lines == 0)[None, :])
    from_below = jnp.pad(from_above[:, 1:], ((0, 0), (0, 1)))
    from_right = jnp.pad(from_left[:, 1:], ((0, 0), (0, 1)))
    shape = (canvases, SIDE, SIDE, 128)
    masks = jnp.concatenate(
        [jnp.broadcast_to(m[:, None, :, None], shape) for m in (from_left, from_right)]
        + [jnp.broadcast_to(m[:, :, None, None], shape) for m in (from_above, from_below)],
        axis=3,
    ).astype(low).reshape(rows, 512)

    flat_in = inputs.reshape(rows, width)
    h_one, vec_one = squeeze(flat_in, w_reduce, (params(gain_one, bias_one), True, 0), min(rows, 512))
    h_two, sides, vec_two, cot_peer = mesh_forward(
        h_one, vec_one, masks, w_spatial.reshape(9 * mid, mid), (params(gain_two, bias_two), True, 1), cot_sent, pixels
    )
    h_three, q_two, vec_three, top_peer = widen(
        h_two, vec_two, w_expand, (params(gain_three, bias_three), True, 2), top_mine, pixels
    )
    out_mine, flow, grad_heads, out_peer, vec_three = crown(
        h_three, flat_in, threshold.reshape(rows, width), cot_mine, cot_peer, top_mine, top_peer, vec_three,
        (vec_three, False, 3), pixels, 256,
    )
    out_peer = out_peer.astype(full)
    first = jnp.where(task == 0, out_mine, out_peer)
    second = jnp.where(task == 0, out_peer, out_mine)
    head_out = jnp.stack([first, second]).reshape(1, 2, canvases, pixels, half)
    flow_two, grad_expand, vec_two = narrow(
        flow, h_three, vec_three, h_two, vec_two, q_two, w_expand, (vec_two, False, 4), min(rows, 512)
    )
    flow_one, grad_spatial, vec_one = mesh_backward(
        flow_two, h_two, vec_two, h_one, vec_one, sides, masks, w_spatial, (vec_one, False, 5), min(rows, 512)
    )
    grad_inputs, grad_reduce = finish(flow_one, h_one, vec_one, flow, flat_in, w_reduce, min(rows, 512))
    grad_heads, grad_expand, grad_spatial, grad_reduce = sum_all(
        [grad_heads, grad_expand, grad_spatial, grad_reduce], [1, 1, 3, 1], [True, True, False, True], 6
    )
    grad_heads = lax.dynamic_slice_in_dim(grad_heads, task * half, half, axis=0)
    return (
        head_out,
        grad_inputs.reshape(inputs.shape),
        grad_reduce.T.astype(full),
        grad_spatial.reshape(w_spatial.shape).astype(full),
        grad_expand.astype(full),
        grad_heads.T.astype(full)[None],
        vec_one[9],
        vec_one[8],
        vec_two[9],
        vec_two[8],
        vec_three[9],
        vec_three[8],
    )


def solution(mesh):
    in_specs = (
        P("task", "batch", None, None),
        P("task", "batch", None),
        P("task", "batch", None, None),
        P(),
        P(),
        P(),
        P("task", None, None),
        P(),
        P(),
        P(),
        P(),
        P(),
        P(),
        P("task", None, "batch", None, None),
    )
    out_specs = (
        P("task", None, "batch", None, None),
        P("task", "batch", None, None),
        P(),
        P(),
        P(),
        P("task", None, None),
        P(),
        P(),
        P(),
        P(),
        P(),
        P(),
    )
    return jax.shard_map(body, mesh=mesh, in_specs=in_specs, out_specs=out_specs, check_vma=False)
```

```python
import functools
import math

import jax
import jax.numpy as jnp
from jax import lax
from jax.experimental import pallas as pl
from jax.experimental.pallas import tpu as pltpu
from jax.sharding import PartitionSpec as P

SIDE = 16
EPS = 1e-05
FLOOR = 0.1
SOFT = 0.25
ROOT_HALF = 0.7071067811865476
DENSITY = 0.3989422804014327
LOG2E = 1.4426950408889634
ERF_P = 0.3275911
ERF_A = (0.254829592, -0.284496736, 1.421413741, -1.453152027, 1.061405429)
ROWS_ROWS = (((0,), (0,)), ((), ()))
COLS_COLS = (((1,), (1,)), ((), ()))
MESH = pl.DeviceIdType.MESH
LOW = 4
VMEM_BYTES = 62 * 2**20


AGENDA = {
    "start": ((0, 0), (1, 0),),
    "lane1": ((0, 1),),
    "lane2": ((1, 1),),
    "sp2": ((2, 0),),
    "sp3": ((0, 2),),
    "sp4": ((2, 1),),
    "sp5": ((3, 0),),
    "sp7": ((1, 2), (3, 1),),
    "sp8": ((4, 0),),
    "tap0": ((0, 3),),
    "tap1": ((4, 1),),
    "tap2": ((2, 2),),
    "tap4": ((1, 3),),
    "tap5": ((0, 4),),
    "tap6": ((3, 2),),
    "tap9": ((1, 4), (4, 2),),
    "tap10": ((2, 3),),
    "xch": ((0, 5), (1, 5), (3, 3), (4, 3),),
    "inner": ((0, 6), (2, 4),),
    "red1": ((1, 6), (5, 0),),
    "red2": ((3, 4), (5, 1),),
    "red3": ((6, 0),),
    "inp0": ((0, 7), (4, 4), (6, 1),),
    "inp2": ((0, 8), (2, 5),),
    "inp3": ((1, 7),),
    "inp5": ((1, 8), (3, 5), (5, 2),),
    "inp7": ((6, 2), (4, 5),),
    "tail": ((2, 6), (3, 6), (5, 3), (6, 3), (4, 6), (5, 4), (2, 7), (6, 4), (2, 8), (3, 7), (5, 5), (3, 8), (6, 5), (4, 7), (5, 6), (4, 8), (6, 6), (5, 7), (5, 8), (6, 7), (6, 8),),
}


class Reduction:
    def __init__(self, grid, work, result, core, first, second, last, done, send, recv, far_send, far_recv, local, wide):
        self.grid, self.work, self.result = grid, work, result
        self.room, self.done = (core, first, second, last), done
        self.send, self.recv, self.far_send, self.far_recv = send, recv, far_send, far_recv
        self.local = local
        self.wide = wide
        self.rows, self.cols = work.shape
        sizes = self.sizes(self.rows, self.cols, wide, grid.far)
        self.pieces = sizes[2][0] // sizes[3][0]
        self.mine = lax.rem(grid.high, self.pieces)

    @staticmethod
    def sizes(rows, cols, wide, far):
        if wide:
            core = (rows, cols // 2)
            first = (rows, cols // 8)
            second = (rows, cols // 16)
        else:
            core = (rows // 2, cols)
            first = (rows // 2, cols // 4)
            second = (rows // 4, cols // 4)
        pieces = max(n for n in range(1, far + 1) if far % n == 0 and second[0] % (8 * n) == 0)
        return core, first, second, (second[0] // pieces, second[1])

    @staticmethod
    def scratch(rows, cols, wide, far):
        core, first, second, last = Reduction.sizes(rows, cols, wide, far)
        return [
            pltpu.VMEM(core, jnp.bfloat16),
            pltpu.VMEM((2,) + first, jnp.bfloat16),
            pltpu.VMEM((2,) + second, jnp.bfloat16),
            pltpu.VMEM((2, far) + last, jnp.bfloat16),
            pltpu.VMEM((2,) + last, jnp.bfloat16),
            pltpu.SemaphoreType.DMA((10,)),
            pltpu.SemaphoreType.DMA((10,)),
            pltpu.SemaphoreType.DMA((4, far)),
            pltpu.SemaphoreType.DMA((4, far)),
            pltpu.SemaphoreType.DMA((2,)),
        ]

    def view(self, core, part=None, first=None, second=None, piece=None, done=False):
        sizes = self.sizes(self.rows, self.cols, self.wide, self.grid.far)
        row = col = 0
        shape = sizes[0]
        if self.wide:
            col = core * (self.cols // 2)
            if part is not None:
                col = col + part * (self.cols // 4) + first * (self.cols // 8)
                shape = sizes[1]
            if second is not None:
                col = col + second * (self.cols // 16)
                shape = sizes[2]
        else:
            row = core * (self.rows // 2)
            if part is not None:
                col = part * (self.cols // 2) + first * (self.cols // 4)
                shape = sizes[1]
            if second is not None:
                row = row + second * (self.rows // 4)
                shape = sizes[2]
        if piece is not None:
            row = row + piece * sizes[3][0]
            shape = sizes[3]
        if not isinstance(row, int):
            row = pl.multiple_of(row, shape[0] & -shape[0])
        if not isinstance(col, int):
            col = pl.multiple_of(col, 128)
        ref = self.result if done else self.work
        return ref.at[pl.ds(row, shape[0]), pl.ds(col, shape[1])]

    def swap(self, index):
        grid = self.grid
        part = (index + 1) % 2
        bits = grid.bits(part)
        if index == 0:
            source, target, device = self.view(1 - grid.core), self.room[0], grid.core_peer
        elif index < 3:
            source, target = self.view(grid.core, part, 1 - bits[0]), self.room[1].at[part]
            device = grid.peers(part)[0]
        elif index < 5:
            source, target = self.view(grid.core, part, bits[0], 1 - bits[1]), self.room[2].at[part]
            device = grid.peers(part)[1]
        elif index < 7:
            source = self.view(grid.core, part, bits[0], bits[1], done=True)
            target, device = source, grid.peers(part)[1]
        elif index < 9:
            source = self.view(grid.core, part, bits[0], done=True)
            target, device = source, grid.peers(part)[0]
        else:
            source = self.view(grid.core, done=True)
            target, device = source, grid.core_peer
        return pltpu.make_async_remote_copy(
            src_ref=source,
            dst_ref=target,
            send_sem=self.send.at[index],
            recv_sem=self.recv.at[index],
            device_id=device,
            device_id_type=MESH,
        )

    def add(self, target, sources):
        rows = target.shape[0]
        step = math.gcd(rows, 64)

        def one(i, carry):
            span = pl.ds(pl.multiple_of(i * step, step), step)
            total = sources[0][span].astype(jnp.float32)
            for source in sources[1:]:
                total = total + source[span].astype(jnp.float32)
            target[span] = total.astype(jnp.bfloat16)
            return carry

        lax.fori_loop(0, rows // step, one, 0)

    def join(self, mine, received):
        self.add(mine, [mine, received])

    def far_copy(self, part, step, back, inward):
        grid = self.grid
        bits = grid.bits(part)
        if back:
            first = grid.high - self.mine
            slot = first + lax.rem(self.mine + step, self.pieces)
            owner = slot if inward else grid.high
            source = self.done.at[part]
            target = self.view(grid.core, part, bits[0], bits[1], lax.rem(owner, self.pieces), True)
        else:
            slot = lax.rem(grid.high + step, grid.far)
            owner = slot if inward else grid.high
            source = self.view(grid.core, part, bits[0], bits[1], lax.rem(slot, self.pieces))
            target = self.room[3].at[part, owner]
        line = 2 * part + (1 if back else 0)
        return pltpu.make_async_remote_copy(
            src_ref=source,
            dst_ref=target,
            send_sem=self.far_send.at[line, step],
            recv_sem=self.far_recv.at[line, owner],
            device_id=(grid.task, slot * LOW + grid.low),
            device_id_type=MESH,
        )

    def far_start(self, back):
        for part in range(2):
            for step in range(1, self.pieces if back else self.grid.far):
                self.far_copy(part, step, back, False).start()

    def far_settle(self, back):
        for part in range(2):
            for step in range(1, self.pieces if back else self.grid.far):
                self.far_copy(part, step, back, True).wait_recv()
                self.far_copy(part, step, back, False).wait_send()

    def keep(self, part):
        bits = self.grid.bits(part)
        mine = self.view(self.grid.core, part, bits[0], bits[1], self.mine, True)
        return pltpu.make_async_copy(self.done.at[part], mine, self.local.at[part])

    def stage(self, index):
        grid = self.grid
        if index == 0:
            self.swap(0).start()
        elif index == 1:
            self.swap(0).wait()
            self.join(self.view(grid.core), self.room[0])
            for part in range(2):
                self.swap(1 + part).start()
        elif index == 2:
            for part in range(2):
                self.swap(1 + part).wait()
                bits = grid.bits(part)
                self.join(self.view(grid.core, part, bits[0]), self.room[1].at[part])
                self.swap(3 + part).start()
        elif index == 3:
            for part in range(2):
                self.swap(3 + part).wait()
                bits = grid.bits(part)
                self.join(self.view(grid.core, part, bits[0], bits[1]), self.room[2].at[part])
            self.far_start(False)
        elif index == 4:
            self.far_settle(False)
            for part in range(2):
                bits = grid.bits(part)
                mine = self.view(grid.core, part, bits[0], bits[1], self.mine)
                self.room[3][part, grid.high] = mine[...]
                self.add(self.done.at[part], [self.room[3].at[part, slot] for slot in range(grid.far)])
                self.keep(part).start()
            self.far_start(True)
        elif index == 5:
            self.far_settle(True)
            for part in range(2):
                self.keep(part).wait()
                self.swap(5 + part).start()
        elif index == 6:
            for part in range(2):
                self.swap(5 + part).wait()
                self.swap(7 + part).start()
        elif index == 7:
            for part in range(2):
                self.swap(7 + part).wait()
            self.swap(9).start()
        elif index == 8:
            self.swap(9).wait()


class Grid:
    def __init__(self, batch):
        self.task = lax.axis_index("task")
        place = lax.axis_index("batch")
        self.far = batch // LOW
        self.high = place // LOW
        self.low = lax.rem(place, LOW)
        self.core = lax.rem(place, 2)
        self.y = lax.rem(place // 2, 2)
        base = place - self.low
        self.core_peer = (self.task, base + self.y * 2 + (1 - self.core))
        self.x_peer = (1 - self.task, place)
        self.y_peer = (self.task, base + (1 - self.y) * 2 + self.core)

    def bits(self, part):
        return (self.task, self.y) if part == 0 else (self.y, self.task)

    def peers(self, part):
        return (self.x_peer, self.y_peer) if part == 0 else (self.y_peer, self.x_peer)


class Exchange:
    def __init__(self, tasks, batch, near, far, near_send, near_recv, far_send, far_recv):
        place = lax.axis_index("batch")
        self.task = lax.axis_index("task")
        self.high = place // LOW
        self.low = lax.rem(place, LOW)
        self.near_size = tasks * LOW
        self.far_size = batch // LOW
        self.me_near = self.task * LOW + self.low
        self.near, self.far = near, far
        self.near_sems, self.far_sems = (near_send, near_recv), (far_send, far_recv)

    @staticmethod
    def scratch(tasks, batch, width):
        near_size, far_size = tasks * LOW, batch // LOW
        return [
            pltpu.VMEM((near_size + 1, 2, width), jnp.float32),
            pltpu.VMEM((far_size + 1, 2, width), jnp.float32),
            pltpu.SemaphoreType.DMA((near_size,)),
            pltpu.SemaphoreType.DMA((near_size,)),
            pltpu.SemaphoreType.DMA((far_size,)),
            pltpu.SemaphoreType.DMA((far_size,)),
        ]

    def near_peer(self, step):
        slot = lax.rem(self.me_near + step, self.near_size)
        return slot, (slot // LOW, self.high * LOW + lax.rem(slot, LOW))

    def far_peer(self, step):
        slot = lax.rem(self.high + step, self.far_size)
        return slot, (self.task, slot * LOW + self.low)

    def peers(self):
        near = [self.near_peer(step)[1] for step in range(1, self.near_size)]
        return near + [self.far_peer(step)[1] for step in range(1, self.far_size)]

    def greet(self):
        barrier = pltpu.get_barrier_semaphore()
        for device in self.peers():
            pl.semaphore_signal(barrier, inc=1, device_id=device, device_id_type=MESH)

    def met(self):
        pl.semaphore_wait(pltpu.get_barrier_semaphore(), self.near_size + self.far_size - 2)

    def hop(self, size, peer, me, held, sems, filler=None):
        def copy(step, slot):
            return pltpu.make_async_remote_copy(
                src_ref=held.at[size],
                dst_ref=held.at[slot],
                send_sem=sems[0].at[step],
                recv_sem=sems[1].at[slot],
                device_id=peer(step)[1],
                device_id_type=MESH,
            )

        for step in range(1, size):
            copy(step, me).start()
        held[me] = held[size]
        if filler is not None:
            filler()
        for step in range(1, size):
            copy(step, peer(step)[0]).wait_recv()
        for step in range(1, size):
            copy(step, me).wait_send()
        return held[:size]

    def run(self, total, spread, rows, forward, fillers=(None, None)):
        self.near[self.near_size, 0:1] = total
        self.near[self.near_size, 1:2] = spread
        held = self.hop(self.near_size, self.near_peer, self.me_near, self.near, self.near_sems, fillers[0])
        total, spread = join(held, float(rows), forward)
        self.far[self.far_size, 0:1] = total
        self.far[self.far_size, 1:2] = spread
        held = self.hop(self.far_size, self.far_peer, self.high, self.far, self.far_sems, fillers[1])
        return join(held, float(rows * self.near_size), forward)


def join(held, share, forward):
    sums = held[:, 0, :]
    total = jnp.sum(sums, axis=0, keepdims=True)
    spread = jnp.sum(held[:, 1, :], axis=0, keepdims=True)
    if forward:
        groups = held.shape[0]
        away = sums * (1.0 / share) - total * (1.0 / (share * groups))
        spread = spread + share * jnp.sum(away * away, axis=0, keepdims=True)
    return total, spread


def settle_stats(exchange, stat_ref, vec_ref, out_ref, rows, count, forward, fillers=(None, None)):
    first = jnp.sum(stat_ref[:8], axis=0, keepdims=True)
    second = jnp.sum(stat_ref[8:16], axis=0, keepdims=True)
    out_ref[:8] = vec_ref[:8]
    if forward:
        local = first + rows * stat_ref[16:17]
        total, spread = exchange.run(local, second - first * first * (1.0 / rows), rows, True, fillers)
        scale = lax.rsqrt(spread * (1.0 / count) + EPS)
        out_ref[0:1] = total * (1.0 / count)
        out_ref[1:2] = scale
        out_ref[4:5] = scale * vec_ref[2:3]
        out_ref[8:] = jnp.zeros_like(out_ref[8:])
    else:
        total, spread = exchange.run(first, second, rows, False, fillers)
        out_ref[5:6] = total * (1.0 / count)
        out_ref[6:7] = spread * (1.0 / count)
        out_ref[8:9] = total
        out_ref[9:10] = spread
        out_ref[10:] = jnp.zeros_like(out_ref[10:])


def tail_and_bell(value):
    bell = jnp.exp2(value * value * (-0.5 * LOG2E))
    away = jnp.abs(value)
    ratio = 1.0 / (1.0 + away * (ERF_P * ROOT_HALF))
    poly = ERF_A[4]
    for factor in ERF_A[3::-1]:
        poly = poly * ratio + factor
    tail = 0.5 * poly * ratio * bell
    return jnp.where(value >= 0, 1.0 - tail, tail), bell


def fold(array):
    total = array[:8]
    for start in range(8, array.shape[0], 8):
        total = total + array[start : start + 8]
    return total


def crown_kernel(
    piece, h_ref, x_ref, thr_ref, cot_ref, cot_peer_ref, top_ref, top_peer_ref, vec_ref,
    out_ref, flow_ref, normed_ref, grad_ref, came_ref, stat_ref, z_ref, acc_ref, sent_ref, sems,
):
    step = pl.program_id(0)
    rows, width = x_ref.shape
    half = cot_ref.shape[1]
    task = lax.axis_index("task")
    last = pl.num_programs(0) - 1

    def send(index):
        span = pl.ds(pl.multiple_of(index * rows, rows), rows)
        return across(sent_ref.at[span], came_ref.at[span], sems.at[index])

    @pl.when(step > 0)
    def _():
        send(step - 1).start()

    @pl.when(step == 0)
    def _():
        stat_ref[...] = jnp.zeros_like(stat_ref)
        acc_ref[...] = jnp.zeros_like(acc_ref)

    for start in range(0, width, piece):
        cols = pl.ds(start, piece)
        g_one = lax.dot_general(
            cot_ref[...], top_ref[cols], COLS_COLS, preferred_element_type=jnp.float32
        ).astype(jnp.bfloat16).astype(jnp.float32)
        g_two = lax.dot_general(
            cot_peer_ref[...], top_peer_ref[cols], COLS_COLS, preferred_element_type=jnp.float32
        ).astype(jnp.bfloat16).astype(jnp.float32)
        total = g_one + g_two
        size = jnp.abs(g_one) + jnp.abs(g_two)
        share = total / jnp.maximum(size, FLOOR)
        limit = thr_ref[:, cols].astype(jnp.float32)
        keep = jnp.clip((0.5 / SOFT) * share + ((0.5 / SOFT + 0.5) - limit * (1.0 / SOFT)), 0.0, 1.0)
        merged = 0.5 * (total - size) + keep * size
        normed = (h_ref[:, cols] - vec_ref[0:1, cols]) * vec_ref[1:2, cols]
        normed_ref[:, cols] = normed.astype(jnp.bfloat16)
        before = normed * vec_ref[2:3, cols] + vec_ref[3:4, cols] + x_ref[:, cols].astype(jnp.float32)
        phi, bell = tail_and_bell(before)
        z_ref[:, cols] = (before * phi).astype(jnp.bfloat16)
        flow = merged * (phi + before * bell * DENSITY)
        flow_ref[:, cols] = flow.astype(flow_ref.dtype)
        stat_ref[:8, cols] += fold(flow)
        stat_ref[8:, cols] += fold(flow * normed)
    out_ref[...] = jnp.dot(z_ref[...], top_ref[...], preferred_element_type=jnp.float32)
    sent_ref[pl.ds(pl.multiple_of(step * rows, rows), rows)] = jnp.dot(
        z_ref[...], top_peer_ref[...], preferred_element_type=jnp.float32
    ).astype(jnp.bfloat16)
    acc_ref[:half] += lax.dot_general(cot_ref[...], z_ref[...], ROWS_ROWS, preferred_element_type=jnp.float32)
    acc_ref[half:] += lax.dot_general(cot_peer_ref[...], z_ref[...], ROWS_ROWS, preferred_element_type=jnp.float32)

    @pl.when(step == last)
    def _():
        mine = pl.multiple_of(task * half, half)
        peer = pl.multiple_of((1 - task) * half, half)
        grad_ref[:, pl.ds(mine, half)] = acc_ref[:half].T.astype(jnp.bfloat16)
        grad_ref[:, pl.ds(peer, half)] = acc_ref[half:].T.astype(jnp.bfloat16)
        send(last).start()

    def after():
        lax.fori_loop(0, last + 1, lambda index, carry: (send(index).wait(), carry)[1], 0)

    return after


def wide(mask, width):
    return jnp.concatenate([mask] * (width // mask.shape[1]), axis=1)


def gather_stats(stat_ref, hidden, first):
    @pl.when(first)
    def _():
        stat_ref[:16] = jnp.zeros_like(stat_ref[:16])
        mean = jnp.sum(hidden, axis=0, keepdims=True) / hidden.shape[0]
        stat_ref[16:] = jnp.broadcast_to(mean, stat_ref[16:].shape)

    away = hidden - stat_ref[16:17]
    stat_ref[:8] += fold(away)
    stat_ref[8:16] += fold(away * away)


def normal(hidden, vec_ref):
    return (hidden - vec_ref[0:1]) * vec_ref[1:2]


def squeeze_kernel(x_ref, w_ref, out_ref, stat_ref):
    hidden = jnp.dot(x_ref[...], w_ref[...], preferred_element_type=jnp.float32)
    out_ref[...] = hidden
    gather_stats(stat_ref, hidden, pl.program_id(0) == 0)


def mesh_kernel(h_ref, vec_ref, mask_ref, w_ref, out_ref, side_ref, stat_ref, pad_ref):
    rows, mid = h_ref.shape
    inner = pl.ds(SIDE, rows)
    before = normal(h_ref[...], vec_ref) * vec_ref[2:3] + vec_ref[3:4]
    phi, _ = tail_and_bell(before)
    low = (before * phi).astype(jnp.bfloat16)
    kept = low.astype(jnp.float32)
    left = wide(mask_ref[:, :128].astype(jnp.float32), mid)
    right = wide(mask_ref[:, 128:256].astype(jnp.float32), mid)

    @pl.when(pl.program_id(0) == 0)
    def _():
        pad_ref[:SIDE] = jnp.zeros_like(pad_ref[:SIDE])
        pad_ref[SIDE + rows :] = jnp.zeros_like(pad_ref[:SIDE])

    pad_ref[inner, :mid] = (pltpu.roll(kept, 1, 0) * left).astype(jnp.bfloat16)
    pad_ref[inner, mid : 2 * mid] = low
    pad_ref[inner, 2 * mid :] = (pltpu.roll(kept, rows - 1, 0) * right).astype(jnp.bfloat16)
    side_ref[...] = pad_ref[inner].T
    above = wide(mask_ref[:, 256:384], 3 * mid)
    below = wide(mask_ref[:, 384:], 3 * mid)
    hidden = jnp.dot(pad_ref[inner], w_ref[3 * mid : 6 * mid], preferred_element_type=jnp.float32)
    hidden += jnp.dot(pad_ref[:rows] * above, w_ref[: 3 * mid], preferred_element_type=jnp.float32)
    hidden += jnp.dot(pad_ref[2 * SIDE :] * below, w_ref[6 * mid :], preferred_element_type=jnp.float32)
    out_ref[...] = hidden
    gather_stats(stat_ref, hidden, pl.program_id(0) == 0)


def widen_kernel(h_ref, vec_ref, w_ref, out_ref, low_ref, stat_ref):
    before = normal(h_ref[...], vec_ref) * vec_ref[2:3] + vec_ref[3:4]
    phi, _ = tail_and_bell(before)
    low = (before * phi).astype(jnp.bfloat16)
    low_ref[...] = low.T
    hidden = jnp.dot(low, w_ref[...], preferred_element_type=jnp.float32)
    out_ref[...] = hidden
    gather_stats(stat_ref, hidden, pl.program_id(0) == 0)


def norm_grad(upstream, normed, vec_ref):
    return vec_ref[4:5] * (upstream - vec_ref[5:6] - normed * vec_ref[6:7])


def act_slope(value):
    phi, bell = tail_and_bell(value)
    return phi + value * bell * DENSITY


def gather_flow(stat_ref, flow, normed, first):
    @pl.when(first)
    def _():
        stat_ref[...] = jnp.zeros_like(stat_ref)

    stat_ref[:8] += fold(flow)
    stat_ref[8:16] += fold(flow * normed)


def narrow_kernel(flow_ref, normed_ref, vec_ref, two_ref, vectwo_ref, low_ref, w_ref, out_ref, grad_ref, stat_ref, dh_ref):
    step = pl.program_id(0)
    rows = flow_ref.shape[0]
    dh = norm_grad(flow_ref[...].astype(jnp.float32), normed_ref[...].astype(jnp.float32), vec_ref)
    low = dh.astype(jnp.bfloat16)
    dh_ref[pl.ds(pl.multiple_of(step * rows, rows), rows)] = low
    dq = lax.dot_general(low, w_ref[...], COLS_COLS, preferred_element_type=jnp.float32)
    normed = normal(two_ref[...], vectwo_ref)
    flow = dq * act_slope(normed * vectwo_ref[2:3] + vectwo_ref[3:4])
    out_ref[...] = flow
    gather_flow(stat_ref, flow, normed, step == 0)


def narrow_fill(flow_ref, normed_ref, vec_ref, two_ref, vectwo_ref, low_ref, w_ref, out_ref, grad_ref, stat_ref, dh_ref):
    half = dh_ref.shape[1] // 2

    def part(index):
        def run():
            def one(i, carry):
                cols = pl.ds(pl.multiple_of(index * half + i * 512, 512), 512)
                grad_ref[:, cols] = jnp.dot(
                    low_ref[...], dh_ref[:, cols], preferred_element_type=jnp.float32
                ).astype(jnp.bfloat16)
                return carry

            lax.fori_loop(0, half // 512, one, 0)

        return run

    return part(0), part(1)


def across(source, target, sems):
    return pltpu.make_async_remote_copy(
        src_ref=source,
        dst_ref=target,
        send_sem=sems.at[0],
        recv_sem=sems.at[1],
        device_id=(1 - lax.axis_index("task"), lax.axis_index("batch")),
        device_id_type=MESH,
    )


def tiled(kernel, tile, moving, flags, outs, fixed, scratch, name, stats=None, send=None, far=(), fill=None, turns=()):
    tasks = lax.axis_size("task")
    batch = lax.axis_size("batch")
    rows = moving[0].shape[0]

    def block(array):
        return pl.BlockSpec((tile,) + array.shape[1:], lambda i: (i,) + (0,) * (len(array.shape) - 1))

    def turned(array):
        return pl.BlockSpec((array.shape[0], tile), lambda i: (0, i))

    def whole(array):
        zeros = (0,) * len(array.shape)
        return pl.BlockSpec(array.shape, lambda i: zeros)

    hbm = pl.BlockSpec(memory_space=pl.ANY)
    operands = list(moving)
    in_specs = [block(a) if m else whole(a) for a, m in zip(moving, flags)]
    out_shape = outs + fixed + list(far)
    out_specs = [turned(a) if i in turns else block(a) for i, a in enumerate(outs)] + [whole(a) for a in fixed] + [hbm for a in far]
    scratch = list(scratch)
    params = dict(vmem_limit_bytes=VMEM_BYTES)
    ins, made, held = len(operands), len(out_shape), len(scratch)
    run = kernel
    if stats is not None:
        vec, forward, ident = stats
        width = vec.shape[1]
        params.update(collective_id=ident, has_side_effects=True)
        operands.append(vec)
        in_specs.append(whole(vec))
        out_shape = out_shape + [shape32(16, width)]
        out_specs = out_specs + [whole(out_shape[-1])]
        scratch = scratch + [pltpu.VMEM((24 if forward else 16, width), jnp.float32)]
        scratch = scratch + Exchange.scratch(tasks, batch, width)
        if send is not None:
            operands.append(send)
            in_specs.append(hbm)
            out_shape = out_shape + [jax.ShapeDtypeStruct(send.shape, send.dtype)]
            out_specs = out_specs + [hbm]
            scratch = scratch + [pltpu.SemaphoreType.DMA((2,))]

        def run(*refs):
            refs = list(refs)
            take = lambda n: [refs.pop(0) for _ in range(n)]
            used = take(ins)
            vec_ref = take(1)[0]
            source = take(1)[0] if send is not None else None
            given = take(made)
            out_ref = take(1)[0]
            target = take(1)[0] if send is not None else None
            own = take(held)
            stat_ref = take(1)[0]
            exchange = Exchange(tasks, batch, *take(6))
            step = pl.program_id(0)
            last = pl.num_programs(0) - 1

            @pl.when(step == 0)
            def _():
                exchange.greet()

            early = send is not None or len(far) > 0
            if early:

                @pl.when(step == 1)
                def _():
                    exchange.met()
                    if send is not None:
                        across(source, target, refs[0]).start()

            after = kernel(*used, *given, stat_ref, *own)

            @pl.when(step == last)
            def _():
                if not early:
                    exchange.met()
                fillers = (None, None) if fill is None else fill(*used, *given, stat_ref, *own)
                settle_stats(exchange, stat_ref, vec_ref, out_ref, rows, rows * tasks * batch, forward, fillers)
                if send is not None:
                    across(source, target, refs[0]).wait()
                if after is not None:
                    after()

    return pl.pallas_call(
        run,
        grid=(rows // tile,),
        out_shape=out_shape,
        in_specs=in_specs,
        out_specs=out_specs,
        scratch_shapes=scratch,
        compiler_params=pltpu.CompilerParams(**params),
        name=name,
    )(*operands)


def shape32(*shape):
    return jax.ShapeDtypeStruct(shape, jnp.float32)


def shape16(*shape):
    return jax.ShapeDtypeStruct(shape, jnp.bfloat16)


def squeeze(flat_in, w_reduce, stats, tile):
    rows, mid = flat_in.shape[0], w_reduce.shape[1]
    return tiled(squeeze_kernel, tile, [flat_in, w_reduce], [1, 0], [shape32(rows, mid)], [], [], "squeeze", stats)


def mesh_forward(h_one, vec, masks, taps, stats, send, tile):
    rows, mid = h_one.shape
    return tiled(
        mesh_kernel, tile, [h_one, vec, masks, taps], [1, 0, 1, 0],
        [shape32(rows, mid), shape16(3 * mid, rows)], [],
        [pltpu.VMEM((tile + 2 * SIDE, 3 * mid), jnp.bfloat16)], "mesh_forward", stats, send, turns=(1,),
    )


def widen(h_two, vec, w_expand, stats, send, tile):
    rows, mid = h_two.shape
    width = w_expand.shape[1]
    return tiled(
        widen_kernel, tile, [h_two, vec, w_expand], [1, 0, 0],
        [shape32(rows, width), shape16(mid, rows)], [], [], "widen", stats, send, turns=(1,),
    )


def narrow(flow, normed, vec_three, h_two, vec_two, q_two, w_expand, stats, tile):
    rows, mid = h_two.shape
    width = w_expand.shape[1]
    return tiled(
        narrow_kernel, tile, [flow, normed, vec_three, h_two, vec_two, q_two, w_expand], [1, 1, 0, 1, 0, 0, 0],
        [shape32(rows, mid)], [shape16(mid, width)], [pltpu.VMEM((rows, width), jnp.bfloat16)], "narrow", stats,
        fill=narrow_fill,
    )


def crown(h_three, flat_in, limits, cot, cot_peer, top, top_peer, vec, stats, tile, piece):
    rows, width = flat_in.shape
    half = cot.shape[1]
    return tiled(
        functools.partial(crown_kernel, piece), tile,
        [h_three, flat_in, limits, cot, cot_peer, top, top_peer, vec], [1, 1, 1, 1, 1, 0, 0, 0],
        [shape32(rows, half), shape16(rows, width), shape16(rows, width)], [shape16(width, 2 * half)],
        [
            pltpu.VMEM((tile, width), jnp.bfloat16),
            pltpu.VMEM((2 * half, width), jnp.float32),
            pltpu.VMEM((rows, half), jnp.bfloat16),
            pltpu.SemaphoreType.DMA((rows // tile, 2)),
        ],
        "crown", stats, None, [shape16(rows, half)],
    )


class Stream:
    def __init__(self, view, held, sems):
        self.view, self.held, self.sems = view, held, sems

    def copy(self, index):
        slot = lax.rem(index, 2)
        return pltpu.make_async_copy(self.view(index), self.held.at[slot], self.sems.at[slot])

    def start(self, index):
        self.copy(index).start()

    def take(self, index, count):
        self.copy(index).wait()

        @pl.when(index + 1 < count)
        def _():
            self.start(index + 1)

        return self.held.at[lax.rem(index, 2)]


def back_kernel(rows, tasks, batch, tile, *refs):
    refs = list(refs)

    def take(count):
        return [refs.pop(0) for _ in range(count)]

    (flow_hbm, two_hbm, one_hbm, side_hbm, mask_hbm, w_hbm, x_hbm, up_hbm, top_hbm, heads_hbm, expand_hbm) = take(11)
    vectwo_ref, vecone_ref = take(2)
    (out_hbm, heads_out, expand_out, spatial_out, reduce_out, vec_ref) = take(6)
    (two_buf, mask_buf, x_buf, up_buf, out_buf) = take(5)
    (side_ref, lane_ref, flow_ref, w_ref, top_ref) = take(5)
    small = up_buf.shape[1]
    heads_work, expand_work, spatial_work, reduce_work, stat_ref = take(5)
    pair_sems, whole_sems, flow_sems = take(3)
    exchange = Exchange(tasks, batch, *take(6))
    grid = Grid(batch)
    mid = flow_hbm.shape[1]
    width = x_hbm.shape[1]
    spans = rows // tile

    def blocks(ref, height):
        return lambda index: ref.at[pl.ds(pl.multiple_of(index * height, height), height)]

    exchange.greet()

    def flow_load(index):
        return pltpu.make_async_copy(
            blocks(flow_hbm, tile)(index), blocks(flow_ref, tile)(index), flow_sems.at[index]
        )

    twos = Stream(blocks(two_hbm, tile), two_buf, pair_sems.at[1])
    masks = Stream(blocks(mask_hbm, tile), mask_buf, pair_sems.at[2])
    ones = Stream(blocks(one_hbm, tile), two_buf, pair_sems.at[3])
    ups = Stream(blocks(up_hbm, small), up_buf, pair_sems.at[4])
    dh_ref, normed_ref, dht_ref = lane_ref.at[:, :mid], lane_ref.at[:, mid : 2 * mid], side_ref.at[:mid]
    across_cols = x_buf.shape[2]
    columns = Stream(
        lambda index: x_hbm.at[:, pl.ds(pl.multiple_of(index * across_cols, across_cols), across_cols)],
        x_buf, pair_sems.at[5],
    )
    loads = [
        pltpu.make_async_copy(source, target, whole_sems.at[index])
        for index, (source, target) in enumerate(
            [(heads_hbm, heads_work), (side_hbm, side_ref), (expand_hbm, expand_work), (w_hbm, w_ref), (top_hbm, top_ref)]
        )
    ]
    heads_load, side_load, expand_load, w_load, top_load = loads
    heads_load.start()
    for stream in (twos, masks):
        stream.start(0)
    for index in range(spans):
        flow_load(index).start()
    for load in loads[1:]:
        load.start()

    third = spatial_work.shape[0] // 3
    works = [(heads_work, heads_out, False), (expand_work, expand_out, True)]
    for index in range(3):
        span = pl.ds(index * third, third)
        works.append((spatial_work.at[span], spatial_out.at[span], False))
    for index in range(2):
        span = pl.ds(index * width // 2, width // 2)
        works.append((reduce_work.at[span], reduce_out.at[span], False))
    reductions = [Reduction(grid, work, out, *take(10), wide) for work, out, wide in works]

    def tick(name):
        for item, stage in AGENDA.get(name, ()):
            reductions[item].stage(stage)

    def ticks(name, index, count, scale=1, shift=0):
        for step in range(count):
            label = "%s%d" % (name, step * scale + shift)
            if label in AGENDA:

                @pl.when(index == step)
                def _():
                    tick(label)

    def lanes(index, carry):
        span = pl.ds(pl.multiple_of(index * tile, tile), tile)
        flow_load(index).wait()
        flow = flow_ref[span]
        normed = normal(twos.take(index, spans)[...], vectwo_ref)
        mask = masks.take(index, spans)
        dh = norm_grad(flow, normed, vectwo_ref)
        above = wide(mask[:, 256:384].astype(jnp.float32), mid)
        below = wide(mask[:, 384:].astype(jnp.float32), mid)
        low = jnp.bfloat16
        zero = jnp.zeros((SIDE, mid), low)
        lane_ref[span, mid : 2 * mid] = dh.astype(low)
        lane_ref[span, :mid] = jnp.concatenate([(dh * above)[SIDE:].astype(low), zero], axis=0)
        lane_ref[span, 2 * mid :] = jnp.concatenate([zero, (dh * below)[: tile - SIDE].astype(low)], axis=0)
        ticks("lane", index, 4)
        return carry

    exchange.met()
    heads_load.wait()
    expand_load.wait()
    tick("start")
    lax.fori_loop(0, spans, lanes, 0)
    masks.start(0)
    ones.start(0)
    side_load.wait()

    def spatial(index, carry):
        a, b = index // 3, lax.rem(index, 3)
        rows_here = pl.ds(pl.multiple_of(b * mid, mid), mid)
        cols = pl.ds(pl.multiple_of(a * mid, mid), mid)
        part = jnp.dot(side_ref[rows_here], lane_ref[:, cols], preferred_element_type=jnp.float32)
        spatial_work[pl.ds(pl.multiple_of(index * mid, mid), mid)] = part.astype(jnp.bfloat16)
        ticks("sp", index, 9)
        return carry

    lax.fori_loop(0, 9, spatial, 0)
    w_load.wait()

    def taps(index, carry):
        span = pl.ds(pl.multiple_of(index * tile, tile), tile)
        mask = masks.take(index, spans)
        pieces = []
        for b in range(3):
            total = None
            for a in range(3):
                part = lax.dot_general(
                    lane_ref[span, a * mid : (a + 1) * mid], w_ref[3 * a + b], COLS_COLS,
                    preferred_element_type=jnp.float32,
                )
                total = part if total is None else total + part
            pieces.append(total)
            if b < 2:
                ticks("tap", index, 4, 3, b)
        left = wide(mask[:, :128].astype(jnp.float32), mid)
        right = wide(mask[:, 128:256].astype(jnp.float32), mid)
        dq = pieces[1] + pltpu.roll(pieces[0] * left, tile - 1, 0) + pltpu.roll(pieces[2] * right, 1, 0)
        normed = normal(ones.take(index, spans)[...], vecone_ref)
        flow = dq * act_slope(normed * vecone_ref[2:3] + vecone_ref[3:4])
        flow_ref[span] = flow
        normed_ref[span] = normed.astype(jnp.bfloat16)
        gather_flow(stat_ref, flow, normed, index == 0)
        ticks("tap", index, 4, 3, 2)
        return carry

    lax.fori_loop(0, spans, taps, 0)
    columns.start(0)
    ups.start(0)
    settle_stats(exchange, stat_ref, vecone_ref, vec_ref, rows, rows * tasks * batch, False)
    tick("xch")

    def inner(index, carry):
        span = pl.ds(pl.multiple_of(index * tile, tile), tile)
        dh = norm_grad(flow_ref[span], normed_ref[span].astype(jnp.float32), vec_ref)
        dh_ref[span] = dh.astype(jnp.bfloat16)
        dht_ref[:, span] = dh.T.astype(jnp.bfloat16)
        return carry

    lax.fori_loop(0, spans, inner, 0)
    tick("inner")
    count = width // across_cols

    def reduce(index, carry):
        part = jnp.dot(dht_ref[...], columns.take(index, count)[...], preferred_element_type=jnp.float32)
        span = pl.ds(pl.multiple_of(index * across_cols, across_cols), across_cols)
        reduce_work[span] = part.T.astype(jnp.bfloat16)
        ticks("red", index, 4)
        return carry

    lax.fori_loop(0, count, reduce, 0)
    top_load.wait()

    def store(index):
        slot = lax.rem(index, 2)
        return pltpu.make_async_copy(out_buf.at[slot], blocks(out_hbm, small)(index), pair_sems.at[6, slot])

    def inputs(index, carry):
        span = pl.ds(pl.multiple_of(index * small, small), small)
        up = ups.take(index, rows // small)

        @pl.when(index >= 2)
        def _():
            store(index - 2).wait()

        slot = lax.rem(index, 2)
        for start in range(0, width, across_cols):
            cols = pl.ds(start, across_cols)
            part = lax.dot_general(dh_ref[span], top_ref[cols], COLS_COLS, preferred_element_type=jnp.float32)
            out_buf[slot, :, cols] = (up[:, cols].astype(jnp.float32) + part).astype(jnp.bfloat16)
        store(index).start()
        ticks("inp", index, 8)
        return carry

    lax.fori_loop(0, rows // small, inputs, 0)
    for index in range(rows // small - 2, rows // small):
        store(index).wait()
    tick("tail")


def back(flow, h_two, vec_two, h_one, vec_one, sides, masks, w_spatial, flat_in, up, w_reduce, heads, expand, ident, tile):
    tasks = lax.axis_size("task")
    batch = lax.axis_size("batch")
    far = batch // LOW
    rows, mid = h_one.shape
    width = flat_in.shape[1]
    full, low = jnp.float32, jnp.bfloat16
    cols = 512
    hbm = pl.BlockSpec(memory_space=pl.ANY)
    vmem = pl.BlockSpec(memory_space=pltpu.VMEM)
    shapes = [(heads.shape, False), (expand.shape, True)] + [((3 * mid, mid), False)] * 3
    shapes += [((width // 2, mid), False)] * 2
    scratch = [
        pltpu.VMEM((2, tile, mid), full),
        pltpu.VMEM((2, tile, 512), low),
        pltpu.VMEM((2, rows, cols), low),
        pltpu.VMEM((2, 256, width), low),
        pltpu.VMEM((2, 256, width), low),
        pltpu.VMEM((3 * mid, rows), low),
        pltpu.VMEM((rows, 3 * mid), low),
        pltpu.VMEM((rows, mid), full),
        pltpu.VMEM(w_spatial.shape, low),
        pltpu.VMEM(w_reduce.shape, low),
        pltpu.VMEM(heads.shape, low),
        pltpu.VMEM(expand.shape, low),
        pltpu.VMEM((9 * mid, mid), low),
        pltpu.VMEM((width, mid), low),
        pltpu.VMEM((16, mid), full),
        pltpu.SemaphoreType.DMA((7, 2)),
        pltpu.SemaphoreType.DMA((5,)),
        pltpu.SemaphoreType.DMA((rows // tile,)),
    ] + Exchange.scratch(tasks, batch, mid)
    for (high, across_), is_wide in shapes:
        scratch += Reduction.scratch(high, across_, is_wide, far)
    return pl.pallas_call(
        functools.partial(back_kernel, rows, tasks, batch, tile),
        out_shape=[
            shape16(rows, width), shape16(*heads.shape), shape16(*expand.shape), shape16(9 * mid, mid),
            shape16(width, mid), shape32(16, mid),
        ],
        in_specs=[hbm] * 11 + [vmem] * 2,
        out_specs=[hbm] * 5 + [vmem],
        scratch_shapes=scratch,
        compiler_params=pltpu.CompilerParams(
            vmem_limit_bytes=VMEM_BYTES, collective_id=ident, has_side_effects=True
        ),
        name="back",
    )(flow, h_two, h_one, sides, masks, w_spatial, flat_in, up, w_reduce, heads, expand, vec_two, vec_one)


def body(
    inputs,
    crop_cuts,
    threshold,
    w_reduce,
    w_spatial,
    w_expand,
    w_heads,
    gain_one,
    bias_one,
    gain_two,
    bias_two,
    gain_three,
    bias_three,
    cotangent,
):
    low = jnp.bfloat16
    full = jnp.float32
    canvases, pixels, width = inputs.shape[1:]
    mid = w_reduce.shape[1]
    rows = canvases * pixels
    half = w_heads.shape[2]
    task = lax.axis_index("task")
    cot = cotangent.reshape(2, rows, half)
    cot_mine = lax.dynamic_index_in_dim(cot, task, 0, keepdims=False)
    cot_sent = lax.dynamic_index_in_dim(cot, 1 - task, 0, keepdims=False)
    top_mine = w_heads[0]

    def params(gain, bias):
        zero = jnp.zeros_like(gain)
        return jnp.stack([zero, zero, gain, bias, zero, zero, zero, zero])

    lines = jnp.arange(SIDE, dtype=jnp.int32)
    cuts = crop_cuts.reshape(canvases, 2)
    from_above = jnp.logical_not((lines == cuts[:, 0:1]) | (lines == 0)[None, :])
    from_left = jnp.logical_not((lines == cuts[:, 1:2]) | (lines == 0)[None, :])
    from_below = jnp.pad(from_above[:, 1:], ((0, 0), (0, 1)))
    from_right = jnp.pad(from_left[:, 1:], ((0, 0), (0, 1)))
    shape = (canvases, SIDE, SIDE, 128)
    masks = jnp.concatenate(
        [jnp.broadcast_to(m[:, None, :, None], shape) for m in (from_left, from_right)]
        + [jnp.broadcast_to(m[:, :, None, None], shape) for m in (from_above, from_below)],
        axis=3,
    ).astype(low).reshape(rows, 512)

    flat_in = inputs.reshape(rows, width)
    h_one, vec_one = squeeze(flat_in, w_reduce, (params(gain_one, bias_one), True, 0), min(rows, 512))
    h_two, sides, vec_two, cot_peer = mesh_forward(
        h_one, vec_one, masks, w_spatial.reshape(9 * mid, mid), (params(gain_two, bias_two), True, 1), cot_sent, pixels
    )
    h_three, q_two, vec_three, top_peer = widen(
        h_two, vec_two, w_expand, (params(gain_three, bias_three), True, 2), top_mine, pixels
    )
    out_mine, flow, normed, grad_heads, out_peer, vec_three = crown(
        h_three, flat_in, threshold.reshape(rows, width), cot_mine, cot_peer, top_mine, top_peer, vec_three,
        (vec_three, False, 3), pixels, 256,
    )
    out_peer = out_peer.astype(full)
    first = jnp.where(task == 0, out_mine, out_peer)
    second = jnp.where(task == 0, out_peer, out_mine)
    head_out = jnp.stack([first, second]).reshape(1, 2, canvases, pixels, half)
    flow_two, grad_expand, vec_two = narrow(
        flow, normed, vec_three, h_two, vec_two, q_two, w_expand, (vec_two, False, 4), min(rows, 512)
    )
    grad_inputs, grad_heads, grad_expand, grad_spatial, grad_reduce, vec_one = back(
        flow_two, h_two, vec_two, h_one, vec_one, sides, masks, w_spatial, flat_in, flow, w_reduce,
        grad_heads, grad_expand, 5, min(rows, 512),
    )
    grad_heads = lax.dynamic_slice_in_dim(grad_heads, task * half, half, axis=1)
    return (
        head_out,
        grad_inputs.reshape(inputs.shape),
        grad_reduce.astype(full),
        grad_spatial.reshape(w_spatial.shape).astype(full),
        grad_expand.astype(full),
        grad_heads.astype(full)[None],
        vec_one[9],
        vec_one[8],
        vec_two[9],
        vec_two[8],
        vec_three[9],
        vec_three[8],
    )


def solution(mesh):
    in_specs = (
        P("task", "batch", None, None),
        P("task", "batch", None),
        P("task", "batch", None, None),
        P(),
        P(),
        P(),
        P("task", None, None),
        P(),
        P(),
        P(),
        P(),
        P(),
        P(),
        P("task", None, "batch", None, None),
    )
    out_specs = (
        P("task", None, "batch", None, None),
        P("task", "batch", None, None),
        P(),
        P(),
        P(),
        P("task", None, None),
        P(),
        P(),
        P(),
        P(),
        P(),
        P(),
    )
    return jax.shard_map(body, mesh=mesh, in_specs=in_specs, out_specs=out_specs, check_vma=False)
```

```python
import functools
import math

import jax
import jax.numpy as jnp
from jax import lax
from jax.experimental import pallas as pl
from jax.experimental.pallas import tpu as pltpu
from jax.sharding import PartitionSpec as P

SIDE = 16
EPS = 1e-05
FLOOR = 0.1
SOFT = 0.25
ROOT_HALF = 0.7071067811865476
DENSITY = 0.3989422804014327
LOG2E = 1.4426950408889634
ERF_P = 0.3275911
ERF_A = (0.254829592, -0.284496736, 1.421413741, -1.453152027, 1.061405429)
ROWS_ROWS = (((0,), (0,)), ((), ()))
COLS_COLS = (((1,), (1,)), ((), ()))
MESH = pl.DeviceIdType.MESH
LOW = 4
VMEM_BYTES = 62 * 2**20


AGENDA = {
    "start": ((0, 0), (1, 0),),
    "lane1": ((0, 1),),
    "lane2": ((1, 1),),
    "sp2": ((2, 0),),
    "sp3": ((0, 2),),
    "sp4": ((2, 1),),
    "sp5": ((3, 0),),
    "sp7": ((1, 2), (3, 1),),
    "sp8": ((4, 0),),
    "tap0": ((0, 3),),
    "tap1": ((4, 1),),
    "tap2": ((2, 2),),
    "tap4": ((1, 3),),
    "tap5": ((0, 4),),
    "tap6": ((3, 2),),
    "tap9": ((1, 4), (4, 2),),
    "tap10": ((2, 3),),
    "xch": ((0, 5), (1, 5), (3, 3), (4, 3),),
    "inner": ((0, 6), (2, 4),),
    "red1": ((1, 6), (5, 0),),
    "red2": ((3, 4), (5, 1),),
    "red3": ((6, 0),),
    "tail": ((4, 4), (0, 7), (6, 1), (0, 8), (2, 5), (1, 7), (3, 5), (5, 2), (1, 8), (6, 2), (4, 5), (2, 6), (3, 6), (5, 3), (6, 3), (4, 6), (5, 4), (2, 7), (6, 4), (2, 8), (3, 7), (5, 5), (3, 8), (6, 5), (4, 7), (5, 6), (4, 8), (6, 6), (5, 7), (5, 8), (6, 7), (6, 8),),
}


class Reduction:
    def __init__(self, grid, work, result, core, first, second, last, done, send, recv, far_send, far_recv, local, wide):
        self.grid, self.work, self.result = grid, work, result
        self.room, self.done = (core, first, second, last), done
        self.send, self.recv, self.far_send, self.far_recv = send, recv, far_send, far_recv
        self.local = local
        self.wide = wide
        self.rows, self.cols = work.shape
        sizes = self.sizes(self.rows, self.cols, wide, grid.far)
        self.pieces = sizes[2][0] // sizes[3][0]
        self.mine = lax.rem(grid.high, self.pieces)

    @staticmethod
    def sizes(rows, cols, wide, far):
        if wide:
            core = (rows, cols // 2)
            first = (rows, cols // 8)
            second = (rows, cols // 16)
        else:
            core = (rows // 2, cols)
            first = (rows // 2, cols // 4)
            second = (rows // 4, cols // 4)
        pieces = max(n for n in range(1, far + 1) if far % n == 0 and second[0] % (8 * n) == 0)
        return core, first, second, (second[0] // pieces, second[1])

    @staticmethod
    def scratch(rows, cols, wide, far):
        core, first, second, last = Reduction.sizes(rows, cols, wide, far)
        return [
            pltpu.VMEM(core, jnp.bfloat16),
            pltpu.VMEM((2,) + first, jnp.bfloat16),
            pltpu.VMEM((2,) + second, jnp.bfloat16),
            pltpu.VMEM((2, far) + last, jnp.bfloat16),
            pltpu.VMEM((2,) + last, jnp.bfloat16),
            pltpu.SemaphoreType.DMA((10,)),
            pltpu.SemaphoreType.DMA((10,)),
            pltpu.SemaphoreType.DMA((4, far)),
            pltpu.SemaphoreType.DMA((4, far)),
            pltpu.SemaphoreType.DMA((2,)),
        ]

    def view(self, core, part=None, first=None, second=None, piece=None, done=False):
        sizes = self.sizes(self.rows, self.cols, self.wide, self.grid.far)
        row = col = 0
        shape = sizes[0]
        if self.wide:
            col = core * (self.cols // 2)
            if part is not None:
                col = col + part * (self.cols // 4) + first * (self.cols // 8)
                shape = sizes[1]
            if second is not None:
                col = col + second * (self.cols // 16)
                shape = sizes[2]
        else:
            row = core * (self.rows // 2)
            if part is not None:
                col = part * (self.cols // 2) + first * (self.cols // 4)
                shape = sizes[1]
            if second is not None:
                row = row + second * (self.rows // 4)
                shape = sizes[2]
        if piece is not None:
            row = row + piece * sizes[3][0]
            shape = sizes[3]
        if not isinstance(row, int):
            row = pl.multiple_of(row, shape[0] & -shape[0])
        if not isinstance(col, int):
            col = pl.multiple_of(col, 128)
        ref = self.result if done else self.work
        return ref.at[pl.ds(row, shape[0]), pl.ds(col, shape[1])]

    def swap(self, index):
        grid = self.grid
        part = (index + 1) % 2
        bits = grid.bits(part)
        if index == 0:
            source, target, device = self.view(1 - grid.core), self.room[0], grid.core_peer
        elif index < 3:
            source, target = self.view(grid.core, part, 1 - bits[0]), self.room[1].at[part]
            device = grid.peers(part)[0]
        elif index < 5:
            source, target = self.view(grid.core, part, bits[0], 1 - bits[1]), self.room[2].at[part]
            device = grid.peers(part)[1]
        elif index < 7:
            source = self.view(grid.core, part, bits[0], bits[1], done=True)
            target, device = source, grid.peers(part)[1]
        elif index < 9:
            source = self.view(grid.core, part, bits[0], done=True)
            target, device = source, grid.peers(part)[0]
        else:
            source = self.view(grid.core, done=True)
            target, device = source, grid.core_peer
        return pltpu.make_async_remote_copy(
            src_ref=source,
            dst_ref=target,
            send_sem=self.send.at[index],
            recv_sem=self.recv.at[index],
            device_id=device,
            device_id_type=MESH,
        )

    def add(self, target, sources):
        rows = target.shape[0]
        step = math.gcd(rows, 64)

        def one(i, carry):
            span = pl.ds(pl.multiple_of(i * step, step), step)
            total = sources[0][span].astype(jnp.float32)
            for source in sources[1:]:
                total = total + source[span].astype(jnp.float32)
            target[span] = total.astype(jnp.bfloat16)
            return carry

        lax.fori_loop(0, rows // step, one, 0)

    def join(self, mine, received):
        self.add(mine, [mine, received])

    def far_copy(self, part, step, back, inward):
        grid = self.grid
        bits = grid.bits(part)
        if back:
            first = grid.high - self.mine
            slot = first + lax.rem(self.mine + step, self.pieces)
            owner = slot if inward else grid.high
            source = self.done.at[part]
            target = self.view(grid.core, part, bits[0], bits[1], lax.rem(owner, self.pieces), True)
        else:
            slot = lax.rem(grid.high + step, grid.far)
            owner = slot if inward else grid.high
            source = self.view(grid.core, part, bits[0], bits[1], lax.rem(slot, self.pieces))
            target = self.room[3].at[part, owner]
        line = 2 * part + (1 if back else 0)
        return pltpu.make_async_remote_copy(
            src_ref=source,
            dst_ref=target,
            send_sem=self.far_send.at[line, step],
            recv_sem=self.far_recv.at[line, owner],
            device_id=(grid.task, slot * LOW + grid.low),
            device_id_type=MESH,
        )

    def far_start(self, back):
        for part in range(2):
            for step in range(1, self.pieces if back else self.grid.far):
                self.far_copy(part, step, back, False).start()

    def far_settle(self, back):
        for part in range(2):
            for step in range(1, self.pieces if back else self.grid.far):
                self.far_copy(part, step, back, True).wait_recv()
                self.far_copy(part, step, back, False).wait_send()

    def keep(self, part):
        bits = self.grid.bits(part)
        mine = self.view(self.grid.core, part, bits[0], bits[1], self.mine, True)
        return pltpu.make_async_copy(self.done.at[part], mine, self.local.at[part])

    def stage(self, index):
        grid = self.grid
        if index == 0:
            self.swap(0).start()
        elif index == 1:
            self.swap(0).wait()
            self.join(self.view(grid.core), self.room[0])
            for part in range(2):
                self.swap(1 + part).start()
        elif index == 2:
            for part in range(2):
                self.swap(1 + part).wait()
                bits = grid.bits(part)
                self.join(self.view(grid.core, part, bits[0]), self.room[1].at[part])
                self.swap(3 + part).start()
        elif index == 3:
            for part in range(2):
                self.swap(3 + part).wait()
                bits = grid.bits(part)
                self.join(self.view(grid.core, part, bits[0], bits[1]), self.room[2].at[part])
            self.far_start(False)
        elif index == 4:
            self.far_settle(False)
            for part in range(2):
                bits = grid.bits(part)
                mine = self.view(grid.core, part, bits[0], bits[1], self.mine)
                self.room[3][part, grid.high] = mine[...]
                self.add(self.done.at[part], [self.room[3].at[part, slot] for slot in range(grid.far)])
                self.keep(part).start()
            self.far_start(True)
        elif index == 5:
            self.far_settle(True)
            for part in range(2):
                self.keep(part).wait()
                self.swap(5 + part).start()
        elif index == 6:
            for part in range(2):
                self.swap(5 + part).wait()
                self.swap(7 + part).start()
        elif index == 7:
            for part in range(2):
                self.swap(7 + part).wait()
            self.swap(9).start()
        elif index == 8:
            self.swap(9).wait()


class Grid:
    def __init__(self, batch):
        self.task = lax.axis_index("task")
        place = lax.axis_index("batch")
        self.far = batch // LOW
        self.high = place // LOW
        self.low = lax.rem(place, LOW)
        self.core = lax.rem(place, 2)
        self.y = lax.rem(place // 2, 2)
        base = place - self.low
        self.core_peer = (self.task, base + self.y * 2 + (1 - self.core))
        self.x_peer = (1 - self.task, place)
        self.y_peer = (self.task, base + (1 - self.y) * 2 + self.core)

    def bits(self, part):
        return (self.task, self.y) if part == 0 else (self.y, self.task)

    def peers(self, part):
        return (self.x_peer, self.y_peer) if part == 0 else (self.y_peer, self.x_peer)


class Exchange:
    def __init__(self, tasks, batch, near, far, near_send, near_recv, far_send, far_recv):
        place = lax.axis_index("batch")
        self.task = lax.axis_index("task")
        self.high = place // LOW
        self.low = lax.rem(place, LOW)
        self.near_size = tasks * LOW
        self.far_size = batch // LOW
        self.me_near = self.task * LOW + self.low
        self.near, self.far = near, far
        self.near_sems, self.far_sems = (near_send, near_recv), (far_send, far_recv)

    @staticmethod
    def scratch(tasks, batch, width):
        near_size, far_size = tasks * LOW, batch // LOW
        return [
            pltpu.VMEM((near_size + 1, 2, width), jnp.float32),
            pltpu.VMEM((far_size + 1, 2, width), jnp.float32),
            pltpu.SemaphoreType.DMA((near_size,)),
            pltpu.SemaphoreType.DMA((near_size,)),
            pltpu.SemaphoreType.DMA((far_size,)),
            pltpu.SemaphoreType.DMA((far_size,)),
        ]

    def near_peer(self, step):
        slot = lax.rem(self.me_near + step, self.near_size)
        return slot, (slot // LOW, self.high * LOW + lax.rem(slot, LOW))

    def far_peer(self, step):
        slot = lax.rem(self.high + step, self.far_size)
        return slot, (self.task, slot * LOW + self.low)

    def peers(self):
        near = [self.near_peer(step)[1] for step in range(1, self.near_size)]
        return near + [self.far_peer(step)[1] for step in range(1, self.far_size)]

    def greet(self):
        barrier = pltpu.get_barrier_semaphore()
        for device in self.peers():
            pl.semaphore_signal(barrier, inc=1, device_id=device, device_id_type=MESH)

    def met(self):
        pl.semaphore_wait(pltpu.get_barrier_semaphore(), self.near_size + self.far_size - 2)

    def hop(self, size, peer, me, held, sems, filler=None):
        def copy(step, slot):
            return pltpu.make_async_remote_copy(
                src_ref=held.at[size],
                dst_ref=held.at[slot],
                send_sem=sems[0].at[step],
                recv_sem=sems[1].at[slot],
                device_id=peer(step)[1],
                device_id_type=MESH,
            )

        for step in range(1, size):
            copy(step, me).start()
        held[me] = held[size]
        if filler is not None:
            filler()
        for step in range(1, size):
            copy(step, peer(step)[0]).wait_recv()
        for step in range(1, size):
            copy(step, me).wait_send()
        return held[:size]

    def run(self, total, spread, rows, forward, fillers=(None, None)):
        self.near[self.near_size, 0:1] = total
        self.near[self.near_size, 1:2] = spread
        held = self.hop(self.near_size, self.near_peer, self.me_near, self.near, self.near_sems, fillers[0])
        total, spread = join(held, float(rows), forward)
        self.far[self.far_size, 0:1] = total
        self.far[self.far_size, 1:2] = spread
        held = self.hop(self.far_size, self.far_peer, self.high, self.far, self.far_sems, fillers[1])
        return join(held, float(rows * self.near_size), forward)


def join(held, share, forward):
    sums = held[:, 0, :]
    total = jnp.sum(sums, axis=0, keepdims=True)
    spread = jnp.sum(held[:, 1, :], axis=0, keepdims=True)
    if forward:
        groups = held.shape[0]
        away = sums * (1.0 / share) - total * (1.0 / (share * groups))
        spread = spread + share * jnp.sum(away * away, axis=0, keepdims=True)
    return total, spread


def settle_stats(exchange, stat_ref, vec_ref, out_ref, rows, count, forward, fillers=(None, None)):
    first = jnp.sum(stat_ref[:8], axis=0, keepdims=True)
    second = jnp.sum(stat_ref[8:16], axis=0, keepdims=True)
    out_ref[:8] = vec_ref[:8]
    if forward:
        local = first + rows * stat_ref[16:17]
        total, spread = exchange.run(local, second - first * first * (1.0 / rows), rows, True, fillers)
        scale = lax.rsqrt(spread * (1.0 / count) + EPS)
        out_ref[0:1] = total * (1.0 / count)
        out_ref[1:2] = scale
        out_ref[4:5] = scale * vec_ref[2:3]
        out_ref[8:] = jnp.zeros_like(out_ref[8:])
    else:
        total, spread = exchange.run(first, second, rows, False, fillers)
        out_ref[5:6] = total * (1.0 / count)
        out_ref[6:7] = spread * (1.0 / count)
        out_ref[8:9] = total
        out_ref[9:10] = spread
        out_ref[10:] = jnp.zeros_like(out_ref[10:])


def tail_and_bell(value):
    bell = jnp.exp2(value * value * (-0.5 * LOG2E))
    away = jnp.abs(value)
    ratio = 1.0 / (1.0 + away * (ERF_P * ROOT_HALF))
    poly = ERF_A[4]
    for factor in ERF_A[3::-1]:
        poly = poly * ratio + factor
    tail = 0.5 * poly * ratio * bell
    return jnp.where(value >= 0, 1.0 - tail, tail), bell


def fold(array):
    total = array[:8]
    for start in range(8, array.shape[0], 8):
        total = total + array[start : start + 8]
    return total


def crown_kernel(
    piece, h_ref, x_ref, thr_ref, cot_hbm, cot_one, cot_two, top_ref, top_one, top_two, vec_ref,
    out_ref, flow_ref, normed_ref, grad_ref, came_ref, stat_ref, z_ref, acc_ref, sent_ref, sems,
    cots_ref, cots_peer_ref, top_peer_ref, local_sems, late_sems,
):
    step = pl.program_id(0)
    rows, width = x_ref.shape
    all_rows, half = cots_ref.shape
    split = all_rows // 4
    task = lax.axis_index("task")
    last = pl.num_programs(0) - 1

    def send(index):
        span = pl.ds(pl.multiple_of(index * rows, rows), rows)
        return across(sent_ref.at[span], came_ref.at[span], sems.at[index])

    core = lax.rem(lax.axis_index("batch"), 2)
    high = top_one.shape[0]
    late = across(cot_hbm.at[1 - task, pl.ds(2 * split, 2 * split)], cots_peer_ref.at[pl.ds(2 * split, 2 * split)], late_sems)

    @pl.when(step == 0)
    def _():
        pairs = [
            (cot_hbm.at[task], cots_ref),
            (cot_one, cots_peer_ref.at[pl.ds(0, split)]),
            (cot_two, cots_peer_ref.at[pl.ds(split, split)]),
            (top_one, top_peer_ref.at[pl.ds(pl.multiple_of(core * high, high), high)]),
            (top_two, top_peer_ref.at[pl.ds(pl.multiple_of((1 - core) * high, high), high)]),
        ]
        copies = [pltpu.make_async_copy(a, b, local_sems.at[i]) for i, (a, b) in enumerate(pairs)]
        for copy in copies:
            copy.start()
        for copy in copies:
            copy.wait()

    @pl.when(step == 1)
    def _():
        late.start()

    @pl.when(step == (last + 1) // 2)
    def _():
        late.wait()

    @pl.when(step > 0)
    def _():
        send(step - 1).start()

    span = pl.ds(pl.multiple_of(step * rows, rows), rows)
    cot_ref, cot_peer_ref = cots_ref.at[span], cots_peer_ref.at[span]

    @pl.when(step == 0)
    def _():
        stat_ref[...] = jnp.zeros_like(stat_ref)
        acc_ref[...] = jnp.zeros_like(acc_ref)

    for start in range(0, width, piece):
        cols = pl.ds(start, piece)
        g_one = lax.dot_general(
            cot_ref[...], top_ref[cols], COLS_COLS, preferred_element_type=jnp.float32
        ).astype(jnp.bfloat16).astype(jnp.float32)
        g_two = lax.dot_general(
            cot_peer_ref[...], top_peer_ref[cols], COLS_COLS, preferred_element_type=jnp.float32
        ).astype(jnp.bfloat16).astype(jnp.float32)
        total = g_one + g_two
        size = jnp.abs(g_one) + jnp.abs(g_two)
        share = total / jnp.maximum(size, FLOOR)
        limit = thr_ref[:, cols].astype(jnp.float32)
        keep = jnp.clip((0.5 / SOFT) * share + ((0.5 / SOFT + 0.5) - limit * (1.0 / SOFT)), 0.0, 1.0)
        merged = 0.5 * (total - size) + keep * size
        normed = (h_ref[:, cols] - vec_ref[0:1, cols]) * vec_ref[1:2, cols]
        normed_ref[:, cols] = normed.astype(jnp.bfloat16)
        before = normed * vec_ref[2:3, cols] + vec_ref[3:4, cols] + x_ref[:, cols].astype(jnp.float32)
        phi, bell = tail_and_bell(before)
        z_ref[:, cols] = (before * phi).astype(jnp.bfloat16)
        flow = merged * (phi + before * bell * DENSITY)
        flow_ref[:, cols] = flow.astype(flow_ref.dtype)
        stat_ref[:8, cols] += fold(flow)
        stat_ref[8:, cols] += fold(flow * normed)
    out_ref[...] = jnp.dot(z_ref[...], top_ref[...], preferred_element_type=jnp.float32)
    sent_ref[pl.ds(pl.multiple_of(step * rows, rows), rows)] = jnp.dot(
        z_ref[...], top_peer_ref[...], preferred_element_type=jnp.float32
    ).astype(jnp.bfloat16)
    acc_ref[:half] += lax.dot_general(cot_ref[...], z_ref[...], ROWS_ROWS, preferred_element_type=jnp.float32)
    acc_ref[half:] += lax.dot_general(cot_peer_ref[...], z_ref[...], ROWS_ROWS, preferred_element_type=jnp.float32)

    @pl.when(step == last)
    def _():
        mine = pl.multiple_of(task * half, half)
        peer = pl.multiple_of((1 - task) * half, half)
        grad_ref[:, pl.ds(mine, half)] = acc_ref[:half].T.astype(jnp.bfloat16)
        grad_ref[:, pl.ds(peer, half)] = acc_ref[half:].T.astype(jnp.bfloat16)
        send(last).start()

    def after():
        lax.fori_loop(0, last + 1, lambda index, carry: (send(index).wait(), carry)[1], 0)

    return after


def wide(mask, width):
    return jnp.concatenate([mask] * (width // mask.shape[1]), axis=1)


def gather_stats(stat_ref, hidden, first):
    @pl.when(first)
    def _():
        stat_ref[:16] = jnp.zeros_like(stat_ref[:16])
        mean = jnp.sum(hidden, axis=0, keepdims=True) / hidden.shape[0]
        stat_ref[16:] = jnp.broadcast_to(mean, stat_ref[16:].shape)

    away = hidden - stat_ref[16:17]
    stat_ref[:8] += fold(away)
    stat_ref[8:16] += fold(away * away)


def normal(hidden, vec_ref):
    return (hidden - vec_ref[0:1]) * vec_ref[1:2]


def squeeze_kernel(x_ref, w_ref, out_ref, stat_ref):
    hidden = jnp.dot(x_ref[...], w_ref[...], preferred_element_type=jnp.float32)
    out_ref[...] = hidden
    gather_stats(stat_ref, hidden, pl.program_id(0) == 0)


def mesh_kernel(h_ref, vec_ref, mask_ref, w_ref, out_ref, side_ref, stat_ref, pad_ref):
    rows, mid = h_ref.shape
    inner = pl.ds(SIDE, rows)
    before = normal(h_ref[...], vec_ref) * vec_ref[2:3] + vec_ref[3:4]
    phi, _ = tail_and_bell(before)
    low = (before * phi).astype(jnp.bfloat16)
    kept = low.astype(jnp.float32)
    left = wide(mask_ref[:, :128].astype(jnp.float32), mid)
    right = wide(mask_ref[:, 128:256].astype(jnp.float32), mid)

    @pl.when(pl.program_id(0) == 0)
    def _():
        pad_ref[:SIDE] = jnp.zeros_like(pad_ref[:SIDE])
        pad_ref[SIDE + rows :] = jnp.zeros_like(pad_ref[:SIDE])

    pad_ref[inner, :mid] = (pltpu.roll(kept, 1, 0) * left).astype(jnp.bfloat16)
    pad_ref[inner, mid : 2 * mid] = low
    pad_ref[inner, 2 * mid :] = (pltpu.roll(kept, rows - 1, 0) * right).astype(jnp.bfloat16)
    side_ref[...] = pad_ref[inner].T
    above = wide(mask_ref[:, 256:384], 3 * mid)
    below = wide(mask_ref[:, 384:], 3 * mid)
    hidden = jnp.dot(pad_ref[inner], w_ref[3 * mid : 6 * mid], preferred_element_type=jnp.float32)
    hidden += jnp.dot(pad_ref[:rows] * above, w_ref[: 3 * mid], preferred_element_type=jnp.float32)
    hidden += jnp.dot(pad_ref[2 * SIDE :] * below, w_ref[6 * mid :], preferred_element_type=jnp.float32)
    out_ref[...] = hidden
    gather_stats(stat_ref, hidden, pl.program_id(0) == 0)


def widen_kernel(h_ref, vec_ref, w_ref, out_ref, low_ref, stat_ref):
    before = normal(h_ref[...], vec_ref) * vec_ref[2:3] + vec_ref[3:4]
    phi, _ = tail_and_bell(before)
    low = (before * phi).astype(jnp.bfloat16)
    low_ref[...] = low.T
    hidden = jnp.dot(low, w_ref[...], preferred_element_type=jnp.float32)
    out_ref[...] = hidden
    gather_stats(stat_ref, hidden, pl.program_id(0) == 0)


def norm_grad(upstream, normed, vec_ref):
    return vec_ref[4:5] * (upstream - vec_ref[5:6] - normed * vec_ref[6:7])


def act_slope(value):
    phi, bell = tail_and_bell(value)
    return phi + value * bell * DENSITY


def gather_flow(stat_ref, flow, normed, first):
    @pl.when(first)
    def _():
        stat_ref[...] = jnp.zeros_like(stat_ref)

    stat_ref[:8] += fold(flow)
    stat_ref[8:16] += fold(flow * normed)


def narrow_kernel(flow_ref, normed_ref, vec_ref, two_ref, vectwo_ref, low_ref, w_ref, out_ref, grad_ref, stat_ref, dh_ref):
    step = pl.program_id(0)
    rows = flow_ref.shape[0]
    dh = norm_grad(flow_ref[...].astype(jnp.float32), normed_ref[...].astype(jnp.float32), vec_ref)
    low = dh.astype(jnp.bfloat16)
    dh_ref[pl.ds(pl.multiple_of(step * rows, rows), rows)] = low
    dq = lax.dot_general(low, w_ref[...], COLS_COLS, preferred_element_type=jnp.float32)
    normed = normal(two_ref[...], vectwo_ref)
    flow = dq * act_slope(normed * vectwo_ref[2:3] + vectwo_ref[3:4])
    out_ref[...] = flow
    gather_flow(stat_ref, flow, normed, step == 0)


def narrow_fill(flow_ref, normed_ref, vec_ref, two_ref, vectwo_ref, low_ref, w_ref, out_ref, grad_ref, stat_ref, dh_ref):
    half = dh_ref.shape[1] // 2

    def part(index):
        def run():
            def one(i, carry):
                cols = pl.ds(pl.multiple_of(index * half + i * 512, 512), 512)
                grad_ref[:, cols] = jnp.dot(
                    low_ref[...], dh_ref[:, cols], preferred_element_type=jnp.float32
                ).astype(jnp.bfloat16)
                return carry

            lax.fori_loop(0, half // 512, one, 0)

        return run

    return part(0), part(1)


def across(source, target, sems, hop="task"):
    task = lax.axis_index("task")
    place = lax.axis_index("batch")
    device = (1 - task, place) if hop == "task" else (task, place + 1 - 2 * lax.rem(place, 2))
    return pltpu.make_async_remote_copy(
        src_ref=source,
        dst_ref=target,
        send_sem=sems.at[0],
        recv_sem=sems.at[1],
        device_id=device,
        device_id_type=MESH,
    )


def tiled(kernel, tile, moving, flags, outs, fixed, scratch, name, stats=None, sends=(), far=(), fill=None, turns=()):
    tasks = lax.axis_size("task")
    batch = lax.axis_size("batch")
    rows = moving[0].shape[0]

    def block(array):
        return pl.BlockSpec((tile,) + array.shape[1:], lambda i: (i,) + (0,) * (len(array.shape) - 1))

    def turned(array):
        return pl.BlockSpec((array.shape[0], tile), lambda i: (0, i))

    def whole(array):
        zeros = (0,) * len(array.shape)
        return pl.BlockSpec(array.shape, lambda i: zeros)

    hbm = pl.BlockSpec(memory_space=pl.ANY)
    operands = list(moving)
    in_specs = [(whole, block, lambda a: hbm)[m](a) for a, m in zip(moving, flags)]
    out_shape = outs + fixed + list(far)
    out_specs = [turned(a) if i in turns else block(a) for i, a in enumerate(outs)] + [whole(a) for a in fixed] + [hbm for a in far]
    scratch = list(scratch)
    params = dict(vmem_limit_bytes=VMEM_BYTES)
    ins, made, held = len(operands), len(out_shape), len(scratch)
    run = kernel
    if stats is not None:
        vec, forward, ident = stats
        width = vec.shape[1]
        params.update(collective_id=ident, has_side_effects=True)
        operands.append(vec)
        in_specs.append(whole(vec))
        out_shape = out_shape + [shape32(16, width)]
        out_specs = out_specs + [whole(out_shape[-1])]
        scratch = scratch + [pltpu.VMEM((24 if forward else 16, width), jnp.float32)]
        scratch = scratch + Exchange.scratch(tasks, batch, width)
        for array, _, shape, _ in sends:
            operands.append(array)
            in_specs.append(hbm)
            out_shape = out_shape + [jax.ShapeDtypeStruct(shape, array.dtype)]
            out_specs = out_specs + [hbm]
            scratch = scratch + [pltpu.SemaphoreType.DMA((2,))]

        def run(*refs):
            refs = list(refs)
            take = lambda n: [refs.pop(0) for _ in range(n)]
            used = take(ins)
            vec_ref = take(1)[0]
            sources = take(len(sends))
            given = take(made)
            out_ref = take(1)[0]
            targets = take(len(sends))
            own = take(held)
            stat_ref = take(1)[0]
            exchange = Exchange(tasks, batch, *take(6))
            step = pl.program_id(0)
            last = pl.num_programs(0) - 1

            @pl.when(step == 0)
            def _():
                exchange.greet()

            early = len(sends) > 0 or len(far) > 0

            def crossing(index):
                _, view, _, hop = sends[index]
                return across(view(sources[index]), targets[index], refs[index], hop)
            if early:

                @pl.when(step == 1)
                def _():
                    exchange.met()
                    for index in range(len(sends)):
                        crossing(index).start()

            after = kernel(*used, *given, stat_ref, *own)

            @pl.when(step == last)
            def _():
                if not early:
                    exchange.met()
                fillers = (None, None) if fill is None else fill(*used, *given, stat_ref, *own)
                settle_stats(exchange, stat_ref, vec_ref, out_ref, rows, rows * tasks * batch, forward, fillers)
                for index in range(len(sends)):
                    crossing(index).wait()
                if after is not None:
                    after()

    return pl.pallas_call(
        run,
        grid=(rows // tile,),
        out_shape=out_shape,
        in_specs=in_specs,
        out_specs=out_specs,
        scratch_shapes=scratch,
        compiler_params=pltpu.CompilerParams(**params),
        name=name,
    )(*operands)


def shape32(*shape):
    return jax.ShapeDtypeStruct(shape, jnp.float32)


def shape16(*shape):
    return jax.ShapeDtypeStruct(shape, jnp.bfloat16)


def squeeze(flat_in, w_reduce, stats, tile):
    rows, mid = flat_in.shape[0], w_reduce.shape[1]
    return tiled(squeeze_kernel, tile, [flat_in, w_reduce], [1, 0], [shape32(rows, mid)], [], [], "squeeze", stats)


def mesh_forward(h_one, vec, masks, taps, stats, sends, tile):
    rows, mid = h_one.shape
    return tiled(
        mesh_kernel, tile, [h_one, vec, masks, taps], [1, 0, 1, 0],
        [shape32(rows, mid), shape16(3 * mid, rows)], [],
        [pltpu.VMEM((tile + 2 * SIDE, 3 * mid), jnp.bfloat16)], "mesh_forward", stats, sends, turns=(1,),
    )


def widen(h_two, vec, w_expand, stats, sends, tile):
    rows, mid = h_two.shape
    width = w_expand.shape[1]
    return tiled(
        widen_kernel, tile, [h_two, vec, w_expand], [1, 0, 0],
        [shape32(rows, width), shape16(mid, rows)], [], [], "widen", stats, sends, turns=(1,),
    )


def narrow(flow, normed, vec_three, h_two, vec_two, q_two, w_expand, stats, tile):
    rows, mid = h_two.shape
    width = w_expand.shape[1]
    return tiled(
        narrow_kernel, tile, [flow, normed, vec_three, h_two, vec_two, q_two, w_expand], [1, 1, 0, 1, 0, 0, 0],
        [shape32(rows, mid)], [shape16(mid, width)], [pltpu.VMEM((rows, width), jnp.bfloat16)], "narrow", stats,
        fill=narrow_fill,
    )


def crown(h_three, flat_in, limits, cots, cot_parts, top, top_parts, vec, stats, tile, piece):
    rows, width = flat_in.shape
    half = cots.shape[2]
    return tiled(
        functools.partial(crown_kernel, piece), tile,
        [h_three, flat_in, limits, cots, *cot_parts, top, *top_parts, vec], [1, 1, 1, 2, 2, 2, 0, 2, 2, 0],
        [shape32(rows, half), shape16(rows, width), shape16(rows, width)], [shape16(width, 2 * half)],
        [
            pltpu.VMEM((tile, width), jnp.bfloat16),
            pltpu.VMEM((2 * half, width), jnp.float32),
            pltpu.VMEM((rows, half), jnp.bfloat16),
            pltpu.SemaphoreType.DMA((rows // tile, 2)),
            pltpu.VMEM((rows, half), jnp.bfloat16),
            pltpu.VMEM((rows, half), jnp.bfloat16),
            pltpu.VMEM((width, half), jnp.bfloat16),
            pltpu.SemaphoreType.DMA((5,)),
            pltpu.SemaphoreType.DMA((2,)),
        ],
        "crown", stats, (), [shape16(rows, half)],
    )


class Stream:
    def __init__(self, view, held, sems):
        self.view, self.held, self.sems = view, held, sems

    def copy(self, index):
        slot = lax.rem(index, 2)
        return pltpu.make_async_copy(self.view(index), self.held.at[slot], self.sems.at[slot])

    def start(self, index):
        self.copy(index).start()

    def take(self, index, count):
        self.copy(index).wait()

        @pl.when(index + 1 < count)
        def _():
            self.start(index + 1)

        return self.held.at[lax.rem(index, 2)]


def back_kernel(rows, tasks, batch, tile, *refs):
    refs = list(refs)

    def take(count):
        return [refs.pop(0) for _ in range(count)]

    (flow_hbm, two_hbm, one_hbm, side_hbm, mask_hbm, w_hbm, x_hbm, heads_hbm, expand_hbm) = take(9)
    vectwo_ref, vecone_ref = take(2)
    (out_hbm, heads_out, expand_out, spatial_out, reduce_out, vec_ref) = take(6)
    (two_buf, mask_buf, x_buf) = take(3)
    (side_ref, lane_ref, flow_ref, w_ref) = take(4)
    heads_work, expand_work, spatial_work, reduce_work, stat_ref = take(5)
    pair_sems, whole_sems, flow_sems = take(3)
    exchange = Exchange(tasks, batch, *take(6))
    grid = Grid(batch)
    mid = flow_hbm.shape[1]
    width = x_hbm.shape[1]
    spans = rows // tile

    def blocks(ref, height):
        return lambda index: ref.at[pl.ds(pl.multiple_of(index * height, height), height)]

    exchange.greet()

    def flow_load(index):
        return pltpu.make_async_copy(
            blocks(flow_hbm, tile)(index), blocks(flow_ref, tile)(index), flow_sems.at[index]
        )

    twos = Stream(blocks(two_hbm, tile), two_buf, pair_sems.at[1])
    masks = Stream(blocks(mask_hbm, tile), mask_buf, pair_sems.at[2])
    ones = Stream(blocks(one_hbm, tile), two_buf, pair_sems.at[3])
    dh_ref, normed_ref, dht_ref = lane_ref.at[:, :mid], lane_ref.at[:, mid : 2 * mid], side_ref.at[:mid]
    across_cols = x_buf.shape[2]
    columns = Stream(
        lambda index: x_hbm.at[:, pl.ds(pl.multiple_of(index * across_cols, across_cols), across_cols)],
        x_buf, pair_sems.at[0],
    )
    loads = [
        pltpu.make_async_copy(source, target, whole_sems.at[index])
        for index, (source, target) in enumerate(
            [(heads_hbm, heads_work), (side_hbm, side_ref), (expand_hbm, expand_work), (w_hbm, w_ref)]
        )
    ]
    heads_load, side_load, expand_load, w_load = loads
    keep = pltpu.make_async_copy(dh_ref, out_hbm, whole_sems.at[4])
    heads_load.start()
    for stream in (twos, masks):
        stream.start(0)
    for index in range(spans):
        flow_load(index).start()
    for load in loads[1:]:
        load.start()

    third = spatial_work.shape[0] // 3
    works = [(heads_work, heads_out, False), (expand_work, expand_out, True)]
    for index in range(3):
        span = pl.ds(index * third, third)
        works.append((spatial_work.at[span], spatial_out.at[span], False))
    for index in range(2):
        span = pl.ds(index * width // 2, width // 2)
        works.append((reduce_work.at[span], reduce_out.at[span], False))
    reductions = [Reduction(grid, work, out, *take(10), wide) for work, out, wide in works]

    def tick(name):
        for item, stage in AGENDA.get(name, ()):
            reductions[item].stage(stage)

    def ticks(name, index, count, scale=1, shift=0):
        for step in range(count):
            label = "%s%d" % (name, step * scale + shift)
            if label in AGENDA:

                @pl.when(index == step)
                def _():
                    tick(label)

    def lanes(index, carry):
        span = pl.ds(pl.multiple_of(index * tile, tile), tile)
        flow_load(index).wait()
        flow = flow_ref[span]
        normed = normal(twos.take(index, spans)[...], vectwo_ref)
        mask = masks.take(index, spans)
        dh = norm_grad(flow, normed, vectwo_ref)
        above = wide(mask[:, 256:384].astype(jnp.float32), mid)
        below = wide(mask[:, 384:].astype(jnp.float32), mid)
        low = jnp.bfloat16
        zero = jnp.zeros((SIDE, mid), low)
        lane_ref[span, mid : 2 * mid] = dh.astype(low)
        lane_ref[span, :mid] = jnp.concatenate([(dh * above)[SIDE:].astype(low), zero], axis=0)
        lane_ref[span, 2 * mid :] = jnp.concatenate([zero, (dh * below)[: tile - SIDE].astype(low)], axis=0)
        ticks("lane", index, 4)
        return carry

    exchange.met()
    heads_load.wait()
    expand_load.wait()
    tick("start")
    lax.fori_loop(0, spans, lanes, 0)
    masks.start(0)
    ones.start(0)
    side_load.wait()

    def spatial(index, carry):
        a, b = index // 3, lax.rem(index, 3)
        rows_here = pl.ds(pl.multiple_of(b * mid, mid), mid)
        cols = pl.ds(pl.multiple_of(a * mid, mid), mid)
        part = jnp.dot(side_ref[rows_here], lane_ref[:, cols], preferred_element_type=jnp.float32)
        spatial_work[pl.ds(pl.multiple_of(index * mid, mid), mid)] = part.astype(jnp.bfloat16)
        ticks("sp", index, 9)
        return carry

    lax.fori_loop(0, 9, spatial, 0)
    w_load.wait()

    def taps(index, carry):
        span = pl.ds(pl.multiple_of(index * tile, tile), tile)
        mask = masks.take(index, spans)
        pieces = []
        for b in range(3):
            total = None
            for a in range(3):
                part = lax.dot_general(
                    lane_ref[span, a * mid : (a + 1) * mid], w_ref[3 * a + b], COLS_COLS,
                    preferred_element_type=jnp.float32,
                )
                total = part if total is None else total + part
            pieces.append(total)
            if b < 2:
                ticks("tap", index, 4, 3, b)
        left = wide(mask[:, :128].astype(jnp.float32), mid)
        right = wide(mask[:, 128:256].astype(jnp.float32), mid)
        dq = pieces[1] + pltpu.roll(pieces[0] * left, tile - 1, 0) + pltpu.roll(pieces[2] * right, 1, 0)
        normed = normal(ones.take(index, spans)[...], vecone_ref)
        flow = dq * act_slope(normed * vecone_ref[2:3] + vecone_ref[3:4])
        flow_ref[span] = flow
        normed_ref[span] = normed.astype(jnp.bfloat16)
        gather_flow(stat_ref, flow, normed, index == 0)
        ticks("tap", index, 4, 3, 2)
        return carry

    lax.fori_loop(0, spans, taps, 0)
    columns.start(0)
    settle_stats(exchange, stat_ref, vecone_ref, vec_ref, rows, rows * tasks * batch, False)
    tick("xch")

    def inner(index, carry):
        span = pl.ds(pl.multiple_of(index * tile, tile), tile)
        dh = norm_grad(flow_ref[span], normed_ref[span].astype(jnp.float32), vec_ref)
        dh_ref[span] = dh.astype(jnp.bfloat16)
        dht_ref[:, span] = dh.T.astype(jnp.bfloat16)
        return carry

    lax.fori_loop(0, spans, inner, 0)
    keep.start()
    tick("inner")
    count = width // across_cols

    def reduce(index, carry):
        part = jnp.dot(dht_ref[...], columns.take(index, count)[...], preferred_element_type=jnp.float32)
        span = pl.ds(pl.multiple_of(index * across_cols, across_cols), across_cols)
        reduce_work[span] = part.T.astype(jnp.bfloat16)
        ticks("red", index, 4)
        return carry

    lax.fori_loop(0, count, reduce, 0)
    keep.wait()
    tick("tail")


def back(flow, h_two, vec_two, h_one, vec_one, sides, masks, w_spatial, flat_in, heads, expand, ident, tile):
    tasks = lax.axis_size("task")
    batch = lax.axis_size("batch")
    far = batch // LOW
    rows, mid = h_one.shape
    width = flat_in.shape[1]
    full, low = jnp.float32, jnp.bfloat16
    cols = 512
    hbm = pl.BlockSpec(memory_space=pl.ANY)
    vmem = pl.BlockSpec(memory_space=pltpu.VMEM)
    shapes = [(heads.shape, False), (expand.shape, True)] + [((3 * mid, mid), False)] * 3
    shapes += [((width // 2, mid), False)] * 2
    scratch = [
        pltpu.VMEM((2, tile, mid), full),
        pltpu.VMEM((2, tile, 512), low),
        pltpu.VMEM((2, rows, cols), low),
        pltpu.VMEM((3 * mid, rows), low),
        pltpu.VMEM((rows, 3 * mid), low),
        pltpu.VMEM((rows, mid), full),
        pltpu.VMEM(w_spatial.shape, low),
        pltpu.VMEM(heads.shape, low),
        pltpu.VMEM(expand.shape, low),
        pltpu.VMEM((9 * mid, mid), low),
        pltpu.VMEM((width, mid), low),
        pltpu.VMEM((16, mid), full),
        pltpu.SemaphoreType.DMA((4, 2)),
        pltpu.SemaphoreType.DMA((5,)),
        pltpu.SemaphoreType.DMA((rows // tile,)),
    ] + Exchange.scratch(tasks, batch, mid)
    for (high, across_), is_wide in shapes:
        scratch += Reduction.scratch(high, across_, is_wide, far)
    return pl.pallas_call(
        functools.partial(back_kernel, rows, tasks, batch, tile),
        out_shape=[
            shape16(rows, mid), shape16(*heads.shape), shape16(*expand.shape), shape16(9 * mid, mid),
            shape16(width, mid), shape32(16, mid),
        ],
        in_specs=[hbm] * 9 + [vmem] * 2,
        out_specs=[hbm] * 5 + [vmem],
        scratch_shapes=scratch,
        compiler_params=pltpu.CompilerParams(
            vmem_limit_bytes=VMEM_BYTES, collective_id=ident, has_side_effects=True
        ),
        name="back",
    )(flow, h_two, h_one, sides, masks, w_spatial, flat_in, heads, expand, vec_two, vec_one)


def finish_kernel(
    dh_ref, up_ref, heads_ref, expand_ref, spatial_ref, reduce_ref, mine_ref, came_ref, w_ref, one_ref, two_ref, three_ref,
    out_ref, heads_out, expand_out, spatial_out, reduce_out, both_ref, *sums,
):
    full = jnp.float32
    task = lax.axis_index("task")
    half = heads_out.shape[1]
    back = lax.dot_general(dh_ref[...], w_ref[...], COLS_COLS, preferred_element_type=full)
    out_ref[...] = (up_ref[...].astype(full) + back).astype(jnp.bfloat16)
    heads_out[...] = jnp.where(task == 0, heads_ref[:, :half], heads_ref[:, half:]).astype(full)
    expand_out[...] = expand_ref[...].astype(full)
    spatial_out[...] = spatial_ref[...].astype(full)
    reduce_out[...] = reduce_ref[...].astype(full)
    both_ref[task] = mine_ref[...]
    both_ref[1 - task] = came_ref[...].astype(full)

    @pl.when(pl.program_id(0) == 0)
    def _():
        for index, vec_ref in enumerate((one_ref, two_ref, three_ref)):
            sums[2 * index][...] = vec_ref[9:10]
            sums[2 * index + 1][...] = vec_ref[8:9]


def finish(dh, up, heads, expand, spatial, reduce, mine, came, w_reduce, vecs, steps):
    def block(array, lead=0):
        zeros = (0,) * (len(array.shape) - 1 - lead)
        height = array.shape[lead] // steps
        return pl.BlockSpec(array.shape[:lead] + (height,) + array.shape[lead + 1 :], lambda i: (0,) * lead + (i,) + zeros)

    def whole(array):
        return pl.BlockSpec(array.shape, lambda i: (0, 0))

    rows, half = mine.shape
    moving = [dh, up, heads, expand, spatial, reduce, mine, came]
    fixed = [w_reduce, *vecs]
    outs = [shape16(*up.shape), shape32(heads.shape[0], half), shape32(*expand.shape), shape32(*spatial.shape), shape32(*reduce.shape)]
    both = shape32(2, rows, half)
    sums = [shape32(1, vec.shape[1]) for vec in vecs for _ in range(2)]
    return pl.pallas_call(
        finish_kernel,
        grid=(steps,),
        out_shape=outs + [both] + sums,
        in_specs=[block(a) for a in moving] + [whole(a) for a in fixed],
        out_specs=[block(a) for a in outs] + [block(both, 1)] + [whole(a) for a in sums],
        compiler_params=pltpu.CompilerParams(vmem_limit_bytes=VMEM_BYTES),
        name="finish",
    )(*moving, *fixed)


def body(
    inputs,
    crop_cuts,
    threshold,
    w_reduce,
    w_spatial,
    w_expand,
    w_heads,
    gain_one,
    bias_one,
    gain_two,
    bias_two,
    gain_three,
    bias_three,
    cotangent,
):
    low = jnp.bfloat16
    full = jnp.float32
    canvases, pixels, width = inputs.shape[1:]
    mid = w_reduce.shape[1]
    rows = canvases * pixels
    half = w_heads.shape[2]
    cots = cotangent.reshape(2, rows, half)
    top_mine = w_heads[0]

    def params(gain, bias):
        zero = jnp.zeros_like(gain)
        return jnp.stack([zero, zero, gain, bias, zero, zero, zero, zero])

    lines = jnp.arange(SIDE, dtype=jnp.int32)
    cuts = crop_cuts.reshape(canvases, 2)
    from_above = jnp.logical_not((lines == cuts[:, 0:1]) | (lines == 0)[None, :])
    from_left = jnp.logical_not((lines == cuts[:, 1:2]) | (lines == 0)[None, :])
    from_below = jnp.pad(from_above[:, 1:], ((0, 0), (0, 1)))
    from_right = jnp.pad(from_left[:, 1:], ((0, 0), (0, 1)))
    shape = (canvases, SIDE, SIDE, 128)
    masks = jnp.concatenate(
        [jnp.broadcast_to(m[:, None, :, None], shape) for m in (from_left, from_right)]
        + [jnp.broadcast_to(m[:, :, None, None], shape) for m in (from_above, from_below)],
        axis=3,
    ).astype(low).reshape(rows, 512)

    flat_in = inputs.reshape(rows, width)
    core = lambda: lax.rem(lax.axis_index("batch"), 2)
    other = lambda: 1 - lax.axis_index("task")
    quarter = rows // 4
    top_rows = width // 2
    h_one, vec_one = squeeze(flat_in, w_reduce, (params(gain_one, bias_one), True, 0), min(rows, 512))
    sends = [
        (top_mine, lambda ref: ref.at[pl.ds(pl.multiple_of(core() * top_rows, top_rows), top_rows)], (top_rows, half), "task"),
        (cots, lambda ref: ref.at[other(), pl.ds(0, quarter)], (quarter, half), "task"),
    ]
    h_two, sides, vec_two, top_one, cot_one = mesh_forward(
        h_one, vec_one, masks, w_spatial.reshape(9 * mid, mid), (params(gain_two, bias_two), True, 1), sends, pixels
    )
    sends = [
        (top_one, lambda ref: ref, (top_rows, half), "core"),
        (cots, lambda ref: ref.at[other(), pl.ds(quarter, quarter)], (quarter, half), "task"),
    ]
    h_three, q_two, vec_three, top_two, cot_two = widen(
        h_two, vec_two, w_expand, (params(gain_three, bias_three), True, 2), sends, pixels
    )
    out_mine, flow, normed, grad_heads, out_peer, vec_three = crown(
        h_three, flat_in, threshold.reshape(rows, width), cots, (cot_one, cot_two), top_mine, (top_one, top_two), vec_three,
        (vec_three, False, 3), pixels, 256,
    )
    flow_two, grad_expand, vec_two = narrow(
        flow, normed, vec_three, h_two, vec_two, q_two, w_expand, (vec_two, False, 4), min(rows, 512)
    )
    dh_one, grad_heads, grad_expand, grad_spatial, grad_reduce, vec_one = back(
        flow_two, h_two, vec_two, h_one, vec_one, sides, masks, w_spatial, flat_in, grad_heads, grad_expand, 5,
        min(rows, 512),
    )
    grad_inputs, grad_heads, grad_expand, grad_spatial, grad_reduce, head_out, *sums = finish(
        dh_one, flow, grad_heads, grad_expand, grad_spatial, grad_reduce, out_mine, out_peer, w_reduce,
        (vec_one, vec_two, vec_three), 8,
    )
    return (
        head_out.reshape(1, 2, canvases, pixels, half),
        grad_inputs.reshape(inputs.shape),
        grad_reduce,
        grad_spatial.reshape(w_spatial.shape),
        grad_expand,
        grad_heads[None],
        *[row.reshape(-1) for row in sums],
    )


def solution(mesh):
    in_specs = (
        P("task", "batch", None, None),
        P("task", "batch", None),
        P("task", "batch", None, None),
        P(),
        P(),
        P(),
        P("task", None, None),
        P(),
        P(),
        P(),
        P(),
        P(),
        P(),
        P("task", None, "batch", None, None),
    )
    out_specs = (
        P("task", None, "batch", None, None),
        P("task", "batch", None, None),
        P(),
        P(),
        P(),
        P("task", None, None),
        P(),
        P(),
        P(),
        P(),
        P(),
        P(),
    )
    return jax.shard_map(body, mesh=mesh, in_specs=in_specs, out_specs=out_specs, check_vma=False)
```

```python
import functools
import math

import jax
import jax.numpy as jnp
from jax import lax
from jax.experimental import pallas as pl
from jax.experimental.pallas import tpu as pltpu
from jax.sharding import PartitionSpec as P

SIDE = 16
EPS = 1e-05
FLOOR = 0.1
SOFT = 0.25
ROOT_HALF = 0.7071067811865476
DENSITY = 0.3989422804014327
LOG2E = 1.4426950408889634
ERF_P = 0.3275911
ERF_A = (0.254829592, -0.284496736, 1.421413741, -1.453152027, 1.061405429)
ROWS_ROWS = (((0,), (0,)), ((), ()))
COLS_COLS = (((1,), (1,)), ((), ()))
MESH = pl.DeviceIdType.MESH
LOW = 4
VMEM_BYTES = 62 * 2**20


AGENDA = {
    "start": ((0, 3),),
    "lane0": ((1, 0),),
    "lane2": ((1, 1),),
    "sp1": ((0, 4),),
    "sp2": ((2, 0),),
    "sp4": ((1, 2), (2, 1),),
    "sp5": ((3, 0),),
    "sp8": ((0, 5), (1, 3), (3, 1), (4, 0),),
    "tap1": ((2, 2), (4, 1),),
    "tap5": ((0, 7), (1, 4),),
    "tap7": ((0, 8), (3, 2),),
    "tap8": ((2, 3),),
    "xch": ((1, 5), (2, 4), (3, 3), (4, 2),),
    "inner": ((1, 6),),
    "red1": ((2, 5), (4, 3), (5, 0),),
    "red3": ((3, 4), (5, 1), (6, 0), (1, 7),),
    "tail": ((2, 6), (6, 1), (4, 4), (1, 8), (5, 2), (3, 5), (2, 7), (2, 8), (6, 2), (4, 5), (5, 3), (3, 6), (6, 3), (4, 6), (5, 4), (3, 7), (6, 4), (3, 8), (5, 5), (4, 7), (6, 5), (5, 6), (4, 8), (6, 6), (5, 7), (5, 8), (6, 7), (6, 8),),
}


class Reduction:
    def __init__(
        self, grid, work, result, core, first_a, first_b, second, last, done, send, recv, far_send, far_recv, local,
        kind, shape=None,
    ):
        self.grid, self.work, self.result = grid, work, result
        self.core_room, self.first_rooms, self.second_room, self.last_room = core, (first_a, first_b), second, last
        self.done = done
        self.send, self.recv, self.far_send, self.far_recv = send, recv, far_send, far_recv
        self.local = local
        self.kind = kind
        self.resumed = shape is not None
        self.rows, self.cols = shape or work.shape
        sizes = self.sizes(self.rows, self.cols, kind, grid.far)
        self.pieces = sizes[3][0] // sizes[4][0]
        self.mine = lax.rem(grid.high, self.pieces)

    @staticmethod
    def sizes(rows, cols, kind, far):
        if kind == "wide":
            core, first, second = (rows, cols // 2), (rows, cols // 8), (rows, cols // 16)
            firsts = first, first
        elif kind == "tall":
            core, first, second = (rows // 2, cols), (rows // 2, cols // 4), (rows // 4, cols // 4)
            firsts = first, first
        else:
            core, second = (rows // 2, cols), (rows // 8, cols // 2)
            firsts = (rows // 4, cols // 2), (rows // 8, cols)
        pieces = max(n for n in range(1, far + 1) if far % n == 0 and second[0] % (8 * n) == 0)
        return core, *firsts, second, (second[0] // pieces, second[1])

    @staticmethod
    def scratch(rows, cols, kind, far, resumed=False):
        core, first_a, first_b, second, last = Reduction.sizes(rows, cols, kind, far)
        if resumed:
            core = first_a = first_b = (16, 128)
        return [
            pltpu.VMEM(core, jnp.bfloat16),
            pltpu.VMEM(first_a, jnp.bfloat16),
            pltpu.VMEM(first_b, jnp.bfloat16),
            pltpu.VMEM((2,) + ((16, 128) if resumed else second), jnp.bfloat16),
            pltpu.VMEM((2, far) + last, jnp.bfloat16),
            pltpu.VMEM((2,) + last, jnp.bfloat16),
            pltpu.SemaphoreType.DMA((10,)),
            pltpu.SemaphoreType.DMA((10,)),
            pltpu.SemaphoreType.DMA((4, far)),
            pltpu.SemaphoreType.DMA((4, far)),
            pltpu.SemaphoreType.DMA((2,)),
        ]

    def view(self, core, part=None, first=None, second=None, piece=None, done=False):
        rows, cols = self.rows, self.cols
        sizes = self.sizes(rows, cols, self.kind, self.grid.far)
        row = col = 0
        shape = sizes[0]
        if self.kind == "wide":
            col = core * (cols // 2)
            if part is not None:
                col = col + part * (cols // 4) + first * (cols // 8)
            if second is not None:
                col = col + second * (cols // 16)
        elif self.kind == "tall":
            row = core * (rows // 2)
            if part is not None:
                col = part * (cols // 2) + first * (cols // 4)
            if second is not None:
                row = row + second * (rows // 4)
        else:
            row = core * (rows // 2)
            if part is not None:
                row = row + part * (rows // 4)
                y, task = (second, first) if part == 0 else (first, second)
                row = row if y is None else row + y * (rows // 8)
                col = 0 if task is None else task * (cols // 2)
            elif done:
                col = self.grid.task * (cols // 2)
                shape = (rows // 2, cols // 2)
        if part is not None:
            shape = sizes[1 + part] if second is None else sizes[3]
        ref = self.result if done else self.work
        if self.resumed and not done:
            ref, row, col = self.work.at[part], 0, 0
        if piece is not None:
            row = row + piece * sizes[4][0]
            shape = sizes[4]
        if not isinstance(row, int):
            row = pl.multiple_of(row, shape[0] & -shape[0])
        if not isinstance(col, int):
            col = pl.multiple_of(col, 128)
        return ref.at[pl.ds(row, shape[0]), pl.ds(col, shape[1])]

    def swap(self, index):
        grid = self.grid
        part = (index + 1) % 2
        bits = grid.bits(part)
        if index == 0:
            source, target, device = self.view(1 - grid.core), self.core_room, grid.core_peer
        elif index < 3:
            source, target = self.view(grid.core, part, 1 - bits[0]), self.first_rooms[part]
            device = grid.peers(part)[0]
        elif index < 5:
            source, target = self.view(grid.core, part, bits[0], 1 - bits[1]), self.second_room.at[part]
            device = grid.peers(part)[1]
        elif index < 7:
            source = self.view(grid.core, part, bits[0], bits[1], done=True)
            target, device = source, grid.y_peer if self.kind == "owner" else grid.peers(part)[1]
        elif index < 9:
            source = self.view(grid.core, part, bits[0], done=True)
            target, device = source, grid.peers(part)[0]
        else:
            source = self.view(grid.core, done=True)
            target, device = source, grid.core_peer
        return pltpu.make_async_remote_copy(
            src_ref=source,
            dst_ref=target,
            send_sem=self.send.at[index],
            recv_sem=self.recv.at[index],
            device_id=device,
            device_id_type=MESH,
        )

    def add(self, target, sources):
        rows = target.shape[0]
        step = math.gcd(rows, 64)

        def one(i, carry):
            span = pl.ds(pl.multiple_of(i * step, step), step)
            total = sources[0][span].astype(jnp.float32)
            for source in sources[1:]:
                total = total + source[span].astype(jnp.float32)
            target[span] = total.astype(jnp.bfloat16)
            return carry

        lax.fori_loop(0, rows // step, one, 0)

    def far_copy(self, part, step, back, inward):
        grid = self.grid
        bits = grid.bits(part)
        if back:
            first = grid.high - self.mine
            slot = first + lax.rem(self.mine + step, self.pieces)
            owner = slot if inward else grid.high
            source = self.done.at[part]
            target = self.view(grid.core, part, bits[0], bits[1], lax.rem(owner, self.pieces), True)
        else:
            slot = lax.rem(grid.high + step, grid.far)
            owner = slot if inward else grid.high
            source = self.view(grid.core, part, bits[0], bits[1], lax.rem(slot, self.pieces))
            target = self.last_room.at[part, owner]
        line = 2 * part + (1 if back else 0)
        return pltpu.make_async_remote_copy(
            src_ref=source,
            dst_ref=target,
            send_sem=self.far_send.at[line, step],
            recv_sem=self.far_recv.at[line, owner],
            device_id=(grid.task, slot * LOW + grid.low),
            device_id_type=MESH,
        )

    def far_start(self, part, back):
        for step in range(1, self.pieces if back else self.grid.far):
            self.far_copy(part, step, back, False).start()

    def far_settle(self, part, back):
        for step in range(1, self.pieces if back else self.grid.far):
            self.far_copy(part, step, back, True).wait_recv()
            self.far_copy(part, step, back, False).wait_send()

    def keep(self, part):
        bits = self.grid.bits(part)
        mine = self.view(self.grid.core, part, bits[0], bits[1], self.mine, True)
        return pltpu.make_async_copy(self.done.at[part], mine, self.local.at[part])

    def finish(self, index, part):
        grid = self.grid
        bits = grid.bits(part)
        if index == 0:
            if part == 0:
                self.swap(0).wait()
                mine = self.view(grid.core)
                self.add(mine, [mine, self.core_room])
        elif index == 1:
            self.swap(1 + part).wait()
            mine = self.view(grid.core, part, bits[0])
            self.add(mine, [mine, self.first_rooms[part]])
        elif index == 2:
            self.swap(3 + part).wait()
            mine = self.view(grid.core, part, bits[0], bits[1])
            self.add(mine, [mine, self.second_room.at[part]])
        elif index == 3:
            self.far_settle(part, False)
            self.last_room[part, grid.high] = self.view(grid.core, part, bits[0], bits[1], self.mine)[...]
            self.add(self.done.at[part], [self.last_room.at[part, slot] for slot in range(grid.far)])
        elif index == 4:
            self.far_settle(part, True)
            self.keep(part).wait()
        elif index < 7:
            self.swap(2 * index - 5 + part).wait()
        elif part == 0:
            self.swap(9).wait()

    def begin(self, index, part):
        if index == 0 or index == 7:
            if part == 0:
                self.swap(9 if index else 0).start()
        elif index < 3:
            self.swap(2 * index - 1 + part).start()
        elif index == 3:
            self.far_start(part, False)
        elif index == 4:
            self.keep(part).start()
            self.far_start(part, True)
        elif index < 7:
            self.swap(2 * index - 5 + part).start()

    def stage(self, index):
        owner = self.kind == "owner"
        if owner and index == 6:
            return
        before = 5 if owner and index == 7 else index - 1
        first = self.resumed and index == 3
        together = index in (1, 7, 8)
        for part in range(2):
            if before >= 0 and not first:
                self.finish(before, part)
            if not together:
                self.begin(index, part)
        if together:
            for part in range(2):
                self.begin(index, part)


class Grid:
    def __init__(self, batch):
        self.task = lax.axis_index("task")
        place = lax.axis_index("batch")
        self.far = batch // LOW
        self.high = place // LOW
        self.low = lax.rem(place, LOW)
        self.core = lax.rem(place, 2)
        self.y = lax.rem(place // 2, 2)
        base = place - self.low
        self.core_peer = (self.task, base + self.y * 2 + (1 - self.core))
        self.x_peer = (1 - self.task, place)
        self.y_peer = (self.task, base + (1 - self.y) * 2 + self.core)

    def bits(self, part):
        return (self.task, self.y) if part == 0 else (self.y, self.task)

    def peers(self, part):
        return (self.x_peer, self.y_peer) if part == 0 else (self.y_peer, self.x_peer)


class Exchange:
    def __init__(self, tasks, batch, near, far, near_send, near_recv, far_send, far_recv):
        place = lax.axis_index("batch")
        self.task = lax.axis_index("task")
        self.high = place // LOW
        self.low = lax.rem(place, LOW)
        self.near_size = tasks * LOW
        self.far_size = batch // LOW
        self.me_near = self.task * LOW + self.low
        self.near, self.far = near, far
        self.near_sems, self.far_sems = (near_send, near_recv), (far_send, far_recv)

    @staticmethod
    def scratch(tasks, batch, width):
        near_size, far_size = tasks * LOW, batch // LOW
        return [
            pltpu.VMEM((near_size + 1, 2, width), jnp.float32),
            pltpu.VMEM((far_size + 1, 2, width), jnp.float32),
            pltpu.SemaphoreType.DMA((near_size,)),
            pltpu.SemaphoreType.DMA((near_size,)),
            pltpu.SemaphoreType.DMA((far_size,)),
            pltpu.SemaphoreType.DMA((far_size,)),
        ]

    def near_peer(self, step):
        slot = lax.rem(self.me_near + step, self.near_size)
        return slot, (slot // LOW, self.high * LOW + lax.rem(slot, LOW))

    def far_peer(self, step):
        slot = lax.rem(self.high + step, self.far_size)
        return slot, (self.task, slot * LOW + self.low)

    def peers(self):
        near = [self.near_peer(step)[1] for step in range(1, self.near_size)]
        return near + [self.far_peer(step)[1] for step in range(1, self.far_size)]

    def greet(self):
        barrier = pltpu.get_barrier_semaphore()
        for device in self.peers():
            pl.semaphore_signal(barrier, inc=1, device_id=device, device_id_type=MESH)

    def met(self):
        pl.semaphore_wait(pltpu.get_barrier_semaphore(), self.near_size + self.far_size - 2)

    def hop(self, size, peer, me, held, sems, filler=None):
        def copy(step, slot):
            return pltpu.make_async_remote_copy(
                src_ref=held.at[size],
                dst_ref=held.at[slot],
                send_sem=sems[0].at[step],
                recv_sem=sems[1].at[slot],
                device_id=peer(step)[1],
                device_id_type=MESH,
            )

        for step in range(1, size):
            copy(step, me).start()
        held[me] = held[size]
        if filler is not None:
            filler()
        for step in range(1, size):
            copy(step, peer(step)[0]).wait_recv()
        for step in range(1, size):
            copy(step, me).wait_send()
        return held[:size]

    def run(self, total, spread, rows, forward, fillers=(None, None)):
        self.near[self.near_size, 0:1] = total
        self.near[self.near_size, 1:2] = spread
        held = self.hop(self.near_size, self.near_peer, self.me_near, self.near, self.near_sems, fillers[0])
        total, spread = join(held, float(rows), forward)
        self.far[self.far_size, 0:1] = total
        self.far[self.far_size, 1:2] = spread
        held = self.hop(self.far_size, self.far_peer, self.high, self.far, self.far_sems, fillers[1])
        return join(held, float(rows * self.near_size), forward)


def join(held, share, forward):
    sums = held[:, 0, :]
    total = jnp.sum(sums, axis=0, keepdims=True)
    spread = jnp.sum(held[:, 1, :], axis=0, keepdims=True)
    if forward:
        groups = held.shape[0]
        away = sums * (1.0 / share) - total * (1.0 / (share * groups))
        spread = spread + share * jnp.sum(away * away, axis=0, keepdims=True)
    return total, spread


def settle_stats(exchange, stat_ref, vec_refs, out_ref, rows, count, forward, fillers=(None, None)):
    first = jnp.sum(stat_ref[:8], axis=0, keepdims=True)
    second = jnp.sum(stat_ref[8:16], axis=0, keepdims=True)
    if forward:
        gain, bias = vec_refs[0][...], vec_refs[1][...]
        out_ref[...] = jnp.zeros_like(out_ref)
        out_ref[2:3] = gain
        out_ref[3:4] = bias
        local = first + rows * stat_ref[16:17]
        total, spread = exchange.run(local, second - first * first * (1.0 / rows), rows, True, fillers)
        scale = lax.rsqrt(spread * (1.0 / count) + EPS)
        out_ref[0:1] = total * (1.0 / count)
        out_ref[1:2] = scale
        out_ref[4:5] = scale * gain
    else:
        out_ref[:8] = vec_refs[0][:8]
        total, spread = exchange.run(first, second, rows, False, fillers)
        out_ref[5:6] = total * (1.0 / count)
        out_ref[6:7] = spread * (1.0 / count)
        out_ref[8:9] = total
        out_ref[9:10] = spread
        out_ref[10:] = jnp.zeros_like(out_ref[10:])


def tail_and_bell(value):
    bell = jnp.exp2(value * value * (-0.5 * LOG2E))
    away = jnp.abs(value)
    ratio = pltpu.reciprocal(1.0 + away * (ERF_P * ROOT_HALF))
    poly = 0.5 * ERF_A[4]
    for factor in ERF_A[3::-1]:
        poly = poly * ratio + 0.5 * factor
    tail = poly * ratio * bell
    return jnp.where(value >= 0, 1.0 - tail, tail), bell


def fold(array):
    total = array[:8]
    for start in range(8, array.shape[0], 8):
        total = total + array[start : start + 8]
    return total


def crown_kernel(
    piece, h_ref, x_ref, thr_ref, cot_hbm, cot_one, cot_two, top_ref, top_one, top_two, vec_ref,
    out_ref, flow_ref, normed_ref, grad_ref, rest_ref, came_ref, stat_ref, z_ref, acc_ref, sent_ref, sems,
    cots_ref, cots_peer_ref, top_peer_ref, local_sems, late_sems, twice_ref,
):
    step = pl.program_id(0)
    rows, width = x_ref.shape
    all_rows, half = cots_ref.shape
    split = all_rows // 4
    task = lax.axis_index("task")
    last = pl.num_programs(0) - 1

    def send(index):
        span = pl.ds(pl.multiple_of(index * rows, rows), rows)
        return across(sent_ref.at[span], came_ref.at[span], sems.at[index])

    core = lax.rem(lax.axis_index("batch"), 2)
    high = top_one.shape[0]
    late = across(cot_hbm.at[1 - task, pl.ds(2 * split, 2 * split)], cots_peer_ref.at[pl.ds(2 * split, 2 * split)], late_sems)

    @pl.when(step == 0)
    def _():
        pairs = [
            (cot_hbm.at[task], cots_ref),
            (cot_one, cots_peer_ref.at[pl.ds(0, split)]),
            (cot_two, cots_peer_ref.at[pl.ds(split, split)]),
            (top_one, top_peer_ref.at[pl.ds(pl.multiple_of(core * high, high), high)]),
            (top_two, top_peer_ref.at[pl.ds(pl.multiple_of((1 - core) * high, high), high)]),
        ]
        copies = [pltpu.make_async_copy(a, b, local_sems.at[i]) for i, (a, b) in enumerate(pairs)]
        for copy in copies:
            copy.start()
        for copy in copies:
            copy.wait()

    @pl.when(step == 1)
    def _():
        late.start()

    @pl.when(step == (last + 1) // 2)
    def _():
        late.wait()

    @pl.when(step > 0)
    def _():
        send(step - 1).start()

    span = pl.ds(pl.multiple_of(step * rows, rows), rows)
    cot_ref, cot_peer_ref = cots_ref.at[span], cots_peer_ref.at[span]
    span = pl.ds(0, rows)
    twice_ref[0] = cot_ref[...] * jnp.bfloat16(2.0)
    twice_ref[1] = cot_peer_ref[...] * jnp.bfloat16(2.0)

    @pl.when(step == 0)
    def _():
        stat_ref[...] = jnp.zeros_like(stat_ref)
        acc_ref[...] = jnp.zeros_like(acc_ref)

    for start in range(0, width, piece):
        cols = pl.ds(start, piece)
        g_one = lax.dot_general(twice_ref[0, span], top_ref[cols], COLS_COLS, preferred_element_type=jnp.float32)
        g_one = g_one.astype(jnp.bfloat16).astype(jnp.float32)
        g_two = lax.dot_general(twice_ref[1, span], top_peer_ref[cols], COLS_COLS, preferred_element_type=jnp.float32)
        g_two = g_two.astype(jnp.bfloat16).astype(jnp.float32)
        total = g_one + g_two
        size = jnp.abs(g_one) + jnp.abs(g_two)
        limit = (thr_ref[:, cols] * jnp.bfloat16(2.0)).astype(jnp.float32)
        share = total * pltpu.reciprocal(jnp.maximum(size, 2.0 * FLOOR))
        merged = 0.25 * total + jnp.clip(share + (1.0 - limit), -SOFT, SOFT) * size
        normed = (h_ref[:, cols] - vec_ref[0:1, cols]) * vec_ref[1:2, cols]
        normed_ref[:, cols] = normed.astype(jnp.bfloat16)
        before = normed * vec_ref[2:3, cols] + vec_ref[3:4, cols] + x_ref[:, cols].astype(jnp.float32)
        phi, bell = tail_and_bell(before)
        z_ref[:, cols] = (before * phi).astype(jnp.bfloat16)
        flow = merged * (phi + before * bell * DENSITY)
        flow_ref[:, cols] = flow.astype(flow_ref.dtype)
        stat_ref[:8, cols] += fold(flow)
        stat_ref[8:, cols] += fold(flow * normed)
    out_ref[...] = jnp.dot(z_ref[...], top_ref[...], preferred_element_type=jnp.float32)
    sent_ref[pl.ds(pl.multiple_of(step * rows, rows), rows)] = jnp.dot(
        z_ref[...], top_peer_ref[...], preferred_element_type=jnp.float32
    ).astype(jnp.bfloat16)
    acc_ref[:half] += lax.dot_general(cot_ref[...], z_ref[...], ROWS_ROWS, preferred_element_type=jnp.float32)
    acc_ref[half:] += lax.dot_general(cot_peer_ref[...], z_ref[...], ROWS_ROWS, preferred_element_type=jnp.float32)

    @pl.when(step == last)
    def _():
        rest_ref[...] = sent_ref[pl.ds(last * rows, rows)]

    def after():
        lax.fori_loop(0, last, lambda index, carry: (send(index).wait(), carry)[1], 0)

    return after


def crown_fill(*refs):
    used, given, own = refs[:10], refs[10:16], refs[17:]
    grad_ref, acc_ref = given[3], own[1]
    half = acc_ref.shape[0] // 2
    task = lax.axis_index("task")

    def part(index):
        def run():
            place = pl.multiple_of((task if index == 0 else 1 - task) * half, half)

            def one(i, carry):
                cols = pl.ds(pl.multiple_of(i * half, half), half)
                turned = acc_ref[pl.ds(index * half, half), cols].T
                grad_ref[cols, pl.ds(place, half)] = turned.astype(jnp.bfloat16)
                return carry

            lax.fori_loop(0, acc_ref.shape[1] // half, one, 0)

        return run

    return part(0), part(1)


def wide(mask, width):
    return jnp.concatenate([mask] * (width // mask.shape[1]), axis=1)


def gather_stats(stat_ref, hidden, first):
    @pl.when(first)
    def _():
        stat_ref[:16] = jnp.zeros_like(stat_ref[:16])
        mean = jnp.sum(hidden, axis=0, keepdims=True) / hidden.shape[0]
        stat_ref[16:] = jnp.broadcast_to(mean, stat_ref[16:].shape)

    away = hidden - stat_ref[16:17]
    stat_ref[:8] += fold(away)
    stat_ref[8:16] += fold(away * away)


def normal(hidden, vec_ref):
    return (hidden - vec_ref[0:1]) * vec_ref[1:2]


def squeeze_kernel(x_ref, w_ref, out_ref, stat_ref):
    hidden = jnp.dot(x_ref[...], w_ref[...], preferred_element_type=jnp.float32)
    out_ref[...] = hidden
    gather_stats(stat_ref, hidden, pl.program_id(0) == 0)


def mesh_kernel(h_ref, vec_ref, mask_ref, w_ref, out_ref, side_ref, stat_ref, pad_ref):
    rows, mid = h_ref.shape
    inner = pl.ds(SIDE, rows)
    before = normal(h_ref[...], vec_ref) * vec_ref[2:3] + vec_ref[3:4]
    phi, _ = tail_and_bell(before)
    low = (before * phi).astype(jnp.bfloat16)
    kept = low.astype(jnp.float32)
    left = wide(mask_ref[:, :128].astype(jnp.float32), mid)
    right = wide(mask_ref[:, 128:256].astype(jnp.float32), mid)

    @pl.when(pl.program_id(0) == 0)
    def _():
        pad_ref[:SIDE] = jnp.zeros_like(pad_ref[:SIDE])
        pad_ref[SIDE + rows :] = jnp.zeros_like(pad_ref[:SIDE])

    pad_ref[inner, :mid] = (pltpu.roll(kept, 1, 0) * left).astype(jnp.bfloat16)
    pad_ref[inner, mid : 2 * mid] = low
    pad_ref[inner, 2 * mid :] = (pltpu.roll(kept, rows - 1, 0) * right).astype(jnp.bfloat16)
    side_ref[...] = pad_ref[inner].T
    above = wide(mask_ref[:, 256:384], 3 * mid)
    below = wide(mask_ref[:, 384:], 3 * mid)
    hidden = jnp.dot(pad_ref[inner], w_ref[3 * mid : 6 * mid], preferred_element_type=jnp.float32)
    hidden += jnp.dot(pad_ref[:rows] * above, w_ref[: 3 * mid], preferred_element_type=jnp.float32)
    hidden += jnp.dot(pad_ref[2 * SIDE :] * below, w_ref[6 * mid :], preferred_element_type=jnp.float32)
    out_ref[...] = hidden
    gather_stats(stat_ref, hidden, pl.program_id(0) == 0)


def widen_kernel(h_ref, vec_ref, w_ref, out_ref, low_ref, stat_ref):
    before = normal(h_ref[...], vec_ref) * vec_ref[2:3] + vec_ref[3:4]
    phi, _ = tail_and_bell(before)
    low = (before * phi).astype(jnp.bfloat16)
    low_ref[...] = low.T
    hidden = jnp.dot(low, w_ref[...], preferred_element_type=jnp.float32)
    out_ref[...] = hidden
    gather_stats(stat_ref, hidden, pl.program_id(0) == 0)


def norm_grad(upstream, normed, vec_ref):
    return vec_ref[4:5] * (upstream - vec_ref[5:6] - normed * vec_ref[6:7])


def act_slope(value):
    phi, bell = tail_and_bell(value)
    return phi + value * bell * DENSITY


def gather_flow(stat_ref, flow, normed, first):
    @pl.when(first)
    def _():
        stat_ref[...] = jnp.zeros_like(stat_ref)

    stat_ref[:8] += fold(flow)
    stat_ref[8:16] += fold(flow * normed)


def narrow_kernel(flow_ref, normed_ref, vec_ref, two_ref, vectwo_ref, low_ref, w_ref, out_ref, grad_ref, stat_ref, dh_ref):
    step = pl.program_id(0)
    rows = flow_ref.shape[0]
    dh = norm_grad(flow_ref[...].astype(jnp.float32), normed_ref[...].astype(jnp.float32), vec_ref)
    low = dh.astype(jnp.bfloat16)
    dh_ref[pl.ds(pl.multiple_of(step * rows, rows), rows)] = low
    dq = lax.dot_general(low, w_ref[...], COLS_COLS, preferred_element_type=jnp.float32)
    normed = normal(two_ref[...], vectwo_ref)
    flow = dq * act_slope(normed * vectwo_ref[2:3] + vectwo_ref[3:4])
    out_ref[...] = flow
    gather_flow(stat_ref, flow, normed, step == 0)


def narrow_fill(flow_ref, normed_ref, vec_ref, two_ref, vectwo_ref, low_ref, w_ref, out_ref, grad_ref, stat_ref, dh_ref):
    half = dh_ref.shape[1] // 2

    def part(index):
        def run():
            def one(i, carry):
                cols = pl.ds(pl.multiple_of(index * half + i * 512, 512), 512)
                grad_ref[:, cols] = jnp.dot(
                    low_ref[...], dh_ref[:, cols], preferred_element_type=jnp.float32
                ).astype(jnp.bfloat16)
                return carry

            lax.fori_loop(0, half // 512, one, 0)

        return run

    return part(0), part(1)


def across(source, target, sems, hop="task"):
    task = lax.axis_index("task")
    place = lax.axis_index("batch")
    device = (1 - task, place) if hop == "task" else (task, place + 1 - 2 * lax.rem(place, 2))
    return pltpu.make_async_remote_copy(
        src_ref=source,
        dst_ref=target,
        send_sem=sems.at[0],
        recv_sem=sems.at[1],
        device_id=device,
        device_id_type=MESH,
    )


def tiled(kernel, tile, moving, flags, outs, fixed, scratch, name, stats=None, sends=(), far=(), fill=None, turns=(), aside=None):
    tasks = lax.axis_size("task")
    batch = lax.axis_size("batch")
    rows = moving[0].shape[0]

    def block(array):
        return pl.BlockSpec((tile,) + array.shape[1:], lambda i: (i,) + (0,) * (len(array.shape) - 1))

    def turned(array):
        return pl.BlockSpec((array.shape[0], tile), lambda i: (0, i))

    def whole(array):
        zeros = (0,) * len(array.shape)
        return pl.BlockSpec(array.shape, lambda i: zeros)

    hbm = pl.BlockSpec(memory_space=pl.ANY)
    operands = list(moving)
    in_specs = [(whole, block, lambda a: hbm)[m](a) for a, m in zip(moving, flags)]
    out_shape = outs + fixed + list(far)
    out_specs = [turned(a) if i in turns else block(a) for i, a in enumerate(outs)] + [whole(a) for a in fixed] + [hbm for a in far]
    scratch = list(scratch)
    params = dict(vmem_limit_bytes=VMEM_BYTES)
    ins, made, held = len(operands), len(out_shape), len(scratch)
    run = kernel
    if stats is not None:
        vecs, forward, ident = stats
        width = vecs[0].shape[1]
        params.update(collective_id=ident, has_side_effects=True)
        operands += vecs
        in_specs += [whole(vec) for vec in vecs]
        out_shape = out_shape + [shape32(16, width)]
        out_specs = out_specs + [whole(out_shape[-1])]
        scratch = scratch + [pltpu.VMEM((24 if forward else 16, width), jnp.float32)]
        scratch = scratch + Exchange.scratch(tasks, batch, width)
        for array, _, shape, _ in sends:
            operands.append(array)
            in_specs.append(hbm)
            out_shape = out_shape + [jax.ShapeDtypeStruct(shape, array.dtype)]
            out_specs = out_specs + [hbm]
            scratch = scratch + [pltpu.SemaphoreType.DMA((2,))]

        if aside is not None:
            operands.append(aside[0])
            in_specs.append(hbm)
            out_shape = out_shape + list(aside[1])
            out_specs = out_specs + [hbm for _ in aside[1]]
            scratch = scratch + list(aside[2])

        def run(*refs):
            refs = list(refs)
            take = lambda n: [refs.pop(0) for _ in range(n)]
            used = take(ins)
            vec_refs = take(len(vecs))
            sources = take(len(sends))
            own_in = take(0 if aside is None else 1)
            given = take(made)
            out_ref = take(1)[0]
            targets = take(len(sends))
            own_out = take(0 if aside is None else len(aside[1]))
            own = take(held)
            stat_ref = take(1)[0]
            exchange = Exchange(tasks, batch, *take(6))
            step = pl.program_id(0)
            last = pl.num_programs(0) - 1

            @pl.when(step == 0)
            def _():
                exchange.greet()

            early = len(sends) > 0 or len(far) > 0

            def crossing(index):
                _, view, _, hop = sends[index]
                return across(view(sources[index]), targets[index], cross_sems[index], hop)

            cross_sems = take(len(sends))
            if early and aside is None:

                @pl.when(step == 1)
                def _():
                    exchange.met()
                    for index in range(len(sends)):
                        crossing(index).start()

            if aside is not None:
                helper = aside[3](exchange, *own_in, *own_out, *refs)
                helper.before(step)

            after = kernel(*used, *given, stat_ref, *own)
            if aside is not None:
                helper.after(step)

                @pl.when(step == 1)
                def _():
                    for index in range(len(sends)):
                        crossing(index).start()

            @pl.when(step == last)
            def _():
                if not early and aside is None:
                    exchange.met()
                fillers = (None, None) if fill is None else fill(*used, *given, stat_ref, *own)
                settle_stats(exchange, stat_ref, vec_refs, out_ref, rows, rows * tasks * batch, forward, fillers)
                for index in range(len(sends)):
                    crossing(index).wait()
                if after is not None:
                    after()
                if aside is not None:
                    helper.end()

    return pl.pallas_call(
        run,
        grid=(rows // tile,),
        out_shape=out_shape,
        in_specs=in_specs,
        out_specs=out_specs,
        scratch_shapes=scratch,
        compiler_params=pltpu.CompilerParams(**params),
        name=name,
    )(*operands)


def shape32(*shape):
    return jax.ShapeDtypeStruct(shape, jnp.float32)


def shape16(*shape):
    return jax.ShapeDtypeStruct(shape, jnp.bfloat16)


def squeeze(flat_in, w_reduce, stats, tile):
    rows, mid = flat_in.shape[0], w_reduce.shape[1]
    return tiled(squeeze_kernel, tile, [flat_in, w_reduce], [1, 0], [shape32(rows, mid)], [], [], "squeeze", stats)


def mesh_forward(h_one, vec, masks, taps, stats, sends, tile):
    rows, mid = h_one.shape
    return tiled(
        mesh_kernel, tile, [h_one, vec, masks, taps], [1, 0, 1, 0],
        [shape32(rows, mid), shape16(3 * mid, rows)], [],
        [pltpu.VMEM((tile + 2 * SIDE, 3 * mid), jnp.bfloat16)], "mesh_forward", stats, sends, turns=(1,),
    )


def widen(h_two, vec, w_expand, stats, sends, tile):
    rows, mid = h_two.shape
    width = w_expand.shape[1]
    return tiled(
        widen_kernel, tile, [h_two, vec, w_expand], [1, 0, 0],
        [shape32(rows, width), shape16(mid, rows)], [], [], "widen", stats, sends, turns=(1,),
    )


class HeadsAside:
    def __init__(self, batch, shape, last, exchange, source, target, work, *room):
        self.exchange, self.work, self.target, self.last = exchange, work, target, last
        self.sum = Reduction(Grid(batch), work, None, *room[:11], "owner")
        self.load = pltpu.make_async_copy(source, work, room[11].at[0])
        self.sems = room[11]

    def before(self, step):
        @pl.when(step == 0)
        def _():
            self.load.start()

    def out(self, part):
        grid = self.sum.grid
        bits = grid.bits(part)
        view = self.sum.view(grid.core, part, bits[0], bits[1])
        return pltpu.make_async_copy(view, self.target.at[part], self.sems.at[1 + part])

    def after(self, step):
        @pl.when(step == 0)
        def _():
            self.exchange.met()
            self.load.wait()
            self.sum.stage(0)

        @pl.when(step == 1)
        def _():
            self.sum.stage(1)

        @pl.when(step == self.last)
        def _():
            self.sum.stage(2)

    def end(self):
        for part in range(2):
            self.sum.finish(2, part)
            self.out(part).start()
        for part in range(2):
            self.out(part).wait()


def narrow(flow, normed, vec_three, h_two, vec_two, q_two, w_expand, heads, rest, stats, tile):
    rows, mid = h_two.shape
    width = w_expand.shape[1]
    batch = lax.axis_size("batch")
    high, across_ = heads.shape
    scratch = [pltpu.VMEM(heads.shape, jnp.bfloat16)] + Reduction.scratch(high, across_, "owner", batch // LOW)
    scratch += [pltpu.SemaphoreType.DMA((3,))]
    helper = functools.partial(HeadsAside, batch, heads.shape, rows // tile - 1)
    return tiled(
        narrow_kernel, tile, [flow, normed, vec_three, h_two, vec_two, q_two, w_expand], [1, 1, 0, 1, 0, 0, 0],
        [shape32(rows, mid)], [shape16(mid, width)], [pltpu.VMEM((rows, width), jnp.bfloat16)], "narrow", stats,
        [(rest, lambda ref: ref, rest.shape, "task")], fill=narrow_fill, aside=(heads, [shape16(2, high // 8, across_ // 2)], scratch, helper),
    )


def crown(h_three, flat_in, limits, cots, cot_parts, top, top_parts, vec, stats, tile, piece):
    rows, width = flat_in.shape
    half = cots.shape[2]
    return tiled(
        functools.partial(crown_kernel, piece), tile,
        [h_three, flat_in, limits, cots, *cot_parts, top, *top_parts, vec], [1, 1, 1, 2, 2, 2, 0, 2, 2, 0],
        [shape32(rows, half), shape16(rows, width), shape16(rows, width)], [shape16(width, 2 * half), shape16(tile, half)],
        [
            pltpu.VMEM((tile, width), jnp.bfloat16),
            pltpu.VMEM((2 * half, width), jnp.float32),
            pltpu.VMEM((rows, half), jnp.bfloat16),
            pltpu.SemaphoreType.DMA((rows // tile, 2)),
            pltpu.VMEM((rows, half), jnp.bfloat16),
            pltpu.VMEM((rows, half), jnp.bfloat16),
            pltpu.VMEM((width, half), jnp.bfloat16),
            pltpu.SemaphoreType.DMA((5,)),
            pltpu.SemaphoreType.DMA((2,)),
            pltpu.VMEM((2, tile, half), jnp.bfloat16),
        ],
        "crown", stats, (), [shape16(rows, half)], crown_fill,
    )


class Stream:
    def __init__(self, view, held, sems):
        self.view, self.held, self.sems = view, held, sems

    def copy(self, index):
        slot = lax.rem(index, 2)
        return pltpu.make_async_copy(self.view(index), self.held.at[slot], self.sems.at[slot])

    def start(self, index):
        self.copy(index).start()

    def take(self, index, count):
        self.copy(index).wait()

        @pl.when(index + 1 < count)
        def _():
            self.start(index + 1)

        return self.held.at[lax.rem(index, 2)]


def back_kernel(rows, tasks, batch, tile, *refs):
    refs = list(refs)

    def take(count):
        return [refs.pop(0) for _ in range(count)]

    (flow_hbm, two_hbm, one_hbm, side_hbm, mask_hbm, w_hbm, x_hbm, heads_hbm, expand_hbm) = take(9)
    vectwo_ref, vecone_ref = take(2)
    (out_hbm, heads_out, expand_out, spatial_out, reduce_out, vec_ref) = take(6)
    (two_buf, mask_buf, x_buf) = take(3)
    (side_ref, lane_ref, flow_ref, w_ref) = take(4)
    heads_work, expand_work, spatial_work, reduce_work, stat_ref = take(5)
    pair_sems, whole_sems, flow_sems = take(3)
    exchange = Exchange(tasks, batch, *take(6))
    grid = Grid(batch)
    mid = flow_hbm.shape[1]
    width = x_hbm.shape[1]
    spans = rows // tile

    def blocks(ref, height):
        return lambda index: ref.at[pl.ds(pl.multiple_of(index * height, height), height)]

    exchange.greet()

    def flow_load(index):
        return pltpu.make_async_copy(
            blocks(flow_hbm, tile)(index), blocks(flow_ref, tile)(index), flow_sems.at[index]
        )

    twos = Stream(blocks(two_hbm, tile), two_buf, pair_sems.at[1])
    masks = Stream(blocks(mask_hbm, tile), mask_buf, pair_sems.at[2])
    ones = Stream(blocks(one_hbm, tile), two_buf, pair_sems.at[3])
    dh_ref, normed_ref, dht_ref = lane_ref.at[:, :mid], lane_ref.at[:, mid : 2 * mid], side_ref.at[:mid]
    across_cols = x_buf.shape[2]
    columns = Stream(
        lambda index: x_hbm.at[:, pl.ds(pl.multiple_of(index * across_cols, across_cols), across_cols)],
        x_buf, pair_sems.at[0],
    )
    loads = [
        pltpu.make_async_copy(source, target, whole_sems.at[index])
        for index, (source, target) in enumerate(
            [(heads_hbm, heads_work), (side_hbm, side_ref), (expand_hbm, expand_work), (w_hbm, w_ref)]
        )
    ]
    heads_load, side_load, expand_load, w_load = loads
    keep = pltpu.make_async_copy(dh_ref, out_hbm, whole_sems.at[4])
    heads_load.start()
    flow_load(0).start()
    for stream in (twos, masks):
        stream.start(0)
    expand_load.start()
    for index in range(1, spans):
        flow_load(index).start()
    side_load.start()
    w_load.start()

    third = spatial_work.shape[0] // 3
    works = [(heads_work, heads_out, "owner"), (expand_work, expand_out, "wide")]
    for index in range(3):
        span = pl.ds(index * third, third)
        works.append((spatial_work.at[span], spatial_out.at[span], "tall"))
    for index in range(2):
        span = pl.ds(index * width // 2, width // 2)
        works.append((reduce_work.at[span], reduce_out.at[span], "tall"))
    reductions = []
    for work, out, kind in works:
        shape = heads_out.shape if kind == "owner" else None
        reductions.append(Reduction(grid, work, out, *take(11), kind, shape))

    def tick(name):
        for item, stage in AGENDA.get(name, ()):
            reductions[item].stage(stage)

    def ticks(name, index, count, scale=1, shift=0):
        for step in range(count):
            label = "%s%d" % (name, step * scale + shift)
            if label in AGENDA:

                @pl.when(index == step)
                def _():
                    tick(label)

    def lanes(index, carry):
        span = pl.ds(pl.multiple_of(index * tile, tile), tile)
        flow_load(index).wait()
        flow = flow_ref[span]
        normed = normal(twos.take(index, spans)[...], vectwo_ref)
        mask = masks.take(index, spans)
        dh = norm_grad(flow, normed, vectwo_ref)
        above = wide(mask[:, 256:384].astype(jnp.float32), mid)
        below = wide(mask[:, 384:].astype(jnp.float32), mid)
        low = jnp.bfloat16
        zero = jnp.zeros((SIDE, mid), low)
        lane_ref[span, mid : 2 * mid] = dh.astype(low)
        lane_ref[span, :mid] = jnp.concatenate([(dh * above)[SIDE:].astype(low), zero], axis=0)
        lane_ref[span, 2 * mid :] = jnp.concatenate([zero, (dh * below)[: tile - SIDE].astype(low)], axis=0)

        @pl.when(index == 0)
        def _():
            expand_load.wait()

        ticks("lane", index, 4)
        return carry

    exchange.met()
    heads_load.wait()
    tick("start")
    lax.fori_loop(0, spans, lanes, 0)
    masks.start(0)
    ones.start(0)
    side_load.wait()

    def spatial(index, carry):
        a, b = index // 3, lax.rem(index, 3)
        rows_here = pl.ds(pl.multiple_of(b * mid, mid), mid)
        cols = pl.ds(pl.multiple_of(a * mid, mid), mid)
        part = jnp.dot(side_ref[rows_here], lane_ref[:, cols], preferred_element_type=jnp.float32)
        spatial_work[pl.ds(pl.multiple_of(index * mid, mid), mid)] = part.astype(jnp.bfloat16)
        ticks("sp", index, 9)
        return carry

    lax.fori_loop(0, 9, spatial, 0)
    w_load.wait()

    def taps(index, carry):
        span = pl.ds(pl.multiple_of(index * tile, tile), tile)
        mask = masks.take(index, spans)
        pieces = []
        for b in range(3):
            total = None
            for a in range(3):
                part = lax.dot_general(
                    lane_ref[span, a * mid : (a + 1) * mid], w_ref[3 * a + b], COLS_COLS,
                    preferred_element_type=jnp.float32,
                )
                total = part if total is None else total + part
            pieces.append(total)
            if b < 2:
                ticks("tap", index, 4, 3, b)
        left = wide(mask[:, :128].astype(jnp.float32), mid)
        right = wide(mask[:, 128:256].astype(jnp.float32), mid)
        dq = pieces[1] + pltpu.roll(pieces[0] * left, tile - 1, 0) + pltpu.roll(pieces[2] * right, 1, 0)
        normed = normal(ones.take(index, spans)[...], vecone_ref)
        flow = dq * act_slope(normed * vecone_ref[2:3] + vecone_ref[3:4])
        flow_ref[span] = flow
        normed_ref[span] = normed.astype(jnp.bfloat16)
        gather_flow(stat_ref, flow, normed, index == 0)
        ticks("tap", index, 4, 3, 2)
        return carry

    lax.fori_loop(0, spans, taps, 0)
    columns.start(0)
    settle_stats(exchange, stat_ref, [vecone_ref], vec_ref, rows, rows * tasks * batch, False)
    tick("xch")

    def inner(index, carry):
        span = pl.ds(pl.multiple_of(index * tile, tile), tile)
        dh = norm_grad(flow_ref[span], normed_ref[span].astype(jnp.float32), vec_ref)
        low = dh.astype(jnp.bfloat16)
        dh_ref[span] = low
        dht_ref[:, span] = low.T
        return carry

    lax.fori_loop(0, spans, inner, 0)
    keep.start()
    tick("inner")
    count = width // across_cols

    def reduce(index, carry):
        part = jnp.dot(dht_ref[...], columns.take(index, count)[...], preferred_element_type=jnp.float32)
        span = pl.ds(pl.multiple_of(index * across_cols, across_cols), across_cols)
        reduce_work[span] = part.T.astype(jnp.bfloat16)
        ticks("red", index, 4)
        return carry

    lax.fori_loop(0, count, reduce, 0)
    keep.wait()
    tick("tail")


def back(flow, h_two, vec_two, h_one, vec_one, sides, masks, w_spatial, flat_in, heads, expand, heads_shape, ident, tile):
    tasks = lax.axis_size("task")
    batch = lax.axis_size("batch")
    far = batch // LOW
    rows, mid = h_one.shape
    width = flat_in.shape[1]
    full, low = jnp.float32, jnp.bfloat16
    cols = 512
    hbm = pl.BlockSpec(memory_space=pl.ANY)
    vmem = pl.BlockSpec(memory_space=pltpu.VMEM)
    shapes = [(heads_shape, "owner"), (expand.shape, "wide")] + [((3 * mid, mid), "tall")] * 3
    shapes += [((width // 2, mid), "tall")] * 2
    scratch = [
        pltpu.VMEM((2, tile, mid), full),
        pltpu.VMEM((2, tile, 512), low),
        pltpu.VMEM((2, rows, cols), low),
        pltpu.VMEM((3 * mid, rows), low),
        pltpu.VMEM((rows, 3 * mid), low),
        pltpu.VMEM((rows, mid), full),
        pltpu.VMEM(w_spatial.shape, low),
        pltpu.VMEM(heads.shape, low),
        pltpu.VMEM(expand.shape, low),
        pltpu.VMEM((9 * mid, mid), low),
        pltpu.VMEM((width, mid), low),
        pltpu.VMEM((16, mid), full),
        pltpu.SemaphoreType.DMA((4, 2)),
        pltpu.SemaphoreType.DMA((5,)),
        pltpu.SemaphoreType.DMA((rows // tile,)),
    ] + Exchange.scratch(tasks, batch, mid)
    for (high, across_), kind in shapes:
        scratch += Reduction.scratch(high, across_, kind, far, kind == "owner")
    return pl.pallas_call(
        functools.partial(back_kernel, rows, tasks, batch, tile),
        out_shape=[
            shape16(rows, mid), shape16(*heads_shape), shape16(*expand.shape), shape16(9 * mid, mid),
            shape16(width, mid), shape32(16, mid),
        ],
        in_specs=[hbm] * 9 + [vmem] * 2,
        out_specs=[hbm] * 5 + [vmem],
        scratch_shapes=scratch,
        compiler_params=pltpu.CompilerParams(
            vmem_limit_bytes=VMEM_BYTES, collective_id=ident, has_side_effects=True
        ),
        name="back",
    )(flow, h_two, h_one, sides, masks, w_spatial, flat_in, heads, expand, vec_two, vec_one)


def finish_kernel(
    dh_ref, up_ref, heads_ref, expand_ref, spatial_ref, reduce_ref, mine_ref, came_ref, rest_ref, w_ref, one_ref, two_ref, three_ref,
    out_ref, heads_out, expand_out, spatial_out, reduce_out, both_ref, *sums,
):
    full = jnp.float32
    task = lax.axis_index("task")
    half = heads_out.shape[1]
    back = lax.dot_general(dh_ref[...], w_ref[...], COLS_COLS, preferred_element_type=full)
    out_ref[...] = (up_ref[...].astype(full) + back).astype(jnp.bfloat16)
    heads_out[...] = jnp.where(task == 0, heads_ref[:, :half], heads_ref[:, half:]).astype(full)
    expand_out[...] = expand_ref[...].astype(full)
    spatial_out[...] = spatial_ref[...].astype(full)
    reduce_out[...] = reduce_ref[...].astype(full)
    both_ref[task] = mine_ref[...]
    ends = pl.program_id(0) == pl.num_programs(0) - 1
    both_ref[1 - task] = jnp.where(ends, rest_ref[...], came_ref[...]).astype(full)

    @pl.when(pl.program_id(0) == 0)
    def _():
        for index, vec_ref in enumerate((one_ref, two_ref, three_ref)):
            sums[2 * index][...] = vec_ref[9:10]
            sums[2 * index + 1][...] = vec_ref[8:9]


def finish(dh, up, heads, expand, spatial, reduce, mine, came, rest, w_reduce, vecs):
    steps = mine.shape[0] // rest.shape[0]

    def block(array, lead=0):
        zeros = (0,) * (len(array.shape) - 1 - lead)
        height = array.shape[lead] // steps
        return pl.BlockSpec(array.shape[:lead] + (height,) + array.shape[lead + 1 :], lambda i: (0,) * lead + (i,) + zeros)

    def whole(array):
        return pl.BlockSpec(array.shape, lambda i: (0, 0))

    rows, half = mine.shape
    moving = [dh, up, heads, expand, spatial, reduce, mine, came]
    fixed = [rest, w_reduce, *vecs]
    outs = [shape16(*up.shape), shape32(heads.shape[0], half), shape32(*expand.shape), shape32(*spatial.shape), shape32(*reduce.shape)]
    both = shape32(2, rows, half)
    sums = [shape32(1, vec.shape[1]) for vec in vecs for _ in range(2)]
    return pl.pallas_call(
        finish_kernel,
        grid=(steps,),
        out_shape=outs + [both] + sums,
        in_specs=[block(a) for a in moving] + [whole(a) for a in fixed],
        out_specs=[block(a) for a in outs] + [block(both, 1)] + [whole(a) for a in sums],
        compiler_params=pltpu.CompilerParams(vmem_limit_bytes=VMEM_BYTES),
        name="finish",
    )(*moving, *fixed)


def body(
    inputs,
    crop_cuts,
    threshold,
    w_reduce,
    w_spatial,
    w_expand,
    w_heads,
    gain_one,
    bias_one,
    gain_two,
    bias_two,
    gain_three,
    bias_three,
    cotangent,
):
    low = jnp.bfloat16
    full = jnp.float32
    canvases, pixels, width = inputs.shape[1:]
    mid = w_reduce.shape[1]
    rows = canvases * pixels
    half = w_heads.shape[2]
    cots = cotangent.reshape(2, rows, half)
    top_mine = w_heads[0]

    def params(gain, bias):
        return [gain.reshape(1, -1), bias.reshape(1, -1)]

    lines = jnp.arange(SIDE, dtype=jnp.int32)
    cuts = crop_cuts.reshape(canvases, 2)
    from_above = jnp.logical_not((lines == cuts[:, 0:1]) | (lines == 0)[None, :])
    from_left = jnp.logical_not((lines == cuts[:, 1:2]) | (lines == 0)[None, :])
    from_below = jnp.pad(from_above[:, 1:], ((0, 0), (0, 1)))
    from_right = jnp.pad(from_left[:, 1:], ((0, 0), (0, 1)))
    shape = (canvases, SIDE, SIDE, 128)
    masks = jnp.concatenate(
        [jnp.broadcast_to(m[:, None, :, None], shape) for m in (from_left, from_right)]
        + [jnp.broadcast_to(m[:, :, None, None], shape) for m in (from_above, from_below)],
        axis=3,
    ).astype(low).reshape(rows, 512)

    flat_in = inputs.reshape(rows, width)
    core = lambda: lax.rem(lax.axis_index("batch"), 2)
    other = lambda: 1 - lax.axis_index("task")
    quarter = rows // 4
    top_rows = width // 2
    h_one, vec_one = squeeze(flat_in, w_reduce, (params(gain_one, bias_one), True, 0), min(rows, 512))
    sends = [
        (top_mine, lambda ref: ref.at[pl.ds(pl.multiple_of(core() * top_rows, top_rows), top_rows)], (top_rows, half), "task"),
        (cots, lambda ref: ref.at[other(), pl.ds(0, quarter)], (quarter, half), "task"),
    ]
    h_two, sides, vec_two, top_one, cot_one = mesh_forward(
        h_one, vec_one, masks, w_spatial.reshape(9 * mid, mid), (params(gain_two, bias_two), True, 1), sends, pixels
    )
    sends = [
        (top_one, lambda ref: ref, (top_rows, half), "core"),
        (cots, lambda ref: ref.at[other(), pl.ds(quarter, quarter)], (quarter, half), "task"),
    ]
    h_three, q_two, vec_three, top_two, cot_two = widen(
        h_two, vec_two, w_expand, (params(gain_three, bias_three), True, 2), sends, pixels
    )
    out_mine, flow, normed, grad_heads, rest, out_peer, vec_three = crown(
        h_three, flat_in, threshold.reshape(rows, width), cots, (cot_one, cot_two), top_mine, (top_one, top_two), vec_three,
        ([vec_three], False, 3), pixels, 256,
    )
    heads_shape = grad_heads.shape
    flow_two, grad_expand, vec_two, rest, grad_heads = narrow(
        flow, normed, vec_three, h_two, vec_two, q_two, w_expand, grad_heads, rest, ([vec_two], False, 4), min(rows, 512)
    )
    dh_one, grad_heads, grad_expand, grad_spatial, grad_reduce, vec_one = back(
        flow_two, h_two, vec_two, h_one, vec_one, sides, masks, w_spatial, flat_in, grad_heads, grad_expand, heads_shape, 5,
        min(rows, 512),
    )
    grad_inputs, grad_heads, grad_expand, grad_spatial, grad_reduce, head_out, *sums = finish(
        dh_one, flow, grad_heads, grad_expand, grad_spatial, grad_reduce, out_mine, out_peer, rest, w_reduce,
        (vec_one, vec_two, vec_three),
    )
    return (
        head_out.reshape(1, 2, canvases, pixels, half),
        grad_inputs.reshape(inputs.shape),
        grad_reduce,
        grad_spatial.reshape(w_spatial.shape),
        grad_expand,
        grad_heads[None],
        *[row.reshape(-1) for row in sums],
    )


def solution(mesh):
    in_specs = (
        P("task", "batch", None, None),
        P("task", "batch", None),
        P("task", "batch", None, None),
        P(),
        P(),
        P(),
        P("task", None, None),
        P(),
        P(),
        P(),
        P(),
        P(),
        P(),
        P("task", None, "batch", None, None),
    )
    out_specs = (
        P("task", None, "batch", None, None),
        P("task", "batch", None, None),
        P(),
        P(),
        P(),
        P("task", None, None),
        P(),
        P(),
        P(),
        P(),
        P(),
        P(),
    )
    return jax.shard_map(body, mesh=mesh, in_specs=in_specs, out_specs=out_specs, check_vma=False)
```

```python
import functools
import math

import jax
import jax.numpy as jnp
from jax import lax
from jax.experimental import pallas as pl
from jax.experimental.pallas import tpu as pltpu
from jax.sharding import PartitionSpec as P

SIDE = 16
EPS = 1e-05
FLOOR = 0.1
SOFT = 0.25
ROOT_HALF = 0.7071067811865476
DENSITY = 0.3989422804014327
LOG2E = 1.4426950408889634
ERF_P = 0.3275911
ERF_A = (0.254829592, -0.284496736, 1.421413741, -1.453152027, 1.061405429)
ROWS_ROWS = (((0,), (0,)), ((), ()))
COLS_COLS = (((1,), (1,)), ((), ()))
MESH = pl.DeviceIdType.MESH
LOW = 4
VMEM_BYTES = 62 * 2**20


AGENDA = {
    "start": ((0, 3),),
    "lane0": ((1, 0),),
    "lane2": ((1, 1),),
    "sp1": ((0, 4),),
    "sp2": ((2, 0),),
    "sp4": ((1, 2), (2, 1),),
    "sp5": ((3, 0),),
    "sp8": ((0, 5), (1, 3), (3, 1), (4, 0),),
    "tap1": ((2, 2), (4, 1),),
    "tap5": ((0, 7), (1, 4),),
    "tap7": ((0, 8), (3, 2),),
    "tap8": ((2, 3),),
    "xch": ((1, 5), (2, 4), (3, 3), (4, 2),),
    "inner": ((1, 6),),
    "red1": ((2, 5), (4, 3), (5, 0),),
    "red3": ((3, 4), (5, 1), (6, 0), (1, 7),),
    "tail": ((2, 6), (6, 1), (4, 4), (1, 8), (5, 2), (3, 5), (2, 7), (2, 8), (6, 2), (4, 5), (5, 3), (3, 6), (6, 3), (4, 6), (5, 4), (3, 7), (6, 4), (3, 8), (5, 5), (4, 7), (6, 5), (5, 6), (4, 8), (6, 6), (5, 7), (5, 8), (6, 7), (6, 8),),
}


class Reduction:
    def __init__(
        self, grid, work, result, core, first_a, first_b, second, last, done, send, recv, far_send, far_recv, local,
        kind, shape=None,
    ):
        self.grid, self.work, self.result = grid, work, result
        self.core_room, self.first_rooms, self.second_room, self.last_room = core, (first_a, first_b), second, last
        self.done = done
        self.send, self.recv, self.far_send, self.far_recv = send, recv, far_send, far_recv
        self.local = local
        self.kind = kind
        self.resumed = shape is not None
        self.rows, self.cols = shape or work.shape
        sizes = self.sizes(self.rows, self.cols, kind, grid.far)
        self.pieces = sizes[3][0] // sizes[4][0]
        self.mine = lax.rem(grid.high, self.pieces)

    @staticmethod
    def sizes(rows, cols, kind, far):
        if kind == "wide":
            core, first, second = (rows, cols // 2), (rows, cols // 8), (rows, cols // 16)
            firsts = first, first
        elif kind == "tall":
            core, first, second = (rows // 2, cols), (rows // 2, cols // 4), (rows // 4, cols // 4)
            firsts = first, first
        else:
            core, second = (rows // 2, cols), (rows // 8, cols // 2)
            firsts = (rows // 4, cols // 2), (rows // 8, cols)
        pieces = max(n for n in range(1, far + 1) if far % n == 0 and second[0] % (8 * n) == 0)
        return core, *firsts, second, (second[0] // pieces, second[1])

    @staticmethod
    def scratch(rows, cols, kind, far, resumed=False):
        core, first_a, first_b, second, last = Reduction.sizes(rows, cols, kind, far)
        if resumed:
            core = first_a = first_b = (16, 128)
        return [
            pltpu.VMEM(core, jnp.bfloat16),
            pltpu.VMEM(first_a, jnp.bfloat16),
            pltpu.VMEM(first_b, jnp.bfloat16),
            pltpu.VMEM((2,) + ((16, 128) if resumed else second), jnp.bfloat16),
            pltpu.VMEM((2, far) + last, jnp.bfloat16),
            pltpu.VMEM((2,) + last, jnp.bfloat16),
            pltpu.SemaphoreType.DMA((10,)),
            pltpu.SemaphoreType.DMA((10,)),
            pltpu.SemaphoreType.DMA((4, far)),
            pltpu.SemaphoreType.DMA((4, far)),
            pltpu.SemaphoreType.DMA((2,)),
        ]

    def view(self, core, part=None, first=None, second=None, piece=None, done=False):
        rows, cols = self.rows, self.cols
        sizes = self.sizes(rows, cols, self.kind, self.grid.far)
        row = col = 0
        shape = sizes[0]
        if self.kind == "wide":
            col = core * (cols // 2)
            if part is not None:
                col = col + part * (cols // 4) + first * (cols // 8)
            if second is not None:
                col = col + second * (cols // 16)
        elif self.kind == "tall":
            row = core * (rows // 2)
            if part is not None:
                col = part * (cols // 2) + first * (cols // 4)
            if second is not None:
                row = row + second * (rows // 4)
        else:
            row = core * (rows // 2)
            if part is not None:
                row = row + part * (rows // 4)
                y, task = (second, first) if part == 0 else (first, second)
                row = row if y is None else row + y * (rows // 8)
                col = 0 if task is None else task * (cols // 2)
            elif done:
                col = self.grid.task * (cols // 2)
                shape = (rows // 2, cols // 2)
        if part is not None:
            shape = sizes[1 + part] if second is None else sizes[3]
        ref = self.result if done else self.work
        if self.resumed and not done:
            ref, row, col = self.work.at[part], 0, 0
        if piece is not None:
            row = row + piece * sizes[4][0]
            shape = sizes[4]
        if not isinstance(row, int):
            row = pl.multiple_of(row, shape[0] & -shape[0])
        if not isinstance(col, int):
            col = pl.multiple_of(col, 128)
        return ref.at[pl.ds(row, shape[0]), pl.ds(col, shape[1])]

    def swap(self, index):
        grid = self.grid
        part = (index + 1) % 2
        bits = grid.bits(part)
        if index == 0:
            source, target, device = self.view(1 - grid.core), self.core_room, grid.core_peer
        elif index < 3:
            source, target = self.view(grid.core, part, 1 - bits[0]), self.first_rooms[part]
            device = grid.peers(part)[0]
        elif index < 5:
            source, target = self.view(grid.core, part, bits[0], 1 - bits[1]), self.second_room.at[part]
            device = grid.peers(part)[1]
        elif index < 7:
            source = self.view(grid.core, part, bits[0], bits[1], done=True)
            target, device = source, grid.y_peer if self.kind == "owner" else grid.peers(part)[1]
        elif index < 9:
            source = self.view(grid.core, part, bits[0], done=True)
            target, device = source, grid.peers(part)[0]
        else:
            source = self.view(grid.core, done=True)
            target, device = source, grid.core_peer
        return pltpu.make_async_remote_copy(
            src_ref=source,
            dst_ref=target,
            send_sem=self.send.at[index],
            recv_sem=self.recv.at[index],
            device_id=device,
            device_id_type=MESH,
        )

    def add(self, target, sources):
        rows = target.shape[0]
        step = math.gcd(rows, 64)

        def one(i, carry):
            span = pl.ds(pl.multiple_of(i * step, step), step)
            total = sources[0][span].astype(jnp.float32)
            for source in sources[1:]:
                total = total + source[span].astype(jnp.float32)
            target[span] = total.astype(jnp.bfloat16)
            return carry

        lax.fori_loop(0, rows // step, one, 0)

    def far_copy(self, part, step, back, inward):
        grid = self.grid
        bits = grid.bits(part)
        if back:
            first = grid.high - self.mine
            slot = first + lax.rem(self.mine + step, self.pieces)
            owner = slot if inward else grid.high
            source = self.done.at[part]
            target = self.view(grid.core, part, bits[0], bits[1], lax.rem(owner, self.pieces), True)
        else:
            slot = lax.rem(grid.high + step, grid.far)
            owner = slot if inward else grid.high
            source = self.view(grid.core, part, bits[0], bits[1], lax.rem(slot, self.pieces))
            target = self.last_room.at[part, owner]
        line = 2 * part + (1 if back else 0)
        return pltpu.make_async_remote_copy(
            src_ref=source,
            dst_ref=target,
            send_sem=self.far_send.at[line, step],
            recv_sem=self.far_recv.at[line, owner],
            device_id=(grid.task, slot * LOW + grid.low),
            device_id_type=MESH,
        )

    def far_start(self, part, back):
        for step in range(1, self.pieces if back else self.grid.far):
            self.far_copy(part, step, back, False).start()

    def far_settle(self, part, back):
        for step in range(1, self.pieces if back else self.grid.far):
            self.far_copy(part, step, back, True).wait_recv()
            self.far_copy(part, step, back, False).wait_send()

    def keep(self, part):
        bits = self.grid.bits(part)
        mine = self.view(self.grid.core, part, bits[0], bits[1], self.mine, True)
        return pltpu.make_async_copy(self.done.at[part], mine, self.local.at[part])

    def finish(self, index, part):
        grid = self.grid
        bits = grid.bits(part)
        if index == 0:
            if part == 0:
                self.swap(0).wait()
                mine = self.view(grid.core)
                self.add(mine, [mine, self.core_room])
        elif index == 1:
            self.swap(1 + part).wait()
            mine = self.view(grid.core, part, bits[0])
            self.add(mine, [mine, self.first_rooms[part]])
        elif index == 2:
            self.swap(3 + part).wait()
            mine = self.view(grid.core, part, bits[0], bits[1])
            self.add(mine, [mine, self.second_room.at[part]])
        elif index == 3:
            self.far_settle(part, False)
            self.last_room[part, grid.high] = self.view(grid.core, part, bits[0], bits[1], self.mine)[...]
            self.add(self.done.at[part], [self.last_room.at[part, slot] for slot in range(grid.far)])
        elif index == 4:
            self.far_settle(part, True)
            self.keep(part).wait()
        elif index < 7:
            self.swap(2 * index - 5 + part).wait()
        elif part == 0:
            self.swap(9).wait()

    def begin(self, index, part):
        if index == 0 or index == 7:
            if part == 0:
                self.swap(9 if index else 0).start()
        elif index < 3:
            self.swap(2 * index - 1 + part).start()
        elif index == 3:
            self.far_start(part, False)
        elif index == 4:
            self.keep(part).start()
            self.far_start(part, True)
        elif index < 7:
            self.swap(2 * index - 5 + part).start()

    def stage(self, index):
        owner = self.kind == "owner"
        if owner and index == 6:
            return
        before = 5 if owner and index == 7 else index - 1
        first = self.resumed and index == 3
        together = index in (1, 7, 8)
        for part in range(2):
            if before >= 0 and not first:
                self.finish(before, part)
            if not together:
                self.begin(index, part)
        if together:
            for part in range(2):
                self.begin(index, part)


class Grid:
    def __init__(self, batch):
        self.task = lax.axis_index("task")
        place = lax.axis_index("batch")
        self.far = batch // LOW
        self.high = place // LOW
        self.low = lax.rem(place, LOW)
        self.core = lax.rem(place, 2)
        self.y = lax.rem(place // 2, 2)
        base = place - self.low
        self.core_peer = (self.task, base + self.y * 2 + (1 - self.core))
        self.x_peer = (1 - self.task, place)
        self.y_peer = (self.task, base + (1 - self.y) * 2 + self.core)

    def bits(self, part):
        return (self.task, self.y) if part == 0 else (self.y, self.task)

    def peers(self, part):
        return (self.x_peer, self.y_peer) if part == 0 else (self.y_peer, self.x_peer)


class Exchange:
    def __init__(self, tasks, batch, near, far, near_send, near_recv, far_send, far_recv):
        place = lax.axis_index("batch")
        self.task = lax.axis_index("task")
        self.high = place // LOW
        self.low = lax.rem(place, LOW)
        self.near_size = tasks * LOW
        self.far_size = batch // LOW
        self.me_near = self.task * LOW + self.low
        self.near, self.far = near, far
        self.near_sems, self.far_sems = (near_send, near_recv), (far_send, far_recv)

    @staticmethod
    def scratch(tasks, batch, width):
        near_size, far_size = tasks * LOW, batch // LOW
        return [
            pltpu.VMEM((near_size + 1, 2 * width // 128, 128), jnp.float32),
            pltpu.VMEM((far_size + 1, 2 * width // 128, 128), jnp.float32),
            pltpu.SemaphoreType.DMA((near_size,)),
            pltpu.SemaphoreType.DMA((near_size,)),
            pltpu.SemaphoreType.DMA((far_size,)),
            pltpu.SemaphoreType.DMA((far_size,)),
        ]

    def near_peer(self, step):
        slot = lax.rem(self.me_near + step, self.near_size)
        return slot, (slot // LOW, self.high * LOW + lax.rem(slot, LOW))

    def far_peer(self, step):
        slot = lax.rem(self.high + step, self.far_size)
        return slot, (self.task, slot * LOW + self.low)

    def peers(self):
        near = [self.near_peer(step)[1] for step in range(1, self.near_size)]
        return near + [self.far_peer(step)[1] for step in range(1, self.far_size)]

    def greet(self):
        barrier = pltpu.get_barrier_semaphore()
        for device in self.peers():
            pl.semaphore_signal(barrier, inc=1, device_id=device, device_id_type=MESH)

    def met(self):
        pl.semaphore_wait(pltpu.get_barrier_semaphore(), self.near_size + self.far_size - 2)

    def hop(self, size, peer, me, held, sems, filler=None):
        def copy(step, slot):
            return pltpu.make_async_remote_copy(
                src_ref=held.at[size],
                dst_ref=held.at[slot],
                send_sem=sems[0].at[step],
                recv_sem=sems[1].at[slot],
                device_id=peer(step)[1],
                device_id_type=MESH,
            )

        for step in range(1, size):
            copy(step, me).start()
        held[me] = held[size]
        if filler is not None:
            filler()
        for step in range(1, size):
            copy(step, peer(step)[0]).wait_recv()
        for step in range(1, size):
            copy(step, me).wait_send()
        return held.at[pl.ds(0, size)]

    def run(self, total, spread, rows, forward, fillers=(None, None)):
        lines = total.shape[1] // 128
        for line in range(lines):
            cols = slice(line * 128, (line + 1) * 128)
            self.near[self.near_size, line : line + 1] = total[:, cols]
            self.near[self.near_size, lines + line : lines + line + 1] = spread[:, cols]
        held = self.hop(self.near_size, self.near_peer, self.me_near, self.near, self.near_sems, fillers[0])
        total, spread = join(held, float(rows), forward)
        self.far[self.far_size, :lines] = total
        self.far[self.far_size, lines:] = spread
        held = self.hop(self.far_size, self.far_peer, self.high, self.far, self.far_sems, fillers[1])
        total, spread = join(held, float(rows * self.near_size), forward)
        flat = lambda array: jnp.concatenate([array[line : line + 1] for line in range(lines)], axis=1)
        return flat(total), flat(spread)


def join(held, share, forward):
    groups, lines = held.shape[0], held.shape[1] // 2
    total = held[0, :lines]
    spread = held[0, lines:]
    for group in range(1, groups):
        total = total + held[group, :lines]
        spread = spread + held[group, lines:]
    if forward:
        centre = total * (1.0 / (share * groups))
        for group in range(groups):
            away = held[group, :lines] * (1.0 / share) - centre
            spread = spread + share * (away * away)
    return total, spread


def settle_stats(exchange, stat_ref, vec_refs, out_ref, rows, count, forward, fillers=(None, None)):
    first = jnp.sum(stat_ref[:8], axis=0, keepdims=True)
    second = jnp.sum(stat_ref[8:16], axis=0, keepdims=True)
    if forward:
        gain, bias = vec_refs[0][...], vec_refs[1][...]
        out_ref[...] = jnp.zeros_like(out_ref)
        out_ref[2:3] = gain
        out_ref[3:4] = bias
        local = first + rows * stat_ref[16:17]
        total, spread = exchange.run(local, second - first * first * (1.0 / rows), rows, True, fillers)
        scale = lax.rsqrt(spread * (1.0 / count) + EPS)
        out_ref[0:1] = total * (1.0 / count)
        out_ref[1:2] = scale
        out_ref[4:5] = scale * gain
    else:
        out_ref[:8] = vec_refs[0][:8]
        total, spread = exchange.run(first, second, rows, False, fillers)
        out_ref[5:6] = total * (1.0 / count)
        out_ref[6:7] = spread * (1.0 / count)
        out_ref[8:9] = total
        out_ref[9:10] = spread
        out_ref[10:] = jnp.zeros_like(out_ref[10:])


def tail_and_bell(value):
    bell = jnp.exp2(value * value * (-0.5 * LOG2E))
    away = jnp.abs(value)
    ratio = pltpu.reciprocal(1.0 + away * (ERF_P * ROOT_HALF))
    poly = 0.5 * ERF_A[4]
    for factor in ERF_A[3::-1]:
        poly = poly * ratio + 0.5 * factor
    tail = poly * ratio * bell
    return jnp.where(value >= 0, 1.0 - tail, tail), bell


def fold(array):
    total = array[:8]
    for start in range(8, array.shape[0], 8):
        total = total + array[start : start + 8]
    return total


def crown_kernel(
    piece, h_ref, x_ref, thr_ref, cot_hbm, cot_one, cot_two, top_ref, top_one, top_two, vec_ref,
    out_ref, flow_ref, normed_ref, grad_ref, rest_ref, came_ref, stat_ref, z_ref, acc_ref, sent_ref, sems,
    cots_ref, cots_peer_ref, top_peer_ref, local_sems, late_sems, twice_ref,
):
    step = pl.program_id(0)
    rows, width = x_ref.shape
    all_rows, half = cots_ref.shape
    split = all_rows // 4
    task = lax.axis_index("task")
    last = pl.num_programs(0) - 1

    def send(index):
        span = pl.ds(pl.multiple_of(index * rows, rows), rows)
        return across(sent_ref.at[span], came_ref.at[span], sems.at[index])

    core = lax.rem(lax.axis_index("batch"), 2)
    high = top_one.shape[0]
    late = across(cot_hbm.at[1 - task, pl.ds(2 * split, 2 * split)], cots_peer_ref.at[pl.ds(2 * split, 2 * split)], late_sems)

    @pl.when(step == 0)
    def _():
        pairs = [
            (cot_hbm.at[task], cots_ref),
            (cot_one, cots_peer_ref.at[pl.ds(0, split)]),
            (cot_two, cots_peer_ref.at[pl.ds(split, split)]),
            (top_one, top_peer_ref.at[pl.ds(pl.multiple_of(core * high, high), high)]),
            (top_two, top_peer_ref.at[pl.ds(pl.multiple_of((1 - core) * high, high), high)]),
        ]
        copies = [pltpu.make_async_copy(a, b, local_sems.at[i]) for i, (a, b) in enumerate(pairs)]
        for copy in copies:
            copy.start()
        for copy in copies:
            copy.wait()

    @pl.when(step == 1)
    def _():
        late.start()

    @pl.when(step == (last + 1) // 2)
    def _():
        late.wait()

    @pl.when(step > 0)
    def _():
        send(step - 1).start()

    span = pl.ds(pl.multiple_of(step * rows, rows), rows)
    cot_ref, cot_peer_ref = cots_ref.at[span], cots_peer_ref.at[span]
    span = pl.ds(0, rows)
    twice_ref[0] = cot_ref[...] * jnp.bfloat16(2.0)
    twice_ref[1] = cot_peer_ref[...] * jnp.bfloat16(2.0)

    @pl.when(step == 0)
    def _():
        stat_ref[...] = jnp.zeros_like(stat_ref)
        acc_ref[...] = jnp.zeros_like(acc_ref)

    for start in range(0, width, piece):
        cols = pl.ds(start, piece)
        g_one = lax.dot_general(twice_ref[0, span], top_ref[cols], COLS_COLS, preferred_element_type=jnp.float32)
        g_one = g_one.astype(jnp.bfloat16).astype(jnp.float32)
        g_two = lax.dot_general(twice_ref[1, span], top_peer_ref[cols], COLS_COLS, preferred_element_type=jnp.float32)
        g_two = g_two.astype(jnp.bfloat16).astype(jnp.float32)
        total = g_one + g_two
        size = jnp.abs(g_one) + jnp.abs(g_two)
        limit = (thr_ref[:, cols] * jnp.bfloat16(2.0)).astype(jnp.float32)
        share = total * pltpu.reciprocal(jnp.maximum(size, 2.0 * FLOOR))
        merged = 0.25 * total + jnp.clip(share + (1.0 - limit), -SOFT, SOFT) * size
        normed = (h_ref[:, cols] - vec_ref[0:1, cols]) * vec_ref[1:2, cols]
        normed_ref[:, cols] = normed.astype(jnp.bfloat16)
        before = normed * vec_ref[2:3, cols] + vec_ref[3:4, cols] + x_ref[:, cols].astype(jnp.float32)
        phi, bell = tail_and_bell(before)
        z_ref[:, cols] = (before * phi).astype(jnp.bfloat16)
        flow = merged * (phi + before * bell * DENSITY)
        flow_ref[:, cols] = flow.astype(flow_ref.dtype)
        stat_ref[:8, cols] += fold(flow)
        stat_ref[8:, cols] += fold(flow * normed)
    out_ref[...] = jnp.dot(z_ref[...], top_ref[...], preferred_element_type=jnp.float32)
    sent_ref[pl.ds(pl.multiple_of(step * rows, rows), rows)] = jnp.dot(
        z_ref[...], top_peer_ref[...], preferred_element_type=jnp.float32
    ).astype(jnp.bfloat16)
    acc_ref[:half] += lax.dot_general(cot_ref[...], z_ref[...], ROWS_ROWS, preferred_element_type=jnp.float32)
    acc_ref[half:] += lax.dot_general(cot_peer_ref[...], z_ref[...], ROWS_ROWS, preferred_element_type=jnp.float32)

    @pl.when(step == last)
    def _():
        rest_ref[...] = sent_ref[pl.ds(last * rows, rows)]

    def after():
        lax.fori_loop(0, last, lambda index, carry: (send(index).wait(), carry)[1], 0)

    return after


def crown_fill(*refs):
    used, given, own = refs[:10], refs[10:16], refs[17:]
    grad_ref, acc_ref = given[3], own[1]
    half = acc_ref.shape[0] // 2
    task = lax.axis_index("task")

    def part(index):
        def run():
            place = pl.multiple_of((task if index == 0 else 1 - task) * half, half)

            def one(i, carry):
                cols = pl.ds(pl.multiple_of(i * half, half), half)
                turned = acc_ref[pl.ds(index * half, half), cols].T
                grad_ref[cols, pl.ds(place, half)] = turned.astype(jnp.bfloat16)
                return carry

            lax.fori_loop(0, acc_ref.shape[1] // half, one, 0)

        return run

    return part(0), part(1)


def wide(mask, width):
    return jnp.concatenate([mask] * (width // mask.shape[1]), axis=1)


def edges(cuts_ref, canvas):
    shape = (SIDE * SIDE, 128)
    pixel = lax.broadcasted_iota(jnp.int32, shape, 0)
    row, col = pixel // SIDE, lax.rem(pixel, SIDE)
    down, right = cuts_ref[canvas, 0], cuts_ref[canvas, 1]
    one, zero = jnp.ones(shape, jnp.float32), jnp.zeros(shape, jnp.float32)
    within = lambda place, rim, cut: jnp.where((place != rim) & (place != cut), one, zero)
    return (
        within(col, 0, right), within(col, SIDE - 1, right - 1), within(row, 0, down), within(row, SIDE - 1, down - 1),
    )


def edges_of(cuts_ref, step, rows):
    count = rows // (SIDE * SIDE)
    parts = [edges(cuts_ref, step * count + index) for index in range(count)]
    return [jnp.concatenate([part[side] for part in parts], axis=0) for side in range(4)]


def gather_stats(stat_ref, hidden, first):
    @pl.when(first)
    def _():
        stat_ref[:16] = jnp.zeros_like(stat_ref[:16])
        mean = jnp.sum(hidden, axis=0, keepdims=True) / hidden.shape[0]
        stat_ref[16:] = jnp.broadcast_to(mean, stat_ref[16:].shape)

    away = hidden - stat_ref[16:17]
    stat_ref[:8] += fold(away)
    stat_ref[8:16] += fold(away * away)


def normal(hidden, vec_ref):
    return (hidden - vec_ref[0:1]) * vec_ref[1:2]


def squeeze_kernel(x_ref, w_ref, out_ref, stat_ref):
    hidden = jnp.dot(x_ref[...], w_ref[...], preferred_element_type=jnp.float32)
    out_ref[...] = hidden
    gather_stats(stat_ref, hidden, pl.program_id(0) == 0)


def mesh_kernel(h_ref, vec_ref, cuts_ref, w_ref, out_ref, side_ref, stat_ref, pad_ref):
    rows, mid = h_ref.shape
    inner = pl.ds(SIDE, rows)
    before = normal(h_ref[...], vec_ref) * vec_ref[2:3] + vec_ref[3:4]
    phi, _ = tail_and_bell(before)
    low = (before * phi).astype(jnp.bfloat16)
    kept = low.astype(jnp.float32)
    left, right, above, below = edges_of(cuts_ref, pl.program_id(0), rows)
    left, right = wide(left, mid), wide(right, mid)

    @pl.when(pl.program_id(0) == 0)
    def _():
        pad_ref[:SIDE] = jnp.zeros_like(pad_ref[:SIDE])
        pad_ref[SIDE + rows :] = jnp.zeros_like(pad_ref[:SIDE])

    pad_ref[inner, :mid] = (pltpu.roll(kept, 1, 0) * left).astype(jnp.bfloat16)
    pad_ref[inner, mid : 2 * mid] = low
    pad_ref[inner, 2 * mid :] = (pltpu.roll(kept, rows - 1, 0) * right).astype(jnp.bfloat16)
    side_ref[...] = pad_ref[inner].T
    above = wide(above.astype(jnp.bfloat16), 3 * mid)
    below = wide(below.astype(jnp.bfloat16), 3 * mid)
    hidden = jnp.dot(pad_ref[inner], w_ref[3 * mid : 6 * mid], preferred_element_type=jnp.float32)
    hidden += jnp.dot(pad_ref[:rows] * above, w_ref[: 3 * mid], preferred_element_type=jnp.float32)
    hidden += jnp.dot(pad_ref[2 * SIDE :] * below, w_ref[6 * mid :], preferred_element_type=jnp.float32)
    out_ref[...] = hidden
    gather_stats(stat_ref, hidden, pl.program_id(0) == 0)


def widen_kernel(h_ref, vec_ref, w_ref, out_ref, low_ref, stat_ref):
    before = normal(h_ref[...], vec_ref) * vec_ref[2:3] + vec_ref[3:4]
    phi, _ = tail_and_bell(before)
    low = (before * phi).astype(jnp.bfloat16)
    low_ref[...] = low.T
    hidden = jnp.dot(low, w_ref[...], preferred_element_type=jnp.float32)
    out_ref[...] = hidden
    gather_stats(stat_ref, hidden, pl.program_id(0) == 0)


def norm_grad(upstream, normed, vec_ref):
    return vec_ref[4:5] * (upstream - vec_ref[5:6] - normed * vec_ref[6:7])


def act_slope(value):
    phi, bell = tail_and_bell(value)
    return phi + value * bell * DENSITY


def gather_flow(stat_ref, flow, normed, first):
    @pl.when(first)
    def _():
        stat_ref[...] = jnp.zeros_like(stat_ref)

    stat_ref[:8] += fold(flow)
    stat_ref[8:16] += fold(flow * normed)


def narrow_kernel(flow_ref, normed_ref, vec_ref, two_ref, vectwo_ref, low_ref, w_ref, out_ref, grad_ref, stat_ref, dh_ref):
    step = pl.program_id(0)
    rows = flow_ref.shape[0]
    dh = norm_grad(flow_ref[...].astype(jnp.float32), normed_ref[...].astype(jnp.float32), vec_ref)
    low = dh.astype(jnp.bfloat16)
    dh_ref[pl.ds(pl.multiple_of(step * rows, rows), rows)] = low
    dq = lax.dot_general(low, w_ref[...], COLS_COLS, preferred_element_type=jnp.float32)
    normed = normal(two_ref[...], vectwo_ref)
    flow = dq * act_slope(normed * vectwo_ref[2:3] + vectwo_ref[3:4])
    out_ref[...] = flow
    gather_flow(stat_ref, flow, normed, step == 0)


def narrow_fill(flow_ref, normed_ref, vec_ref, two_ref, vectwo_ref, low_ref, w_ref, out_ref, grad_ref, stat_ref, dh_ref):
    half = dh_ref.shape[1] // 2

    def part(index):
        def run():
            def one(i, carry):
                cols = pl.ds(pl.multiple_of(index * half + i * 512, 512), 512)
                grad_ref[:, cols] = jnp.dot(
                    low_ref[...], dh_ref[:, cols], preferred_element_type=jnp.float32
                ).astype(jnp.bfloat16)
                return carry

            lax.fori_loop(0, half // 512, one, 0)

        return run

    return part(0), part(1)


def across(source, target, sems, hop="task"):
    task = lax.axis_index("task")
    place = lax.axis_index("batch")
    device = (1 - task, place) if hop == "task" else (task, place + 1 - 2 * lax.rem(place, 2))
    return pltpu.make_async_remote_copy(
        src_ref=source,
        dst_ref=target,
        send_sem=sems.at[0],
        recv_sem=sems.at[1],
        device_id=device,
        device_id_type=MESH,
    )


def tiled(kernel, tile, moving, flags, outs, fixed, scratch, name, stats=None, sends=(), far=(), fill=None, turns=(), aside=None):
    tasks = lax.axis_size("task")
    batch = lax.axis_size("batch")
    rows = moving[0].shape[0]

    def block(array):
        return pl.BlockSpec((tile,) + array.shape[1:], lambda i: (i,) + (0,) * (len(array.shape) - 1))

    def turned(array):
        return pl.BlockSpec((array.shape[0], tile), lambda i: (0, i))

    def whole(array):
        zeros = (0,) * len(array.shape)
        return pl.BlockSpec(array.shape, lambda i: zeros)

    hbm = pl.BlockSpec(memory_space=pl.ANY)
    operands = list(moving)
    in_specs = [(whole, block, lambda a: hbm, lambda a: pl.BlockSpec(memory_space=pltpu.SMEM))[m](a) for a, m in zip(moving, flags)]
    out_shape = outs + fixed + list(far)
    out_specs = [turned(a) if i in turns else block(a) for i, a in enumerate(outs)] + [whole(a) for a in fixed] + [hbm for a in far]
    scratch = list(scratch)
    params = dict(vmem_limit_bytes=VMEM_BYTES)
    ins, made, held = len(operands), len(out_shape), len(scratch)
    run = kernel
    if stats is not None:
        vecs, forward, ident = stats
        width = vecs[0].shape[1]
        params.update(collective_id=ident, has_side_effects=True)
        operands += vecs
        in_specs += [whole(vec) for vec in vecs]
        out_shape = out_shape + [shape32(16, width)]
        out_specs = out_specs + [whole(out_shape[-1])]
        scratch = scratch + [pltpu.VMEM((24 if forward else 16, width), jnp.float32)]
        scratch = scratch + Exchange.scratch(tasks, batch, width)
        for array, _, shape, _ in sends:
            operands.append(array)
            in_specs.append(hbm)
            out_shape = out_shape + [jax.ShapeDtypeStruct(shape, array.dtype)]
            out_specs = out_specs + [hbm]
            scratch = scratch + [pltpu.SemaphoreType.DMA((2,))]

        if aside is not None:
            operands.append(aside[0])
            in_specs.append(hbm)
            out_shape = out_shape + list(aside[1])
            out_specs = out_specs + [hbm for _ in aside[1]]
            scratch = scratch + list(aside[2])

        def run(*refs):
            refs = list(refs)
            take = lambda n: [refs.pop(0) for _ in range(n)]
            used = take(ins)
            vec_refs = take(len(vecs))
            sources = take(len(sends))
            own_in = take(0 if aside is None else 1)
            given = take(made)
            out_ref = take(1)[0]
            targets = take(len(sends))
            own_out = take(0 if aside is None else len(aside[1]))
            own = take(held)
            stat_ref = take(1)[0]
            exchange = Exchange(tasks, batch, *take(6))
            step = pl.program_id(0)
            last = pl.num_programs(0) - 1

            @pl.when(step == 0)
            def _():
                exchange.greet()

            early = len(sends) > 0 or len(far) > 0

            def crossing(index):
                _, view, _, hop = sends[index]
                return across(view(sources[index]), targets[index], cross_sems[index], hop)

            cross_sems = take(len(sends))
            if early and aside is None:

                @pl.when(step == 1)
                def _():
                    exchange.met()
                    for index in range(len(sends)):
                        crossing(index).start()

            if aside is not None:
                helper = aside[3](exchange, *own_in, *own_out, *refs)
                helper.before(step)

            after = kernel(*used, *given, stat_ref, *own)
            if aside is not None:
                helper.after(step)

                @pl.when(step == 1)
                def _():
                    for index in range(len(sends)):
                        crossing(index).start()

            @pl.when(step == last)
            def _():
                if not early and aside is None:
                    exchange.met()
                fillers = (None, None) if fill is None else fill(*used, *given, stat_ref, *own)
                settle_stats(exchange, stat_ref, vec_refs, out_ref, rows, rows * tasks * batch, forward, fillers)
                for index in range(len(sends)):
                    crossing(index).wait()
                if after is not None:
                    after()
                if aside is not None:
                    helper.end()

    return pl.pallas_call(
        run,
        grid=(rows // tile,),
        out_shape=out_shape,
        in_specs=in_specs,
        out_specs=out_specs,
        scratch_shapes=scratch,
        compiler_params=pltpu.CompilerParams(**params),
        name=name,
    )(*operands)


def shape32(*shape):
    return jax.ShapeDtypeStruct(shape, jnp.float32)


def shape16(*shape):
    return jax.ShapeDtypeStruct(shape, jnp.bfloat16)


def squeeze(flat_in, w_reduce, stats, tile):
    rows, mid = flat_in.shape[0], w_reduce.shape[1]
    return tiled(squeeze_kernel, tile, [flat_in, w_reduce], [1, 0], [shape32(rows, mid)], [], [], "squeeze", stats)


def mesh_forward(h_one, vec, cuts, taps, stats, sends, tile):
    rows, mid = h_one.shape
    return tiled(
        mesh_kernel, tile, [h_one, vec, cuts, taps], [1, 0, 3, 0],
        [shape32(rows, mid), shape16(3 * mid, rows)], [],
        [pltpu.VMEM((tile + 2 * SIDE, 3 * mid), jnp.bfloat16)], "mesh_forward", stats, sends, turns=(1,),
    )


def widen(h_two, vec, w_expand, stats, sends, tile):
    rows, mid = h_two.shape
    width = w_expand.shape[1]
    return tiled(
        widen_kernel, tile, [h_two, vec, w_expand], [1, 0, 0],
        [shape32(rows, width), shape16(mid, rows)], [], [], "widen", stats, sends, turns=(1,),
    )


class HeadsAside:
    def __init__(self, batch, shape, last, exchange, source, target, work, *room):
        self.exchange, self.work, self.target, self.last = exchange, work, target, last
        self.sum = Reduction(Grid(batch), work, None, *room[:11], "owner")
        self.load = pltpu.make_async_copy(source, work, room[11].at[0])
        self.sems = room[11]

    def before(self, step):
        @pl.when(step == 0)
        def _():
            self.load.start()

    def out(self, part):
        grid = self.sum.grid
        bits = grid.bits(part)
        view = self.sum.view(grid.core, part, bits[0], bits[1])
        return pltpu.make_async_copy(view, self.target.at[part], self.sems.at[1 + part])

    def after(self, step):
        @pl.when(step == 0)
        def _():
            self.exchange.met()
            self.load.wait()
            self.sum.stage(0)

        @pl.when(step == 1)
        def _():
            self.sum.stage(1)

        @pl.when(step == self.last)
        def _():
            self.sum.stage(2)

    def end(self):
        for part in range(2):
            self.sum.finish(2, part)
            self.out(part).start()
        for part in range(2):
            self.out(part).wait()


def narrow(flow, normed, vec_three, h_two, vec_two, q_two, w_expand, heads, rest, stats, tile):
    rows, mid = h_two.shape
    width = w_expand.shape[1]
    batch = lax.axis_size("batch")
    high, across_ = heads.shape
    scratch = [pltpu.VMEM(heads.shape, jnp.bfloat16)] + Reduction.scratch(high, across_, "owner", batch // LOW)
    scratch += [pltpu.SemaphoreType.DMA((3,))]
    helper = functools.partial(HeadsAside, batch, heads.shape, rows // tile - 1)
    return tiled(
        narrow_kernel, tile, [flow, normed, vec_three, h_two, vec_two, q_two, w_expand], [1, 1, 0, 1, 0, 0, 0],
        [shape32(rows, mid)], [shape16(mid, width)], [pltpu.VMEM((rows, width), jnp.bfloat16)], "narrow", stats,
        [(rest, lambda ref: ref, rest.shape, "task")], fill=narrow_fill, aside=(heads, [shape16(2, high // 8, across_ // 2)], scratch, helper),
    )


def crown(h_three, flat_in, limits, cots, cot_parts, top, top_parts, vec, stats, tile, piece):
    rows, width = flat_in.shape
    half = cots.shape[2]
    return tiled(
        functools.partial(crown_kernel, piece), tile,
        [h_three, flat_in, limits, cots, *cot_parts, top, *top_parts, vec], [1, 1, 1, 2, 2, 2, 0, 2, 2, 0],
        [shape32(rows, half), shape16(rows, width), shape16(rows, width)], [shape16(width, 2 * half), shape16(tile, half)],
        [
            pltpu.VMEM((tile, width), jnp.bfloat16),
            pltpu.VMEM((2 * half, width), jnp.float32),
            pltpu.VMEM((rows, half), jnp.bfloat16),
            pltpu.SemaphoreType.DMA((rows // tile, 2)),
            pltpu.VMEM((rows, half), jnp.bfloat16),
            pltpu.VMEM((rows, half), jnp.bfloat16),
            pltpu.VMEM((width, half), jnp.bfloat16),
            pltpu.SemaphoreType.DMA((5,)),
            pltpu.SemaphoreType.DMA((2,)),
            pltpu.VMEM((2, tile, half), jnp.bfloat16),
        ],
        "crown", stats, (), [shape16(rows, half)], crown_fill,
    )


class Stream:
    def __init__(self, view, held, sems):
        self.view, self.held, self.sems = view, held, sems

    def copy(self, index):
        slot = lax.rem(index, 2)
        return pltpu.make_async_copy(self.view(index), self.held.at[slot], self.sems.at[slot])

    def start(self, index):
        self.copy(index).start()

    def take(self, index, count):
        self.copy(index).wait()

        @pl.when(index + 1 < count)
        def _():
            self.start(index + 1)

        return self.held.at[lax.rem(index, 2)]


def back_kernel(rows, tasks, batch, tile, *refs):
    refs = list(refs)

    def take(count):
        return [refs.pop(0) for _ in range(count)]

    (flow_hbm, two_hbm, one_hbm, side_hbm, w_hbm, x_hbm, heads_hbm, expand_hbm) = take(8)
    vectwo_ref, vecone_ref, cuts_ref = take(3)
    (out_hbm, heads_out, expand_out, spatial_out, reduce_out, vec_ref) = take(6)
    (two_buf, x_buf) = take(2)
    (side_ref, lane_ref, flow_ref, w_ref) = take(4)
    heads_work, expand_work, spatial_work, reduce_work, stat_ref = take(5)
    pair_sems, whole_sems, flow_sems = take(3)
    exchange = Exchange(tasks, batch, *take(6))
    grid = Grid(batch)
    mid = flow_hbm.shape[1]
    width = x_hbm.shape[1]
    spans = rows // tile

    def blocks(ref, height):
        return lambda index: ref.at[pl.ds(pl.multiple_of(index * height, height), height)]

    exchange.greet()

    def flow_load(index):
        return pltpu.make_async_copy(
            blocks(flow_hbm, tile)(index), blocks(flow_ref, tile)(index), flow_sems.at[index]
        )

    twos = Stream(blocks(two_hbm, tile), two_buf, pair_sems.at[1])
    ones = Stream(blocks(one_hbm, tile), two_buf, pair_sems.at[3])
    dh_ref, normed_ref, dht_ref = lane_ref.at[:, :mid], lane_ref.at[:, mid : 2 * mid], side_ref.at[:mid]
    across_cols = x_buf.shape[2]
    columns = Stream(
        lambda index: x_hbm.at[:, pl.ds(pl.multiple_of(index * across_cols, across_cols), across_cols)],
        x_buf, pair_sems.at[0],
    )
    loads = [
        pltpu.make_async_copy(source, target, whole_sems.at[index])
        for index, (source, target) in enumerate(
            [(heads_hbm, heads_work), (side_hbm, side_ref), (expand_hbm, expand_work), (w_hbm, w_ref)]
        )
    ]
    heads_load, side_load, expand_load, w_load = loads
    keep = pltpu.make_async_copy(dh_ref, out_hbm, whole_sems.at[4])
    heads_load.start()
    flow_load(0).start()
    twos.start(0)
    expand_load.start()
    for index in range(1, spans):
        flow_load(index).start()
    side_load.start()
    w_load.start()

    third = spatial_work.shape[0] // 3
    works = [(heads_work, heads_out, "owner"), (expand_work, expand_out, "wide")]
    for index in range(3):
        span = pl.ds(index * third, third)
        works.append((spatial_work.at[span], spatial_out.at[span], "tall"))
    for index in range(2):
        span = pl.ds(index * width // 2, width // 2)
        works.append((reduce_work.at[span], reduce_out.at[span], "tall"))
    reductions = []
    for work, out, kind in works:
        shape = heads_out.shape if kind == "owner" else None
        reductions.append(Reduction(grid, work, out, *take(11), kind, shape))

    def tick(name):
        for item, stage in AGENDA.get(name, ()):
            reductions[item].stage(stage)

    def ticks(name, index, count, scale=1, shift=0):
        for step in range(count):
            label = "%s%d" % (name, step * scale + shift)
            if label in AGENDA:

                @pl.when(index == step)
                def _():
                    tick(label)

    def lanes(index, carry):
        span = pl.ds(pl.multiple_of(index * tile, tile), tile)
        flow_load(index).wait()
        flow = flow_ref[span]
        normed = normal(twos.take(index, spans)[...], vectwo_ref)
        dh = norm_grad(flow, normed, vectwo_ref)
        _, _, above, below = edges_of(cuts_ref, index, tile)
        above, below = wide(above, mid), wide(below, mid)
        low = jnp.bfloat16
        zero = jnp.zeros((SIDE, mid), low)
        lane_ref[span, mid : 2 * mid] = dh.astype(low)
        lane_ref[span, :mid] = jnp.concatenate([(dh * above)[SIDE:].astype(low), zero], axis=0)
        lane_ref[span, 2 * mid :] = jnp.concatenate([zero, (dh * below)[: tile - SIDE].astype(low)], axis=0)

        @pl.when(index == 0)
        def _():
            expand_load.wait()

        ticks("lane", index, 4)
        return carry

    exchange.met()
    heads_load.wait()
    tick("start")
    lax.fori_loop(0, spans, lanes, 0)
    ones.start(0)
    side_load.wait()

    def spatial(index, carry):
        a, b = index // 3, lax.rem(index, 3)
        rows_here = pl.ds(pl.multiple_of(b * mid, mid), mid)
        cols = pl.ds(pl.multiple_of(a * mid, mid), mid)
        part = jnp.dot(side_ref[rows_here], lane_ref[:, cols], preferred_element_type=jnp.float32)
        spatial_work[pl.ds(pl.multiple_of(index * mid, mid), mid)] = part.astype(jnp.bfloat16)
        ticks("sp", index, 9)
        return carry

    lax.fori_loop(0, 9, spatial, 0)
    w_load.wait()

    def taps(index, carry):
        span = pl.ds(pl.multiple_of(index * tile, tile), tile)
        pieces = []
        for b in range(3):
            total = None
            for a in range(3):
                part = lax.dot_general(
                    lane_ref[span, a * mid : (a + 1) * mid], w_ref[3 * a + b], COLS_COLS,
                    preferred_element_type=jnp.float32,
                )
                total = part if total is None else total + part
            pieces.append(total)
            if b < 2:
                ticks("tap", index, 4, 3, b)
        left, right, _, _ = edges_of(cuts_ref, index, tile)
        left, right = wide(left, mid), wide(right, mid)
        dq = pieces[1] + pltpu.roll(pieces[0] * left, tile - 1, 0) + pltpu.roll(pieces[2] * right, 1, 0)
        normed = normal(ones.take(index, spans)[...], vecone_ref)
        flow = dq * act_slope(normed * vecone_ref[2:3] + vecone_ref[3:4])
        flow_ref[span] = flow
        normed_ref[span] = normed.astype(jnp.bfloat16)
        gather_flow(stat_ref, flow, normed, index == 0)
        ticks("tap", index, 4, 3, 2)
        return carry

    lax.fori_loop(0, spans, taps, 0)
    columns.start(0)
    settle_stats(exchange, stat_ref, [vecone_ref], vec_ref, rows, rows * tasks * batch, False)
    tick("xch")

    def inner(index, carry):
        span = pl.ds(pl.multiple_of(index * tile, tile), tile)
        dh = norm_grad(flow_ref[span], normed_ref[span].astype(jnp.float32), vec_ref)
        low = dh.astype(jnp.bfloat16)
        dh_ref[span] = low
        dht_ref[:, span] = low.T
        return carry

    lax.fori_loop(0, spans, inner, 0)
    keep.start()
    tick("inner")
    count = width // across_cols

    def reduce(index, carry):
        part = jnp.dot(dht_ref[...], columns.take(index, count)[...], preferred_element_type=jnp.float32)
        span = pl.ds(pl.multiple_of(index * across_cols, across_cols), across_cols)
        reduce_work[span] = part.T.astype(jnp.bfloat16)
        ticks("red", index, 4)
        return carry

    lax.fori_loop(0, count, reduce, 0)
    keep.wait()
    tick("tail")


def back(flow, h_two, vec_two, h_one, vec_one, sides, cuts, w_spatial, flat_in, heads, expand, heads_shape, ident, tile):
    tasks = lax.axis_size("task")
    batch = lax.axis_size("batch")
    far = batch // LOW
    rows, mid = h_one.shape
    width = flat_in.shape[1]
    full, low = jnp.float32, jnp.bfloat16
    cols = 512
    hbm = pl.BlockSpec(memory_space=pl.ANY)
    vmem = pl.BlockSpec(memory_space=pltpu.VMEM)
    shapes = [(heads_shape, "owner"), (expand.shape, "wide")] + [((3 * mid, mid), "tall")] * 3
    shapes += [((width // 2, mid), "tall")] * 2
    scratch = [
        pltpu.VMEM((2, tile, mid), full),
        pltpu.VMEM((2, rows, cols), low),
        pltpu.VMEM((3 * mid, rows), low),
        pltpu.VMEM((rows, 3 * mid), low),
        pltpu.VMEM((rows, mid), full),
        pltpu.VMEM(w_spatial.shape, low),
        pltpu.VMEM(heads.shape, low),
        pltpu.VMEM(expand.shape, low),
        pltpu.VMEM((9 * mid, mid), low),
        pltpu.VMEM((width, mid), low),
        pltpu.VMEM((16, mid), full),
        pltpu.SemaphoreType.DMA((4, 2)),
        pltpu.SemaphoreType.DMA((5,)),
        pltpu.SemaphoreType.DMA((rows // tile,)),
    ] + Exchange.scratch(tasks, batch, mid)
    for (high, across_), kind in shapes:
        scratch += Reduction.scratch(high, across_, kind, far, kind == "owner")
    return pl.pallas_call(
        functools.partial(back_kernel, rows, tasks, batch, tile),
        out_shape=[
            shape16(rows, mid), shape16(*heads_shape), shape16(*expand.shape), shape16(9 * mid, mid),
            shape16(width, mid), shape32(16, mid),
        ],
        in_specs=[hbm] * 8 + [vmem] * 2 + [pl.BlockSpec(memory_space=pltpu.SMEM)],
        out_specs=[hbm] * 5 + [vmem],
        scratch_shapes=scratch,
        compiler_params=pltpu.CompilerParams(
            vmem_limit_bytes=VMEM_BYTES, collective_id=ident, has_side_effects=True
        ),
        name="back",
    )(flow, h_two, h_one, sides, w_spatial, flat_in, heads, expand, vec_two, vec_one, cuts)


def finish_kernel(
    dh_ref, up_ref, heads_ref, expand_ref, spatial_ref, reduce_ref, mine_ref, came_ref, rest_ref, w_ref, one_ref, two_ref, three_ref,
    out_ref, heads_out, expand_out, spatial_out, reduce_out, both_ref, *sums,
):
    full = jnp.float32
    task = lax.axis_index("task")
    half = heads_out.shape[1]
    back = lax.dot_general(dh_ref[...], w_ref[...], COLS_COLS, preferred_element_type=full)
    out_ref[...] = (up_ref[...].astype(full) + back).astype(jnp.bfloat16)
    heads_out[...] = jnp.where(task == 0, heads_ref[:, :half], heads_ref[:, half:]).astype(full)
    expand_out[...] = expand_ref[...].astype(full)
    spatial_out[...] = spatial_ref[...].astype(full)
    reduce_out[...] = reduce_ref[...].astype(full)
    both_ref[task] = mine_ref[...]
    both_ref[1 - task] = came_ref[...].astype(full)

    @pl.when(pl.program_id(0) == pl.num_programs(0) - 1)
    def _():
        height = rest_ref.shape[0]
        both_ref[1 - task, both_ref.shape[1] - height :] = rest_ref[...].astype(full)


    @pl.when(pl.program_id(0) == 0)
    def _():
        for index, vec_ref in enumerate((one_ref, two_ref, three_ref)):
            sums[2 * index][...] = vec_ref[9:10]
            sums[2 * index + 1][...] = vec_ref[8:9]


def finish(dh, up, heads, expand, spatial, reduce, mine, came, rest, w_reduce, vecs, steps):

    def block(array, lead=0):
        zeros = (0,) * (len(array.shape) - 1 - lead)
        height = array.shape[lead] // steps
        return pl.BlockSpec(array.shape[:lead] + (height,) + array.shape[lead + 1 :], lambda i: (0,) * lead + (i,) + zeros)

    def whole(array):
        return pl.BlockSpec(array.shape, lambda i: (0, 0))

    rows, half = mine.shape
    moving = [dh, up, heads, expand, spatial, reduce, mine, came]
    fixed = [rest, w_reduce, *vecs]
    outs = [shape16(*up.shape), shape32(heads.shape[0], half), shape32(*expand.shape), shape32(*spatial.shape), shape32(*reduce.shape)]
    both = shape32(2, rows, half)
    sums = [shape32(1, vec.shape[1]) for vec in vecs for _ in range(2)]
    return pl.pallas_call(
        finish_kernel,
        grid=(steps,),
        out_shape=outs + [both] + sums,
        in_specs=[block(a) for a in moving] + [whole(a) for a in fixed],
        out_specs=[block(a) for a in outs] + [block(both, 1)] + [whole(a) for a in sums],
        compiler_params=pltpu.CompilerParams(vmem_limit_bytes=VMEM_BYTES),
        name="finish",
    )(*moving, *fixed)


def body(
    inputs,
    crop_cuts,
    threshold,
    w_reduce,
    w_spatial,
    w_expand,
    w_heads,
    gain_one,
    bias_one,
    gain_two,
    bias_two,
    gain_three,
    bias_three,
    cotangent,
):
    canvases, pixels, width = inputs.shape[1:]
    mid = w_reduce.shape[1]
    rows = canvases * pixels
    half = w_heads.shape[2]
    cots = cotangent.reshape(2, rows, half)
    top_mine = w_heads[0]

    def params(gain, bias):
        return [gain.reshape(1, -1), bias.reshape(1, -1)]

    cuts = crop_cuts.reshape(canvases, 2)
    flat_in = inputs.reshape(rows, width)
    core = lambda: lax.rem(lax.axis_index("batch"), 2)
    other = lambda: 1 - lax.axis_index("task")
    quarter = rows // 4
    top_rows = width // 2
    h_one, vec_one = squeeze(flat_in, w_reduce, (params(gain_one, bias_one), True, 0), min(rows, 512))
    sends = [
        (top_mine, lambda ref: ref.at[pl.ds(pl.multiple_of(core() * top_rows, top_rows), top_rows)], (top_rows, half), "task"),
        (cots, lambda ref: ref.at[other(), pl.ds(0, quarter)], (quarter, half), "task"),
    ]
    h_two, sides, vec_two, top_one, cot_one = mesh_forward(
        h_one, vec_one, cuts, w_spatial.reshape(9 * mid, mid), (params(gain_two, bias_two), True, 1), sends, pixels
    )
    sends = [
        (top_one, lambda ref: ref, (top_rows, half), "core"),
        (cots, lambda ref: ref.at[other(), pl.ds(quarter, quarter)], (quarter, half), "task"),
    ]
    h_three, q_two, vec_three, top_two, cot_two = widen(
        h_two, vec_two, w_expand, (params(gain_three, bias_three), True, 2), sends, pixels
    )
    out_mine, flow, normed, grad_heads, rest, out_peer, vec_three = crown(
        h_three, flat_in, threshold.reshape(rows, width), cots, (cot_one, cot_two), top_mine, (top_one, top_two), vec_three,
        ([vec_three], False, 3), pixels, 256,
    )
    heads_shape = grad_heads.shape
    flow_two, grad_expand, vec_two, rest, grad_heads = narrow(
        flow, normed, vec_three, h_two, vec_two, q_two, w_expand, grad_heads, rest, ([vec_two], False, 4), min(rows, 512)
    )
    dh_one, grad_heads, grad_expand, grad_spatial, grad_reduce, vec_one = back(
        flow_two, h_two, vec_two, h_one, vec_one, sides, cuts, w_spatial, flat_in, grad_heads, grad_expand, heads_shape, 5,
        min(rows, 512),
    )
    grad_inputs, grad_heads, grad_expand, grad_spatial, grad_reduce, head_out, *sums = finish(
        dh_one, flow, grad_heads, grad_expand, grad_spatial, grad_reduce, out_mine, out_peer, rest, w_reduce,
        (vec_one, vec_two, vec_three), 2,
    )
    return (
        head_out.reshape(1, 2, canvases, pixels, half),
        grad_inputs.reshape(inputs.shape),
        grad_reduce,
        grad_spatial.reshape(w_spatial.shape),
        grad_expand,
        grad_heads[None],
        *[row.reshape(-1) for row in sums],
    )


def solution(mesh):
    in_specs = (
        P("task", "batch", None, None),
        P("task", "batch", None),
        P("task", "batch", None, None),
        P(),
        P(),
        P(),
        P("task", None, None),
        P(),
        P(),
        P(),
        P(),
        P(),
        P(),
        P("task", None, "batch", None, None),
    )
    out_specs = (
        P("task", None, "batch", None, None),
        P("task", "batch", None, None),
        P(),
        P(),
        P(),
        P("task", None, None),
        P(),
        P(),
        P(),
        P(),
        P(),
        P(),
    )
    return jax.shard_map(body, mesh=mesh, in_specs=in_specs, out_specs=out_specs, check_vma=False)
```

```python
import functools
import math

import jax
import jax.numpy as jnp
from jax import lax
from jax.experimental import pallas as pl
from jax.experimental.pallas import tpu as pltpu
from jax.sharding import PartitionSpec as P

SIDE = 16
EPS = 1e-05
FLOOR = 0.1
SOFT = 0.25
ROOT_HALF = 0.7071067811865476
DENSITY = 0.3989422804014327
LOG2E = 1.4426950408889634
ERF_P = 0.3275911
ERF_A = (0.254829592, -0.284496736, 1.421413741, -1.453152027, 1.061405429)
ROWS_ROWS = (((0,), (0,)), ((), ()))
COLS_COLS = (((1,), (1,)), ((), ()))
MESH = pl.DeviceIdType.MESH
LOW = 4
VMEM_BYTES = 62 * 2**20


AGENDA = {
    "start": ((0, 3),),
    "lane0": ((1, 0),),
    "lane2": ((1, 1),),
    "sp1": ((0, 4),),
    "sp2": ((2, 0),),
    "sp4": ((1, 2), (2, 1),),
    "sp5": ((3, 0),),
    "sp8": ((0, 5), (1, 3), (3, 1), (4, 0),),
    "tap2": ((2, 2), (4, 1),),
    "tap5": ((0, 7), (1, 4),),
    "tap8": ((0, 8), (3, 2), (2, 3),),
    "xb": ((1, 5), (2, 4), (3, 3), (4, 2),),
    "xch": ((1, 6),),
    "inner": ((2, 5), (4, 3),),
    "red1": ((1, 7), (3, 4), (5, 0),),
    "red2": ((2, 6),),
    "red3": ((1, 8), (4, 4), (5, 1), (6, 0),),
    "tail": ((6, 1), (3, 5), (2, 7), (2, 8), (5, 2), (4, 5), (6, 2), (3, 6), (5, 3), (4, 6), (6, 3), (5, 4), (3, 7), (6, 4), (3, 8), (4, 7), (5, 5), (4, 8), (6, 5), (5, 6), (6, 6), (5, 7), (5, 8), (6, 7), (6, 8),),
}


class Reduction:
    def __init__(
        self, grid, work, result, core, first_a, first_b, second, last, done, send, recv, far_send, far_recv, local,
        kind, shape=None,
    ):
        self.grid, self.work, self.result = grid, work, result
        self.core_room, self.first_rooms, self.second_room, self.last_room = core, (first_a, first_b), second, last
        self.done = done
        self.send, self.recv, self.far_send, self.far_recv = send, recv, far_send, far_recv
        self.local = local
        self.kind = kind
        self.resumed = shape is not None
        self.rows, self.cols = shape or work.shape
        sizes = self.sizes(self.rows, self.cols, kind, grid.far)
        self.pieces = sizes[3][0] // sizes[4][0]
        self.mine = lax.rem(grid.high, self.pieces)

    @staticmethod
    def sizes(rows, cols, kind, far):
        if kind == "wide":
            core, first, second = (rows, cols // 2), (rows, cols // 8), (rows, cols // 16)
            firsts = first, first
        elif kind == "tall":
            core, first, second = (rows // 2, cols), (rows // 2, cols // 4), (rows // 4, cols // 4)
            firsts = first, first
        else:
            core, second = (rows // 2, cols), (rows // 8, cols // 2)
            firsts = (rows // 4, cols // 2), (rows // 8, cols)
        pieces = max(n for n in range(1, far + 1) if far % n == 0 and second[0] % (8 * n) == 0)
        return core, *firsts, second, (second[0] // pieces, second[1])

    @staticmethod
    def scratch(rows, cols, kind, far, resumed=False):
        core, first_a, first_b, second, last = Reduction.sizes(rows, cols, kind, far)
        if resumed:
            core = first_a = first_b = (16, 128)
        return [
            pltpu.VMEM(core, jnp.bfloat16),
            pltpu.VMEM(first_a, jnp.bfloat16),
            pltpu.VMEM(first_b, jnp.bfloat16),
            pltpu.VMEM((2,) + ((16, 128) if resumed else second), jnp.bfloat16),
            pltpu.VMEM((2, far) + last, jnp.bfloat16),
            pltpu.VMEM((2,) + last, jnp.bfloat16),
            pltpu.SemaphoreType.DMA((10,)),
            pltpu.SemaphoreType.DMA((10,)),
            pltpu.SemaphoreType.DMA((4, far)),
            pltpu.SemaphoreType.DMA((4, far)),
            pltpu.SemaphoreType.DMA((2,)),
        ]

    def view(self, core, part=None, first=None, second=None, piece=None, done=False):
        rows, cols = self.rows, self.cols
        sizes = self.sizes(rows, cols, self.kind, self.grid.far)
        row = col = 0
        shape = sizes[0]
        if self.kind == "wide":
            col = core * (cols // 2)
            if part is not None:
                col = col + part * (cols // 4) + first * (cols // 8)
            if second is not None:
                col = col + second * (cols // 16)
        elif self.kind == "tall":
            row = core * (rows // 2)
            if part is not None:
                col = part * (cols // 2) + first * (cols // 4)
            if second is not None:
                row = row + second * (rows // 4)
        else:
            row = core * (rows // 2)
            if part is not None:
                row = row + part * (rows // 4)
                y, task = (second, first) if part == 0 else (first, second)
                row = row if y is None else row + y * (rows // 8)
                col = 0 if task is None else task * (cols // 2)
            elif done:
                col = self.grid.task * (cols // 2)
                shape = (rows // 2, cols // 2)
        if part is not None:
            shape = sizes[1 + part] if second is None else sizes[3]
        ref = self.result if done else self.work
        if self.resumed and not done:
            ref, row, col = self.work.at[part], 0, 0
        if piece is not None:
            row = row + piece * sizes[4][0]
            shape = sizes[4]
        if not isinstance(row, int):
            row = pl.multiple_of(row, shape[0] & -shape[0])
        if not isinstance(col, int):
            col = pl.multiple_of(col, 128)
        return ref.at[pl.ds(row, shape[0]), pl.ds(col, shape[1])]

    def swap(self, index):
        grid = self.grid
        part = (index + 1) % 2
        bits = grid.bits(part)
        if index == 0:
            source, target, device = self.view(1 - grid.core), self.core_room, grid.core_peer
        elif index < 3:
            source, target = self.view(grid.core, part, 1 - bits[0]), self.first_rooms[part]
            device = grid.peers(part)[0]
        elif index < 5:
            source, target = self.view(grid.core, part, bits[0], 1 - bits[1]), self.second_room.at[part]
            device = grid.peers(part)[1]
        elif index < 7:
            source = self.view(grid.core, part, bits[0], bits[1], done=True)
            target, device = source, grid.y_peer if self.kind == "owner" else grid.peers(part)[1]
        elif index < 9:
            source = self.view(grid.core, part, bits[0], done=True)
            target, device = source, grid.peers(part)[0]
        else:
            source = self.view(grid.core, done=True)
            target, device = source, grid.core_peer
        return pltpu.make_async_remote_copy(
            src_ref=source,
            dst_ref=target,
            send_sem=self.send.at[index],
            recv_sem=self.recv.at[index],
            device_id=device,
            device_id_type=MESH,
        )

    def add(self, target, sources):
        rows = target.shape[0]
        step = math.gcd(rows, 64)

        def one(i, carry):
            span = pl.ds(pl.multiple_of(i * step, step), step)
            total = sources[0][span].astype(jnp.float32)
            for source in sources[1:]:
                total = total + source[span].astype(jnp.float32)
            target[span] = total.astype(jnp.bfloat16)
            return carry

        lax.fori_loop(0, rows // step, one, 0)

    def far_copy(self, part, step, back, inward):
        grid = self.grid
        bits = grid.bits(part)
        if back:
            first = grid.high - self.mine
            slot = first + lax.rem(self.mine + step, self.pieces)
            owner = slot if inward else grid.high
            source = self.done.at[part]
            target = self.view(grid.core, part, bits[0], bits[1], lax.rem(owner, self.pieces), True)
        else:
            slot = lax.rem(grid.high + step, grid.far)
            owner = slot if inward else grid.high
            source = self.view(grid.core, part, bits[0], bits[1], lax.rem(slot, self.pieces))
            target = self.last_room.at[part, owner]
        line = 2 * part + (1 if back else 0)
        return pltpu.make_async_remote_copy(
            src_ref=source,
            dst_ref=target,
            send_sem=self.far_send.at[line, step],
            recv_sem=self.far_recv.at[line, owner],
            device_id=(grid.task, slot * LOW + grid.low),
            device_id_type=MESH,
        )

    def far_start(self, part, back):
        for step in range(1, self.pieces if back else self.grid.far):
            self.far_copy(part, step, back, False).start()

    def far_settle(self, part, back):
        for step in range(1, self.pieces if back else self.grid.far):
            self.far_copy(part, step, back, True).wait_recv()
            self.far_copy(part, step, back, False).wait_send()

    def keep(self, part):
        bits = self.grid.bits(part)
        mine = self.view(self.grid.core, part, bits[0], bits[1], self.mine, True)
        return pltpu.make_async_copy(self.done.at[part], mine, self.local.at[part])

    def finish(self, index, part):
        grid = self.grid
        bits = grid.bits(part)
        if index == 0:
            if part == 0:
                self.swap(0).wait()
                mine = self.view(grid.core)
                self.add(mine, [mine, self.core_room])
        elif index == 1:
            self.swap(1 + part).wait()
            mine = self.view(grid.core, part, bits[0])
            self.add(mine, [mine, self.first_rooms[part]])
        elif index == 2:
            self.swap(3 + part).wait()
            mine = self.view(grid.core, part, bits[0], bits[1])
            self.add(mine, [mine, self.second_room.at[part]])
        elif index == 3:
            self.far_settle(part, False)
            self.last_room[part, grid.high] = self.view(grid.core, part, bits[0], bits[1], self.mine)[...]
            self.add(self.done.at[part], [self.last_room.at[part, slot] for slot in range(grid.far)])
        elif index == 4:
            self.far_settle(part, True)
            self.keep(part).wait()
        elif index < 7:
            self.swap(2 * index - 5 + part).wait()
        elif part == 0:
            self.swap(9).wait()

    def begin(self, index, part):
        if index == 0 or index == 7:
            if part == 0:
                self.swap(9 if index else 0).start()
        elif index < 3:
            self.swap(2 * index - 1 + part).start()
        elif index == 3:
            self.far_start(part, False)
        elif index == 4:
            self.keep(part).start()
            self.far_start(part, True)
        elif index < 7:
            self.swap(2 * index - 5 + part).start()

    def stage(self, index):
        owner = self.kind == "owner"
        if owner and index == 6:
            return
        before = 5 if owner and index == 7 else index - 1
        first = self.resumed and index == 3
        together = index in (1, 7, 8)
        for part in range(2):
            if before >= 0 and not first:
                self.finish(before, part)
            if not together:
                self.begin(index, part)
        if together:
            for part in range(2):
                self.begin(index, part)


class Grid:
    def __init__(self, batch):
        self.task = lax.axis_index("task")
        place = lax.axis_index("batch")
        self.far = batch // LOW
        self.high = place // LOW
        self.low = lax.rem(place, LOW)
        self.core = lax.rem(place, 2)
        self.y = lax.rem(place // 2, 2)
        base = place - self.low
        self.core_peer = (self.task, base + self.y * 2 + (1 - self.core))
        self.x_peer = (1 - self.task, place)
        self.y_peer = (self.task, base + (1 - self.y) * 2 + self.core)

    def bits(self, part):
        return (self.task, self.y) if part == 0 else (self.y, self.task)

    def peers(self, part):
        return (self.x_peer, self.y_peer) if part == 0 else (self.y_peer, self.x_peer)


class Exchange:
    def __init__(self, tasks, batch, near, far, near_send, near_recv, far_send, far_recv):
        place = lax.axis_index("batch")
        self.task = lax.axis_index("task")
        self.high = place // LOW
        self.low = lax.rem(place, LOW)
        self.near_size = tasks * LOW
        self.far_size = batch // LOW
        self.me_near = self.task * LOW + self.low
        self.near, self.far = near, far
        self.near_sems, self.far_sems = (near_send, near_recv), (far_send, far_recv)

    @staticmethod
    def scratch(tasks, batch, width):
        near_size, far_size = tasks * LOW, batch // LOW
        return [
            pltpu.VMEM((near_size + 1, 2 * width // 128, 128), jnp.float32),
            pltpu.VMEM((far_size + 1, 2 * width // 128, 128), jnp.float32),
            pltpu.SemaphoreType.DMA((near_size,)),
            pltpu.SemaphoreType.DMA((near_size,)),
            pltpu.SemaphoreType.DMA((far_size,)),
            pltpu.SemaphoreType.DMA((far_size,)),
        ]

    def near_peer(self, step):
        slot = lax.rem(self.me_near + step, self.near_size)
        return slot, (slot // LOW, self.high * LOW + lax.rem(slot, LOW))

    def far_peer(self, step):
        slot = lax.rem(self.high + step, self.far_size)
        return slot, (self.task, slot * LOW + self.low)

    def peers(self):
        near = [self.near_peer(step)[1] for step in range(1, self.near_size)]
        return near + [self.far_peer(step)[1] for step in range(1, self.far_size)]

    def greet(self):
        barrier = pltpu.get_barrier_semaphore()
        for device in self.peers():
            pl.semaphore_signal(barrier, inc=1, device_id=device, device_id_type=MESH)

    def met(self):
        pl.semaphore_wait(pltpu.get_barrier_semaphore(), self.near_size + self.far_size - 2)

    def hop(self, size, peer, me, held, sems, filler=None):
        def copy(step, slot):
            return pltpu.make_async_remote_copy(
                src_ref=held.at[size],
                dst_ref=held.at[slot],
                send_sem=sems[0].at[step],
                recv_sem=sems[1].at[slot],
                device_id=peer(step)[1],
                device_id_type=MESH,
            )

        for step in range(1, size):
            copy(step, me).start()
        held[me] = held[size]
        if filler is not None:
            filler()
        for step in range(1, size):
            copy(step, peer(step)[0]).wait_recv()
        for step in range(1, size):
            copy(step, me).wait_send()
        return held.at[pl.ds(0, size)]

    def run(self, total, spread, rows, forward, fillers=(None, None)):
        lines = total.shape[1] // 128
        for line in range(lines):
            cols = slice(line * 128, (line + 1) * 128)
            self.near[self.near_size, line : line + 1] = total[:, cols]
            self.near[self.near_size, lines + line : lines + line + 1] = spread[:, cols]
        held = self.hop(self.near_size, self.near_peer, self.me_near, self.near, self.near_sems, fillers[0])
        total, spread = join(held, float(rows), forward)
        self.far[self.far_size, :lines] = total
        self.far[self.far_size, lines:] = spread
        held = self.hop(self.far_size, self.far_peer, self.high, self.far, self.far_sems, fillers[1])
        total, spread = join(held, float(rows * self.near_size), forward)
        flat = lambda array: jnp.concatenate([array[line : line + 1] for line in range(lines)], axis=1)
        return flat(total), flat(spread)


def join(held, share, forward):
    groups, lines = held.shape[0], held.shape[1] // 2
    total = held[0, :lines]
    spread = held[0, lines:]
    for group in range(1, groups):
        total = total + held[group, :lines]
        spread = spread + held[group, lines:]
    if forward:
        centre = total * (1.0 / (share * groups))
        for group in range(groups):
            away = held[group, :lines] * (1.0 / share) - centre
            spread = spread + share * (away * away)
    return total, spread


def settle_stats(exchange, stat_ref, vec_refs, out_ref, rows, count, forward, fillers=(None, None)):
    first = jnp.sum(stat_ref[:8], axis=0, keepdims=True)
    second = jnp.sum(stat_ref[8:16], axis=0, keepdims=True)
    if forward:
        gain, bias = vec_refs[0][...], vec_refs[1][...]
        out_ref[...] = jnp.zeros_like(out_ref)
        out_ref[2:3] = gain
        out_ref[3:4] = bias
        local = first + rows * stat_ref[16:17]
        total, spread = exchange.run(local, second - first * first * (1.0 / rows), rows, True, fillers)
        scale = lax.rsqrt(spread * (1.0 / count) + EPS)
        out_ref[0:1] = total * (1.0 / count)
        out_ref[1:2] = scale
        out_ref[4:5] = scale * gain
    else:
        out_ref[:8] = vec_refs[0][:8]
        total, spread = exchange.run(first, second, rows, False, fillers)
        out_ref[5:6] = total * (1.0 / count)
        out_ref[6:7] = spread * (1.0 / count)
        out_ref[8:9] = total
        out_ref[9:10] = spread
        out_ref[10:] = jnp.zeros_like(out_ref[10:])


def tail_and_bell(value):
    bell = jnp.exp2(value * value * (-0.5 * LOG2E))
    away = jnp.abs(value)
    ratio = pltpu.reciprocal(1.0 + away * (ERF_P * ROOT_HALF))
    poly = 0.5 * ERF_A[4]
    for factor in ERF_A[3::-1]:
        poly = poly * ratio + 0.5 * factor
    tail = poly * ratio * bell
    return jnp.where(value >= 0, 1.0 - tail, tail), bell


def fold(array):
    total = array[:8]
    for start in range(8, array.shape[0], 8):
        total = total + array[start : start + 8]
    return total


def crown_kernel(
    piece, h_ref, x_ref, thr_ref, cot_hbm, cot_one, cot_two, top_ref, top_one, top_two, vec_ref,
    out_ref, flow_ref, normed_ref, grad_ref, rest_ref, came_ref, stat_ref, z_ref, acc_ref, sent_ref, sems,
    cots_ref, cots_peer_ref, top_peer_ref, local_sems, late_sems, twice_ref,
):
    step = pl.program_id(0)
    rows, width = x_ref.shape
    all_rows, half = cots_ref.shape
    split = all_rows // 4
    task = lax.axis_index("task")
    last = pl.num_programs(0) - 1

    def send(index):
        span = pl.ds(pl.multiple_of(index * rows, rows), rows)
        return across(sent_ref.at[span], came_ref.at[span], sems.at[index])

    core = lax.rem(lax.axis_index("batch"), 2)
    high = top_one.shape[0]
    late = across(cot_hbm.at[1 - task, pl.ds(2 * split, 2 * split)], cots_peer_ref.at[pl.ds(2 * split, 2 * split)], late_sems)

    @pl.when(step == 0)
    def _():
        pairs = [
            (cot_hbm.at[task], cots_ref),
            (cot_one, cots_peer_ref.at[pl.ds(0, split)]),
            (cot_two, cots_peer_ref.at[pl.ds(split, split)]),
            (top_one, top_peer_ref.at[pl.ds(pl.multiple_of(core * high, high), high)]),
            (top_two, top_peer_ref.at[pl.ds(pl.multiple_of((1 - core) * high, high), high)]),
        ]
        copies = [pltpu.make_async_copy(a, b, local_sems.at[i]) for i, (a, b) in enumerate(pairs)]
        for copy in copies:
            copy.start()
        for copy in copies:
            copy.wait()

    @pl.when(step == 1)
    def _():
        late.start()

    @pl.when(step == (last + 1) // 2)
    def _():
        late.wait()

    @pl.when(step > 0)
    def _():
        send(step - 1).start()

    span = pl.ds(pl.multiple_of(step * rows, rows), rows)
    cot_ref, cot_peer_ref = cots_ref.at[span], cots_peer_ref.at[span]
    span = pl.ds(0, rows)
    twice_ref[0] = cot_ref[...] * jnp.bfloat16(2.0)
    twice_ref[1] = cot_peer_ref[...] * jnp.bfloat16(2.0)

    @pl.when(step == 0)
    def _():
        stat_ref[...] = jnp.zeros_like(stat_ref)
        acc_ref[...] = jnp.zeros_like(acc_ref)

    for start in range(0, width, piece):
        cols = pl.ds(start, piece)
        g_one = lax.dot_general(twice_ref[0, span], top_ref[cols], COLS_COLS, preferred_element_type=jnp.float32)
        g_one = g_one.astype(jnp.bfloat16).astype(jnp.float32)
        g_two = lax.dot_general(twice_ref[1, span], top_peer_ref[cols], COLS_COLS, preferred_element_type=jnp.float32)
        g_two = g_two.astype(jnp.bfloat16).astype(jnp.float32)
        total = g_one + g_two
        size = jnp.abs(g_one) + jnp.abs(g_two)
        limit = (thr_ref[:, cols] * jnp.bfloat16(2.0)).astype(jnp.float32)
        share = total * pltpu.reciprocal(jnp.maximum(size, 2.0 * FLOOR))
        merged = 0.25 * total + jnp.clip(share + (1.0 - limit), -SOFT, SOFT) * size
        normed = (h_ref[:, cols] - vec_ref[0:1, cols]) * vec_ref[1:2, cols]
        normed_ref[:, cols] = normed.astype(jnp.bfloat16)
        before = normed * vec_ref[2:3, cols] + vec_ref[3:4, cols] + x_ref[:, cols].astype(jnp.float32)
        phi, bell = tail_and_bell(before)
        z_ref[:, cols] = (before * phi).astype(jnp.bfloat16)
        flow = merged * (phi + before * bell * DENSITY)
        flow_ref[:, cols] = flow.astype(flow_ref.dtype)
        stat_ref[:8, cols] += fold(flow)
        stat_ref[8:, cols] += fold(flow * normed)
    out_ref[...] = jnp.dot(z_ref[...], top_ref[...], preferred_element_type=jnp.float32)
    sent_ref[pl.ds(pl.multiple_of(step * rows, rows), rows)] = jnp.dot(
        z_ref[...], top_peer_ref[...], preferred_element_type=jnp.float32
    ).astype(jnp.bfloat16)
    acc_ref[:half] += lax.dot_general(cot_ref[...], z_ref[...], ROWS_ROWS, preferred_element_type=jnp.float32)
    acc_ref[half:] += lax.dot_general(cot_peer_ref[...], z_ref[...], ROWS_ROWS, preferred_element_type=jnp.float32)

    @pl.when(step == last)
    def _():
        rest_ref[...] = sent_ref[pl.ds(last * rows, rows)]

    def after():
        lax.fori_loop(0, last, lambda index, carry: (send(index).wait(), carry)[1], 0)

    return after


def crown_fill(*refs):
    used, given, own = refs[:10], refs[10:16], refs[17:]
    grad_ref, acc_ref = given[3], own[1]
    half = acc_ref.shape[0] // 2
    task = lax.axis_index("task")

    def part(index):
        def run():
            place = pl.multiple_of((task if index == 0 else 1 - task) * half, half)

            def one(i, carry):
                cols = pl.ds(pl.multiple_of(i * half, half), half)
                turned = acc_ref[pl.ds(index * half, half), cols].T
                grad_ref[cols, pl.ds(place, half)] = turned.astype(jnp.bfloat16)
                return carry

            lax.fori_loop(0, acc_ref.shape[1] // half, one, 0)

        return run

    return part(0), part(1)


def wide(mask, width):
    return jnp.concatenate([mask] * (width // mask.shape[1]), axis=1)


def edges(cuts_ref, canvas):
    shape = (SIDE * SIDE, 128)
    pixel = lax.broadcasted_iota(jnp.int32, shape, 0)
    row, col = pixel // SIDE, lax.rem(pixel, SIDE)
    down, right = cuts_ref[canvas, 0], cuts_ref[canvas, 1]
    one, zero = jnp.ones(shape, jnp.float32), jnp.zeros(shape, jnp.float32)
    within = lambda place, rim, cut: jnp.where((place != rim) & (place != cut), one, zero)
    return (
        within(col, 0, right), within(col, SIDE - 1, right - 1), within(row, 0, down), within(row, SIDE - 1, down - 1),
    )


def edges_of(cuts_ref, step, rows):
    count = rows // (SIDE * SIDE)
    parts = [edges(cuts_ref, step * count + index) for index in range(count)]
    return [jnp.concatenate([part[side] for part in parts], axis=0) for side in range(4)]


def gather_stats(stat_ref, hidden, first):
    @pl.when(False if first is None else first)
    def _():
        stat_ref[:16] = jnp.zeros_like(stat_ref[:16])
        mean = jnp.sum(hidden, axis=0, keepdims=True) / hidden.shape[0]
        stat_ref[16:] = jnp.broadcast_to(mean, stat_ref[16:].shape)

    away = hidden - stat_ref[16:17]
    stat_ref[:8] += fold(away)
    stat_ref[8:16] += fold(away * away)


def normal(hidden, vec_ref):
    return (hidden - vec_ref[0:1]) * vec_ref[1:2]


def squeeze_kernel(x_ref, w_ref, out_ref, stat_ref):
    hidden = jnp.dot(x_ref[...], w_ref[...], preferred_element_type=jnp.float32)
    out_ref[...] = hidden
    gather_stats(stat_ref, hidden, pl.program_id(0) == 0)


def mesh_kernel(h_ref, vec_ref, cuts_ref, w_ref, out_ref, side_ref, stat_ref, pad_ref):
    rows, mid = h_ref.shape
    inner = pl.ds(SIDE, rows)
    before = normal(h_ref[...], vec_ref) * vec_ref[2:3] + vec_ref[3:4]
    phi, _ = tail_and_bell(before)
    low = (before * phi).astype(jnp.bfloat16)
    kept = low.astype(jnp.float32)
    left, right, above, below = edges_of(cuts_ref, pl.program_id(0), rows)
    left, right = wide(left, mid), wide(right, mid)

    @pl.when(pl.program_id(0) == 0)
    def _():
        pad_ref[:SIDE] = jnp.zeros_like(pad_ref[:SIDE])
        pad_ref[SIDE + rows :] = jnp.zeros_like(pad_ref[:SIDE])

    pad_ref[inner, :mid] = (pltpu.roll(kept, 1, 0) * left).astype(jnp.bfloat16)
    pad_ref[inner, mid : 2 * mid] = low
    pad_ref[inner, 2 * mid :] = (pltpu.roll(kept, rows - 1, 0) * right).astype(jnp.bfloat16)
    side_ref[...] = pad_ref[inner].T
    above = wide(above.astype(jnp.bfloat16), 3 * mid)
    below = wide(below.astype(jnp.bfloat16), 3 * mid)
    hidden = jnp.dot(pad_ref[inner], w_ref[3 * mid : 6 * mid], preferred_element_type=jnp.float32)
    hidden += jnp.dot(pad_ref[:rows] * above, w_ref[: 3 * mid], preferred_element_type=jnp.float32)
    hidden += jnp.dot(pad_ref[2 * SIDE :] * below, w_ref[6 * mid :], preferred_element_type=jnp.float32)
    out_ref[...] = hidden
    gather_stats(stat_ref, hidden, pl.program_id(0) == 0)


def widen_kernel(h_ref, vec_ref, w_ref, out_ref, low_ref, stat_ref):
    rows = h_ref.shape[0]
    spans = [pl.ds(start, rows // 2) for start in (0, rows // 2)]
    lows = []
    for span in spans:
        before = normal(h_ref[span], vec_ref) * vec_ref[2:3] + vec_ref[3:4]
        phi, _ = tail_and_bell(before)
        low = (before * phi).astype(jnp.bfloat16)
        low_ref[:, span] = low.T
        lows.append(low)
    for index, span in enumerate(spans):
        hidden = jnp.dot(lows[index], w_ref[...], preferred_element_type=jnp.float32)
        out_ref[span] = hidden
        gather_stats(stat_ref, hidden, (pl.program_id(0) == 0) if index == 0 else None)


def norm_grad(upstream, normed, vec_ref):
    return vec_ref[4:5] * (upstream - vec_ref[5:6] - normed * vec_ref[6:7])


def act_slope(value):
    phi, bell = tail_and_bell(value)
    return phi + value * bell * DENSITY


def gather_flow(stat_ref, flow, normed, first):
    @pl.when(first)
    def _():
        stat_ref[...] = jnp.zeros_like(stat_ref)

    stat_ref[:8] += fold(flow)
    stat_ref[8:16] += fold(flow * normed)


def narrow_kernel(flow_ref, normed_ref, vec_ref, two_ref, vectwo_ref, low_ref, w_ref, out_ref, grad_ref, stat_ref, dh_ref):
    step = pl.program_id(0)
    rows = flow_ref.shape[0]
    dh = norm_grad(flow_ref[...].astype(jnp.float32), normed_ref[...].astype(jnp.float32), vec_ref)
    low = dh.astype(jnp.bfloat16)
    dh_ref[pl.ds(pl.multiple_of(step * rows, rows), rows)] = low
    dq = lax.dot_general(low, w_ref[...], COLS_COLS, preferred_element_type=jnp.float32)
    normed = normal(two_ref[...], vectwo_ref)
    flow = dq * act_slope(normed * vectwo_ref[2:3] + vectwo_ref[3:4])
    out_ref[...] = flow
    gather_flow(stat_ref, flow, normed, step == 0)


def narrow_fill(flow_ref, normed_ref, vec_ref, two_ref, vectwo_ref, low_ref, w_ref, out_ref, grad_ref, stat_ref, dh_ref):
    half = dh_ref.shape[1] // 2

    def part(index):
        def run():
            def one(i, carry):
                cols = pl.ds(pl.multiple_of(index * half + i * 512, 512), 512)
                grad_ref[:, cols] = jnp.dot(
                    low_ref[...], dh_ref[:, cols], preferred_element_type=jnp.float32
                ).astype(jnp.bfloat16)
                return carry

            lax.fori_loop(0, half // 512, one, 0)

        return run

    return part(0), part(1)


def across(source, target, sems, hop="task"):
    task = lax.axis_index("task")
    place = lax.axis_index("batch")
    device = (1 - task, place) if hop == "task" else (task, place + 1 - 2 * lax.rem(place, 2))
    return pltpu.make_async_remote_copy(
        src_ref=source,
        dst_ref=target,
        send_sem=sems.at[0],
        recv_sem=sems.at[1],
        device_id=device,
        device_id_type=MESH,
    )


def tiled(kernel, tile, moving, flags, outs, fixed, scratch, name, stats=None, sends=(), far=(), fill=None, turns=(), aside=None):
    tasks = lax.axis_size("task")
    batch = lax.axis_size("batch")
    rows = moving[0].shape[0]

    def block(array):
        return pl.BlockSpec((tile,) + array.shape[1:], lambda i: (i,) + (0,) * (len(array.shape) - 1))

    def turned(array):
        return pl.BlockSpec((array.shape[0], tile), lambda i: (0, i))

    def whole(array):
        zeros = (0,) * len(array.shape)
        return pl.BlockSpec(array.shape, lambda i: zeros)

    hbm = pl.BlockSpec(memory_space=pl.ANY)
    operands = list(moving)
    in_specs = [(whole, block, lambda a: hbm, lambda a: pl.BlockSpec(memory_space=pltpu.SMEM))[m](a) for a, m in zip(moving, flags)]
    out_shape = outs + fixed + list(far)
    out_specs = [turned(a) if i in turns else block(a) for i, a in enumerate(outs)] + [whole(a) for a in fixed] + [hbm for a in far]
    scratch = list(scratch)
    params = dict(vmem_limit_bytes=VMEM_BYTES)
    ins, made, held = len(operands), len(out_shape), len(scratch)
    run = kernel
    if stats is not None:
        vecs, forward, ident = stats
        width = vecs[0].shape[1]
        params.update(collective_id=ident, has_side_effects=True)
        operands += vecs
        in_specs += [whole(vec) for vec in vecs]
        out_shape = out_shape + [shape32(16, width)]
        out_specs = out_specs + [whole(out_shape[-1])]
        scratch = scratch + [pltpu.VMEM((24 if forward else 16, width), jnp.float32)]
        scratch = scratch + Exchange.scratch(tasks, batch, width)
        for array, _, shape, _ in sends:
            operands.append(array)
            in_specs.append(hbm)
            out_shape = out_shape + [jax.ShapeDtypeStruct(shape, array.dtype)]
            out_specs = out_specs + [hbm]
            scratch = scratch + [pltpu.SemaphoreType.DMA((2,))]

        if aside is not None:
            operands.append(aside[0])
            in_specs.append(hbm)
            out_shape = out_shape + list(aside[1])
            out_specs = out_specs + [hbm for _ in aside[1]]
            scratch = scratch + list(aside[2])

        def run(*refs):
            refs = list(refs)
            take = lambda n: [refs.pop(0) for _ in range(n)]
            used = take(ins)
            vec_refs = take(len(vecs))
            sources = take(len(sends))
            own_in = take(0 if aside is None else 1)
            given = take(made)
            out_ref = take(1)[0]
            targets = take(len(sends))
            own_out = take(0 if aside is None else len(aside[1]))
            own = take(held)
            stat_ref = take(1)[0]
            exchange = Exchange(tasks, batch, *take(6))
            step = pl.program_id(0)
            last = pl.num_programs(0) - 1

            @pl.when(step == 0)
            def _():
                exchange.greet()

            early = len(sends) > 0 or len(far) > 0

            def crossing(index):
                _, view, _, hop = sends[index]
                return across(view(sources[index]), targets[index], cross_sems[index], hop)

            cross_sems = take(len(sends))
            if early and aside is None:

                @pl.when(step == 1)
                def _():
                    exchange.met()
                    for index in range(len(sends)):
                        crossing(index).start()

            if aside is not None:
                helper = aside[3](exchange, *own_in, *own_out, *refs)
                helper.before(step)

            after = kernel(*used, *given, stat_ref, *own)
            if aside is not None:
                helper.after(step)

                @pl.when(step == 1)
                def _():
                    for index in range(len(sends)):
                        crossing(index).start()

            @pl.when(step == last)
            def _():
                if not early and aside is None:
                    exchange.met()
                fillers = (None, None) if fill is None else fill(*used, *given, stat_ref, *own)
                settle_stats(exchange, stat_ref, vec_refs, out_ref, rows, rows * tasks * batch, forward, fillers)
                for index in range(len(sends)):
                    crossing(index).wait()
                if after is not None:
                    after()
                if aside is not None:
                    helper.end()

    return pl.pallas_call(
        run,
        grid=(rows // tile,),
        out_shape=out_shape,
        in_specs=in_specs,
        out_specs=out_specs,
        scratch_shapes=scratch,
        compiler_params=pltpu.CompilerParams(**params),
        name=name,
    )(*operands)


def shape32(*shape):
    return jax.ShapeDtypeStruct(shape, jnp.float32)


def shape16(*shape):
    return jax.ShapeDtypeStruct(shape, jnp.bfloat16)


def squeeze(flat_in, w_reduce, stats, tile):
    rows, mid = flat_in.shape[0], w_reduce.shape[1]
    return tiled(squeeze_kernel, tile, [flat_in, w_reduce], [1, 0], [shape32(rows, mid)], [], [], "squeeze", stats)


def mesh_forward(h_one, vec, cuts, taps, stats, sends, tile):
    rows, mid = h_one.shape
    return tiled(
        mesh_kernel, tile, [h_one, vec, cuts, taps], [1, 0, 3, 0],
        [shape32(rows, mid), shape16(3 * mid, rows)], [],
        [pltpu.VMEM((tile + 2 * SIDE, 3 * mid), jnp.bfloat16)], "mesh_forward", stats, sends, turns=(1,),
    )


def widen(h_two, vec, w_expand, stats, sends, tile):
    rows, mid = h_two.shape
    width = w_expand.shape[1]
    return tiled(
        widen_kernel, tile, [h_two, vec, w_expand], [1, 0, 0],
        [shape32(rows, width), shape16(mid, rows)], [], [], "widen", stats, sends, turns=(1,),
    )


class HeadsAside:
    def __init__(self, batch, shape, last, exchange, source, target, work, *room):
        self.exchange, self.work, self.target, self.last = exchange, work, target, last
        self.sum = Reduction(Grid(batch), work, None, *room[:11], "owner")
        self.load = pltpu.make_async_copy(source, work, room[11].at[0])
        self.sems = room[11]

    def before(self, step):
        @pl.when(step == 0)
        def _():
            self.load.start()

    def out(self, part):
        grid = self.sum.grid
        bits = grid.bits(part)
        view = self.sum.view(grid.core, part, bits[0], bits[1])
        return pltpu.make_async_copy(view, self.target.at[part], self.sems.at[1 + part])

    def after(self, step):
        @pl.when(step == 0)
        def _():
            self.exchange.met()
            self.load.wait()
            self.sum.stage(0)

        @pl.when(step == 1)
        def _():
            self.sum.stage(1)

        @pl.when(step == self.last)
        def _():
            self.sum.stage(2)

    def end(self):
        for part in range(2):
            self.sum.finish(2, part)
            self.out(part).start()
        for part in range(2):
            self.out(part).wait()


def narrow(flow, normed, vec_three, h_two, vec_two, q_two, w_expand, heads, rest, stats, tile):
    rows, mid = h_two.shape
    width = w_expand.shape[1]
    batch = lax.axis_size("batch")
    high, across_ = heads.shape
    scratch = [pltpu.VMEM(heads.shape, jnp.bfloat16)] + Reduction.scratch(high, across_, "owner", batch // LOW)
    scratch += [pltpu.SemaphoreType.DMA((3,))]
    helper = functools.partial(HeadsAside, batch, heads.shape, rows // tile - 1)
    return tiled(
        narrow_kernel, tile, [flow, normed, vec_three, h_two, vec_two, q_two, w_expand], [1, 1, 0, 1, 0, 0, 0],
        [shape32(rows, mid)], [shape16(mid, width)], [pltpu.VMEM((rows, width), jnp.bfloat16)], "narrow", stats,
        [(rest, lambda ref: ref, rest.shape, "task")], fill=narrow_fill, aside=(heads, [shape16(2, high // 8, across_ // 2)], scratch, helper),
    )


def crown(h_three, flat_in, limits, cots, cot_parts, top, top_parts, vec, stats, tile, piece):
    rows, width = flat_in.shape
    half = cots.shape[2]
    return tiled(
        functools.partial(crown_kernel, piece), tile,
        [h_three, flat_in, limits, cots, *cot_parts, top, *top_parts, vec], [1, 1, 1, 2, 2, 2, 0, 2, 2, 0],
        [shape32(rows, half), shape16(rows, width), shape16(rows, width)], [shape16(width, 2 * half), shape16(tile, half)],
        [
            pltpu.VMEM((tile, width), jnp.bfloat16),
            pltpu.VMEM((2 * half, width), jnp.float32),
            pltpu.VMEM((rows, half), jnp.bfloat16),
            pltpu.SemaphoreType.DMA((rows // tile, 2)),
            pltpu.VMEM((rows, half), jnp.bfloat16),
            pltpu.VMEM((rows, half), jnp.bfloat16),
            pltpu.VMEM((width, half), jnp.bfloat16),
            pltpu.SemaphoreType.DMA((5,)),
            pltpu.SemaphoreType.DMA((2,)),
            pltpu.VMEM((2, tile, half), jnp.bfloat16),
        ],
        "crown", stats, (), [shape16(rows, half)], crown_fill,
    )


class Stream:
    def __init__(self, view, held, sems):
        self.view, self.held, self.sems = view, held, sems

    def copy(self, index):
        slot = lax.rem(index, 2)
        return pltpu.make_async_copy(self.view(index), self.held.at[slot], self.sems.at[slot])

    def start(self, index):
        self.copy(index).start()

    def take(self, index, count):
        self.copy(index).wait()

        @pl.when(index + 1 < count)
        def _():
            self.start(index + 1)

        return self.held.at[lax.rem(index, 2)]


def back_kernel(rows, tasks, batch, tile, *refs):
    refs = list(refs)

    def take(count):
        return [refs.pop(0) for _ in range(count)]

    (flow_hbm, two_hbm, one_hbm, side_hbm, w_hbm, x_hbm, heads_hbm, expand_hbm) = take(8)
    vectwo_ref, vecone_ref, cuts_ref = take(3)
    (out_hbm, heads_out, expand_out, spatial_out, reduce_out, vec_ref) = take(6)
    (two_buf, x_buf) = take(2)
    (side_ref, lane_ref, flow_ref, w_ref) = take(4)
    heads_work, expand_work, spatial_work, reduce_work, total_ref, stat_ref = take(6)
    pair_sems, whole_sems, flow_sems = take(3)
    exchange = Exchange(tasks, batch, *take(6))
    grid = Grid(batch)
    mid = flow_hbm.shape[1]
    width = x_hbm.shape[1]
    spans = rows // tile

    def blocks(ref, height):
        return lambda index: ref.at[pl.ds(pl.multiple_of(index * height, height), height)]

    exchange.greet()

    def flow_load(index):
        return pltpu.make_async_copy(
            blocks(flow_hbm, tile)(index), blocks(flow_ref, tile)(index), flow_sems.at[index]
        )

    twos = Stream(blocks(two_hbm, tile), two_buf, pair_sems.at[1])
    ones = Stream(blocks(one_hbm, tile), two_buf, pair_sems.at[3])
    dh_ref, normed_ref, dht_ref = lane_ref.at[:, :mid], lane_ref.at[:, mid : 2 * mid], side_ref.at[:mid]
    across_cols = x_buf.shape[2]
    columns = Stream(
        lambda index: x_hbm.at[:, pl.ds(pl.multiple_of(index * across_cols, across_cols), across_cols)],
        x_buf, pair_sems.at[0],
    )
    loads = [
        pltpu.make_async_copy(source, target, whole_sems.at[index])
        for index, (source, target) in enumerate(
            [(heads_hbm, heads_work), (side_hbm, side_ref), (expand_hbm, expand_work), (w_hbm, w_ref)]
        )
    ]
    heads_load, side_load, expand_load, w_load = loads
    keep = pltpu.make_async_copy(dh_ref, out_hbm, whole_sems.at[4])
    heads_load.start()
    flow_load(0).start()
    twos.start(0)
    expand_load.start()
    for index in range(1, spans):
        flow_load(index).start()
    side_load.start()
    w_load.start()

    third = spatial_work.shape[0] // 3
    works = [(heads_work, heads_out, "owner"), (expand_work, expand_out, "wide")]
    for index in range(3):
        span = pl.ds(index * third, third)
        works.append((spatial_work.at[span], spatial_out.at[span], "tall"))
    for index in range(2):
        span = pl.ds(index * width // 2, width // 2)
        works.append((reduce_work.at[span], total_ref.at[span], "tall"))
    reductions = []
    for work, out, kind in works:
        shape = heads_out.shape if kind == "owner" else None
        reductions.append(Reduction(grid, work, out, *take(11), kind, shape))

    def tick(name):
        for item, stage in AGENDA.get(name, ()):
            reductions[item].stage(stage)

    def ticks(name, index, count, scale=1, shift=0):
        for step in range(count):
            label = "%s%d" % (name, step * scale + shift)
            if label in AGENDA:

                @pl.when(index == step)
                def _():
                    tick(label)

    def lanes(index, carry):
        span = pl.ds(pl.multiple_of(index * tile, tile), tile)
        flow_load(index).wait()
        flow = flow_ref[span]
        normed = normal(twos.take(index, spans)[...], vectwo_ref)
        dh = norm_grad(flow, normed, vectwo_ref)
        _, _, above, below = edges_of(cuts_ref, index, tile)
        above, below = wide(above, mid), wide(below, mid)
        low = jnp.bfloat16
        zero = jnp.zeros((SIDE, mid), low)
        lane_ref[span, mid : 2 * mid] = dh.astype(low)
        lane_ref[span, :mid] = jnp.concatenate([(dh * above)[SIDE:].astype(low), zero], axis=0)
        lane_ref[span, 2 * mid :] = jnp.concatenate([zero, (dh * below)[: tile - SIDE].astype(low)], axis=0)

        @pl.when(index == 0)
        def _():
            expand_load.wait()

        ticks("lane", index, 4)
        return carry

    exchange.met()
    heads_load.wait()
    tick("start")
    lax.fori_loop(0, spans, lanes, 0)
    ones.start(0)
    side_load.wait()

    def spatial(index, carry):
        a, b = index // 3, lax.rem(index, 3)
        rows_here = pl.ds(pl.multiple_of(b * mid, mid), mid)
        cols = pl.ds(pl.multiple_of(a * mid, mid), mid)
        part = jnp.dot(side_ref[rows_here], lane_ref[:, cols], preferred_element_type=jnp.float32)
        spatial_work[pl.ds(pl.multiple_of(index * mid, mid), mid)] = part.astype(jnp.bfloat16)
        ticks("sp", index, 9)
        return carry

    lax.fori_loop(0, 9, spatial, 0)
    w_load.wait()

    def taps(index, carry):
        span = pl.ds(pl.multiple_of(index * tile, tile), tile)
        pieces = []
        for b in range(3):
            total = None
            for a in range(3):
                part = lax.dot_general(
                    lane_ref[span, a * mid : (a + 1) * mid], w_ref[3 * a + b], COLS_COLS,
                    preferred_element_type=jnp.float32,
                )
                total = part if total is None else total + part
            pieces.append(total)
            if b < 2:
                ticks("tap", index, 4, 3, b)
        left, right, _, _ = edges_of(cuts_ref, index, tile)
        left, right = wide(left, mid), wide(right, mid)
        dq = pieces[1] + pltpu.roll(pieces[0] * left, tile - 1, 0) + pltpu.roll(pieces[2] * right, 1, 0)
        normed = normal(ones.take(index, spans)[...], vecone_ref)
        flow = dq * act_slope(normed * vecone_ref[2:3] + vecone_ref[3:4])
        flow_ref[span] = flow
        normed_ref[span] = normed.astype(jnp.bfloat16)
        gather_flow(stat_ref, flow, normed, index == 0)
        ticks("tap", index, 4, 3, 2)
        return carry

    lax.fori_loop(0, spans, taps, 0)
    columns.start(0)
    settle_stats(
        exchange, stat_ref, [vecone_ref], vec_ref, rows, rows * tasks * batch, False,
        (lambda: tick("xa"), lambda: tick("xb")),
    )
    tick("xch")

    def inner(index, carry):
        span = pl.ds(pl.multiple_of(index * tile, tile), tile)
        dh = norm_grad(flow_ref[span], normed_ref[span].astype(jnp.float32), vec_ref)
        low = dh.astype(jnp.bfloat16)
        dh_ref[span] = low
        dht_ref[:, span] = low.T
        return carry

    lax.fori_loop(0, spans, inner, 0)
    keep.start()
    tick("inner")
    count = width // across_cols

    def reduce(index, carry):
        part = jnp.dot(dht_ref[...], columns.take(index, count)[...], preferred_element_type=jnp.float32)
        span = pl.ds(pl.multiple_of(index * across_cols, across_cols), across_cols)
        reduce_work[span] = part.T.astype(jnp.bfloat16)
        ticks("red", index, 4)
        return carry

    lax.fori_loop(0, count, reduce, 0)
    keep.wait()
    tick("tail")
    store = pltpu.make_async_copy(total_ref, reduce_out, whole_sems.at[0])
    store.start()
    store.wait()


def back(flow, h_two, vec_two, h_one, vec_one, sides, cuts, w_spatial, flat_in, heads, expand, heads_shape, ident, tile):
    tasks = lax.axis_size("task")
    batch = lax.axis_size("batch")
    far = batch // LOW
    rows, mid = h_one.shape
    width = flat_in.shape[1]
    full, low = jnp.float32, jnp.bfloat16
    cols = 512
    hbm = pl.BlockSpec(memory_space=pl.ANY)
    vmem = pl.BlockSpec(memory_space=pltpu.VMEM)
    shapes = [(heads_shape, "owner"), (expand.shape, "wide")] + [((3 * mid, mid), "tall")] * 3
    shapes += [((width // 2, mid), "tall")] * 2
    scratch = [
        pltpu.VMEM((2, tile, mid), full),
        pltpu.VMEM((2, rows, cols), low),
        pltpu.VMEM((3 * mid, rows), low),
        pltpu.VMEM((rows, 3 * mid), low),
        pltpu.VMEM((rows, mid), full),
        pltpu.VMEM(w_spatial.shape, low),
        pltpu.VMEM(heads.shape, low),
        pltpu.VMEM(expand.shape, low),
        pltpu.VMEM((9 * mid, mid), low),
        pltpu.VMEM((width, mid), low),
        pltpu.VMEM((width, mid), low),
        pltpu.VMEM((16, mid), full),
        pltpu.SemaphoreType.DMA((4, 2)),
        pltpu.SemaphoreType.DMA((5,)),
        pltpu.SemaphoreType.DMA((rows // tile,)),
    ] + Exchange.scratch(tasks, batch, mid)
    for (high, across_), kind in shapes:
        scratch += Reduction.scratch(high, across_, kind, far, kind == "owner")
    return pl.pallas_call(
        functools.partial(back_kernel, rows, tasks, batch, tile),
        out_shape=[
            shape16(rows, mid), shape16(*heads_shape), shape16(*expand.shape), shape16(9 * mid, mid),
            shape16(width, mid), shape32(16, mid),
        ],
        in_specs=[hbm] * 8 + [vmem] * 2 + [pl.BlockSpec(memory_space=pltpu.SMEM)],
        out_specs=[hbm] * 5 + [vmem],
        scratch_shapes=scratch,
        compiler_params=pltpu.CompilerParams(
            vmem_limit_bytes=VMEM_BYTES, collective_id=ident, has_side_effects=True
        ),
        name="back",
    )(flow, h_two, h_one, sides, w_spatial, flat_in, heads, expand, vec_two, vec_one, cuts)


def finish_kernel(
    dh_ref, up_ref, heads_ref, expand_ref, spatial_ref, reduce_ref, mine_ref, came_ref, rest_ref, w_ref, one_ref, two_ref, three_ref,
    out_ref, heads_out, expand_out, spatial_out, reduce_out, both_ref, *sums,
):
    full = jnp.float32
    task = lax.axis_index("task")
    half = heads_out.shape[1]
    back = lax.dot_general(dh_ref[...], w_ref[...], COLS_COLS, preferred_element_type=full)
    out_ref[...] = (up_ref[...].astype(full) + back).astype(jnp.bfloat16)
    heads_out[...] = jnp.where(task == 0, heads_ref[:, :half], heads_ref[:, half:]).astype(full)
    expand_out[...] = expand_ref[...].astype(full)
    spatial_out[...] = spatial_ref[...].astype(full)
    reduce_out[...] = reduce_ref[...].astype(full)
    both_ref[task] = mine_ref[...]
    both_ref[1 - task] = came_ref[...].astype(full)

    @pl.when(pl.program_id(0) == pl.num_programs(0) - 1)
    def _():
        height = rest_ref.shape[0]
        both_ref[1 - task, both_ref.shape[1] - height :] = rest_ref[...].astype(full)


    @pl.when(pl.program_id(0) == 0)
    def _():
        for index, vec_ref in enumerate((one_ref, two_ref, three_ref)):
            sums[2 * index][...] = vec_ref[9:10]
            sums[2 * index + 1][...] = vec_ref[8:9]


def finish(dh, up, heads, expand, spatial, reduce, mine, came, rest, w_reduce, vecs, steps):

    def block(array, lead=0):
        zeros = (0,) * (len(array.shape) - 1 - lead)
        height = array.shape[lead] // steps
        return pl.BlockSpec(array.shape[:lead] + (height,) + array.shape[lead + 1 :], lambda i: (0,) * lead + (i,) + zeros)

    def whole(array):
        return pl.BlockSpec(array.shape, lambda i: (0, 0))

    rows, half = mine.shape
    moving = [dh, up, heads, expand, spatial, reduce, mine, came]
    fixed = [rest, w_reduce, *vecs]
    outs = [shape16(*up.shape), shape32(heads.shape[0], half), shape32(*expand.shape), shape32(*spatial.shape), shape32(*reduce.shape)]
    both = shape32(2, rows, half)
    sums = [shape32(1, vec.shape[1]) for vec in vecs for _ in range(2)]
    return pl.pallas_call(
        finish_kernel,
        grid=(steps,),
        out_shape=outs + [both] + sums,
        in_specs=[block(a) for a in moving] + [whole(a) for a in fixed],
        out_specs=[block(a) for a in outs] + [block(both, 1)] + [whole(a) for a in sums],
        compiler_params=pltpu.CompilerParams(vmem_limit_bytes=VMEM_BYTES),
        name="finish",
    )(*moving, *fixed)


def body(
    inputs,
    crop_cuts,
    threshold,
    w_reduce,
    w_spatial,
    w_expand,
    w_heads,
    gain_one,
    bias_one,
    gain_two,
    bias_two,
    gain_three,
    bias_three,
    cotangent,
):
    canvases, pixels, width = inputs.shape[1:]
    mid = w_reduce.shape[1]
    rows = canvases * pixels
    half = w_heads.shape[2]
    cots = cotangent.reshape(2, rows, half)
    top_mine = w_heads[0]

    def params(gain, bias):
        return [gain.reshape(1, -1), bias.reshape(1, -1)]

    cuts = crop_cuts.reshape(canvases, 2)
    flat_in = inputs.reshape(rows, width)
    core = lambda: lax.rem(lax.axis_index("batch"), 2)
    other = lambda: 1 - lax.axis_index("task")
    quarter = rows // 4
    top_rows = width // 2
    h_one, vec_one = squeeze(flat_in, w_reduce, (params(gain_one, bias_one), True, 0), min(rows, 512))
    sends = [
        (top_mine, lambda ref: ref.at[pl.ds(pl.multiple_of(core() * top_rows, top_rows), top_rows)], (top_rows, half), "task"),
        (cots, lambda ref: ref.at[other(), pl.ds(0, quarter)], (quarter, half), "task"),
    ]
    h_two, sides, vec_two, top_one, cot_one = mesh_forward(
        h_one, vec_one, cuts, w_spatial.reshape(9 * mid, mid), (params(gain_two, bias_two), True, 1), sends, pixels
    )
    sends = [
        (top_one, lambda ref: ref, (top_rows, half), "core"),
        (cots, lambda ref: ref.at[other(), pl.ds(quarter, quarter)], (quarter, half), "task"),
    ]
    h_three, q_two, vec_three, top_two, cot_two = widen(
        h_two, vec_two, w_expand, (params(gain_three, bias_three), True, 2), sends, min(rows, 2 * pixels)
    )
    out_mine, flow, normed, grad_heads, rest, out_peer, vec_three = crown(
        h_three, flat_in, threshold.reshape(rows, width), cots, (cot_one, cot_two), top_mine, (top_one, top_two), vec_three,
        ([vec_three], False, 3), pixels, 256,
    )
    heads_shape = grad_heads.shape
    flow_two, grad_expand, vec_two, rest, grad_heads = narrow(
        flow, normed, vec_three, h_two, vec_two, q_two, w_expand, grad_heads, rest, ([vec_two], False, 4), min(rows, 512)
    )
    dh_one, grad_heads, grad_expand, grad_spatial, grad_reduce, vec_one = back(
        flow_two, h_two, vec_two, h_one, vec_one, sides, cuts, w_spatial, flat_in, grad_heads, grad_expand, heads_shape, 5,
        min(rows, 512),
    )
    grad_inputs, grad_heads, grad_expand, grad_spatial, grad_reduce, head_out, *sums = finish(
        dh_one, flow, grad_heads, grad_expand, grad_spatial, grad_reduce, out_mine, out_peer, rest, w_reduce,
        (vec_one, vec_two, vec_three), 2,
    )
    return (
        head_out.reshape(1, 2, canvases, pixels, half),
        grad_inputs.reshape(inputs.shape),
        grad_reduce,
        grad_spatial.reshape(w_spatial.shape),
        grad_expand,
        grad_heads[None],
        *[row.reshape(-1) for row in sums],
    )


def solution(mesh):
    in_specs = (
        P("task", "batch", None, None),
        P("task", "batch", None),
        P("task", "batch", None, None),
        P(),
        P(),
        P(),
        P("task", None, None),
        P(),
        P(),
        P(),
        P(),
        P(),
        P(),
        P("task", None, "batch", None, None),
    )
    out_specs = (
        P("task", None, "batch", None, None),
        P("task", "batch", None, None),
        P(),
        P(),
        P(),
        P("task", None, None),
        P(),
        P(),
        P(),
        P(),
        P(),
        P(),
    )
    return jax.shard_map(body, mesh=mesh, in_specs=in_specs, out_specs=out_specs, check_vma=False)
```

```python
import functools
import math

import jax
import jax.numpy as jnp
from jax import lax
from jax.experimental import pallas as pl
from jax.experimental.pallas import tpu as pltpu
from jax.sharding import PartitionSpec as P

SIDE = 16
EPS = 1e-05
FLOOR = 0.1
SOFT = 0.25
ROOT_HALF = 0.7071067811865476
DENSITY = 0.3989422804014327
LOG2E = 1.4426950408889634
ERF_P = 0.3275911
ERF_A = (0.254829592, -0.284496736, 1.421413741, -1.453152027, 1.061405429)
ROWS_ROWS = (((0,), (0,)), ((), ()))
COLS_COLS = (((1,), (1,)), ((), ()))
MESH = pl.DeviceIdType.MESH
LOW = 4
VMEM_BYTES = 62 * 2**20


AGENDA = {
    "start": ((0, 3),),
    "lane0": ((1, 0),),
    "lane2": ((1, 1),),
    "sp1": ((0, 4),),
    "sp2": ((2, 0),),
    "sp4": ((1, 2), (2, 1),),
    "sp5": ((3, 0),),
    "sp8": ((0, 5), (1, 3), (3, 1), (4, 0),),
    "tap2": ((2, 2), (4, 1),),
    "tap5": ((0, 7), (1, 4),),
    "tap8": ((0, 8), (3, 2), (2, 3),),
    "xb": ((1, 5), (2, 4), (3, 3), (4, 2),),
    "xch": ((1, 6),),
    "inner": ((2, 5), (4, 3),),
    "red1": ((1, 7), (3, 4), (5, 0),),
    "red2": ((2, 6),),
    "red3": ((1, 8), (4, 4), (5, 1), (6, 0),),
    "tail": ((6, 1), (3, 5), (2, 7), (2, 8), (5, 2), (4, 5), (6, 2), (3, 6), (5, 3), (4, 6), (6, 3), (5, 4), (3, 7), (6, 4), (3, 8), (4, 7), (5, 5), (4, 8), (6, 5), (5, 6), (6, 6), (5, 7), (5, 8), (6, 7), (6, 8),),
}


class Reduction:
    def __init__(
        self, grid, work, result, core, first_a, first_b, second, last, done, send, recv, far_send, far_recv, local,
        kind, shape=None,
    ):
        self.grid, self.work, self.result = grid, work, result
        self.core_room, self.first_rooms, self.second_room, self.last_room = core, (first_a, first_b), second, last
        self.done = done
        self.send, self.recv, self.far_send, self.far_recv = send, recv, far_send, far_recv
        self.local = local
        self.kind = kind
        self.resumed = shape is not None
        self.rows, self.cols = shape or work.shape
        sizes = self.sizes(self.rows, self.cols, kind, grid.far)
        self.pieces = sizes[3][0] // sizes[4][0]
        self.mine = lax.rem(grid.high, self.pieces)

    @staticmethod
    def sizes(rows, cols, kind, far):
        if kind == "wide":
            core, first, second = (rows, cols // 2), (rows, cols // 8), (rows, cols // 16)
            firsts = first, first
        elif kind == "tall":
            core, first, second = (rows // 2, cols), (rows // 2, cols // 4), (rows // 4, cols // 4)
            firsts = first, first
        else:
            core, second = (rows // 2, cols), (rows // 8, cols // 2)
            firsts = (rows // 4, cols // 2), (rows // 8, cols)
        pieces = max(n for n in range(1, far + 1) if far % n == 0 and second[0] % (8 * n) == 0)
        return core, *firsts, second, (second[0] // pieces, second[1])

    @staticmethod
    def scratch(rows, cols, kind, far, resumed=False):
        core, first_a, first_b, second, last = Reduction.sizes(rows, cols, kind, far)
        if resumed:
            core = first_a = first_b = (16, 128)
        return [
            pltpu.VMEM(core, jnp.bfloat16),
            pltpu.VMEM(first_a, jnp.bfloat16),
            pltpu.VMEM(first_b, jnp.bfloat16),
            pltpu.VMEM((2,) + ((16, 128) if resumed else second), jnp.bfloat16),
            pltpu.VMEM((2, far) + last, jnp.bfloat16),
            pltpu.VMEM((2,) + last, jnp.bfloat16),
            pltpu.SemaphoreType.DMA((10,)),
            pltpu.SemaphoreType.DMA((10,)),
            pltpu.SemaphoreType.DMA((4, far)),
            pltpu.SemaphoreType.DMA((4, far)),
            pltpu.SemaphoreType.DMA((2,)),
        ]

    def view(self, core, part=None, first=None, second=None, piece=None, done=False):
        rows, cols = self.rows, self.cols
        sizes = self.sizes(rows, cols, self.kind, self.grid.far)
        row = col = 0
        shape = sizes[0]
        if self.kind == "wide":
            col = core * (cols // 2)
            if part is not None:
                col = col + part * (cols // 4) + first * (cols // 8)
            if second is not None:
                col = col + second * (cols // 16)
        elif self.kind == "tall":
            row = core * (rows // 2)
            if part is not None:
                col = part * (cols // 2) + first * (cols // 4)
            if second is not None:
                row = row + second * (rows // 4)
        else:
            row = core * (rows // 2)
            if part is not None:
                row = row + part * (rows // 4)
                y, task = (second, first) if part == 0 else (first, second)
                row = row if y is None else row + y * (rows // 8)
                col = 0 if task is None else task * (cols // 2)
            elif done:
                col = self.grid.task * (cols // 2)
                shape = (rows // 2, cols // 2)
        if part is not None:
            shape = sizes[1 + part] if second is None else sizes[3]
        ref = self.result if done else self.work
        if self.resumed and not done:
            ref, row, col = self.work.at[part], 0, 0
        if piece is not None:
            row = row + piece * sizes[4][0]
            shape = sizes[4]
        if not isinstance(row, int):
            row = pl.multiple_of(row, shape[0] & -shape[0])
        if not isinstance(col, int):
            col = pl.multiple_of(col, 128)
        return ref.at[pl.ds(row, shape[0]), pl.ds(col, shape[1])]

    def swap(self, index):
        grid = self.grid
        part = (index + 1) % 2
        bits = grid.bits(part)
        if index == 0:
            source, target, device = self.view(1 - grid.core), self.core_room, grid.core_peer
        elif index < 3:
            source, target = self.view(grid.core, part, 1 - bits[0]), self.first_rooms[part]
            device = grid.peers(part)[0]
        elif index < 5:
            source, target = self.view(grid.core, part, bits[0], 1 - bits[1]), self.second_room.at[part]
            device = grid.peers(part)[1]
        elif index < 7:
            source = self.view(grid.core, part, bits[0], bits[1], done=True)
            target, device = source, grid.y_peer if self.kind == "owner" else grid.peers(part)[1]
        elif index < 9:
            source = self.view(grid.core, part, bits[0], done=True)
            target, device = source, grid.peers(part)[0]
        else:
            source = self.view(grid.core, done=True)
            target, device = source, grid.core_peer
        return pltpu.make_async_remote_copy(
            src_ref=source,
            dst_ref=target,
            send_sem=self.send.at[index],
            recv_sem=self.recv.at[index],
            device_id=device,
            device_id_type=MESH,
        )

    def add(self, target, sources):
        rows = target.shape[0]
        step = math.gcd(rows, 64)

        def one(i, carry):
            span = pl.ds(pl.multiple_of(i * step, step), step)
            total = sources[0][span].astype(jnp.float32)
            for source in sources[1:]:
                total = total + source[span].astype(jnp.float32)
            target[span] = total.astype(jnp.bfloat16)
            return carry

        lax.fori_loop(0, rows // step, one, 0)

    def far_copy(self, part, step, back, inward):
        grid = self.grid
        bits = grid.bits(part)
        if back:
            first = grid.high - self.mine
            slot = first + lax.rem(self.mine + step, self.pieces)
            owner = slot if inward else grid.high
            source = self.done.at[part]
            target = self.view(grid.core, part, bits[0], bits[1], lax.rem(owner, self.pieces), True)
        else:
            slot = lax.rem(grid.high + step, grid.far)
            owner = slot if inward else grid.high
            source = self.view(grid.core, part, bits[0], bits[1], lax.rem(slot, self.pieces))
            target = self.last_room.at[part, owner]
        line = 2 * part + (1 if back else 0)
        return pltpu.make_async_remote_copy(
            src_ref=source,
            dst_ref=target,
            send_sem=self.far_send.at[line, step],
            recv_sem=self.far_recv.at[line, owner],
            device_id=(grid.task, slot * LOW + grid.low),
            device_id_type=MESH,
        )

    def far_start(self, part, back):
        for step in range(1, self.pieces if back else self.grid.far):
            self.far_copy(part, step, back, False).start()

    def far_settle(self, part, back):
        for step in range(1, self.pieces if back else self.grid.far):
            self.far_copy(part, step, back, True).wait_recv()
            self.far_copy(part, step, back, False).wait_send()

    def keep(self, part):
        bits = self.grid.bits(part)
        mine = self.view(self.grid.core, part, bits[0], bits[1], self.mine, True)
        return pltpu.make_async_copy(self.done.at[part], mine, self.local.at[part])

    def finish(self, index, part):
        grid = self.grid
        bits = grid.bits(part)
        if index == 0:
            if part == 0:
                self.swap(0).wait()
                mine = self.view(grid.core)
                self.add(mine, [mine, self.core_room])
        elif index == 1:
            self.swap(1 + part).wait()
            mine = self.view(grid.core, part, bits[0])
            self.add(mine, [mine, self.first_rooms[part]])
        elif index == 2:
            self.swap(3 + part).wait()
            mine = self.view(grid.core, part, bits[0], bits[1])
            self.add(mine, [mine, self.second_room.at[part]])
        elif index == 3:
            self.far_settle(part, False)
            self.last_room[part, grid.high] = self.view(grid.core, part, bits[0], bits[1], self.mine)[...]
            self.add(self.done.at[part], [self.last_room.at[part, slot] for slot in range(grid.far)])
        elif index == 4:
            self.far_settle(part, True)
            self.keep(part).wait()
        elif index < 7:
            self.swap(2 * index - 5 + part).wait()
        elif part == 0:
            self.swap(9).wait()

    def begin(self, index, part):
        if index == 0 or index == 7:
            if part == 0:
                self.swap(9 if index else 0).start()
        elif index < 3:
            self.swap(2 * index - 1 + part).start()
        elif index == 3:
            self.far_start(part, False)
        elif index == 4:
            self.keep(part).start()
            self.far_start(part, True)
        elif index < 7:
            self.swap(2 * index - 5 + part).start()

    def stage(self, index):
        owner = self.kind == "owner"
        if owner and index == 6:
            return
        before = 5 if owner and index == 7 else index - 1
        first = self.resumed and index == 3
        together = index in (1, 7, 8)
        for part in range(2):
            if before >= 0 and not first:
                self.finish(before, part)
            if not together:
                self.begin(index, part)
        if together:
            for part in range(2):
                self.begin(index, part)


class Grid:
    def __init__(self, batch):
        self.task = lax.axis_index("task")
        place = lax.axis_index("batch")
        self.far = batch // LOW
        self.high = place // LOW
        self.low = lax.rem(place, LOW)
        self.core = lax.rem(place, 2)
        self.y = lax.rem(place // 2, 2)
        base = place - self.low
        self.core_peer = (self.task, base + self.y * 2 + (1 - self.core))
        self.x_peer = (1 - self.task, place)
        self.y_peer = (self.task, base + (1 - self.y) * 2 + self.core)

    def bits(self, part):
        return (self.task, self.y) if part == 0 else (self.y, self.task)

    def peers(self, part):
        return (self.x_peer, self.y_peer) if part == 0 else (self.y_peer, self.x_peer)


class Exchange:
    def __init__(self, tasks, batch, near, far, near_send, near_recv, far_send, far_recv):
        place = lax.axis_index("batch")
        self.task = lax.axis_index("task")
        self.high = place // LOW
        self.low = lax.rem(place, LOW)
        self.near_size = tasks * LOW
        self.far_size = batch // LOW
        self.me_near = self.task * LOW + self.low
        self.near, self.far = near, far
        self.near_sems, self.far_sems = (near_send, near_recv), (far_send, far_recv)

    @staticmethod
    def scratch(tasks, batch, width):
        near_size, far_size = tasks * LOW, batch // LOW
        return [
            pltpu.VMEM((near_size + 1, 2 * width // 128, 128), jnp.float32),
            pltpu.VMEM((far_size + 1, 2 * width // 128, 128), jnp.float32),
            pltpu.SemaphoreType.DMA((near_size,)),
            pltpu.SemaphoreType.DMA((near_size,)),
            pltpu.SemaphoreType.DMA((far_size,)),
            pltpu.SemaphoreType.DMA((far_size,)),
        ]

    def near_peer(self, step):
        slot = lax.rem(self.me_near + step, self.near_size)
        return slot, (slot // LOW, self.high * LOW + lax.rem(slot, LOW))

    def far_peer(self, step):
        slot = lax.rem(self.high + step, self.far_size)
        return slot, (self.task, slot * LOW + self.low)

    def peers(self):
        near = [self.near_peer(step)[1] for step in range(1, self.near_size)]
        return near + [self.far_peer(step)[1] for step in range(1, self.far_size)]

    def greet(self):
        barrier = pltpu.get_barrier_semaphore()
        for device in self.peers():
            pl.semaphore_signal(barrier, inc=1, device_id=device, device_id_type=MESH)

    def met(self):
        pl.semaphore_wait(pltpu.get_barrier_semaphore(), self.near_size + self.far_size - 2)

    def hop(self, size, peer, me, held, sems, filler=None):
        def copy(step, slot):
            return pltpu.make_async_remote_copy(
                src_ref=held.at[size],
                dst_ref=held.at[slot],
                send_sem=sems[0].at[step],
                recv_sem=sems[1].at[slot],
                device_id=peer(step)[1],
                device_id_type=MESH,
            )

        for step in range(1, size):
            copy(step, me).start()
        held[me] = held[size]
        if filler is not None:
            filler()
        for step in range(1, size):
            copy(step, peer(step)[0]).wait_recv()
        for step in range(1, size):
            copy(step, me).wait_send()
        return held.at[pl.ds(0, size)]

    def run(self, total, spread, rows, forward, fillers=(None, None)):
        lines = total.shape[1] // 128
        for line in range(lines):
            cols = slice(line * 128, (line + 1) * 128)
            self.near[self.near_size, line : line + 1] = total[:, cols]
            self.near[self.near_size, lines + line : lines + line + 1] = spread[:, cols]
        held = self.hop(self.near_size, self.near_peer, self.me_near, self.near, self.near_sems, fillers[0])
        total, spread = join(held, float(rows), forward)
        self.far[self.far_size, :lines] = total
        self.far[self.far_size, lines:] = spread
        held = self.hop(self.far_size, self.far_peer, self.high, self.far, self.far_sems, fillers[1])
        total, spread = join(held, float(rows * self.near_size), forward)
        flat = lambda array: jnp.concatenate([array[line : line + 1] for line in range(lines)], axis=1)
        return flat(total), flat(spread)


def join(held, share, forward):
    groups, lines = held.shape[0], held.shape[1] // 2
    total = held[0, :lines]
    spread = held[0, lines:]
    for group in range(1, groups):
        total = total + held[group, :lines]
        spread = spread + held[group, lines:]
    if forward:
        centre = total * (1.0 / (share * groups))
        for group in range(groups):
            away = held[group, :lines] * (1.0 / share) - centre
            spread = spread + share * (away * away)
    return total, spread


def settle_stats(exchange, stat_ref, vec_refs, out_ref, rows, count, forward, fillers=(None, None)):
    first = jnp.sum(stat_ref[:8], axis=0, keepdims=True)
    second = jnp.sum(stat_ref[8:16], axis=0, keepdims=True)
    if forward:
        gain, bias = vec_refs[0][...], vec_refs[1][...]
        out_ref[...] = jnp.zeros_like(out_ref)
        out_ref[2:3] = gain
        out_ref[3:4] = bias
        local = first + rows * stat_ref[16:17]
        total, spread = exchange.run(local, second - first * first * (1.0 / rows), rows, True, fillers)
        scale = lax.rsqrt(spread * (1.0 / count) + EPS)
        out_ref[0:1] = total * (1.0 / count)
        out_ref[1:2] = scale
        out_ref[4:5] = scale * gain
    else:
        out_ref[:8] = vec_refs[0][:8]
        total, spread = exchange.run(first, second, rows, False, fillers)
        out_ref[5:6] = total * (1.0 / count)
        out_ref[6:7] = spread * (1.0 / count)
        out_ref[8:9] = total
        out_ref[9:10] = spread
        out_ref[10:] = jnp.zeros_like(out_ref[10:])


def tail_and_bell(value):
    bell = jnp.exp2(value * value * (-0.5 * LOG2E))
    away = jnp.abs(value)
    ratio = pltpu.reciprocal(1.0 + away * (ERF_P * ROOT_HALF))
    poly = 0.5 * ERF_A[4]
    for factor in ERF_A[3::-1]:
        poly = poly * ratio + 0.5 * factor
    tail = poly * ratio * bell
    return jnp.where(value >= 0, 1.0 - tail, tail), bell


def fold(array):
    total = array[:8]
    for start in range(8, array.shape[0], 8):
        total = total + array[start : start + 8]
    return total


def crown_kernel(
    piece, h_ref, x_ref, thr_ref, cot_hbm, cot_one, cot_two, top_ref, top_one, top_two, vec_ref,
    out_ref, flow_ref, normed_ref, grad_ref, rest_ref, came_ref, stat_ref, z_ref, acc_ref, sent_ref, sems,
    cots_ref, cots_peer_ref, top_peer_ref, local_sems, late_sems, twice_ref,
):
    step = pl.program_id(0)
    rows, width = x_ref.shape
    all_rows, half = cots_ref.shape
    split = all_rows // 4
    task = lax.axis_index("task")
    last = pl.num_programs(0) - 1

    def send(index):
        span = pl.ds(pl.multiple_of(index * rows, rows), rows)
        return across(sent_ref.at[span], came_ref.at[span], sems.at[index])

    core = lax.rem(lax.axis_index("batch"), 2)
    high = top_one.shape[0]
    late = across(cot_hbm.at[1 - task, pl.ds(2 * split, 2 * split)], cots_peer_ref.at[pl.ds(2 * split, 2 * split)], late_sems)

    @pl.when(step == 0)
    def _():
        pairs = [
            (cot_hbm.at[task], cots_ref),
            (cot_one, cots_peer_ref.at[pl.ds(0, split)]),
            (cot_two, cots_peer_ref.at[pl.ds(split, split)]),
            (top_one, top_peer_ref.at[pl.ds(pl.multiple_of(core * high, high), high)]),
            (top_two, top_peer_ref.at[pl.ds(pl.multiple_of((1 - core) * high, high), high)]),
        ]
        copies = [pltpu.make_async_copy(a, b, local_sems.at[i]) for i, (a, b) in enumerate(pairs)]
        for copy in copies:
            copy.start()
        for copy in copies:
            copy.wait()

    @pl.when(step == 1)
    def _():
        late.start()

    @pl.when(step == (last + 1) // 2)
    def _():
        late.wait()

    @pl.when(step > 0)
    def _():
        send(step - 1).start()

    span = pl.ds(pl.multiple_of(step * rows, rows), rows)
    cot_ref, cot_peer_ref = cots_ref.at[span], cots_peer_ref.at[span]
    span = pl.ds(0, rows)
    twice_ref[0] = cot_ref[...] * jnp.bfloat16(2.0)
    twice_ref[1] = cot_peer_ref[...] * jnp.bfloat16(2.0)

    @pl.when(step == 0)
    def _():
        stat_ref[...] = jnp.zeros_like(stat_ref)
        acc_ref[...] = jnp.zeros_like(acc_ref)

    for start in range(0, width, piece):
        cols = pl.ds(start, piece)
        g_one = lax.dot_general(twice_ref[0, span], top_ref[cols], COLS_COLS, preferred_element_type=jnp.float32)
        g_one = g_one.astype(jnp.bfloat16).astype(jnp.float32)
        g_two = lax.dot_general(twice_ref[1, span], top_peer_ref[cols], COLS_COLS, preferred_element_type=jnp.float32)
        g_two = g_two.astype(jnp.bfloat16).astype(jnp.float32)
        total = g_one + g_two
        size = jnp.abs(g_one) + jnp.abs(g_two)
        limit = (thr_ref[:, cols] * jnp.bfloat16(2.0)).astype(jnp.float32)
        share = total * pltpu.reciprocal(jnp.maximum(size, 2.0 * FLOOR))
        merged = 0.25 * total + jnp.clip(share + (1.0 - limit), -SOFT, SOFT) * size
        normed = (h_ref[:, cols] - vec_ref[0:1, cols]) * vec_ref[1:2, cols]
        normed_ref[:, cols] = normed.astype(jnp.bfloat16)
        before = normed * vec_ref[2:3, cols] + vec_ref[3:4, cols] + x_ref[:, cols].astype(jnp.float32)
        phi, bell = tail_and_bell(before)
        z_ref[:, cols] = (before * phi).astype(jnp.bfloat16)
        flow = merged * (phi + before * bell * DENSITY)
        flow_ref[:, cols] = flow.astype(flow_ref.dtype)
        stat_ref[:8, cols] += fold(flow)
        stat_ref[8:, cols] += fold(flow * normed)
    out_ref[...] = jnp.dot(z_ref[...], top_ref[...], preferred_element_type=jnp.float32)
    sent_ref[pl.ds(pl.multiple_of(step * rows, rows), rows)] = jnp.dot(
        z_ref[...], top_peer_ref[...], preferred_element_type=jnp.float32
    ).astype(jnp.bfloat16)
    acc_ref[:half] += lax.dot_general(cot_ref[...], z_ref[...], ROWS_ROWS, preferred_element_type=jnp.float32)
    acc_ref[half:] += lax.dot_general(cot_peer_ref[...], z_ref[...], ROWS_ROWS, preferred_element_type=jnp.float32)

    @pl.when(step == last)
    def _():
        rest_ref[...] = sent_ref[pl.ds(last * rows, rows)]

    def after():
        lax.fori_loop(0, last, lambda index, carry: (send(index).wait(), carry)[1], 0)

    return after


def crown_fill(*refs):
    used, given, own = refs[:10], refs[10:16], refs[17:]
    grad_ref, acc_ref = given[3], own[1]
    half = acc_ref.shape[0] // 2
    task = lax.axis_index("task")

    def part(index):
        def run():
            place = pl.multiple_of((task if index == 0 else 1 - task) * half, half)

            def one(i, carry):
                cols = pl.ds(pl.multiple_of(i * half, half), half)
                turned = acc_ref[pl.ds(index * half, half), cols].T
                grad_ref[cols, pl.ds(place, half)] = turned.astype(jnp.bfloat16)
                return carry

            lax.fori_loop(0, acc_ref.shape[1] // half, one, 0)

        return run

    return part(0), part(1)


def wide(mask, width):
    return jnp.concatenate([mask] * (width // mask.shape[1]), axis=1)


def edges(cuts_ref, canvas):
    shape = (SIDE * SIDE, 128)
    pixel = lax.broadcasted_iota(jnp.int32, shape, 0)
    row, col = pixel // SIDE, lax.rem(pixel, SIDE)
    down, right = cuts_ref[canvas, 0], cuts_ref[canvas, 1]
    one, zero = jnp.ones(shape, jnp.float32), jnp.zeros(shape, jnp.float32)
    within = lambda place, rim, cut: jnp.where((place != rim) & (place != cut), one, zero)
    return (
        within(col, 0, right), within(col, SIDE - 1, right - 1), within(row, 0, down), within(row, SIDE - 1, down - 1),
    )


def edges_of(cuts_ref, step, rows):
    count = rows // (SIDE * SIDE)
    parts = [edges(cuts_ref, step * count + index) for index in range(count)]
    return [jnp.concatenate([part[side] for part in parts], axis=0) for side in range(4)]


def gather_stats(stat_ref, hidden, first):
    @pl.when(False if first is None else first)
    def _():
        stat_ref[:16] = jnp.zeros_like(stat_ref[:16])
        mean = jnp.sum(hidden, axis=0, keepdims=True) / hidden.shape[0]
        stat_ref[16:] = jnp.broadcast_to(mean, stat_ref[16:].shape)

    away = hidden - stat_ref[16:17]
    stat_ref[:8] += fold(away)
    stat_ref[8:16] += fold(away * away)


def normal(hidden, vec_ref):
    return (hidden - vec_ref[0:1]) * vec_ref[1:2]


def squeeze_kernel(x_ref, w_ref, out_ref, stat_ref):
    hidden = jnp.dot(x_ref[...], w_ref[...], preferred_element_type=jnp.float32)
    out_ref[...] = hidden
    gather_stats(stat_ref, hidden, pl.program_id(0) == 0)


def mesh_kernel(h_ref, vec_ref, cuts_ref, w_ref, out_ref, side_ref, stat_ref, pad_ref):
    rows, mid = h_ref.shape
    inner = pl.ds(SIDE, rows)
    before = normal(h_ref[...], vec_ref) * vec_ref[2:3] + vec_ref[3:4]
    phi, _ = tail_and_bell(before)
    low = (before * phi).astype(jnp.bfloat16)
    kept = low.astype(jnp.float32)
    left, right, above, below = edges_of(cuts_ref, pl.program_id(0), rows)
    left, right = wide(left, mid), wide(right, mid)

    @pl.when(pl.program_id(0) == 0)
    def _():
        pad_ref[:SIDE] = jnp.zeros_like(pad_ref[:SIDE])
        pad_ref[SIDE + rows :] = jnp.zeros_like(pad_ref[:SIDE])

    pad_ref[inner, :mid] = (pltpu.roll(kept, 1, 0) * left).astype(jnp.bfloat16)
    pad_ref[inner, mid : 2 * mid] = low
    pad_ref[inner, 2 * mid :] = (pltpu.roll(kept, rows - 1, 0) * right).astype(jnp.bfloat16)
    side_ref[...] = pad_ref[inner].T
    above = wide(above.astype(jnp.bfloat16), 3 * mid)
    below = wide(below.astype(jnp.bfloat16), 3 * mid)
    hidden = jnp.dot(pad_ref[inner], w_ref[3 * mid : 6 * mid], preferred_element_type=jnp.float32)
    hidden += jnp.dot(pad_ref[:rows] * above, w_ref[: 3 * mid], preferred_element_type=jnp.float32)
    hidden += jnp.dot(pad_ref[2 * SIDE :] * below, w_ref[6 * mid :], preferred_element_type=jnp.float32)
    out_ref[...] = hidden
    gather_stats(stat_ref, hidden, pl.program_id(0) == 0)


def widen_kernel(h_ref, vec_ref, w_ref, out_ref, low_ref, stat_ref):
    rows = h_ref.shape[0]
    spans = [pl.ds(start, rows // 2) for start in (0, rows // 2)]
    lows = []
    for span in spans:
        before = normal(h_ref[span], vec_ref) * vec_ref[2:3] + vec_ref[3:4]
        phi, _ = tail_and_bell(before)
        low = (before * phi).astype(jnp.bfloat16)
        low_ref[:, span] = low.T
        lows.append(low)
    for index, span in enumerate(spans):
        hidden = jnp.dot(lows[index], w_ref[...], preferred_element_type=jnp.float32)
        out_ref[span] = hidden
        gather_stats(stat_ref, hidden, (pl.program_id(0) == 0) if index == 0 else None)


def norm_grad(upstream, normed, vec_ref):
    return vec_ref[4:5] * (upstream - vec_ref[5:6] - normed * vec_ref[6:7])


def act_slope(value):
    phi, bell = tail_and_bell(value)
    return phi + value * bell * DENSITY


def gather_flow(stat_ref, flow, normed, first):
    @pl.when(first)
    def _():
        stat_ref[...] = jnp.zeros_like(stat_ref)

    stat_ref[:8] += fold(flow)
    stat_ref[8:16] += fold(flow * normed)


def narrow_kernel(flow_ref, normed_ref, vec_ref, two_ref, vectwo_ref, low_ref, w_ref, out_ref, grad_ref, stat_ref, dh_ref):
    step = pl.program_id(0)
    rows = flow_ref.shape[0]
    dh = norm_grad(flow_ref[...].astype(jnp.float32), normed_ref[...].astype(jnp.float32), vec_ref)
    low = dh.astype(jnp.bfloat16)
    dh_ref[pl.ds(pl.multiple_of(step * rows, rows), rows)] = low
    dq = lax.dot_general(low, w_ref[...], COLS_COLS, preferred_element_type=jnp.float32)
    normed = normal(two_ref[...], vectwo_ref)
    flow = dq * act_slope(normed * vectwo_ref[2:3] + vectwo_ref[3:4])
    out_ref[...] = flow
    gather_flow(stat_ref, flow, normed, step == 0)


def narrow_fill(flow_ref, normed_ref, vec_ref, two_ref, vectwo_ref, low_ref, w_ref, out_ref, grad_ref, stat_ref, dh_ref):
    half = dh_ref.shape[1] // 2

    def part(index):
        def run():
            def one(i, carry):
                cols = pl.ds(pl.multiple_of(index * half + i * 512, 512), 512)
                grad_ref[:, cols] = jnp.dot(
                    low_ref[...], dh_ref[:, cols], preferred_element_type=jnp.float32
                ).astype(jnp.bfloat16)
                return carry

            lax.fori_loop(0, half // 512, one, 0)

        return run

    return part(0), part(1)


def across(source, target, sems, hop="task"):
    task = lax.axis_index("task")
    place = lax.axis_index("batch")
    device = (1 - task, place) if hop == "task" else (task, place + 1 - 2 * lax.rem(place, 2))
    return pltpu.make_async_remote_copy(
        src_ref=source,
        dst_ref=target,
        send_sem=sems.at[0],
        recv_sem=sems.at[1],
        device_id=device,
        device_id_type=MESH,
    )


def tiled(kernel, tile, moving, flags, outs, fixed, scratch, name, stats=None, sends=(), far=(), fill=None, turns=(), aside=None):
    tasks = lax.axis_size("task")
    batch = lax.axis_size("batch")
    rows = moving[0].shape[0]

    def block(array):
        return pl.BlockSpec((tile,) + array.shape[1:], lambda i: (i,) + (0,) * (len(array.shape) - 1))

    def turned(array):
        return pl.BlockSpec((array.shape[0], tile), lambda i: (0, i))

    def whole(array):
        zeros = (0,) * len(array.shape)
        return pl.BlockSpec(array.shape, lambda i: zeros)

    hbm = pl.BlockSpec(memory_space=pl.ANY)
    operands = list(moving)
    in_specs = [(whole, block, lambda a: hbm, lambda a: pl.BlockSpec(memory_space=pltpu.SMEM))[m](a) for a, m in zip(moving, flags)]
    out_shape = outs + fixed + list(far)
    out_specs = [turned(a) if i in turns else block(a) for i, a in enumerate(outs)] + [whole(a) for a in fixed] + [hbm for a in far]
    scratch = list(scratch)
    params = dict(vmem_limit_bytes=VMEM_BYTES)
    ins, made, held = len(operands), len(out_shape), len(scratch)
    run = kernel
    if stats is not None:
        vecs, forward, ident = stats
        width = vecs[0].shape[1]
        params.update(collective_id=ident, has_side_effects=True)
        operands += vecs
        in_specs += [whole(vec) for vec in vecs]
        out_shape = out_shape + [shape32(16, width)]
        out_specs = out_specs + [whole(out_shape[-1])]
        scratch = scratch + [pltpu.VMEM((24 if forward else 16, width), jnp.float32)]
        scratch = scratch + Exchange.scratch(tasks, batch, width)
        for array, _, shape, _ in sends:
            operands.append(array)
            in_specs.append(hbm)
            out_shape = out_shape + [jax.ShapeDtypeStruct(shape, array.dtype)]
            out_specs = out_specs + [hbm]
            scratch = scratch + [pltpu.SemaphoreType.DMA((2,))]

        if aside is not None:
            operands.append(aside[0])
            in_specs.append(hbm)
            out_shape = out_shape + list(aside[1])
            out_specs = out_specs + [hbm for _ in aside[1]]
            scratch = scratch + list(aside[2])

        def run(*refs):
            refs = list(refs)
            take = lambda n: [refs.pop(0) for _ in range(n)]
            used = take(ins)
            vec_refs = take(len(vecs))
            sources = take(len(sends))
            own_in = take(0 if aside is None else 1)
            given = take(made)
            out_ref = take(1)[0]
            targets = take(len(sends))
            own_out = take(0 if aside is None else len(aside[1]))
            own = take(held)
            stat_ref = take(1)[0]
            exchange = Exchange(tasks, batch, *take(6))
            step = pl.program_id(0)
            last = pl.num_programs(0) - 1

            @pl.when(step == 0)
            def _():
                exchange.greet()

            early = len(sends) > 0 or len(far) > 0

            def crossing(index):
                _, view, _, hop = sends[index]
                return across(view(sources[index]), targets[index], cross_sems[index], hop)

            cross_sems = take(len(sends))
            if early and aside is None:

                @pl.when(step == 1)
                def _():
                    exchange.met()
                    for index in range(len(sends)):
                        crossing(index).start()

            if aside is not None:
                helper = aside[3](exchange, *own_in, *own_out, *refs)
                helper.before(step)

            after = kernel(*used, *given, stat_ref, *own)
            if aside is not None:
                helper.after(step)

                @pl.when(step == 1)
                def _():
                    for index in range(len(sends)):
                        crossing(index).start()

            @pl.when(step == last)
            def _():
                if not early and aside is None:
                    exchange.met()
                fillers = (None, None) if fill is None else fill(*used, *given, stat_ref, *own)
                settle_stats(exchange, stat_ref, vec_refs, out_ref, rows, rows * tasks * batch, forward, fillers)
                for index in range(len(sends)):
                    crossing(index).wait()
                if after is not None:
                    after()
                if aside is not None:
                    helper.end()

    return pl.pallas_call(
        run,
        grid=(rows // tile,),
        out_shape=out_shape,
        in_specs=in_specs,
        out_specs=out_specs,
        scratch_shapes=scratch,
        compiler_params=pltpu.CompilerParams(**params),
        name=name,
    )(*operands)


def shape32(*shape):
    return jax.ShapeDtypeStruct(shape, jnp.float32)


def shape16(*shape):
    return jax.ShapeDtypeStruct(shape, jnp.bfloat16)


def squeeze(flat_in, w_reduce, stats, tile):
    rows, mid = flat_in.shape[0], w_reduce.shape[1]
    return tiled(squeeze_kernel, tile, [flat_in, w_reduce], [1, 0], [shape32(rows, mid)], [], [], "squeeze", stats)


def mesh_forward(h_one, vec, cuts, taps, stats, sends, tile):
    rows, mid = h_one.shape
    return tiled(
        mesh_kernel, tile, [h_one, vec, cuts, taps], [1, 0, 3, 0],
        [shape32(rows, mid), shape16(3 * mid, rows)], [],
        [pltpu.VMEM((tile + 2 * SIDE, 3 * mid), jnp.bfloat16)], "mesh_forward", stats, sends, turns=(1,),
    )


def widen(h_two, vec, w_expand, stats, sends, tile):
    rows, mid = h_two.shape
    width = w_expand.shape[1]
    return tiled(
        widen_kernel, tile, [h_two, vec, w_expand], [1, 0, 0],
        [shape32(rows, width), shape16(mid, rows)], [], [], "widen", stats, sends, turns=(1,),
    )


class HeadsAside:
    def __init__(self, batch, shape, last, exchange, source, target, work, *room):
        self.exchange, self.work, self.target, self.last = exchange, work, target, last
        self.sum = Reduction(Grid(batch), work, None, *room[:11], "owner")
        self.load = pltpu.make_async_copy(source, work, room[11].at[0])
        self.sems = room[11]

    def before(self, step):
        @pl.when(step == 0)
        def _():
            self.load.start()

    def out(self, part):
        grid = self.sum.grid
        bits = grid.bits(part)
        view = self.sum.view(grid.core, part, bits[0], bits[1])
        return pltpu.make_async_copy(view, self.target.at[part], self.sems.at[1 + part])

    def after(self, step):
        @pl.when(step == 0)
        def _():
            self.exchange.met()
            self.load.wait()
            self.sum.stage(0)

        @pl.when(step == 1)
        def _():
            self.sum.stage(1)

        @pl.when(step == max(self.last - 2, 1))
        def _():
            self.sum.stage(2)

    def end(self):
        for part in range(2):
            self.sum.finish(2, part)
            self.out(part).start()
        for part in range(2):
            self.out(part).wait()


def narrow(flow, normed, vec_three, h_two, vec_two, q_two, w_expand, heads, rest, stats, tile):
    rows, mid = h_two.shape
    width = w_expand.shape[1]
    batch = lax.axis_size("batch")
    high, across_ = heads.shape
    scratch = [pltpu.VMEM(heads.shape, jnp.bfloat16)] + Reduction.scratch(high, across_, "owner", batch // LOW)
    scratch += [pltpu.SemaphoreType.DMA((3,))]
    helper = functools.partial(HeadsAside, batch, heads.shape, rows // tile - 1)
    return tiled(
        narrow_kernel, tile, [flow, normed, vec_three, h_two, vec_two, q_two, w_expand], [1, 1, 0, 1, 0, 0, 0],
        [shape32(rows, mid)], [shape16(mid, width)], [pltpu.VMEM((rows, width), jnp.bfloat16)], "narrow", stats,
        [(rest, lambda ref: ref, rest.shape, "task")], fill=narrow_fill, aside=(heads, [shape16(2, high // 8, across_ // 2)], scratch, helper),
    )


def crown(h_three, flat_in, limits, cots, cot_parts, top, top_parts, vec, stats, tile, piece):
    rows, width = flat_in.shape
    half = cots.shape[2]
    return tiled(
        functools.partial(crown_kernel, piece), tile,
        [h_three, flat_in, limits, cots, *cot_parts, top, *top_parts, vec], [1, 1, 1, 2, 2, 2, 0, 2, 2, 0],
        [shape32(rows, half), shape16(rows, width), shape16(rows, width)], [shape16(width, 2 * half), shape16(tile, half)],
        [
            pltpu.VMEM((tile, width), jnp.bfloat16),
            pltpu.VMEM((2 * half, width), jnp.float32),
            pltpu.VMEM((rows, half), jnp.bfloat16),
            pltpu.SemaphoreType.DMA((rows // tile, 2)),
            pltpu.VMEM((rows, half), jnp.bfloat16),
            pltpu.VMEM((rows, half), jnp.bfloat16),
            pltpu.VMEM((width, half), jnp.bfloat16),
            pltpu.SemaphoreType.DMA((5,)),
            pltpu.SemaphoreType.DMA((2,)),
            pltpu.VMEM((2, tile, half), jnp.bfloat16),
        ],
        "crown", stats, (), [shape16(rows, half)], crown_fill,
    )


class Stream:
    def __init__(self, view, held, sems):
        self.view, self.held, self.sems = view, held, sems

    def copy(self, index):
        slot = lax.rem(index, 2)
        return pltpu.make_async_copy(self.view(index), self.held.at[slot], self.sems.at[slot])

    def start(self, index):
        self.copy(index).start()

    def take(self, index, count):
        self.copy(index).wait()

        @pl.when(index + 1 < count)
        def _():
            self.start(index + 1)

        return self.held.at[lax.rem(index, 2)]


def back_kernel(rows, tasks, batch, tile, *refs):
    refs = list(refs)

    def take(count):
        return [refs.pop(0) for _ in range(count)]

    (flow_hbm, two_hbm, one_hbm, side_hbm, w_hbm, x_hbm, heads_hbm, expand_hbm) = take(8)
    vectwo_ref, vecone_ref, cuts_ref = take(3)
    (out_hbm, heads_out, expand_out, spatial_out, reduce_out, vec_ref) = take(6)
    (two_buf, x_buf) = take(2)
    (side_ref, lane_ref, flow_ref, w_ref) = take(4)
    heads_work, expand_work, spatial_work, reduce_work, total_ref, stat_ref = take(6)
    pair_sems, whole_sems, flow_sems = take(3)
    exchange = Exchange(tasks, batch, *take(6))
    grid = Grid(batch)
    mid = flow_hbm.shape[1]
    width = x_hbm.shape[1]
    spans = rows // tile

    def blocks(ref, height):
        return lambda index: ref.at[pl.ds(pl.multiple_of(index * height, height), height)]

    exchange.greet()

    def flow_load(index):
        return pltpu.make_async_copy(
            blocks(flow_hbm, tile)(index), blocks(flow_ref, tile)(index), flow_sems.at[index]
        )

    twos = Stream(blocks(two_hbm, tile), two_buf, pair_sems.at[1])
    ones = Stream(blocks(one_hbm, tile), two_buf, pair_sems.at[3])
    dh_ref, normed_ref, dht_ref = lane_ref.at[:, :mid], lane_ref.at[:, mid : 2 * mid], side_ref.at[:mid]
    across_cols = x_buf.shape[2]
    columns = Stream(
        lambda index: x_hbm.at[:, pl.ds(pl.multiple_of(index * across_cols, across_cols), across_cols)],
        x_buf, pair_sems.at[0],
    )
    loads = [
        pltpu.make_async_copy(source, target, whole_sems.at[index])
        for index, (source, target) in enumerate(
            [(heads_hbm, heads_work), (side_hbm, side_ref), (expand_hbm, expand_work), (w_hbm, w_ref)]
        )
    ]
    heads_load, side_load, expand_load, w_load = loads
    keep = pltpu.make_async_copy(dh_ref, out_hbm, whole_sems.at[4])
    heads_load.start()
    flow_load(0).start()
    twos.start(0)
    expand_load.start()
    for index in range(1, spans):
        flow_load(index).start()
    side_load.start()
    w_load.start()

    third = spatial_work.shape[0] // 3
    works = [(heads_work, heads_out, "owner"), (expand_work, expand_out, "wide")]
    for index in range(3):
        span = pl.ds(index * third, third)
        works.append((spatial_work.at[span], spatial_out.at[span], "tall"))
    for index in range(2):
        span = pl.ds(index * width // 2, width // 2)
        works.append((reduce_work.at[span], total_ref.at[span], "tall"))
    reductions = []
    for work, out, kind in works:
        shape = heads_out.shape if kind == "owner" else None
        reductions.append(Reduction(grid, work, out, *take(11), kind, shape))

    def tick(name):
        for item, stage in AGENDA.get(name, ()):
            reductions[item].stage(stage)

    def ticks(name, index, count, scale=1, shift=0):
        for step in range(count):
            label = "%s%d" % (name, step * scale + shift)
            if label in AGENDA:

                @pl.when(index == step)
                def _():
                    tick(label)

    def lanes(index, carry):
        span = pl.ds(pl.multiple_of(index * tile, tile), tile)
        flow_load(index).wait()
        flow = flow_ref[span]
        normed = normal(twos.take(index, spans)[...], vectwo_ref)
        dh = norm_grad(flow, normed, vectwo_ref)
        _, _, above, below = edges_of(cuts_ref, index, tile)
        above, below = wide(above, mid), wide(below, mid)
        low = jnp.bfloat16
        zero = jnp.zeros((SIDE, mid), low)
        lane_ref[span, mid : 2 * mid] = dh.astype(low)
        lane_ref[span, :mid] = jnp.concatenate([(dh * above)[SIDE:].astype(low), zero], axis=0)
        lane_ref[span, 2 * mid :] = jnp.concatenate([zero, (dh * below)[: tile - SIDE].astype(low)], axis=0)

        @pl.when(index == 0)
        def _():
            expand_load.wait()

        ticks("lane", index, 4)
        return carry

    exchange.met()
    heads_load.wait()
    tick("start")
    lax.fori_loop(0, spans, lanes, 0)
    ones.start(0)
    side_load.wait()

    def spatial(index, carry):
        a, b = index // 3, lax.rem(index, 3)
        rows_here = pl.ds(pl.multiple_of(b * mid, mid), mid)
        cols = pl.ds(pl.multiple_of(a * mid, mid), mid)
        part = jnp.dot(side_ref[rows_here], lane_ref[:, cols], preferred_element_type=jnp.float32)
        spatial_work[pl.ds(pl.multiple_of(index * mid, mid), mid)] = part.astype(jnp.bfloat16)
        ticks("sp", index, 9)
        return carry

    lax.fori_loop(0, 9, spatial, 0)
    w_load.wait()

    def taps(index, carry):
        span = pl.ds(pl.multiple_of(index * tile, tile), tile)
        pieces = []
        for b in range(3):
            total = None
            for a in range(3):
                part = lax.dot_general(
                    lane_ref[span, a * mid : (a + 1) * mid], w_ref[3 * a + b], COLS_COLS,
                    preferred_element_type=jnp.float32,
                )
                total = part if total is None else total + part
            pieces.append(total)
            if b < 2:
                ticks("tap", index, 4, 3, b)
        left, right, _, _ = edges_of(cuts_ref, index, tile)
        left, right = wide(left, mid), wide(right, mid)
        dq = pieces[1] + pltpu.roll(pieces[0] * left, tile - 1, 0) + pltpu.roll(pieces[2] * right, 1, 0)
        normed = normal(ones.take(index, spans)[...], vecone_ref)
        flow = dq * act_slope(normed * vecone_ref[2:3] + vecone_ref[3:4])
        flow_ref[span] = flow
        normed_ref[span] = normed.astype(jnp.bfloat16)
        gather_flow(stat_ref, flow, normed, index == 0)
        ticks("tap", index, 4, 3, 2)
        return carry

    lax.fori_loop(0, spans, taps, 0)
    columns.start(0)
    settle_stats(
        exchange, stat_ref, [vecone_ref], vec_ref, rows, rows * tasks * batch, False,
        (lambda: tick("xa"), lambda: tick("xb")),
    )
    tick("xch")

    def inner(index, carry):
        span = pl.ds(pl.multiple_of(index * tile, tile), tile)
        dh = norm_grad(flow_ref[span], normed_ref[span].astype(jnp.float32), vec_ref)
        low = dh.astype(jnp.bfloat16)
        dh_ref[span] = low
        dht_ref[:, span] = low.T
        return carry

    lax.fori_loop(0, spans, inner, 0)
    keep.start()
    tick("inner")
    count = width // across_cols

    def reduce(index, carry):
        part = jnp.dot(dht_ref[...], columns.take(index, count)[...], preferred_element_type=jnp.float32)
        span = pl.ds(pl.multiple_of(index * across_cols, across_cols), across_cols)
        reduce_work[span] = part.T.astype(jnp.bfloat16)
        ticks("red", index, 4)
        return carry

    lax.fori_loop(0, count, reduce, 0)
    keep.wait()
    tick("tail")
    store = pltpu.make_async_copy(total_ref, reduce_out, whole_sems.at[0])
    store.start()
    store.wait()


def back(flow, h_two, vec_two, h_one, vec_one, sides, cuts, w_spatial, flat_in, heads, expand, heads_shape, ident, tile):
    tasks = lax.axis_size("task")
    batch = lax.axis_size("batch")
    far = batch // LOW
    rows, mid = h_one.shape
    width = flat_in.shape[1]
    full, low = jnp.float32, jnp.bfloat16
    cols = 512
    hbm = pl.BlockSpec(memory_space=pl.ANY)
    vmem = pl.BlockSpec(memory_space=pltpu.VMEM)
    shapes = [(heads_shape, "owner"), (expand.shape, "wide")] + [((3 * mid, mid), "tall")] * 3
    shapes += [((width // 2, mid), "tall")] * 2
    scratch = [
        pltpu.VMEM((2, tile, mid), full),
        pltpu.VMEM((2, rows, cols), low),
        pltpu.VMEM((3 * mid, rows), low),
        pltpu.VMEM((rows, 3 * mid), low),
        pltpu.VMEM((rows, mid), full),
        pltpu.VMEM(w_spatial.shape, low),
        pltpu.VMEM(heads.shape, low),
        pltpu.VMEM(expand.shape, low),
        pltpu.VMEM((9 * mid, mid), low),
        pltpu.VMEM((width, mid), low),
        pltpu.VMEM((width, mid), low),
        pltpu.VMEM((16, mid), full),
        pltpu.SemaphoreType.DMA((4, 2)),
        pltpu.SemaphoreType.DMA((5,)),
        pltpu.SemaphoreType.DMA((rows // tile,)),
    ] + Exchange.scratch(tasks, batch, mid)
    for (high, across_), kind in shapes:
        scratch += Reduction.scratch(high, across_, kind, far, kind == "owner")
    return pl.pallas_call(
        functools.partial(back_kernel, rows, tasks, batch, tile),
        out_shape=[
            shape16(rows, mid), shape16(*heads_shape), shape16(*expand.shape), shape16(9 * mid, mid),
            shape16(width, mid), shape32(16, mid),
        ],
        in_specs=[hbm] * 8 + [vmem] * 2 + [pl.BlockSpec(memory_space=pltpu.SMEM)],
        out_specs=[hbm] * 5 + [vmem],
        scratch_shapes=scratch,
        compiler_params=pltpu.CompilerParams(
            vmem_limit_bytes=VMEM_BYTES, collective_id=ident, has_side_effects=True
        ),
        name="back",
    )(flow, h_two, h_one, sides, w_spatial, flat_in, heads, expand, vec_two, vec_one, cuts)


def finish_kernel(
    dh_ref, up_ref, heads_ref, expand_ref, spatial_ref, reduce_ref, mine_ref, came_ref, rest_ref, w_ref, one_ref, two_ref, three_ref,
    out_ref, heads_out, expand_out, spatial_out, reduce_out, both_ref, *sums,
):
    full = jnp.float32
    task = lax.axis_index("task")
    half = heads_out.shape[1]
    back = lax.dot_general(dh_ref[...], w_ref[...], COLS_COLS, preferred_element_type=full)
    out_ref[...] = (up_ref[...].astype(full) + back).astype(jnp.bfloat16)
    heads_out[...] = jnp.where(task == 0, heads_ref[:, :half], heads_ref[:, half:]).astype(full)
    expand_out[...] = expand_ref[...].astype(full)
    spatial_out[...] = spatial_ref[...].astype(full)
    reduce_out[...] = reduce_ref[...].astype(full)
    both_ref[task] = mine_ref[...]
    both_ref[1 - task] = came_ref[...].astype(full)

    @pl.when(pl.program_id(0) == pl.num_programs(0) - 1)
    def _():
        height = rest_ref.shape[0]
        both_ref[1 - task, both_ref.shape[1] - height :] = rest_ref[...].astype(full)


    @pl.when(pl.program_id(0) == 0)
    def _():
        for index, vec_ref in enumerate((one_ref, two_ref, three_ref)):
            sums[2 * index][...] = vec_ref[9:10]
            sums[2 * index + 1][...] = vec_ref[8:9]


def finish(dh, up, heads, expand, spatial, reduce, mine, came, rest, w_reduce, vecs, steps):

    def block(array, lead=0):
        zeros = (0,) * (len(array.shape) - 1 - lead)
        height = array.shape[lead] // steps
        return pl.BlockSpec(array.shape[:lead] + (height,) + array.shape[lead + 1 :], lambda i: (0,) * lead + (i,) + zeros)

    def whole(array):
        return pl.BlockSpec(array.shape, lambda i: (0, 0))

    rows, half = mine.shape
    moving = [dh, up, heads, expand, spatial, reduce, mine, came]
    fixed = [rest, w_reduce, *vecs]
    outs = [shape16(*up.shape), shape32(heads.shape[0], half), shape32(*expand.shape), shape32(*spatial.shape), shape32(*reduce.shape)]
    both = shape32(2, rows, half)
    sums = [shape32(1, vec.shape[1]) for vec in vecs for _ in range(2)]
    return pl.pallas_call(
        finish_kernel,
        grid=(steps,),
        out_shape=outs + [both] + sums,
        in_specs=[block(a) for a in moving] + [whole(a) for a in fixed],
        out_specs=[block(a) for a in outs] + [block(both, 1)] + [whole(a) for a in sums],
        compiler_params=pltpu.CompilerParams(vmem_limit_bytes=VMEM_BYTES),
        name="finish",
    )(*moving, *fixed)


def body(
    inputs,
    crop_cuts,
    threshold,
    w_reduce,
    w_spatial,
    w_expand,
    w_heads,
    gain_one,
    bias_one,
    gain_two,
    bias_two,
    gain_three,
    bias_three,
    cotangent,
):
    canvases, pixels, width = inputs.shape[1:]
    mid = w_reduce.shape[1]
    rows = canvases * pixels
    half = w_heads.shape[2]
    cots = cotangent.reshape(2, rows, half)
    top_mine = w_heads[0]

    def params(gain, bias):
        return [gain.reshape(1, -1), bias.reshape(1, -1)]

    cuts = crop_cuts.reshape(canvases, 2)
    flat_in = inputs.reshape(rows, width)
    core = lambda: lax.rem(lax.axis_index("batch"), 2)
    other = lambda: 1 - lax.axis_index("task")
    quarter = rows // 4
    top_rows = width // 2
    h_one, vec_one = squeeze(flat_in, w_reduce, (params(gain_one, bias_one), True, 0), min(rows, 512))
    sends = [
        (top_mine, lambda ref: ref.at[pl.ds(pl.multiple_of(core() * top_rows, top_rows), top_rows)], (top_rows, half), "task"),
        (cots, lambda ref: ref.at[other(), pl.ds(0, quarter)], (quarter, half), "task"),
    ]
    h_two, sides, vec_two, top_one, cot_one = mesh_forward(
        h_one, vec_one, cuts, w_spatial.reshape(9 * mid, mid), (params(gain_two, bias_two), True, 1), sends, pixels
    )
    sends = [
        (top_one, lambda ref: ref, (top_rows, half), "core"),
        (cots, lambda ref: ref.at[other(), pl.ds(quarter, quarter)], (quarter, half), "task"),
    ]
    h_three, q_two, vec_three, top_two, cot_two = widen(
        h_two, vec_two, w_expand, (params(gain_three, bias_three), True, 2), sends, min(rows, 2 * pixels)
    )
    out_mine, flow, normed, grad_heads, rest, out_peer, vec_three = crown(
        h_three, flat_in, threshold.reshape(rows, width), cots, (cot_one, cot_two), top_mine, (top_one, top_two), vec_three,
        ([vec_three], False, 3), pixels, 256,
    )
    heads_shape = grad_heads.shape
    flow_two, grad_expand, vec_two, rest, grad_heads = narrow(
        flow, normed, vec_three, h_two, vec_two, q_two, w_expand, grad_heads, rest, ([vec_two], False, 4), pixels
    )
    dh_one, grad_heads, grad_expand, grad_spatial, grad_reduce, vec_one = back(
        flow_two, h_two, vec_two, h_one, vec_one, sides, cuts, w_spatial, flat_in, grad_heads, grad_expand, heads_shape, 5,
        min(rows, 512),
    )
    grad_inputs, grad_heads, grad_expand, grad_spatial, grad_reduce, head_out, *sums = finish(
        dh_one, flow, grad_heads, grad_expand, grad_spatial, grad_reduce, out_mine, out_peer, rest, w_reduce,
        (vec_one, vec_two, vec_three), 2,
    )
    return (
        head_out.reshape(1, 2, canvases, pixels, half),
        grad_inputs.reshape(inputs.shape),
        grad_reduce,
        grad_spatial.reshape(w_spatial.shape),
        grad_expand,
        grad_heads[None],
        *[row.reshape(-1) for row in sums],
    )


def solution(mesh):
    in_specs = (
        P("task", "batch", None, None),
        P("task", "batch", None),
        P("task", "batch", None, None),
        P(),
        P(),
        P(),
        P("task", None, None),
        P(),
        P(),
        P(),
        P(),
        P(),
        P(),
        P("task", None, "batch", None, None),
    )
    out_specs = (
        P("task", None, "batch", None, None),
        P("task", "batch", None, None),
        P(),
        P(),
        P(),
        P("task", None, None),
        P(),
        P(),
        P(),
        P(),
        P(),
        P(),
    )
    return jax.shard_map(body, mesh=mesh, in_specs=in_specs, out_specs=out_specs, check_vma=False)
```
